32 devices in a mesh: batch: 4 (over y, x), frame: 8 (over z, core).
Axes of the slice: x: 2, y: 2, z: 4, core: 2. Of those that a mesh axis runs over, the one named last changes fastest.
Arguments:
- pixels: bfloat16 [4, 8, 400, 1536], P('batch', 'frame'), may hold values from -6 to 6
- res_class: int32 [4], P('batch'), may hold values from 0 to 2
- valid_tubelet_count: int32 [4], replicated, may hold values from 6 to 8
- positive: int32 [4], P('batch'), may hold values from 0 to 3, as said below
- negatives: int32 [4, 4], P('batch'), may hold values from 0 to 3, as said below
- master: float32 [9253632], P(('batch', 'frame'))
- first_moment: float32 [9253632], P(('batch', 'frame')), may hold values from -2.670288e-05 to 2.670288e-05
- second_moment: float32 [9253632], P(('batch', 'frame')), may hold values from 2.7016418e-13 to 1.0806567e-12
- adam_step: int32 [1], replicated, may hold values from 2 to 20
Outputs:
- new_master: float32 [9253632], P(('batch', 'frame'))
- new_first: float32 [9253632], P(('batch', 'frame'))
- new_second: float32 [9253632], P(('batch', 'frame'))
- master_low: bfloat16 [9253632], P(('batch', 'frame'))
- loss: float32 [], replicated
- grad_norm: float32 [], replicated
The draws below stay inside these ranges and needn't reach their ends.
Inputs may be any that keep to these rules, and one draw needn't show every extreme that they name: `res_class`: class 0, 1, 2 gives 100, 196, 400 patches a tubelet. `valid_tubelet_count`: a clip's valid tubelets are its first ones. `positive`: never the clip itself. `negatives`: never the clip itself; repeats may occur.
All inputs are finite; a program needn't handle non-finite values.
Results may differ from the reference program's by a relative error of at most 0.0092.
Values may be sent and summed in bfloat16 or wider, within the bound.
A program may use at most 384 MiB of HBM per device.

```python
import math
import jax
import jax.numpy as jnp
from jax import lax

HEAD_COUNT = 12
HEAD_FEATURES = 64
FFW = 3072
TUBELET_PIXELS = 1536
EMB = 512
NMAP = 8
P0 = 100
P1 = 196
PATCHES_THIRD_2 = 400
TMAX = 64
NVEC = 13
NNEG = 4
TS = 8
CLIPS = 4
NPARAM = 9253632


def master_piece(key_one, dims_of, spread):
    return jax.random.normal(key_one, dims_of, jnp.float32) * spread


def draw_pixels(key, part):
    pattern_key = jax.random.fold_in(key, 11)
    chosen_key = jax.random.fold_in(key, 13)
    noise_key = jax.random.fold_in(key, 17)
    pattern_table = jax.random.normal(pattern_key, (64, TUBELET_PIXELS), jnp.float32)
    chosen_rows = jax.random.randint(chosen_key, (CLIPS, TS, PATCHES_THIRD_2), 0, 64, dtype=jnp.int32)
    noise_part = jax.random.normal(noise_key, (CLIPS, TS, PATCHES_THIRD_2, TUBELET_PIXELS), jnp.float32)
    return jnp.clip(1.5 * pattern_table[chosen_rows] + noise_part, -6.0, 6.0).astype(jnp.bfloat16)


def draw_master(key, part):
    width_of_model = HEAD_COUNT * HEAD_FEATURES
    key_list = jax.random.split(key, 11)
    pieces = [master_piece(key_list[0], (TUBELET_PIXELS * width_of_model,), TUBELET_PIXELS ** (-0.5)), master_piece(key_list[1], (3 * width_of_model * width_of_model,), width_of_model ** (-0.5)), master_piece(key_list[2], (width_of_model * width_of_model,), 3.0 * width_of_model ** (-0.5)), master_piece(key_list[3], (width_of_model * FFW,), width_of_model ** (-0.5)), master_piece(key_list[4], (FFW * width_of_model,), 1.5 * FFW ** (-0.5)), master_piece(key_list[5], (width_of_model * EMB,), width_of_model ** (-0.5)), master_piece(key_list[6], (width_of_model * NMAP,), 2.0 * width_of_model ** (-0.5)), master_piece(key_list[7], ((P0 + P1 + PATCHES_THIRD_2) * width_of_model,), 0.2), master_piece(key_list[8], (TMAX * width_of_model,), 0.2)]
    row_ids = jnp.arange(NVEC)
    gain_rows = ((row_ids < 8) & (row_ids % 2 == 0)).astype(jnp.float32)
    vector_rows = master_piece(key_list[9], (NVEC, width_of_model), 0.1) + gain_rows[:, None]
    pieces.append(vector_rows.reshape(NVEC * width_of_model))
    pieces.append(master_piece(key_list[10], (FFW,), 0.1))
    return jnp.concatenate(pieces)


def draw_positive(key, part):
    clip_ids = jnp.arange(CLIPS, dtype=jnp.int32)
    jump_by = jax.random.randint(jax.random.fold_in(key, 3), (CLIPS,), 1, CLIPS, dtype=jnp.int32)
    return (clip_ids + jump_by) % CLIPS


def draw_negatives(key, part):
    clip_ids = jnp.arange(CLIPS, dtype=jnp.int32)
    jump_by = jax.random.randint(jax.random.fold_in(key, 7), (CLIPS, NNEG), 1, CLIPS, dtype=jnp.int32)
    return (clip_ids[:, None] + jump_by) % CLIPS


def with_ends(entries, rng, low, high):
    longest = entries.shape.index(max(entries.shape))
    spots = []
    for shift in (0, 1):
        where = [jax.random.randint(jax.random.fold_in(rng, axis), (), 0, length) for axis, length in enumerate(entries.shape)]
        where[longest] = (where[longest] + shift) % entries.shape[longest]
        spots.append(tuple(where))
    return entries.at[spots[0]].set(low).at[spots[1]].set(high)


def level_of(key, dims, shards, least, largest):
    factor_of, own = 1.0, jax.random.fold_in(key, 6)
    for axis_at, blocks in shards:
        draws = jnp.exp(jax.random.uniform(jax.random.fold_in(own, axis_at), (blocks,), jnp.float32, least / len(shards), largest / len(shards)))
        factor_of = factor_of * jnp.repeat(draws, dims[axis_at] // blocks).reshape([-1 if axis == axis_at else 1 for axis in range(len(dims))])
    return factor_of


def gaussian(key, extent, width, bound, cuts=(), kind=jnp.bfloat16):
    array = width * jax.random.normal(key, extent, jnp.float32)
    if cuts:
        array = array * level_of(key, extent, cuts, -0.22, 0.18)
    return jnp.clip(array, -bound, bound).astype(kind)


def setup_inputs(seed: int = 0) -> dict:
    arg_keys = jax.random.split(jax.random.key(seed), 10)
    pixels = draw_pixels(jax.random.fold_in(arg_keys[9], 71), 0)
    res_class = with_ends(jax.random.randint(arg_keys[1], (CLIPS,), 0, 3), jax.random.fold_in(arg_keys[1], 1), 0, 2).astype(jnp.int32)
    valid_tubelet_count = with_ends(jax.random.randint(arg_keys[2], (CLIPS,), 3 * TS // 4, TS + 1), jax.random.fold_in(arg_keys[2], 1), 3 * TS // 4, TS).astype(jnp.int32)
    positive = draw_positive(jax.random.fold_in(arg_keys[9], 71), 0)
    negatives = draw_negatives(jax.random.fold_in(arg_keys[9], 71), 0)
    master = draw_master(jax.random.fold_in(arg_keys[9], 71), 0)
    first_moment = gaussian(arg_keys[6], (NPARAM,), (0.0055 / NPARAM ** 0.5), 2.6702880859375e-05, ((0, 32),), jnp.float32)
    second_moment = jnp.clip(jnp.exp(math.log(1.0806567229612596e-12) - 1.3862944 * jax.random.uniform(arg_keys[7], (NPARAM,), jnp.float32) ** level_of(arg_keys[7], (NPARAM,), ((0, 32),), -0.2, 0.2)), 2.701641807403149e-13, 1.0806567229612596e-12)
    adam_step = jax.random.randint(arg_keys[8], (1,), 2, 21).astype(jnp.int32)
    return {"pixels": pixels, "res_class": res_class, "valid_tubelet_count": valid_tubelet_count, "positive": positive, "negatives": negatives, "master": master, "first_moment": first_moment, "second_moment": second_moment, "adam_step": adam_step}


@jax.custom_vjp
def low(v):
    return lax.optimization_barrier(v.astype(jnp.bfloat16)).astype(jnp.float32)

@jax.custom_vjp
def low_back(v):
    return v

def low_keep(v):
    return (low(v), None)

def low_pass(kept, grad):
    return (grad,)

def back_keep(v):
    return (v, None)

def back_low(kept, grad):
    return (low(grad),)
low.defvjp(low_keep, low_pass)
low_back.defvjp(back_keep, back_low)
EPSILON = 1e-05
SOFTMAX_TEMPER = 0.02
DECAY_PENALTY = 1.0
CLIP_AT = 0.05
RATE = 0.03
DECAY = 0.05
BETA_ONE = 0.9
BETA_TWO = 0.999
ADAM_EPS = 1e-08
HIGH_ACCURACY = lax.Precision.HIGHEST

def matmul_hi(left, right):
    return jnp.dot(left, right, precision=HIGH_ACCURACY, preferred_element_type=jnp.float32)

def unpack_flat(flat_vector):
    width_of_model = HEAD_COUNT * HEAD_FEATURES
    dims_list = [(TUBELET_PIXELS, width_of_model), (width_of_model, 3 * width_of_model), (width_of_model, width_of_model), (width_of_model, FFW), (FFW, width_of_model), (width_of_model, EMB), (width_of_model, NMAP), (P0 + P1 + PATCHES_THIRD_2, width_of_model), (TMAX, width_of_model), (NVEC, width_of_model), (FFW,)]
    pieces = []
    offset = 0
    for dims_of in dims_list:
        length = math.prod(dims_of)
        pieces.append(flat_vector[offset:offset + length].reshape(dims_of))
        offset += length
    return pieces

def layer_norm(inputs, gain_row, shift_row):
    center = inputs - lax.optimization_barrier(jnp.mean(inputs, -1, keepdims=True))
    return center * lax.rsqrt(lax.optimization_barrier(jnp.mean(center * center, -1, keepdims=True)) + EPSILON) * gain_row + shift_row

def attend_block(query_block, head_keys, head_values, key_valid):
    scores = low_back(jnp.einsum('hqd,hkd->hqk', query_block, head_keys, precision=HIGH_ACCURACY) * HEAD_FEATURES ** (-0.5))
    scores = jnp.where(key_valid[None, None, :], scores, -1e+30)
    weights = jax.nn.softmax(scores, axis=-1)
    return jnp.einsum('hqk,hkd->hqd', low(weights), head_values, precision=HIGH_ACCURACY)

def clip_forward(param_list, pixel_clip, resolution, tubelet_stack):
    w_embed, w_qkv, w_out, w_up, w_down, w_proj, w_map, pos_space, pos_time, vectors, bias_up = param_list
    width_of_model = HEAD_COUNT * HEAD_FEATURES
    seq_len = TS * PATCHES_THIRD_2
    patches = jnp.where(resolution == 0, P0, jnp.where(resolution == 1, P1, PATCHES_THIRD_2)).astype(jnp.int32)
    start_row = jnp.where(resolution == 0, 0, jnp.where(resolution == 1, P0, P0 + P1)).astype(jnp.int32)
    patch_pos = lax.dynamic_slice_in_dim(pos_space, start_row, PATCHES_THIRD_2, 0)
    valid_patch = jnp.arange(PATCHES_THIRD_2, dtype=jnp.int32) < patches
    valid_slot = jnp.arange(TS, dtype=jnp.int32) < tubelet_stack
    key_valid = (valid_slot[:, None] & valid_patch[None, :]).reshape(seq_len)
    embedded = low_back(matmul_hi(pixel_clip.reshape(seq_len, TUBELET_PIXELS), w_embed))
    first_in = (embedded.reshape(TS, PATCHES_THIRD_2, width_of_model) + vectors[8] + patch_pos[None] + pos_time[:TS, None]).reshape(seq_len, width_of_model)
    normed_one = low(layer_norm(first_in, vectors[0], vectors[1]))
    zero_row = jnp.zeros_like(vectors[9])
    projection_output = matmul_hi(normed_one, w_qkv) + jnp.concatenate([vectors[9], zero_row, vectors[10]])
    projection_output = low(low_back(projection_output))
    heads_all = projection_output.reshape(seq_len, 3, HEAD_COUNT, HEAD_FEATURES).transpose(1, 2, 0, 3)
    blocks = TS // 2
    query_blocks = heads_all[0].reshape(HEAD_COUNT, blocks, 2 * PATCHES_THIRD_2, HEAD_FEATURES).transpose(1, 0, 2, 3)
    attend_saved = jax.checkpoint(attend_block)
    attended = lax.map(lambda query_block: attend_saved(query_block, heads_all[1], heads_all[2], key_valid), query_blocks)
    attended = attended.transpose(0, 2, 1, 3).reshape(seq_len, width_of_model)
    attended = low(low_back(attended))
    second_in = first_in + low_back(matmul_hi(attended, w_out) + vectors[11])
    normed_two = low(layer_norm(second_in, vectors[2], vectors[3]))
    hidden_pre = low_back(matmul_hi(normed_two, w_up) + bias_up)
    hidden_act = low(jax.nn.gelu(hidden_pre, approximate=False))
    block_out = second_in + low_back(matmul_hi(hidden_act, w_down) + vectors[12])
    frames_out = block_out.reshape(TS, PATCHES_THIRD_2, width_of_model)
    map_logits = jnp.einsum('tpd,dm->tpm', layer_norm(frames_out, vectors[4], vectors[5]), w_map, precision=HIGH_ACCURACY)
    map_logits = jnp.where(valid_patch[None, :, None], map_logits, -1e+30)
    token_maps = jax.nn.softmax(map_logits, axis=1)
    slot_weight = valid_slot.astype(jnp.float32)
    pooled = jnp.einsum('t,tpm,tpd->d', slot_weight, token_maps, frames_out, precision=HIGH_ACCURACY) / (NMAP * tubelet_stack).astype(jnp.float32)
    gram_matrix = jnp.einsum('tpm,tpn->tmn', token_maps, token_maps, precision=HIGH_ACCURACY)
    correlation = jnp.sum(slot_weight * (lax.optimization_barrier(jnp.sum(gram_matrix, axis=(1, 2))) - jnp.trace(gram_matrix, axis1=1, axis2=2)))
    final_norm = layer_norm(pooled, vectors[6], vectors[7])
    embedding = matmul_hi(final_norm[None], w_proj)[0]
    return (embedding * lax.rsqrt(jnp.sum(embedding * embedding) + 1e-06), correlation)

def total_loss(master_full, pixels_full, res_class, valid_tubelet_count, positive, negatives):
    param_list = unpack_flat(low(master_full))

    def one_clip(inputs):
        return clip_forward(param_list, inputs[0], inputs[1], inputs[2])
    normalized_embedding, correlations = lax.map(one_clip, (pixels_full, res_class, valid_tubelet_count))
    selected_rows = jnp.concatenate([positive[:, None], negatives], axis=1)
    similarity_matrix = jnp.einsum('yg,yeg->ye', normalized_embedding, normalized_embedding[selected_rows], precision=HIGH_ACCURACY) / SOFTMAX_TEMPER
    contrast = jnp.mean(jax.nn.logsumexp(similarity_matrix, axis=1) - similarity_matrix[:, 0])
    return contrast + DECAY_PENALTY * jnp.sum(correlations) / jnp.sum(valid_tubelet_count).astype(jnp.float32)

def reference(pixels, res_class, valid_tubelet_count, positive, negatives, master, first_moment, second_moment, adam_step):
    pixels_full = pixels.astype(jnp.float32)
    loss_value, pullback = jax.vjp(lambda master_full: total_loss(master_full, pixels_full, res_class, valid_tubelet_count, positive, negatives), master)
    gradient, = pullback(jnp.ones_like(loss_value))
    grad_norm = jnp.sqrt(jnp.sum(gradient * gradient))
    clipped = gradient * jnp.minimum(1.0, CLIP_AT / grad_norm)
    new_first = BETA_ONE * first_moment + (1.0 - BETA_ONE) * clipped
    new_second = BETA_TWO * second_moment + (1.0 - BETA_TWO) * clipped * clipped
    step_count = adam_step[0].astype(jnp.float32)
    update = new_first / (1.0 - BETA_ONE ** step_count) / (jnp.sqrt(new_second / (1.0 - BETA_TWO ** step_count)) + ADAM_EPS)
    new_master = master - RATE * (update + DECAY * master)
    return (new_master, new_first, new_second, new_master.astype(jnp.bfloat16), loss_value, grad_norm)
```

```python
from functools import partial
import math

import jax
import jax.numpy as jnp
from jax import lax
from jax.experimental import pallas as pl
from jax.experimental.pallas import tpu as pltpu
from jax.sharding import PartitionSpec as P

HEAD_COUNT = 12
HEAD_FEATURES = 64
FFW = 3072
TUBELET_PIXELS = 1536
EMB = 512
NMAP = 8
P0 = 100
P1 = 196
PATCHES_THIRD_2 = 400
TMAX = 64
NVEC = 13
CLIPS_PER_BATCH = 1


EPSILON = 1e-05
SOFTMAX_TEMPER = 0.02
DECAY_PENALTY = 1.0
CLIP_AT = 0.05
RATE = 0.03
DECAY = 0.05
BETA_ONE = 0.9
BETA_TWO = 0.999
ADAM_EPS = 1e-08
HIGH_ACCURACY = lax.Precision.HIGHEST


def to_bfloat(values):
    return values.astype(jnp.bfloat16)


def unpack_flat(flat_vector):
    width_of_model = HEAD_COUNT * HEAD_FEATURES
    dims_list = [
        (TUBELET_PIXELS, width_of_model),
        (width_of_model, 3 * width_of_model),
        (width_of_model, width_of_model),
        (width_of_model, FFW),
        (FFW, width_of_model),
        (width_of_model, EMB),
        (width_of_model, NMAP),
        (P0 + P1 + PATCHES_THIRD_2, width_of_model),
        (TMAX, width_of_model),
        (NVEC, width_of_model),
        (FFW,),
    ]
    pieces = []
    offset = 0
    for dims_of in dims_list:
        length = math.prod(dims_of)
        pieces.append(flat_vector[offset : offset + length].reshape(dims_of))
        offset += length
    return pieces


def norm_forward(inputs, gain_row, shift_row):
    center = inputs - jnp.mean(inputs, -1, keepdims=True)
    inverse = lax.rsqrt(jnp.mean(center * center, -1, keepdims=True) + EPSILON)
    normed = center * inverse
    return (normed * gain_row + shift_row, (normed, inverse))


def norm_backward(grad_out, gain_row, saved_parts):
    normed, inverse = saved_parts
    scaled = grad_out * gain_row
    grad_in = inverse * (
        scaled
        - jnp.mean(scaled, -1, keepdims=True)
        - normed * jnp.mean(scaled * normed, -1, keepdims=True)
    )
    lead_axes = tuple(range(grad_out.ndim - 1))
    return (grad_in, jnp.sum(grad_out * normed, lead_axes), jnp.sum(grad_out, lead_axes))


def block_plan(total_rows):
    shards = total_rows // PATCHES_THIRD_2
    group_size = 4
    return (shards // group_size, group_size * PATCHES_THIRD_2)


def local_any_mesh(
    pixels,
    res_class,
    valid_tubelet_count,
    positive,
    negatives,
    master,
    first_moment,
    second_moment,
    adam_step,
):
    width_of_model = HEAD_COUNT * HEAD_FEATURES
    score_scale = HEAD_FEATURES ** (-0.5)
    every_clip_rows = CLIPS_PER_BATCH * lax.axis_size("batch")
    index_of_batch = lax.axis_index("batch")
    frame_index = lax.axis_index("frame")
    gathered = lax.all_gather(to_bfloat(master), ("batch", "frame"), axis=0, tiled=True)
    w_embed, w_qkv, w_out, w_up, w_down, w_proj, w_map, pos_space, pos_time, vectors, bias_up = (
        unpack_flat(gathered)
    )
    vec_f = vectors.astype(jnp.float32)
    tubelet_stack = lax.dynamic_slice_in_dim(
        valid_tubelet_count, index_of_batch * CLIPS_PER_BATCH, CLIPS_PER_BATCH, 0
    )
    patches = jnp.where(res_class == 0, P0, jnp.where(res_class == 1, P1, PATCHES_THIRD_2)).astype(
        jnp.int32
    )
    start_rows = jnp.where(res_class == 0, 0, jnp.where(res_class == 1, P0, P0 + P1)).astype(
        jnp.int32
    )
    patch_pos = jnp.stack(
        [lax.dynamic_slice_in_dim(pos_space, start_rows[0], PATCHES_THIRD_2, 0)]
    ).astype(jnp.float32)
    time_row = lax.dynamic_slice_in_dim(pos_time, frame_index, 1, 0).astype(jnp.float32)
    rows_of_pixels = pixels.reshape(CLIPS_PER_BATCH * PATCHES_THIRD_2, TUBELET_PIXELS)
    embedded = jnp.dot(rows_of_pixels, w_embed, preferred_element_type=jnp.float32).reshape(
        CLIPS_PER_BATCH, PATCHES_THIRD_2, width_of_model
    )
    first_in = embedded + vec_f[8] + patch_pos + time_row
    normed_one, saved_one = norm_forward(first_in, vec_f[0], vec_f[1])
    normed_one = to_bfloat(normed_one)
    qkv_bias = jnp.concatenate([vec_f[9], jnp.zeros_like(vec_f[9]), vec_f[10]])
    projection_output = to_bfloat(
        jnp.einsum("cpd,de->cpe", normed_one, w_qkv, preferred_element_type=jnp.float32) + qkv_bias
    )
    query_matrix = projection_output[..., :width_of_model].reshape(
        CLIPS_PER_BATCH, PATCHES_THIRD_2, HEAD_COUNT, HEAD_FEATURES
    )
    kv_local = projection_output[..., width_of_model:]

    def key_mask(row_start, count_of_rows):
        row_ids = row_start + jnp.arange(count_of_rows, dtype=jnp.int32)
        return ((row_ids // PATCHES_THIRD_2)[None, :] < tubelet_stack[:, None]) & (
            (row_ids % PATCHES_THIRD_2)[None, :] < patches[:, None]
        )

    def block_scores(key_value_block, block_start):
        count_of_rows = key_value_block.shape[1]
        head_keys = key_value_block[..., :width_of_model].reshape(
            CLIPS_PER_BATCH, count_of_rows, HEAD_COUNT, HEAD_FEATURES
        )
        head_values = key_value_block[..., width_of_model:].reshape(
            CLIPS_PER_BATCH, count_of_rows, HEAD_COUNT, HEAD_FEATURES
        )
        key_ok = key_mask(block_start, count_of_rows)[:, None, None, :]
        scores = (
            jnp.einsum(
                "cqhd,ckhd->chqk", query_matrix, head_keys, preferred_element_type=jnp.float32
            )
            * score_scale
        )
        return (jnp.where(key_ok, scores, -1e30), key_ok, head_keys, head_values)

    forward_init = (
        jnp.full((CLIPS_PER_BATCH, HEAD_COUNT, PATCHES_THIRD_2), -1e30, jnp.float32),
        jnp.zeros((CLIPS_PER_BATCH, HEAD_COUNT, PATCHES_THIRD_2), jnp.float32),
        jnp.zeros((CLIPS_PER_BATCH, HEAD_COUNT, PATCHES_THIRD_2, HEAD_FEATURES), jnp.float32),
    )
    kv_piece = lax.all_gather(kv_local, "frame", axis=1, tiled=True)
    count_blocks, block_rows = block_plan(kv_piece.shape[1])

    def forward_one_block(block_index, running):
        run_max, run_sum, run_acc = running
        block_start = block_index * block_rows
        key_value_block = lax.dynamic_slice_in_dim(
            kv_piece, block_index * block_rows, block_rows, 1
        )
        scores, key_ok, head_keys, head_values = block_scores(key_value_block, block_start)
        new_max = jnp.maximum(run_max, jnp.max(scores, -1))
        factor = jnp.exp(run_max - new_max)
        prob_tile = jnp.where(key_ok, jnp.exp(scores - new_max[..., None]), 0.0)
        run_acc = run_acc * factor[..., None] + jnp.einsum(
            "chqk,ckhd->chqd", to_bfloat(prob_tile), head_values, preferred_element_type=jnp.float32
        )
        return (new_max, run_sum * factor + jnp.sum(prob_tile, -1), run_acc)

    run_max, run_sum, run_acc = lax.fori_loop(0, count_blocks, forward_one_block, forward_init)
    log_sum = run_max + jnp.log(run_sum)
    head_attended_rows = run_acc / run_sum[..., None]
    attended_reduced = to_bfloat(
        head_attended_rows.transpose(0, 2, 1, 3).reshape(
            CLIPS_PER_BATCH, PATCHES_THIRD_2, width_of_model
        )
    )
    second_in = (
        first_in
        + jnp.einsum("cpe,ed->cpd", attended_reduced, w_out, preferred_element_type=jnp.float32)
        + vec_f[11]
    )
    normed_two, saved_two = norm_forward(second_in, vec_f[2], vec_f[3])
    normed_two = to_bfloat(normed_two)
    hidden_pre = jnp.einsum(
        "cpd,df->cpf", normed_two, w_up, preferred_element_type=jnp.float32
    ) + bias_up.astype(jnp.float32)
    hidden_act, gelu_pull = jax.vjp(partial(jax.nn.gelu, approximate=False), hidden_pre)
    hidden_low = to_bfloat(hidden_act)
    block_out = (
        second_in
        + jnp.einsum("cpf,fd->cpd", hidden_low, w_down, preferred_element_type=jnp.float32)
        + vec_f[12]
    )
    valid_patch = jnp.arange(PATCHES_THIRD_2, dtype=jnp.int32)[None, :] < patches[:, None]
    slot_weight = (frame_index < tubelet_stack).astype(jnp.float32)

    def learner(block_in, gain_row, shift_row, map_weight):
        normed, unused = norm_forward(block_in, gain_row, shift_row)
        logits = jnp.einsum("cpd,dm->cpm", normed, map_weight, precision=HIGH_ACCURACY)
        logits = jnp.where(valid_patch[..., None], logits, -1e30)
        token_maps = jax.nn.softmax(logits, axis=1)
        pooled_part = jnp.einsum(
            "c,cpm,cpd->cd", slot_weight, token_maps, block_in, precision=HIGH_ACCURACY
        )
        gram_matrix = jnp.einsum("cpm,cpn->cmn", token_maps, token_maps, precision=HIGH_ACCURACY)
        correlation_part = slot_weight * (
            jnp.sum(gram_matrix, axis=(1, 2)) - jnp.trace(gram_matrix, axis1=1, axis2=2)
        )
        return (pooled_part, correlation_part)

    (pooled_part, correlation_part), learner_pull = jax.vjp(
        learner, block_out, vec_f[4], vec_f[5], w_map.astype(jnp.float32)
    )
    pooled_sum, correlation_sum = lax.psum((pooled_part, correlation_part), "frame")

    def head_map(pooled_in, gain_row, shift_row, proj_weight):
        pooled_mean = pooled_in / (NMAP * tubelet_stack).astype(jnp.float32)[:, None]
        normed, unused = norm_forward(pooled_mean, gain_row, shift_row)
        embedding = jnp.dot(
            normed, proj_weight, precision=HIGH_ACCURACY, preferred_element_type=jnp.float32
        )
        return embedding * lax.rsqrt(jnp.sum(embedding * embedding, -1, keepdims=True) + 1e-06)

    normalized_embedding, head_pull = jax.vjp(
        head_map, pooled_sum, vec_f[6], vec_f[7], w_proj.astype(jnp.float32)
    )
    embed_all, correlation_all = (
        lax.all_gather(normalized_embedding, "batch", axis=0, tiled=True),
        lax.all_gather(correlation_sum, "batch", axis=0, tiled=True),
    )
    selected_rows = jnp.concatenate([positive[:, None], negatives], axis=1)

    def contrast(embedding_input):
        local_row_set = lax.dynamic_slice_in_dim(
            embedding_input, index_of_batch * CLIPS_PER_BATCH, CLIPS_PER_BATCH, 0
        )
        similarity_matrix = (
            jnp.einsum(
                "yg,yeg->ye", local_row_set, embedding_input[selected_rows], precision=HIGH_ACCURACY
            )
            / SOFTMAX_TEMPER
        )
        return (
            jnp.sum(jax.nn.logsumexp(similarity_matrix, axis=1) - similarity_matrix[:, 0])
            / every_clip_rows
        )

    contrast_part, contrast_pull = jax.vjp(contrast, embed_all)
    (grad_embed_all,) = contrast_pull(jnp.ones_like(contrast_part))
    grad_unit = lax.psum_scatter(grad_embed_all, "batch", scatter_dimension=0, tiled=True)
    frame_total_count = jnp.sum(valid_tubelet_count).astype(jnp.float32)
    head_mask = (frame_index == 0).astype(jnp.float32)
    pooled_gradient, grad_final_gain, grad_final_shift, grad_proj = head_pull(grad_unit)
    grad_block, grad_learn_gain, grad_learn_shift, grad_map = learner_pull(
        (
            pooled_gradient,
            jnp.full((CLIPS_PER_BATCH,), DECAY_PENALTY / frame_total_count, jnp.float32),
        )
    )
    grad_mlp = to_bfloat(grad_block)
    grad_down_bias = jnp.sum(grad_mlp.astype(jnp.float32), (0, 1))
    grad_w_down = jnp.einsum(
        "cpf,cpd->fd", hidden_low, grad_mlp, preferred_element_type=jnp.float32
    )
    grad_hidden = jnp.einsum("cpd,fd->cpf", grad_mlp, w_down, preferred_element_type=jnp.float32)
    (grad_pre,) = gelu_pull(grad_hidden)
    grad_pre_low = to_bfloat(grad_pre)
    grad_up_bias = jnp.sum(grad_pre_low.astype(jnp.float32), (0, 1))
    grad_w_up = jnp.einsum(
        "cpd,cpf->df", normed_two, grad_pre_low, preferred_element_type=jnp.float32
    )
    grad_normed_two = jnp.einsum(
        "cpf,df->cpd", grad_pre_low, w_up, preferred_element_type=jnp.float32
    )
    grad_in_two, grad_gain_two, grad_shift_two = norm_backward(grad_normed_two, vec_f[2], saved_two)
    grad_second = grad_block + grad_in_two
    grad_attn = to_bfloat(grad_second)
    grad_out_bias = jnp.sum(grad_attn.astype(jnp.float32), (0, 1))
    grad_w_out = jnp.einsum(
        "cpe,cpd->ed", attended_reduced, grad_attn, preferred_element_type=jnp.float32
    )
    grad_attended = to_bfloat(
        jnp.einsum("cpd,ed->cpe", grad_attn, w_out, preferred_element_type=jnp.float32)
    ).reshape(CLIPS_PER_BATCH, PATCHES_THIRD_2, HEAD_COUNT, HEAD_FEATURES)
    row_delta = jnp.einsum("cqhd,chqd->chq", grad_attended.astype(jnp.float32), head_attended_rows)
    zeroed_query = jnp.zeros(
        (CLIPS_PER_BATCH, PATCHES_THIRD_2, HEAD_COUNT, HEAD_FEATURES), jnp.float32
    )
    query_kv_piece = lax.all_gather(kv_local, "frame", axis=1, tiled=True)
    count_blocks, query_block_rows = block_plan(query_kv_piece.shape[1])

    def query_one_block(block_index, query_gradient):
        block_start = block_index * query_block_rows
        key_value_block = lax.dynamic_slice_in_dim(
            query_kv_piece, block_index * query_block_rows, query_block_rows, 1
        )
        scores, key_ok, head_keys, head_values = block_scores(key_value_block, block_start)
        prob_tile = jnp.where(key_ok, jnp.exp(scores - log_sum[..., None]), 0.0)
        grad_prob = jnp.einsum(
            "cqhd,ckhd->chqk", grad_attended, head_values, preferred_element_type=jnp.float32
        )
        grad_score = to_bfloat(prob_tile * (grad_prob - row_delta[..., None]))
        return (
            query_gradient
            + jnp.einsum(
                "chqk,ckhd->cqhd", grad_score, head_keys, preferred_element_type=jnp.float32
            )
            * score_scale
        )

    query_gradient = lax.fori_loop(0, count_blocks, query_one_block, zeroed_query)
    own_keys = kv_local[..., :width_of_model].reshape(
        CLIPS_PER_BATCH, PATCHES_THIRD_2, HEAD_COUNT, HEAD_FEATURES
    )
    own_values = kv_local[..., width_of_model:].reshape(
        CLIPS_PER_BATCH, PATCHES_THIRD_2, HEAD_COUNT, HEAD_FEATURES
    )
    own_ok = key_mask(frame_index * PATCHES_THIRD_2, PATCHES_THIRD_2)[:, None, None, :]
    row_pieces = (
        query_matrix.astype(jnp.float32),
        grad_attended.astype(jnp.float32),
        log_sum.transpose(0, 2, 1),
        row_delta.transpose(0, 2, 1),
    )
    query_piece = lax.all_gather(
        row_pieces[0].astype(jnp.bfloat16), "frame", axis=1, tiled=True
    ).astype(jnp.float32)
    grad_out_piece = lax.all_gather(
        row_pieces[1].astype(jnp.bfloat16), "frame", axis=1, tiled=True
    ).astype(jnp.float32)
    lse_piece = lax.all_gather(
        row_pieces[2].astype(jnp.bfloat16), "frame", axis=1, tiled=True
    ).astype(jnp.float32)
    delta_piece = lax.all_gather(
        row_pieces[3].astype(jnp.bfloat16), "frame", axis=1, tiled=True
    ).astype(jnp.float32)
    count_blocks, own_block_rows = block_plan(query_piece.shape[1])

    def own_one_block(block_index, running):
        key_gradient, value_gradient = running
        offset = block_index * own_block_rows
        query_block = to_bfloat(lax.dynamic_slice_in_dim(query_piece, offset, own_block_rows, 1))
        grad_out_block = to_bfloat(
            lax.dynamic_slice_in_dim(grad_out_piece, offset, own_block_rows, 1)
        )
        lse_block = lax.dynamic_slice_in_dim(lse_piece, offset, own_block_rows, 1).transpose(
            0, 2, 1
        )
        delta_block = lax.dynamic_slice_in_dim(delta_piece, offset, own_block_rows, 1).transpose(
            0, 2, 1
        )
        scores = (
            jnp.einsum("cqhd,ckhd->chqk", query_block, own_keys, preferred_element_type=jnp.float32)
            * score_scale
        )
        scores = jnp.where(own_ok, scores, -1e30)
        prob_tile = jnp.where(own_ok, jnp.exp(scores - lse_block[..., None]), 0.0)
        grad_prob = jnp.einsum(
            "cqhd,ckhd->chqk", grad_out_block, own_values, preferred_element_type=jnp.float32
        )
        grad_score = to_bfloat(prob_tile * (grad_prob - delta_block[..., None]))
        key_gradient = (
            key_gradient
            + jnp.einsum(
                "chqk,cqhd->ckhd", grad_score, query_block, preferred_element_type=jnp.float32
            )
            * score_scale
        )
        value_gradient = value_gradient + jnp.einsum(
            "chqk,cqhd->ckhd",
            to_bfloat(prob_tile),
            grad_out_block,
            preferred_element_type=jnp.float32,
        )
        return (key_gradient, value_gradient)

    grad_key_own, grad_value_own = lax.fori_loop(
        0, count_blocks, own_one_block, (zeroed_query, zeroed_query)
    )
    gradient_key_value_local = to_bfloat(
        jnp.concatenate(
            [
                grad_key_own.reshape(CLIPS_PER_BATCH, PATCHES_THIRD_2, width_of_model),
                grad_value_own.reshape(CLIPS_PER_BATCH, PATCHES_THIRD_2, width_of_model),
            ],
            -1,
        )
    )
    gradient_query_key_value = jnp.concatenate(
        [
            to_bfloat(query_gradient).reshape(CLIPS_PER_BATCH, PATCHES_THIRD_2, width_of_model),
            gradient_key_value_local,
        ],
        -1,
    )
    grad_query_bias = jnp.sum(
        gradient_query_key_value[..., :width_of_model].astype(jnp.float32), (0, 1)
    )
    grad_value_bias = jnp.sum(
        gradient_query_key_value[..., 2 * width_of_model :].astype(jnp.float32), (0, 1)
    )
    grad_w_qkv = jnp.einsum(
        "cpd,cpe->de", normed_one, gradient_query_key_value, preferred_element_type=jnp.float32
    )
    grad_normed_one = jnp.einsum(
        "cpe,de->cpd", gradient_query_key_value, w_qkv, preferred_element_type=jnp.float32
    )
    grad_in_one, grad_gain_one, grad_shift_one = norm_backward(grad_normed_one, vec_f[0], saved_one)
    gradient_entry = grad_second + grad_in_one
    gradient_entry_low = to_bfloat(gradient_entry).reshape(
        CLIPS_PER_BATCH * PATCHES_THIRD_2, width_of_model
    )
    grad_w_embed = jnp.einsum(
        "rt,rd->td", rows_of_pixels, gradient_entry_low, preferred_element_type=jnp.float32
    )
    grad_embed_bias = jnp.sum(gradient_entry, (0, 1))
    grad_pos_space = jnp.zeros((P0 + P1 + PATCHES_THIRD_2, width_of_model), jnp.float32)
    current = lax.dynamic_slice_in_dim(grad_pos_space, start_rows[0], PATCHES_THIRD_2, 0)
    grad_pos_space = lax.dynamic_update_slice_in_dim(
        grad_pos_space, current + gradient_entry[0], start_rows[0], 0
    )
    grad_pos_time = lax.dynamic_update_slice_in_dim(
        jnp.zeros((TMAX, width_of_model), jnp.float32), grad_embed_bias[None], frame_index, 0
    )
    grad_vectors = jnp.stack(
        [
            grad_gain_one,
            grad_shift_one,
            grad_gain_two,
            grad_shift_two,
            grad_learn_gain,
            grad_learn_shift,
            grad_final_gain * head_mask,
            grad_final_shift * head_mask,
            grad_embed_bias,
            grad_query_bias,
            grad_value_bias,
            grad_out_bias,
            grad_down_bias,
        ]
    )
    flat_grad = jnp.concatenate(
        [
            piece_grad.reshape(-1)
            for piece_grad in (
                grad_w_embed,
                grad_w_qkv,
                grad_w_out,
                grad_w_up,
                grad_w_down,
                grad_proj * head_mask,
                grad_map,
                grad_pos_space,
                grad_pos_time,
                grad_vectors,
                grad_up_bias,
            )
        ]
    )
    grad_shard = lax.psum_scatter(flat_grad, ("batch", "frame"), scatter_dimension=0, tiled=True)
    contrast_keep = jnp.where(frame_index == 0, contrast_part, 0.0)
    square_sum, contrast_total = lax.psum(
        (jnp.sum(grad_shard * grad_shard), contrast_keep), ("batch", "frame")
    )
    grad_norm = jnp.sqrt(square_sum)
    loss_value = contrast_total + DECAY_PENALTY * jnp.sum(correlation_all) / frame_total_count
    clipped = grad_shard * jnp.minimum(1.0, CLIP_AT / grad_norm)
    new_first = BETA_ONE * first_moment + (1.0 - BETA_ONE) * clipped
    new_second = BETA_TWO * second_moment + (1.0 - BETA_TWO) * clipped * clipped
    step_count = adam_step[0].astype(jnp.float32)
    update = (
        new_first
        / (1.0 - BETA_ONE**step_count)
        / (jnp.sqrt(new_second / (1.0 - BETA_TWO**step_count)) + ADAM_EPS)
    )
    new_master = master - RATE * (update + DECAY * master)
    return (new_master, new_first, new_second, to_bfloat(new_master), loss_value, grad_norm)


MESH = pl.DeviceIdType.MESH
T=144
SPA=32

class Sends:
    def __init__(self, sem): self.sem=sem; self.n=0; self.items=[]
    def go(self, src, dst, rsem, dev, pred=None):
        c = pltpu.make_async_remote_copy(src_ref=src, dst_ref=dst, send_sem=self.sem.at[self.n], recv_sem=rsem, device_id=dev, device_id_type=MESH)
        self.n += 1
        if pred is None: c.start()
        else:
            @pl.when(pred)
            def _(): c.start()
        self.items.append((c,pred))
    def drain(self):
        for c,pred in self.items:
            if pred is None: c.wait_send()
            else:
                @pl.when(pred)
                def _(): c.wait_send()

def both(a,b):
    if a is None: return b
    if b is None: return a
    return jnp.logical_and(a,b)

def make_ag(spa=SPA):
    A=(0,spa); A1=(0,spa//2); A2=(spa//2,spa//2)
    nb=T-spa
    B=(spa,nb); B1=(spa,nb//2); B2=(spa+nb//2,nb//2)
    FULL=(0,T)
    def kernel(x_ref, out, ssem, lsem, zB, xB, yB, xBh, yBh, pA, zA, pown, pzB, pxB, pyB, pxBh, pyBh, ppA, pzA):
        b=lax.axis_index("batch"); f=lax.axis_index("frame")
        x=b%2; y=b//2; z=f//2; c=f%2
        bx=y*2+(1-x); by=(1-y)*2+x; bd=(1-y)*2+(1-x)
        X=(bx,f); Y=(by,f); Pn=(b,z*2+(1-c)); UP=(b,f+2); DN=(b,f-2)
        up=z<3; dn=z>0
        bar=pltpu.get_barrier_semaphore()
        for d,p in ((X,None),(Y,None),(Pn,None),(UP,up),(DN,dn)):
            if p is None: pl.semaphore_signal(bar,inc=1,device_id=d,device_id_type=MESH)
            else:
                @pl.when(p)
                def _(): pl.semaphore_signal(bar,inc=1,device_id=d,device_id_type=MESH)
        pl.semaphore_wait(bar, 4+(z*(3-z)+1)//3)
        S=Sends(ssem)
        def blk(bb,zz,part): return out.at[bb*8+zz*2+c, pl.ds(part[0],part[1])]
        def send(bb,zz,part,rsem,dev,pred=None,own=False):
            dst=blk(bb,zz,part)
            src=x_ref.at[pl.ds(part[0],part[1])] if own else dst
            S.go(src,dst,rsem,dev,pred)
        def wait(bb,zz,part,rsem):
            r=blk(bb,zz,part)
            pltpu.make_async_remote_copy(src_ref=r,dst_ref=r,send_sem=ssem.at[0],recv_sem=rsem,device_id=Pn,device_id_type=MESH).wait_recv()
        def waitp(pred,*a):
            if pred is None: wait(*a)
            else:
                @pl.when(pred)
                def _(): wait(*a)
        lc=pltpu.make_async_copy(x_ref, blk(b,z,FULL), lsem);
        send(b,z,A,pA.at[0],X,own=True); send(b,z,A,pA.at[1],Y,own=True)
        send(b,z,B,zB.at[z],UP,up,True); send(b,z,B,zB.at[z],DN,dn,True)
        send(b,z,B,xB.at[z],X,own=True); send(b,z,B,yB.at[z],Y,own=True)
        send(b,z,A,zA.at[z,0],UP,up,True); send(b,z,A,zA.at[z,0],DN,dn,True)
        send(b,z,FULL,pown.at[0],Pn,own=True)
        lc.start()
        pz=[]
        def pwait(*a): pz.append(a)
        pwait(None,b,z,FULL,pown.at[0])
        def zfwdA(bb,part,i,ps):
            send(bb,z,part,zA.at[z,i],UP,up); send(bb,z,part,zA.at[z,i],DN,dn)
            send(bb,z,part,ps,Pn); pwait(None,bb,z,part,ps)
        wait(bx,z,A,pA.at[0]); send(bx,z,A1,pA.at[2],Y); zfwdA(bx,A,1,ppA.at[0])
        wait(by,z,A,pA.at[1]); send(by,z,A2,pA.at[3],X); zfwdA(by,A,2,ppA.at[1])
        wait(bd,z,A1,pA.at[2]); zfwdA(bd,A1,3,ppA.at[2])
        wait(bd,z,A2,pA.at[3]); zfwdA(bd,A2,4,ppA.at[3])
        def xyB(zz,pred):
            waitp(pred,bx,zz,B,xB.at[zz]); send(bx,zz,B1,yBh.at[zz],Y,pred); send(bx,zz,B,pxB.at[zz],Pn,pred); pwait(pred,bx,zz,B,pxB.at[zz])
            waitp(pred,by,zz,B,yB.at[zz]); send(by,zz,B2,xBh.at[zz],X,pred); send(by,zz,B,pyB.at[zz],Pn,pred); pwait(pred,by,zz,B,pyB.at[zz])
        xyB(z,None)
        for d in (1,2,3):
            for s in (1,-1):
                zz=z+s*d
                pred=(zz<4) if s>0 else (zz>=0)
                nxt,np_=(DN,dn) if s>0 else (UP,up)
                waitp(pred,b,zz,B,zB.at[zz])
                send(b,zz,B,zB.at[zz],nxt,both(pred,np_))
                send(b,zz,B,xB.at[zz],X,pred); send(b,zz,B,yB.at[zz],Y,pred)
                send(b,zz,B,pzB.at[zz],Pn,pred); pwait(pred,b,zz,B,pzB.at[zz])
            for s in (1,-1):
                zz=z+s*d
                pred=(zz<4) if s>0 else (zz>=0)
                nxt,np_=(DN,dn) if s>0 else (UP,up)
                for i,(bb,part) in enumerate(((b,A),(bx,A),(by,A),(bd,A1),(bd,A2))):
                    waitp(pred,bb,zz,part,zA.at[zz,i]); send(bb,zz,part,zA.at[zz,i],nxt,both(pred,np_))
                    send(bb,zz,part,pzA.at[zz,i],Pn,pred); pwait(pred,bb,zz,part,pzA.at[zz,i])
            for s in (1,-1):
                zz=z+s*d
                pred=(zz<4) if s>0 else (zz>=0)
                xyB(zz,pred)
        for zz in range(4):
            wait(bd,zz,B1,yBh.at[zz]); send(bd,zz,B1,pyBh.at[zz],Pn); pwait(None,bd,zz,B1,pyBh.at[zz])
            wait(bd,zz,B2,xBh.at[zz]); send(bd,zz,B2,pxBh.at[zz],Pn); pwait(None,bd,zz,B2,pxBh.at[zz])
        for a in pz: waitp(*a)
        lc.wait()
        S.drain()
    D=pltpu.SemaphoreType.DMA
    def ag(xin, cid=0):
        return pl.pallas_call(kernel, out_shape=jax.ShapeDtypeStruct((32,T,16,128),jnp.bfloat16),
            in_specs=[pl.BlockSpec(memory_space=pltpu.VMEM)], out_specs=pl.BlockSpec(memory_space=pl.ANY),
            scratch_shapes=[D((160,)),D]+[D((4,))]*5+[D((4,)),D((4,5)),D((1,))]+[D((4,))]*5+[D((4,)),D((4,5))],
            compiler_params=pltpu.CompilerParams(collective_id=cid,has_side_effects=True))(xin)
    return ag


def make_rs(spa=32):
    nb=T-spa
    A=(0,spa); A1=(0,spa//2); A2=(spa//2,spa//2)
    B=(spa,nb); B1=(spa,nb//2); B2=(spa+nb//2,nb//2)
    FULL=(0,T)
    def kernel(g, out, P, R, LX, LY, LHX, LHY, LZB, LZA, LPA, ssem, lsem, psem, s_hx, s_hy, s_x, s_y, s_zb, s_za, s_pa):
        b=lax.axis_index("batch"); f=lax.axis_index("frame")
        x=b%2; y=b//2; z=f//2; c=f%2
        bx=y*2+(1-x); by=(1-y)*2+x; bd=(1-y)*2+(1-x)
        X=(bx,f); Y=(by,f); Pn=(b,z*2+(1-c)); UP=(b,f+2); DN=(b,f-2)
        up=z<3; dn=z>0
        t=z//2
        zo=[3*(1-t), 2-t, (1-z)*(1-t)+(5-z)*t, z]
        loads=[]
        order=[]
        for zz in zo: order += [(bd,zz)]
        for zz in zo: order += [(bx,zz),(by,zz)]
        for zz in zo: order += [(b,zz)]
        for i,(bb,zz) in enumerate(order):
            cp=pltpu.make_async_copy(g.at[bb*8+zz*2+c], P.at[bb,zz], lsem.at[i]); cp.start(); loads.append(cp)
        bar=pltpu.get_barrier_semaphore()
        for d,p in ((X,None),(Y,None),(Pn,None),(UP,up),(DN,dn)):
            if p is None: pl.semaphore_signal(bar,inc=1,device_id=d,device_id_type=MESH)
            else:
                @pl.when(p)
                def _(): pl.semaphore_signal(bar,inc=1,device_id=d,device_id_type=MESH)
        pl.semaphore_wait(bar, 4+(z*(3-z)+1)//3)
        S=Sends(ssem)
        for i,(bb,zz) in enumerate(order):
            S.go(g.at[bb*8+zz*2+(1-c)], R.at[bb,zz], psem.at[bb,zz], Pn)
        def acc(dst, srcs, n, step=8):
            def body(i,_):
                ds=pl.ds(i*step,step)
                v=srcs[0][ds].astype(jnp.float32)
                for s in srcs[1:]: v=v+s[ds].astype(jnp.float32)
                dst[ds]=v.astype(dst.dtype)
                return 0
            lax.fori_loop(0,n//step,body,0)
        def sub(ref,part): return ref.at[pl.ds(part[0],part[1])]
        have=set()
        def ready(i):
            bb,zz=order[i]
            loads[i].wait()
            pltpu.make_async_remote_copy(src_ref=R.at[bb,zz],dst_ref=R.at[bb,zz],send_sem=ssem.at[0],recv_sem=psem.at[bb,zz],device_id=Pn,device_id_type=MESH).wait_recv()
        def wrecv(ref,sem):
            pltpu.make_async_remote_copy(src_ref=ref,dst_ref=ref,send_sem=ssem.at[0],recv_sem=sem,device_id=Pn,device_id_type=MESH).wait_recv()
        for i,zz in enumerate(zo):
            ready(i)
            acc(sub(P.at[bd,zz],B), [sub(P.at[bd,zz],B), sub(R.at[bd,zz],B)], nb)
            S.go(sub(P.at[bd,zz],B1), LHY.at[zz], s_hy.at[zz], Y)
            S.go(sub(P.at[bd,zz],B2), LHX.at[zz], s_hx.at[zz], X)
        def chainA(bi,bb):
            for d in (3,2,1):
                for s in (1,-1):
                    zz=z+s*d
                    pred=(zz<4) if s>0 else (zz>=0)
                    frm=dn if s>0 else up
                    dev=UP if s>0 else DN
                    di=0 if s>0 else 1
                    @pl.when(jnp.logical_and(pred,frm))
                    def _():
                        wrecv(LZA.at[di,zz,bi], s_za.at[di,zz,bi])
                        acc(sub(P.at[bb,zz],A),[sub(P.at[bb,zz],A),sub(R.at[bb,zz],A),LZA.at[di,zz,bi]],spa)
                    @pl.when(jnp.logical_and(pred,jnp.logical_not(frm)))
                    def _():
                        acc(sub(P.at[bb,zz],A),[sub(P.at[bb,zz],A),sub(R.at[bb,zz],A)],spa)
                    S.go(sub(P.at[bb,zz],A), LZA.at[di,zz,bi], s_za.at[di,zz,bi], dev, pred)
        chainA(0,bd)
        for i,zz in enumerate(zo):
            ready(4+2*i); ready(5+2*i)
            wrecv(LHY.at[zz], s_hy.at[zz])
            acc(sub(P.at[bx,zz],B1),[sub(P.at[bx,zz],B1),sub(R.at[bx,zz],B1),LHY.at[zz]],nb//2)
            acc(sub(P.at[bx,zz],B2),[sub(P.at[bx,zz],B2),sub(R.at[bx,zz],B2)],nb//2)
            S.go(sub(P.at[bx,zz],B), LX.at[zz], s_x.at[zz], X)
            wrecv(LHX.at[zz], s_hx.at[zz])
            acc(sub(P.at[by,zz],B2),[sub(P.at[by,zz],B2),sub(R.at[by,zz],B2),LHX.at[zz]],nb//2)
            acc(sub(P.at[by,zz],B1),[sub(P.at[by,zz],B1),sub(R.at[by,zz],B1)],nb//2)
            S.go(sub(P.at[by,zz],B), LY.at[zz], s_y.at[zz], Y)
        chainA(1,bx); chainA(2,by)
        for i in range(4): ready(12+i)
        chainA(3,b)
        for i,zz in enumerate(zo[:3]):
            wrecv(LX.at[zz],s_x.at[zz]); wrecv(LY.at[zz],s_y.at[zz])
            isup=zz>z
            inc=jnp.logical_or(jnp.logical_and(isup,dn),jnp.logical_and(jnp.logical_not(isup),up))
            di=jnp.where(isup,0,1)
            base=[sub(P.at[b,zz],B),sub(R.at[b,zz],B),LX.at[zz],LY.at[zz]]
            @pl.when(inc)
            def _():
                wrecv(LZB.at[di,zz],s_zb.at[di,zz])
                acc(sub(P.at[b,zz],B),base+[LZB.at[di,zz]],nb)
            @pl.when(jnp.logical_not(inc))
            def _(): acc(sub(P.at[b,zz],B),base,nb)
            S.go(sub(P.at[b,zz],B),LZB.at[0,zz],s_zb.at[0,zz],UP,isup)
            S.go(sub(P.at[b,zz],B),LZB.at[1,zz],s_zb.at[1,zz],DN,jnp.logical_not(isup))
        def totA(bi,bb,part,extra=(),dst=None):
            dst = dst if dst is not None else sub(P.at[bb,z],part)
            srcs=[sub(P.at[bb,z],part),sub(R.at[bb,z],part)]+list(extra)
            o=part[0]; n=part[1]
            l0=LZA.at[0,z,bi,pl.ds(o,n)]; l1=LZA.at[1,z,bi,pl.ds(o,n)]
            @pl.when(jnp.logical_and(up,dn))
            def _(): acc(dst,srcs+[l0,l1],n)
            @pl.when(jnp.logical_not(up))
            def _(): acc(dst,srcs+[l0],n)
            @pl.when(jnp.logical_not(dn))
            def _(): acc(dst,srcs+[l1],n)
        for bi in range(4):
            @pl.when(dn)
            def _(): wrecv(LZA.at[0,z,bi],s_za.at[0,z,bi])
            @pl.when(up)
            def _(): wrecv(LZA.at[1,z,bi],s_za.at[1,z,bi])
            if bi==0:
                totA(0,bd,A1); S.go(sub(P.at[bd,z],A1),LPA.at[0,pl.ds(0,spa//2)],s_pa.at[0],Y)
                totA(0,bd,A2); S.go(sub(P.at[bd,z],A2),LPA.at[1,pl.ds(0,spa//2)],s_pa.at[1],X)
            if bi==1:
                totA(1,bx,A2)
                wrecv(LPA.at[0,pl.ds(0,spa//2)],s_pa.at[0])
                totA(1,bx,A1,[LPA.at[0,pl.ds(0,spa//2)]])
                S.go(sub(P.at[bx,z],A),LPA.at[2],s_pa.at[2],X)
            if bi==2:
                totA(2,by,A1)
                wrecv(LPA.at[1,pl.ds(0,spa//2)],s_pa.at[1])
                totA(2,by,A2,[LPA.at[1,pl.ds(0,spa//2)]])
                S.go(sub(P.at[by,z],A),LPA.at[3],s_pa.at[3],Y)
        wrecv(LX.at[z],s_x.at[z]); wrecv(LY.at[z],s_y.at[z])
        base=[sub(P.at[b,z],B),sub(R.at[b,z],B),LX.at[z],LY.at[z]]
        @pl.when(dn)
        def _(): wrecv(LZB.at[0,z],s_zb.at[0,z])
        @pl.when(up)
        def _(): wrecv(LZB.at[1,z],s_zb.at[1,z])
        @pl.when(jnp.logical_and(up,dn))
        def _(): acc(sub(out,B),base+[LZB.at[0,z],LZB.at[1,z]],nb)
        @pl.when(jnp.logical_not(up))
        def _(): acc(sub(out,B),base+[LZB.at[0,z]],nb)
        @pl.when(jnp.logical_not(dn))
        def _(): acc(sub(out,B),base+[LZB.at[1,z]],nb)
        wrecv(LPA.at[2],s_pa.at[2]); wrecv(LPA.at[3],s_pa.at[3])
        totA(3,b,A,[LPA.at[2],LPA.at[3]],dst=sub(out,A))
        S.drain()
    D=pltpu.SemaphoreType.DMA
    V=lambda *s: pltpu.VMEM(s+(16,128),jnp.bfloat16)
    def rs(g, cid=1):
        return pl.pallas_call(kernel, out_shape=jax.ShapeDtypeStruct((T,16,128),jnp.float32),
            in_specs=[pl.BlockSpec(memory_space=pl.ANY)], out_specs=pl.BlockSpec(memory_space=pltpu.VMEM),
            scratch_shapes=[V(4,4,T),V(4,4,T),V(4,nb),V(4,nb),V(4,nb//2),V(4,nb//2),V(2,4,nb),V(2,4,4,spa),V(4,spa),
              D((80,)),D((16,)),D((4,4)),D((4,)),D((4,)),D((4,)),D((4,)),D((2,4)),D((2,4,4)),D((4,))],
            compiler_params=pltpu.CompilerParams(collective_id=cid,has_side_effects=True,vmem_limit_bytes=60*1024*1024))(g)
    return rs


TOK=400; CB=208; NK=3200; NQ=1600; SUB=80; PADQ=512
ROWS={"q":0,"k":400,"v":800,"qc":1200,"kc":1408,"vc":1616}
NT=(((1,),(1,)),((),())); NN=(((1,),(0,)),((),())); TN=(((0,),(0,)),((),()))
f32=jnp.float32; bf16=jnp.bfloat16

def dot(a,b,dims): return lax.dot_general(a,b,dims,preferred_element_type=f32)

def mesh_pos():
    b=lax.axis_index("batch"); f=lax.axis_index("frame")
    return b,f//2,f%2

def zbarrier(b,z,c):
    bar=pltpu.get_barrier_semaphore()
    for d in (1,2,3):
        pl.semaphore_signal(bar,inc=1,device_id=(b,((z+d)%4)*2+c),device_id_type=MESH)
    pl.semaphore_signal(bar,inc=1,device_id=(b,z*2+1-c),device_id_type=MESH)
    pl.semaphore_wait(bar,4)

def wrecv(ref,sem,dev):
    pltpu.make_async_remote_copy(src_ref=ref,dst_ref=ref,send_sem=sem,recv_sem=sem,device_id=dev,device_id_type=MESH).wait_recv()

def others(z):
    return [((z+d)%4) for d in (2,1,3)]

def unpack_c(src, dst, row):
    v=src.astype(f32)
    lane=lax.broadcasted_iota(jnp.int32,(CB,128),1)
    lo=jnp.where(lane<64,v,0.0)
    hi=jnp.where(lane<64,pltpu.roll(v,64,1),0.0)
    dst[pl.ds(row,CB)]=lo.astype(bf16)
    dst[pl.ds(row+CB,TOK-CB)]=hi[:TOK-CB].astype(bf16)

def pack_c(lo, hi):
    hi=jnp.concatenate([hi,jnp.zeros((2*CB-TOK,128),f32)],0)
    lane=lax.broadcasted_iota(jnp.int32,(CB,128),1)
    return jnp.where(lane<64,lo,pltpu.roll(hi,64,1)).astype(bf16)

def fwd_kernel(sp, bias, og, Q, K, V, QC, KC, VC, OA, OC, LA, LC,
               QCp, KCp, VCp, OB, OCp, S, Pb, ssem, lsem, rq, rk, rv, rqc, rkc, rvc, pk, pv, pkc, pvc, ro, roc):
    b,z,c=mesh_pos()
    Pn=(b,z*2+1-c)
    dev=lambda zz:(b,zz*2+c)
    row=lambda zz: pl.multiple_of(zz*TOK,16)
    krow=lambda zz: pl.multiple_of((c*4+zz)*TOK,16)
    pkrow=lambda zz: pl.multiple_of(((1-c)*4+zz)*TOK,16)
    zbarrier(b,z,c)
    X=Sends(ssem)
    part=lambda g,n,ln: sp.at[g,pl.ds(ROWS[n],ln)]
    loc=[]
    def lcopy(src,dst):
        cp=pltpu.make_async_copy(src,dst,lsem.at[len(loc)]); cp.start(); loc.append(cp)
    for zz in others(z):
        X.go(part(zz,"k",TOK),K.at[pl.ds(krow(z),TOK)],rk.at[z],dev(zz))
        X.go(part(zz,"q",TOK),Q.at[pl.ds(row(z),TOK)],rq.at[z],dev(zz))
        X.go(part(zz,"v",TOK),V.at[pl.ds(krow(z),TOK)],rv.at[z],dev(zz))
    lcopy(part(z,"k",TOK),K.at[pl.ds(krow(z),TOK)])
    lcopy(part(z,"q",TOK),Q.at[pl.ds(row(z),TOK)])
    lcopy(part(z,"v",TOK),V.at[pl.ds(krow(z),TOK)])
    lcopy(part(z,"kc",CB),KCp.at[c*4+z]); lcopy(part(z,"qc",CB),QCp.at[z]); lcopy(part(z,"vc",CB),VCp.at[c*4+z])
    X.go(part(z,"k",TOK),K.at[pl.ds(krow(z),TOK)],pk.at[z],Pn)
    X.go(part(z,"v",TOK),V.at[pl.ds(krow(z),TOK)],pv.at[z],Pn)
    X.go(part(z,"kc",CB),KCp.at[c*4+z],pkc.at[z],Pn)
    X.go(part(z,"vc",CB),VCp.at[c*4+z],pvc.at[z],Pn)
    for zz in others(z):
        X.go(part(zz,"kc",CB),KCp.at[c*4+z],rkc.at[z],dev(zz))
        X.go(part(zz,"qc",CB),QCp.at[z],rqc.at[z],dev(zz))
        X.go(part(zz,"vc",CB),VCp.at[c*4+z],rvc.at[z],dev(zz))
    for zz in [((z+d)%4) for d in (1,3,2)]:
        kr=K.at[pl.ds(krow(zz),TOK)]; vr=V.at[pl.ds(krow(zz),TOK)]
        wrecv(kr,rk.at[zz],Pn); X.go(kr,kr,pk.at[zz],Pn)
        wrecv(vr,rv.at[zz],Pn); X.go(vr,vr,pv.at[zz],Pn)
    for zz in range(4):
        r=K.at[pl.ds(pkrow(zz),TOK)]; wrecv(r,pk.at[zz],Pn)
        r=V.at[pl.ds(pkrow(zz),TOK)]; wrecv(r,pv.at[zz],Pn)
    for zz in [((z+d)%4) for d in (1,2,3)]:
        wrecv(Q.at[pl.ds(row(zz),TOK)],rq.at[zz],Pn)
    for cp in loc: cp.wait()
    lane=lax.broadcasted_iota(jnp.int32,(TOK,128),1)
    lane8=lax.broadcasted_iota(jnp.int32,(SUB,128),1)
    def softmax(slot):
        def sub(i,carry):
            ds=pl.ds(pl.multiple_of(i*SUB,16),SUB)
            s=S[slot,ds,:]+bias[...]
            m=jnp.max(s,-1,keepdims=True)
            p=jnp.exp(s-m)
            l=jnp.sum(p,-1,keepdims=True)
            Pb[slot,ds,:]=p.astype(bf16)
            return m,l
        ms=[];ls=[]
        for i in range(TOK//SUB):
            m,l=sub(i,0); ms.append(m); ls.append(l)
        return jnp.concatenate(ms,0),jnp.concatenate(ls,0)
    def pairblock(i,_):
        ds=pl.ds(pl.multiple_of(i*TOK,16),TOK)
        q=Q[ds]
        zero=jnp.zeros_like(q)
        S[0]=dot(jnp.where(lane<64,q,zero),K[...],NT)
        S[1]=dot(jnp.where(lane<64,zero,q),K[...],NT)
        ma,la=softmax(0); mb,lb=softmax(1)
        oa=dot(Pb[0],V[...],NN)/la; ob=dot(Pb[1],V[...],NN)/lb
        o=jnp.where(lane<64,oa,ob)
        OA[ds]=o; OB[ds]=o.astype(bf16)
        LA[ds]=jnp.where(lane<64,ma+jnp.log(la),mb+jnp.log(lb))
        return 0
    lax.fori_loop(0,4,pairblock,0)
    for zz in [((z+d)%4) for d in (1,3,2)]:
        kr=KCp.at[c*4+zz]; vr=VCp.at[c*4+zz]
        wrecv(kr,rkc.at[zz],Pn); X.go(kr,kr,pkc.at[zz],Pn)
        wrecv(vr,rvc.at[zz],Pn); X.go(vr,vr,pvc.at[zz],Pn)
        wrecv(QCp.at[zz],rqc.at[zz],Pn)
    for zz in others(z):
        X.go(OB.at[pl.ds(row(zz),TOK)],og.at[z,pl.ds(0,TOK)],ro.at[z],dev(zz))
    lo=pltpu.make_async_copy(OB.at[pl.ds(row(z),TOK)],og.at[z,pl.ds(0,TOK)],lsem.at[6]); lo.start()
    for zz in range(4):
        wrecv(KCp.at[(1-c)*4+zz],pkc.at[zz],Pn); wrecv(VCp.at[(1-c)*4+zz],pvc.at[zz],Pn)
    def unp(i,_):
        r=pl.multiple_of(i*TOK,16)
        unpack_c(KCp[i],KC,r); unpack_c(VCp[i],VC,r)
        return 0
    lax.fori_loop(0,8,unp,0)
    def unq(i,_):
        unpack_c(QCp[i],QC,pl.multiple_of(i*TOK,16)); return 0
    lax.fori_loop(0,4,unq,0)
    def cblock(i,_):
        ds=pl.ds(pl.multiple_of(i*TOK,16),TOK)
        S[0]=dot(QC[ds],KC[...],NT)
        ma,la=softmax(0)
        o=dot(Pb[0],VC[...],NN)/la
        OC[ds]=o
        LC[ds]=jnp.broadcast_to(ma+jnp.log(la),(TOK,128))
        OCp[i]=pack_c(o[:CB],o[CB:])
        return 0
    lax.fori_loop(0,4,cblock,0)
    for zz in others(z):
        X.go(OCp.at[zz],og.at[z,pl.ds(TOK,CB)],roc.at[z],dev(zz))
    lc=pltpu.make_async_copy(OCp.at[z],og.at[z,pl.ds(TOK,CB)],lsem.at[7]); lc.start()
    for d in (1,2,3):
        zz=(z+d)%4
        wrecv(og.at[zz,pl.ds(0,TOK)],ro.at[zz],Pn)
        wrecv(og.at[zz,pl.ds(TOK,CB)],roc.at[zz],Pn)
    lo.wait(); lc.wait()
    X.drain()

D=pltpu.SemaphoreType.DMA
def vb(*s): return pltpu.VMEM(s,bf16)
def vf(*s): return pltpu.VMEM(s,f32)
VM=pl.BlockSpec(memory_space=pltpu.VMEM)
def sds(*s,d=bf16): return jax.ShapeDtypeStruct(s,d)

def attn_fwd(sp,bias,cid):
    return pl.pallas_call(fwd_kernel,
        out_shape=(sds(4,TOK+CB,128),sds(NQ,128),sds(NK,128),sds(NK,128),sds(NQ,128),sds(NK,128),sds(NK,128),
                   sds(NQ,128,d=f32),sds(NQ,128,d=f32),sds(NQ,128,d=f32),sds(NQ,128,d=f32)),
        in_specs=[VM,VM],out_specs=[VM]*11,
        scratch_shapes=[vb(4,CB,128),vb(8,CB,128),vb(8,CB,128),vb(NQ,128),vb(4,CB,128),vf(2,TOK,NK),vb(2,TOK,NK),
            D((48,)),D((8,))]+[D((4,))]*12,
        compiler_params=pltpu.CompilerParams(collective_id=cid,has_side_effects=True,vmem_limit_bytes=60*1024*1024))(sp,bias)

def bwd_kernel(dog, bias, Q, K, V, QC, KC, VC, OA, OC, LA, LC, dsp,
               DO, DOCp, DOC, S, P, DS, DKT, DVT, TT, DQ, DQC, XK, XV, YK, YV, SK, SV, HK, HV, XKC, XVC, YKC, YVC, HKC, HVC,
               ssem, lsem, rd, rdc, px, ho):
    b,z,c=mesh_pos()
    Pn=(b,z*2+1-c)
    dev=lambda zz:(b,zz*2+c)
    row=lambda zz: pl.multiple_of(zz*TOK,16)
    zbarrier(b,z,c)
    X=Sends(ssem)
    loc=[]
    def lcopy(src,dst):
        cp=pltpu.make_async_copy(src,dst,lsem.at[len(loc)]); cp.start(); loc.append(cp); return cp
    for zz in others(z):
        X.go(dog.at[zz,pl.ds(0,TOK)],DO.at[pl.ds(row(z),TOK)],rd.at[z],dev(zz))
    for zz in others(z):
        X.go(dog.at[zz,pl.ds(TOK,CB)],DOCp.at[z],rdc.at[z],dev(zz))
    l1=lcopy(dog.at[z,pl.ds(0,TOK)],DO.at[pl.ds(row(z),TOK)])
    l2=lcopy(dog.at[z,pl.ds(TOK,CB)],DOCp.at[z])
    l1.wait(); l2.wait()
    lane=lax.broadcasted_iota(jnp.int32,(TOK,128),1)
    def zero(ref):
        def bodyz(i,_):
            ref[:,pl.ds(pl.multiple_of(i*640,128),640)]=jnp.zeros((128,640),f32); return 0
        lax.fori_loop(0,NK//640,bodyz,0)
    def grads(q,k,v,do,lse,delta):
        S[0]=dot(q,k[...],NT)
        S[1]=dot(do,v[...],NT)
        for i in range(TOK//SUB):
            ds=pl.ds(i*SUB,SUB); sl=slice(i*SUB,(i+1)*SUB)
            p=jnp.exp(S[0,ds,:]+bias[...]-lse[sl])
            P[ds,:]=p.astype(bf16)
            DS[ds,:]=(p*(S[1,ds,:]-delta[sl])).astype(bf16)
        tail=jnp.zeros((PADQ-TOK,128),bf16)
        DKT[...]+=dot(jnp.concatenate([q,tail],0),DS[...],TN)
        DVT[...]+=dot(jnp.concatenate([do,tail],0),P[...],TN)
        return dot(DS[pl.ds(0,TOK)],k[...],NN)
    def home(src,r0,n,si):
        for zz in others(z):
            X.go(src(zz),dsp.at[z,pl.ds(r0,n)],ho.at[si,z],dev(zz))
        lcopy(src(z),dsp.at[z,pl.ds(r0,n)])
    mine=c*NQ; theirs=(1-c)*NQ
    def split(acc, x, own):
        def tr(i,_):
            TT[pl.ds(pl.multiple_of(i*640,16),640)]=acc[:,pl.ds(pl.multiple_of(i*640,128),640)].T
            return 0
        lax.fori_loop(0,NK//640,tr,0)
        def cut(i,_):
            r=pl.multiple_of(i*TOK,16)
            x[pl.ds(r,TOK)]=TT[pl.ds(pl.multiple_of(theirs+i*TOK,16),TOK)].astype(bf16)
            own[pl.ds(r,TOK)]=TT[pl.ds(pl.multiple_of(mine+i*TOK,16),TOK)]
            return 0
        lax.fori_loop(0,4,cut,0)
    P[pl.ds(TOK,PADQ-TOK)]=jnp.zeros((PADQ-TOK,NK),bf16)
    DS[pl.ds(TOK,PADQ-TOK)]=jnp.zeros((PADQ-TOK,NK),bf16)
    zero(DKT); zero(DVT)
    def pairblock(i,_):
        zz=(z+i)%4
        @pl.when(i>0)
        def _(): wrecv(DO.at[pl.ds(row(zz),TOK)],rd.at[zz],Pn)
        ds=pl.ds(row(zz),TOK)
        q=Q[ds]; do=DO[ds]; zero_=jnp.zeros_like(q)
        dof=do.astype(f32)*OA[ds]
        da=jnp.sum(jnp.where(lane<64,dof,0.0),-1,keepdims=True)
        db=jnp.sum(jnp.where(lane<64,0.0,dof),-1,keepdims=True)
        ga=grads(jnp.where(lane<64,q,zero_),K,V,jnp.where(lane<64,do,zero_),LA[ds,0:1],da)
        gb=grads(jnp.where(lane<64,zero_,q),K,V,jnp.where(lane<64,zero_,do),LA[ds,64:65],db)
        DQ[ds]=(jnp.where(lane<64,ga,gb)*0.125).astype(bf16)
        return 0
    lax.fori_loop(0,4,pairblock,0)
    home(lambda zz: DQ.at[pl.ds(row(zz),TOK)],0,TOK,0)
    split(DKT,XK,SK); X.go(XK,YK,px.at[0],Pn)
    split(DVT,XV,SV); X.go(XV,YV,px.at[1],Pn)
    zero(DKT); zero(DVT)
    def cblock(i,_):
        zz=(z+i)%4
        @pl.when(i>0)
        def _(): wrecv(DOCp.at[zz],rdc.at[zz],Pn)
        unpack_c(DOCp[zz],DOC,0)
        ds=pl.ds(row(zz),TOK)
        do=DOC[...]
        delta=jnp.sum(do.astype(f32)*OC[ds],-1,keepdims=True)
        g=grads(QC[ds],KC,VC,do,LC[ds,0:1],delta)*0.125
        DQC[zz]=pack_c(g[:CB],g[CB:])
        return 0
    lax.fori_loop(0,4,cblock,0)
    home(lambda zz: DQC.at[zz],ROWS["qc"],CB,1)
    wrecv(YK,px.at[0],Pn); wrecv(YV,px.at[1],Pn)
    def addp(i,_):
        ds=pl.ds(pl.multiple_of(i*TOK,16),TOK)
        HK[ds]=(SK[ds]+YK[ds].astype(f32)).astype(bf16)
        HV[ds]=(SV[ds]+YV[ds].astype(f32)).astype(bf16)
        return 0
    lax.fori_loop(0,4,addp,0)
    home(lambda zz: HK.at[pl.ds(row(zz),TOK)],ROWS["k"],TOK,2)
    home(lambda zz: HV.at[pl.ds(row(zz),TOK)],ROWS["v"],TOK,3)
    def splitc(acc, x, own):
        def tr(i,_):
            TT[pl.ds(pl.multiple_of(i*640,16),640)]=acc[:,pl.ds(pl.multiple_of(i*640,128),640)].T
            return 0
        lax.fori_loop(0,NK//640,tr,0)
        def cut(i,_):
            r=theirs+i*TOK
            x[i]=pack_c(TT[pl.ds(pl.multiple_of(r,16),CB)],TT[pl.ds(pl.multiple_of(r+CB,16),TOK-CB)])
            own[pl.ds(pl.multiple_of(i*TOK,16),TOK)]=TT[pl.ds(pl.multiple_of(mine+i*TOK,16),TOK)]
            return 0
        lax.fori_loop(0,4,cut,0)
    splitc(DKT,XKC,SK); X.go(XKC,YKC,px.at[2],Pn)
    splitc(DVT,XVC,SV); X.go(XVC,YVC,px.at[3],Pn)
    def addc(y,own,h):
        def body(i,_):
            unpack_c(y[i],DOC,0)
            r=i*TOK
            t=own[pl.ds(pl.multiple_of(r,16),TOK)]+DOC[...].astype(f32)
            h[i]=pack_c(t[:CB],t[CB:])
            return 0
        lax.fori_loop(0,4,body,0)
    wrecv(YKC,px.at[2],Pn); addc(YKC,SK,HKC)
    home(lambda zz: HKC.at[zz],ROWS["kc"],CB,4)
    wrecv(YVC,px.at[3],Pn); addc(YVC,SV,HVC)
    home(lambda zz: HVC.at[zz],ROWS["vc"],CB,5)
    for si,(r0,n) in enumerate(((0,TOK),(ROWS["qc"],CB),(ROWS["k"],TOK),(ROWS["v"],TOK),(ROWS["kc"],CB),(ROWS["vc"],CB))):
        for d in (1,2,3):
            zz=(z+d)%4
            wrecv(dsp.at[zz,pl.ds(r0,n)],ho.at[si,zz],Pn)
    for cp in loc[2:]: cp.wait()
    X.drain()

def attn_bwd(dog,bias,saved,cid):
    return pl.pallas_call(bwd_kernel,
        out_shape=sds(4,3*(TOK+CB),128),
        in_specs=[VM]*12,out_specs=VM,
        scratch_shapes=[vb(NQ,128),vb(4,CB,128),vb(TOK,128),vf(2,TOK,NK),vb(PADQ,NK),vb(PADQ,NK),vf(128,NK),vf(128,NK),vf(NK,128),
            vb(NQ,128),vb(4,CB,128)]+[vb(NQ,128)]*4+[vf(NQ,128)]*2+[vb(NQ,128)]*2+[vb(4,CB,128)]*6+[
            D((32,)),D((10,)),D((4,)),D((4,)),D((4,)),D((6,4))],
        compiler_params=pltpu.CompilerParams(collective_id=cid,has_side_effects=True,vmem_limit_bytes=60*1024*1024))(dog,bias,*saved)

PAIR=(0,256,384,640); CC=(128,192,512,576)
def pack_group(x,g):
    p=x[:,PAIR[g]:PAIR[g]+128]; ch=x[:,CC[g]:CC[g]+64]
    c=jnp.concatenate([ch[:CB],jnp.pad(ch[CB:],((0,2*CB-TOK),(0,0)))],1)
    return p,c
def pack_qkv(q,k,v):
    out=[]
    for g in range(4):
        qp,qc=pack_group(q,g); kp,kc=pack_group(k,g); vp,vc=pack_group(v,g)
        out.append(jnp.concatenate([qp,kp,vp,qc,kc,vc],0))
    return jnp.stack(out)
def unpack_group(p,c):
    ch=jnp.concatenate([c[:,:64],c[:TOK-CB,64:]],0)
    return p,ch
def unpack_x(ps,cs):
    u=[unpack_group(ps[g],cs[g])[1] for g in range(4)]
    return jnp.concatenate([ps[0],u[0],u[1],ps[1],ps[2],u[2],u[3],ps[3]],1)


SHARD = 289176
BLOCK = 294912
SLIDE = BLOCK - SHARD
CARRY = 32 * SLIDE
KEY_ORDER_C = 2


def to_tiles(matrix):
    rows, width = matrix.shape
    m = width // 128
    return matrix.reshape(rows // 16, 16, m, 128).transpose(0, 2, 1, 3).reshape(-1, 16, 128)


def from_tiles(tiles, width):
    m = width // 128
    return tiles.reshape(-1, m, 16, 128).transpose(0, 2, 1, 3).reshape(-1, width)


def block_to_tiles(flat, k):
    def of(width):
        return lambda v: to_tiles(v.reshape(-1, width))

    def split29(v):
        return jnp.concatenate([to_tiles(v[: 48 * 2048].reshape(-1, 512)), v[48 * 2048 :].reshape(-1, 16, 128)])

    branch = class_of(k)
    return lax.switch(branch, [of(768), of(2304), of(3072), of(512), split29, of(128)], flat)


def class_of(k):
    return jnp.where(
        k < 4, 0, jnp.where(k < 10, 1, jnp.where(k < 12, 0, jnp.where(k < 20, 2, jnp.where(k < 28, 0, jnp.where(k == 28, 3, jnp.where(k == 29, 4, 5))))))
    )


def tiles_to_block(tiles, k):
    def of(width):
        return lambda v: from_tiles(v, width).reshape(-1)

    def split29(v):
        return jnp.concatenate([from_tiles(v[:48], 512).reshape(-1), v[48:].reshape(-1)])

    return lax.switch(class_of(k), [of(768), of(2304), of(3072), of(512), split29, of(128)], tiles)


def local_4x8(
    pixels,
    res_class,
    valid_tubelet_count,
    positive,
    negatives,
    master,
    first_moment,
    second_moment,
    adam_step,
):
    D = HEAD_COUNT * HEAD_FEATURES
    both_axes = ("batch", "frame")
    bi = lax.axis_index("batch")
    fi = lax.axis_index("frame")
    k = bi * 8 + fi
    low = to_bfloat(master)
    nxt = lax.ppermute(low[:CARRY], both_axes, [(i + 1, i) for i in range(31)])
    block = lax.dynamic_slice(jnp.concatenate([low, nxt]), (SLIDE * k,), (BLOCK,))
    G = make_ag()(block_to_tiles(block, k), 0)
    w_embed = from_tiles(G[0:4].reshape(-1, 16, 128), D)
    w_qkv = from_tiles(G[4:10].reshape(-1, 16, 128), 3 * D)
    w_out = from_tiles(G[10:12].reshape(-1, 16, 128), D)
    w_up = from_tiles(G[12:20].reshape(-1, 16, 128), FFW)
    w_down = from_tiles(G[20:28].reshape(-1, 16, 128), D)
    rest = G[28:].reshape(-1, 16, 128)
    w_proj = from_tiles(rest[:192], EMB)
    tail = rest[192:].reshape(-1)
    w_map = tail[: D * NMAP].reshape(D, NMAP)
    off = D * NMAP
    pos_space = tail[off : off + 696 * D].reshape(696, D)
    off += 696 * D
    pos_time = tail[off : off + TMAX * D].reshape(TMAX, D)
    off += TMAX * D
    vec_f = tail[off : off + NVEC * D].reshape(NVEC, D).astype(jnp.float32)
    off += NVEC * D
    bias_up = tail[off : off + FFW]

    tubelets = lax.dynamic_slice_in_dim(valid_tubelet_count, bi, 1, 0)
    patches = jnp.where(res_class == 0, P0, jnp.where(res_class == 1, P1, PATCHES_THIRD_2)).astype(jnp.int32)
    start_rows = jnp.where(res_class == 0, 0, jnp.where(res_class == 1, P0, P0 + P1)).astype(jnp.int32)
    patch_pos = lax.dynamic_slice_in_dim(pos_space, start_rows[0], 400, 0).astype(jnp.float32)
    time_row = lax.dynamic_slice_in_dim(pos_time, fi, 1, 0).astype(jnp.float32)
    pix = pixels.reshape(400, TUBELET_PIXELS)
    first_in = jnp.dot(pix, w_embed, preferred_element_type=jnp.float32) + vec_f[8] + patch_pos + time_row
    h1, saved_one = norm_forward(first_in, vec_f[0], vec_f[1])
    h1 = to_bfloat(h1)
    qkv_bias = jnp.concatenate([vec_f[9], jnp.zeros_like(vec_f[9]), vec_f[10]])
    qkv = to_bfloat(jnp.dot(h1, w_qkv, preferred_element_type=jnp.float32) + qkv_bias)
    slot = jnp.arange(8, dtype=jnp.int32)
    slot_tubelet = (slot % 4) * 2 + slot // 4
    key_ok = (slot_tubelet[:, None] < tubelets[0]) & (jnp.arange(400, dtype=jnp.int32)[None] < patches[0])
    bias = jnp.where(key_ok.reshape(1, 3200), 0.0, -1e30).astype(jnp.float32)
    sp = pack_qkv((qkv[:, :D] * 0.125).astype(jnp.bfloat16), qkv[:, D : 2 * D], qkv[:, 2 * D :])
    og, *saved_attn = attn_fwd(sp, bias, 2)
    attended = unpack_x(og[:, :400], og[:, 400:])
    second_in = first_in + jnp.dot(attended, w_out, preferred_element_type=jnp.float32) + vec_f[11]
    h2, saved_two = norm_forward(second_in, vec_f[2], vec_f[3])
    h2 = to_bfloat(h2)
    hidden_pre = jnp.dot(h2, w_up, preferred_element_type=jnp.float32) + bias_up.astype(jnp.float32)
    hidden_act, gelu_pull = jax.vjp(partial(jax.nn.gelu, approximate=False), hidden_pre)
    hidden_low = to_bfloat(hidden_act)
    block_out = second_in + jnp.dot(hidden_low, w_down, preferred_element_type=jnp.float32) + vec_f[12]
    valid_patch = jnp.arange(400, dtype=jnp.int32) < patches[0]
    slot_weight = (fi < tubelets[0]).astype(jnp.float32)

    def learner(block_in, gain_row, shift_row, map_weight):
        normed, unused = norm_forward(block_in, gain_row, shift_row)
        logits = jnp.dot(normed, map_weight, precision=HIGH_ACCURACY)
        logits = jnp.where(valid_patch[:, None], logits, -1e30)
        token_maps = jax.nn.softmax(logits, axis=0)
        pooled_part = slot_weight * jnp.einsum("pm,pd->d", token_maps, block_in, precision=HIGH_ACCURACY)
        gram = jnp.einsum("pm,pn->mn", token_maps, token_maps, precision=HIGH_ACCURACY)
        return pooled_part, slot_weight * (jnp.sum(gram) - jnp.trace(gram))

    (pooled_part, correlation_part), learner_pull = jax.vjp(
        learner, block_out, vec_f[4], vec_f[5], w_map.astype(jnp.float32)
    )
    slots = jnp.zeros((4, D + 128), jnp.float32)
    mine = jnp.concatenate([pooled_part, jnp.full((128,), correlation_part)])
    totals = lax.psum(lax.dynamic_update_slice(slots, mine[None], (bi, 0)), both_axes)
    pooled_all, corr_all = totals[:, :D], totals[:, D]
    ids = lax.all_gather(jnp.concatenate([positive[:, None], negatives], axis=1).astype(jnp.float32), "batch", axis=0, tiled=True).astype(jnp.int32)
    total_count = jnp.sum(valid_tubelet_count).astype(jnp.float32)

    def head(pooled_in, gain_row, shift_row, proj_weight):
        pooled_mean = pooled_in / (NMAP * valid_tubelet_count).astype(jnp.float32)[:, None]
        normed, unused = norm_forward(pooled_mean, gain_row, shift_row)
        e = jnp.dot(normed, proj_weight, precision=HIGH_ACCURACY, preferred_element_type=jnp.float32)
        unit = e * lax.rsqrt(jnp.sum(e * e, -1, keepdims=True) + 1e-06)
        sim = jnp.einsum("yg,yeg->ye", unit, unit[ids], precision=HIGH_ACCURACY) / SOFTMAX_TEMPER
        return jnp.mean(jax.nn.logsumexp(sim, axis=1) - sim[:, 0])

    contrast, head_pull = jax.vjp(head, pooled_all, vec_f[6], vec_f[7], w_proj.astype(jnp.float32))
    d_pooled, g_final_gain, g_final_shift, g_proj = head_pull(jnp.ones_like(contrast))
    loss_value = contrast + DECAY_PENALTY * jnp.sum(corr_all) / total_count
    head_mask = (k == 0).astype(jnp.float32)
    d_mine = lax.dynamic_slice_in_dim(d_pooled, bi, 1, 0)[0]
    grad_block, g_learn_gain, g_learn_shift, g_map = learner_pull((d_mine, DECAY_PENALTY / total_count))
    g_mlp = to_bfloat(grad_block)
    g_down_bias = jnp.sum(g_mlp.astype(jnp.float32), 0)
    tn = (((0,), (0,)), ((), ()))
    nt = (((1,), (1,)), ((), ()))

    def mm(a, b_, dims):
        return lax.dot_general(a, b_, dims, preferred_element_type=jnp.float32)

    gw_down = mm(hidden_low, g_mlp, tn)
    (g_pre,) = gelu_pull(mm(g_mlp, w_down, nt))
    g_pre = to_bfloat(g_pre)
    g_up_bias = jnp.sum(g_pre.astype(jnp.float32), 0)
    gw_up = mm(h2, g_pre, tn)
    g_in_two, g_gain_two, g_shift_two = norm_backward(mm(g_pre, w_up, nt), vec_f[2], saved_two)
    g_second = grad_block + g_in_two
    g_attn = to_bfloat(g_second)
    g_out_bias = jnp.sum(g_attn.astype(jnp.float32), 0)
    gw_out = mm(attended, g_attn, tn)
    g_att = to_bfloat(mm(g_attn, w_out, nt))
    dog = jnp.stack([jnp.concatenate(pack_group(g_att, g), 0) for g in range(4)])
    dsp = attn_bwd(dog, bias, saved_attn, 3)
    g_qkv = jnp.concatenate(
        [
            unpack_x(dsp[:, ROWS[a] : ROWS[a] + TOK], dsp[:, ROWS[c] : ROWS[c] + CB])
            for a, c in (("q", "qc"), ("k", "kc"), ("v", "vc"))
        ],
        1,
    )
    g_query_bias = jnp.sum(g_qkv[:, :D].astype(jnp.float32), 0)
    g_value_bias = jnp.sum(g_qkv[:, 2 * D :].astype(jnp.float32), 0)
    gw_qkv = mm(h1, g_qkv, tn)
    g_in_one, g_gain_one, g_shift_one = norm_backward(mm(g_qkv, w_qkv, nt), vec_f[0], saved_one)
    g_entry = g_second + g_in_one
    gw_embed = mm(pix, to_bfloat(g_entry), tn)
    g_embed_bias = jnp.sum(g_entry, 0)
    g_pos = lax.dynamic_update_slice_in_dim(jnp.zeros((696, D), jnp.float32), g_entry, start_rows[0], 0)
    g_time = lax.dynamic_update_slice_in_dim(jnp.zeros((TMAX, D), jnp.float32), g_embed_bias[None], fi, 0)
    g_vec = jnp.stack(
        [g_gain_one, g_shift_one, g_gain_two, g_shift_two, g_learn_gain, g_learn_shift, g_final_gain * head_mask, g_final_shift * head_mask,
         g_embed_bias, g_query_bias, g_value_bias, g_out_bias, g_down_bias]
    )
    flat_tail = jnp.concatenate([v.reshape(-1).astype(jnp.bfloat16) for v in (g_map, g_pos, g_time, g_vec, g_up_bias)])
    flat_tail = jnp.pad(flat_tail, (0, 6144 * 128 - flat_tail.shape[0]))
    gtiles = jnp.concatenate(
        [to_tiles(w.astype(jnp.bfloat16)) for w in (gw_embed, gw_qkv, gw_out, gw_up, gw_down, g_proj * head_mask)]
        + [flat_tail.reshape(-1, 16, 128)]
    ).reshape(32, 144, 16, 128)
    summed = tiles_to_block(make_rs()(gtiles, 1), k)
    prev = lax.ppermute(summed[BLOCK - CARRY :], both_axes, [(i, i + 1) for i in range(31)])
    grad = lax.dynamic_slice(jnp.concatenate([prev, summed]), (CARRY - SLIDE * k,), (SHARD,))
    grad_norm = jnp.sqrt(lax.psum(jnp.sum(grad * grad), both_axes))
    clipped = grad * jnp.minimum(1.0, CLIP_AT / grad_norm)
    new_first = BETA_ONE * first_moment + (1.0 - BETA_ONE) * clipped
    new_second = BETA_TWO * second_moment + (1.0 - BETA_TWO) * clipped * clipped
    step = adam_step[0].astype(jnp.float32)
    update = new_first / (1.0 - BETA_ONE**step) / (jnp.sqrt(new_second / (1.0 - BETA_TWO**step)) + ADAM_EPS)
    new_master = master - RATE * (update + DECAY * master)
    return (new_master, new_first, new_second, to_bfloat(new_master), loss_value, grad_norm)


def solution(mesh):
    fast = dict(mesh.shape) == {"batch": 4, "frame": 8}
    return jax.shard_map(
        local_4x8 if fast else local_any_mesh,
        mesh=mesh,
        in_specs=(
            P("batch", "frame", None, None),
            P("batch"),
            P(),
            P("batch"),
            P("batch", None),
            P(("batch", "frame")),
            P(("batch", "frame")),
            P(("batch", "frame")),
            P(),
        ),
        out_specs=(
            P(("batch", "frame")),
            P(("batch", "frame")),
            P(("batch", "frame")),
            P(("batch", "frame")),
            P(),
            P(),
        ),
        check_vma=False,
    )
```

```python
from functools import partial
import math

import jax
import jax.numpy as jnp
from jax import lax
from jax.experimental import pallas as pl
from jax.experimental.pallas import tpu as pltpu
from jax.sharding import PartitionSpec as P

HEAD_COUNT = 12
HEAD_FEATURES = 64
FFW = 3072
TUBELET_PIXELS = 1536
EMB = 512
NMAP = 8
P0 = 100
P1 = 196
PATCHES_THIRD_2 = 400
TMAX = 64
NVEC = 13
CLIPS_PER_BATCH = 1


EPSILON = 1e-05
SOFTMAX_TEMPER = 0.02
DECAY_PENALTY = 1.0
CLIP_AT = 0.05
RATE = 0.03
DECAY = 0.05
BETA_ONE = 0.9
BETA_TWO = 0.999
ADAM_EPS = 1e-08
HIGH_ACCURACY = lax.Precision.HIGHEST


def to_bfloat(values):
    return values.astype(jnp.bfloat16)


def unpack_flat(flat_vector):
    width_of_model = HEAD_COUNT * HEAD_FEATURES
    dims_list = [
        (TUBELET_PIXELS, width_of_model),
        (width_of_model, 3 * width_of_model),
        (width_of_model, width_of_model),
        (width_of_model, FFW),
        (FFW, width_of_model),
        (width_of_model, EMB),
        (width_of_model, NMAP),
        (P0 + P1 + PATCHES_THIRD_2, width_of_model),
        (TMAX, width_of_model),
        (NVEC, width_of_model),
        (FFW,),
    ]
    pieces = []
    offset = 0
    for dims_of in dims_list:
        length = math.prod(dims_of)
        pieces.append(flat_vector[offset : offset + length].reshape(dims_of))
        offset += length
    return pieces


def norm_forward(inputs, gain_row, shift_row):
    center = inputs - jnp.mean(inputs, -1, keepdims=True)
    inverse = lax.rsqrt(jnp.mean(center * center, -1, keepdims=True) + EPSILON)
    normed = center * inverse
    return (normed * gain_row + shift_row, (normed, inverse))


def norm_backward(grad_out, gain_row, saved_parts):
    normed, inverse = saved_parts
    scaled = grad_out * gain_row
    grad_in = inverse * (
        scaled
        - jnp.mean(scaled, -1, keepdims=True)
        - normed * jnp.mean(scaled * normed, -1, keepdims=True)
    )
    lead_axes = tuple(range(grad_out.ndim - 1))
    return (grad_in, jnp.sum(grad_out * normed, lead_axes), jnp.sum(grad_out, lead_axes))


def block_plan(total_rows):
    shards = total_rows // PATCHES_THIRD_2
    group_size = 4
    return (shards // group_size, group_size * PATCHES_THIRD_2)


def local_any_mesh(
    pixels,
    res_class,
    valid_tubelet_count,
    positive,
    negatives,
    master,
    first_moment,
    second_moment,
    adam_step,
):
    width_of_model = HEAD_COUNT * HEAD_FEATURES
    score_scale = HEAD_FEATURES ** (-0.5)
    every_clip_rows = CLIPS_PER_BATCH * lax.axis_size("batch")
    index_of_batch = lax.axis_index("batch")
    frame_index = lax.axis_index("frame")
    gathered = lax.all_gather(to_bfloat(master), ("batch", "frame"), axis=0, tiled=True)
    w_embed, w_qkv, w_out, w_up, w_down, w_proj, w_map, pos_space, pos_time, vectors, bias_up = (
        unpack_flat(gathered)
    )
    vec_f = vectors.astype(jnp.float32)
    tubelet_stack = lax.dynamic_slice_in_dim(
        valid_tubelet_count, index_of_batch * CLIPS_PER_BATCH, CLIPS_PER_BATCH, 0
    )
    patches = jnp.where(res_class == 0, P0, jnp.where(res_class == 1, P1, PATCHES_THIRD_2)).astype(
        jnp.int32
    )
    start_rows = jnp.where(res_class == 0, 0, jnp.where(res_class == 1, P0, P0 + P1)).astype(
        jnp.int32
    )
    patch_pos = jnp.stack(
        [lax.dynamic_slice_in_dim(pos_space, start_rows[0], PATCHES_THIRD_2, 0)]
    ).astype(jnp.float32)
    time_row = lax.dynamic_slice_in_dim(pos_time, frame_index, 1, 0).astype(jnp.float32)
    rows_of_pixels = pixels.reshape(CLIPS_PER_BATCH * PATCHES_THIRD_2, TUBELET_PIXELS)
    embedded = jnp.dot(rows_of_pixels, w_embed, preferred_element_type=jnp.float32).reshape(
        CLIPS_PER_BATCH, PATCHES_THIRD_2, width_of_model
    )
    first_in = embedded + vec_f[8] + patch_pos + time_row
    normed_one, saved_one = norm_forward(first_in, vec_f[0], vec_f[1])
    normed_one = to_bfloat(normed_one)
    qkv_bias = jnp.concatenate([vec_f[9], jnp.zeros_like(vec_f[9]), vec_f[10]])
    projection_output = to_bfloat(
        jnp.einsum("cpd,de->cpe", normed_one, w_qkv, preferred_element_type=jnp.float32) + qkv_bias
    )
    query_matrix = projection_output[..., :width_of_model].reshape(
        CLIPS_PER_BATCH, PATCHES_THIRD_2, HEAD_COUNT, HEAD_FEATURES
    )
    kv_local = projection_output[..., width_of_model:]

    def key_mask(row_start, count_of_rows):
        row_ids = row_start + jnp.arange(count_of_rows, dtype=jnp.int32)
        return ((row_ids // PATCHES_THIRD_2)[None, :] < tubelet_stack[:, None]) & (
            (row_ids % PATCHES_THIRD_2)[None, :] < patches[:, None]
        )

    def block_scores(key_value_block, block_start):
        count_of_rows = key_value_block.shape[1]
        head_keys = key_value_block[..., :width_of_model].reshape(
            CLIPS_PER_BATCH, count_of_rows, HEAD_COUNT, HEAD_FEATURES
        )
        head_values = key_value_block[..., width_of_model:].reshape(
            CLIPS_PER_BATCH, count_of_rows, HEAD_COUNT, HEAD_FEATURES
        )
        key_ok = key_mask(block_start, count_of_rows)[:, None, None, :]
        scores = (
            jnp.einsum(
                "cqhd,ckhd->chqk", query_matrix, head_keys, preferred_element_type=jnp.float32
            )
            * score_scale
        )
        return (jnp.where(key_ok, scores, -1e30), key_ok, head_keys, head_values)

    forward_init = (
        jnp.full((CLIPS_PER_BATCH, HEAD_COUNT, PATCHES_THIRD_2), -1e30, jnp.float32),
        jnp.zeros((CLIPS_PER_BATCH, HEAD_COUNT, PATCHES_THIRD_2), jnp.float32),
        jnp.zeros((CLIPS_PER_BATCH, HEAD_COUNT, PATCHES_THIRD_2, HEAD_FEATURES), jnp.float32),
    )
    kv_piece = lax.all_gather(kv_local, "frame", axis=1, tiled=True)
    count_blocks, block_rows = block_plan(kv_piece.shape[1])

    def forward_one_block(block_index, running):
        run_max, run_sum, run_acc = running
        block_start = block_index * block_rows
        key_value_block = lax.dynamic_slice_in_dim(
            kv_piece, block_index * block_rows, block_rows, 1
        )
        scores, key_ok, head_keys, head_values = block_scores(key_value_block, block_start)
        new_max = jnp.maximum(run_max, jnp.max(scores, -1))
        factor = jnp.exp(run_max - new_max)
        prob_tile = jnp.where(key_ok, jnp.exp(scores - new_max[..., None]), 0.0)
        run_acc = run_acc * factor[..., None] + jnp.einsum(
            "chqk,ckhd->chqd", to_bfloat(prob_tile), head_values, preferred_element_type=jnp.float32
        )
        return (new_max, run_sum * factor + jnp.sum(prob_tile, -1), run_acc)

    run_max, run_sum, run_acc = lax.fori_loop(0, count_blocks, forward_one_block, forward_init)
    log_sum = run_max + jnp.log(run_sum)
    head_attended_rows = run_acc / run_sum[..., None]
    attended_reduced = to_bfloat(
        head_attended_rows.transpose(0, 2, 1, 3).reshape(
            CLIPS_PER_BATCH, PATCHES_THIRD_2, width_of_model
        )
    )
    second_in = (
        first_in
        + jnp.einsum("cpe,ed->cpd", attended_reduced, w_out, preferred_element_type=jnp.float32)
        + vec_f[11]
    )
    normed_two, saved_two = norm_forward(second_in, vec_f[2], vec_f[3])
    normed_two = to_bfloat(normed_two)
    hidden_pre = jnp.einsum(
        "cpd,df->cpf", normed_two, w_up, preferred_element_type=jnp.float32
    ) + bias_up.astype(jnp.float32)
    hidden_act, gelu_pull = jax.vjp(partial(jax.nn.gelu, approximate=False), hidden_pre)
    hidden_low = to_bfloat(hidden_act)
    block_out = (
        second_in
        + jnp.einsum("cpf,fd->cpd", hidden_low, w_down, preferred_element_type=jnp.float32)
        + vec_f[12]
    )
    valid_patch = jnp.arange(PATCHES_THIRD_2, dtype=jnp.int32)[None, :] < patches[:, None]
    slot_weight = (frame_index < tubelet_stack).astype(jnp.float32)

    def learner(block_in, gain_row, shift_row, map_weight):
        normed, unused = norm_forward(block_in, gain_row, shift_row)
        logits = jnp.einsum("cpd,dm->cpm", normed, map_weight, precision=HIGH_ACCURACY)
        logits = jnp.where(valid_patch[..., None], logits, -1e30)
        token_maps = jax.nn.softmax(logits, axis=1)
        pooled_part = jnp.einsum(
            "c,cpm,cpd->cd", slot_weight, token_maps, block_in, precision=HIGH_ACCURACY
        )
        gram_matrix = jnp.einsum("cpm,cpn->cmn", token_maps, token_maps, precision=HIGH_ACCURACY)
        correlation_part = slot_weight * (
            jnp.sum(gram_matrix, axis=(1, 2)) - jnp.trace(gram_matrix, axis1=1, axis2=2)
        )
        return (pooled_part, correlation_part)

    (pooled_part, correlation_part), learner_pull = jax.vjp(
        learner, block_out, vec_f[4], vec_f[5], w_map.astype(jnp.float32)
    )
    pooled_sum, correlation_sum = lax.psum((pooled_part, correlation_part), "frame")

    def head_map(pooled_in, gain_row, shift_row, proj_weight):
        pooled_mean = pooled_in / (NMAP * tubelet_stack).astype(jnp.float32)[:, None]
        normed, unused = norm_forward(pooled_mean, gain_row, shift_row)
        embedding = jnp.dot(
            normed, proj_weight, precision=HIGH_ACCURACY, preferred_element_type=jnp.float32
        )
        return embedding * lax.rsqrt(jnp.sum(embedding * embedding, -1, keepdims=True) + 1e-06)

    normalized_embedding, head_pull = jax.vjp(
        head_map, pooled_sum, vec_f[6], vec_f[7], w_proj.astype(jnp.float32)
    )
    embed_all, correlation_all = (
        lax.all_gather(normalized_embedding, "batch", axis=0, tiled=True),
        lax.all_gather(correlation_sum, "batch", axis=0, tiled=True),
    )
    selected_rows = jnp.concatenate([positive[:, None], negatives], axis=1)

    def contrast(embedding_input):
        local_row_set = lax.dynamic_slice_in_dim(
            embedding_input, index_of_batch * CLIPS_PER_BATCH, CLIPS_PER_BATCH, 0
        )
        similarity_matrix = (
            jnp.einsum(
                "yg,yeg->ye", local_row_set, embedding_input[selected_rows], precision=HIGH_ACCURACY
            )
            / SOFTMAX_TEMPER
        )
        return (
            jnp.sum(jax.nn.logsumexp(similarity_matrix, axis=1) - similarity_matrix[:, 0])
            / every_clip_rows
        )

    contrast_part, contrast_pull = jax.vjp(contrast, embed_all)
    (grad_embed_all,) = contrast_pull(jnp.ones_like(contrast_part))
    grad_unit = lax.psum_scatter(grad_embed_all, "batch", scatter_dimension=0, tiled=True)
    frame_total_count = jnp.sum(valid_tubelet_count).astype(jnp.float32)
    head_mask = (frame_index == 0).astype(jnp.float32)
    pooled_gradient, grad_final_gain, grad_final_shift, grad_proj = head_pull(grad_unit)
    grad_block, grad_learn_gain, grad_learn_shift, grad_map = learner_pull(
        (
            pooled_gradient,
            jnp.full((CLIPS_PER_BATCH,), DECAY_PENALTY / frame_total_count, jnp.float32),
        )
    )
    grad_mlp = to_bfloat(grad_block)
    grad_down_bias = jnp.sum(grad_mlp.astype(jnp.float32), (0, 1))
    grad_w_down = jnp.einsum(
        "cpf,cpd->fd", hidden_low, grad_mlp, preferred_element_type=jnp.float32
    )
    grad_hidden = jnp.einsum("cpd,fd->cpf", grad_mlp, w_down, preferred_element_type=jnp.float32)
    (grad_pre,) = gelu_pull(grad_hidden)
    grad_pre_low = to_bfloat(grad_pre)
    grad_up_bias = jnp.sum(grad_pre_low.astype(jnp.float32), (0, 1))
    grad_w_up = jnp.einsum(
        "cpd,cpf->df", normed_two, grad_pre_low, preferred_element_type=jnp.float32
    )
    grad_normed_two = jnp.einsum(
        "cpf,df->cpd", grad_pre_low, w_up, preferred_element_type=jnp.float32
    )
    grad_in_two, grad_gain_two, grad_shift_two = norm_backward(grad_normed_two, vec_f[2], saved_two)
    grad_second = grad_block + grad_in_two
    grad_attn = to_bfloat(grad_second)
    grad_out_bias = jnp.sum(grad_attn.astype(jnp.float32), (0, 1))
    grad_w_out = jnp.einsum(
        "cpe,cpd->ed", attended_reduced, grad_attn, preferred_element_type=jnp.float32
    )
    grad_attended = to_bfloat(
        jnp.einsum("cpd,ed->cpe", grad_attn, w_out, preferred_element_type=jnp.float32)
    ).reshape(CLIPS_PER_BATCH, PATCHES_THIRD_2, HEAD_COUNT, HEAD_FEATURES)
    row_delta = jnp.einsum("cqhd,chqd->chq", grad_attended.astype(jnp.float32), head_attended_rows)
    zeroed_query = jnp.zeros(
        (CLIPS_PER_BATCH, PATCHES_THIRD_2, HEAD_COUNT, HEAD_FEATURES), jnp.float32
    )
    query_kv_piece = lax.all_gather(kv_local, "frame", axis=1, tiled=True)
    count_blocks, query_block_rows = block_plan(query_kv_piece.shape[1])

    def query_one_block(block_index, query_gradient):
        block_start = block_index * query_block_rows
        key_value_block = lax.dynamic_slice_in_dim(
            query_kv_piece, block_index * query_block_rows, query_block_rows, 1
        )
        scores, key_ok, head_keys, head_values = block_scores(key_value_block, block_start)
        prob_tile = jnp.where(key_ok, jnp.exp(scores - log_sum[..., None]), 0.0)
        grad_prob = jnp.einsum(
            "cqhd,ckhd->chqk", grad_attended, head_values, preferred_element_type=jnp.float32
        )
        grad_score = to_bfloat(prob_tile * (grad_prob - row_delta[..., None]))
        return (
            query_gradient
            + jnp.einsum(
                "chqk,ckhd->cqhd", grad_score, head_keys, preferred_element_type=jnp.float32
            )
            * score_scale
        )

    query_gradient = lax.fori_loop(0, count_blocks, query_one_block, zeroed_query)
    own_keys = kv_local[..., :width_of_model].reshape(
        CLIPS_PER_BATCH, PATCHES_THIRD_2, HEAD_COUNT, HEAD_FEATURES
    )
    own_values = kv_local[..., width_of_model:].reshape(
        CLIPS_PER_BATCH, PATCHES_THIRD_2, HEAD_COUNT, HEAD_FEATURES
    )
    own_ok = key_mask(frame_index * PATCHES_THIRD_2, PATCHES_THIRD_2)[:, None, None, :]
    row_pieces = (
        query_matrix.astype(jnp.float32),
        grad_attended.astype(jnp.float32),
        log_sum.transpose(0, 2, 1),
        row_delta.transpose(0, 2, 1),
    )
    query_piece = lax.all_gather(
        row_pieces[0].astype(jnp.bfloat16), "frame", axis=1, tiled=True
    ).astype(jnp.float32)
    grad_out_piece = lax.all_gather(
        row_pieces[1].astype(jnp.bfloat16), "frame", axis=1, tiled=True
    ).astype(jnp.float32)
    lse_piece = lax.all_gather(
        row_pieces[2].astype(jnp.bfloat16), "frame", axis=1, tiled=True
    ).astype(jnp.float32)
    delta_piece = lax.all_gather(
        row_pieces[3].astype(jnp.bfloat16), "frame", axis=1, tiled=True
    ).astype(jnp.float32)
    count_blocks, own_block_rows = block_plan(query_piece.shape[1])

    def own_one_block(block_index, running):
        key_gradient, value_gradient = running
        offset = block_index * own_block_rows
        query_block = to_bfloat(lax.dynamic_slice_in_dim(query_piece, offset, own_block_rows, 1))
        grad_out_block = to_bfloat(
            lax.dynamic_slice_in_dim(grad_out_piece, offset, own_block_rows, 1)
        )
        lse_block = lax.dynamic_slice_in_dim(lse_piece, offset, own_block_rows, 1).transpose(
            0, 2, 1
        )
        delta_block = lax.dynamic_slice_in_dim(delta_piece, offset, own_block_rows, 1).transpose(
            0, 2, 1
        )
        scores = (
            jnp.einsum("cqhd,ckhd->chqk", query_block, own_keys, preferred_element_type=jnp.float32)
            * score_scale
        )
        scores = jnp.where(own_ok, scores, -1e30)
        prob_tile = jnp.where(own_ok, jnp.exp(scores - lse_block[..., None]), 0.0)
        grad_prob = jnp.einsum(
            "cqhd,ckhd->chqk", grad_out_block, own_values, preferred_element_type=jnp.float32
        )
        grad_score = to_bfloat(prob_tile * (grad_prob - delta_block[..., None]))
        key_gradient = (
            key_gradient
            + jnp.einsum(
                "chqk,cqhd->ckhd", grad_score, query_block, preferred_element_type=jnp.float32
            )
            * score_scale
        )
        value_gradient = value_gradient + jnp.einsum(
            "chqk,cqhd->ckhd",
            to_bfloat(prob_tile),
            grad_out_block,
            preferred_element_type=jnp.float32,
        )
        return (key_gradient, value_gradient)

    grad_key_own, grad_value_own = lax.fori_loop(
        0, count_blocks, own_one_block, (zeroed_query, zeroed_query)
    )
    gradient_key_value_local = to_bfloat(
        jnp.concatenate(
            [
                grad_key_own.reshape(CLIPS_PER_BATCH, PATCHES_THIRD_2, width_of_model),
                grad_value_own.reshape(CLIPS_PER_BATCH, PATCHES_THIRD_2, width_of_model),
            ],
            -1,
        )
    )
    gradient_query_key_value = jnp.concatenate(
        [
            to_bfloat(query_gradient).reshape(CLIPS_PER_BATCH, PATCHES_THIRD_2, width_of_model),
            gradient_key_value_local,
        ],
        -1,
    )
    grad_query_bias = jnp.sum(
        gradient_query_key_value[..., :width_of_model].astype(jnp.float32), (0, 1)
    )
    grad_value_bias = jnp.sum(
        gradient_query_key_value[..., 2 * width_of_model :].astype(jnp.float32), (0, 1)
    )
    grad_w_qkv = jnp.einsum(
        "cpd,cpe->de", normed_one, gradient_query_key_value, preferred_element_type=jnp.float32
    )
    grad_normed_one = jnp.einsum(
        "cpe,de->cpd", gradient_query_key_value, w_qkv, preferred_element_type=jnp.float32
    )
    grad_in_one, grad_gain_one, grad_shift_one = norm_backward(grad_normed_one, vec_f[0], saved_one)
    gradient_entry = grad_second + grad_in_one
    gradient_entry_low = to_bfloat(gradient_entry).reshape(
        CLIPS_PER_BATCH * PATCHES_THIRD_2, width_of_model
    )
    grad_w_embed = jnp.einsum(
        "rt,rd->td", rows_of_pixels, gradient_entry_low, preferred_element_type=jnp.float32
    )
    grad_embed_bias = jnp.sum(gradient_entry, (0, 1))
    grad_pos_space = jnp.zeros((P0 + P1 + PATCHES_THIRD_2, width_of_model), jnp.float32)
    current = lax.dynamic_slice_in_dim(grad_pos_space, start_rows[0], PATCHES_THIRD_2, 0)
    grad_pos_space = lax.dynamic_update_slice_in_dim(
        grad_pos_space, current + gradient_entry[0], start_rows[0], 0
    )
    grad_pos_time = lax.dynamic_update_slice_in_dim(
        jnp.zeros((TMAX, width_of_model), jnp.float32), grad_embed_bias[None], frame_index, 0
    )
    grad_vectors = jnp.stack(
        [
            grad_gain_one,
            grad_shift_one,
            grad_gain_two,
            grad_shift_two,
            grad_learn_gain,
            grad_learn_shift,
            grad_final_gain * head_mask,
            grad_final_shift * head_mask,
            grad_embed_bias,
            grad_query_bias,
            grad_value_bias,
            grad_out_bias,
            grad_down_bias,
        ]
    )
    flat_grad = jnp.concatenate(
        [
            piece_grad.reshape(-1)
            for piece_grad in (
                grad_w_embed,
                grad_w_qkv,
                grad_w_out,
                grad_w_up,
                grad_w_down,
                grad_proj * head_mask,
                grad_map,
                grad_pos_space,
                grad_pos_time,
                grad_vectors,
                grad_up_bias,
            )
        ]
    )
    grad_shard = lax.psum_scatter(flat_grad, ("batch", "frame"), scatter_dimension=0, tiled=True)
    contrast_keep = jnp.where(frame_index == 0, contrast_part, 0.0)
    square_sum, contrast_total = lax.psum(
        (jnp.sum(grad_shard * grad_shard), contrast_keep), ("batch", "frame")
    )
    grad_norm = jnp.sqrt(square_sum)
    loss_value = contrast_total + DECAY_PENALTY * jnp.sum(correlation_all) / frame_total_count
    clipped = grad_shard * jnp.minimum(1.0, CLIP_AT / grad_norm)
    new_first = BETA_ONE * first_moment + (1.0 - BETA_ONE) * clipped
    new_second = BETA_TWO * second_moment + (1.0 - BETA_TWO) * clipped * clipped
    step_count = adam_step[0].astype(jnp.float32)
    update = (
        new_first
        / (1.0 - BETA_ONE**step_count)
        / (jnp.sqrt(new_second / (1.0 - BETA_TWO**step_count)) + ADAM_EPS)
    )
    new_master = master - RATE * (update + DECAY * master)
    return (new_master, new_first, new_second, to_bfloat(new_master), loss_value, grad_norm)


MESH = pl.DeviceIdType.MESH
T=144
SPA=32

class Sends:
    def __init__(self, sem): self.sem=sem; self.n=0; self.items=[]
    def go(self, src, dst, rsem, dev, pred=None):
        c = pltpu.make_async_remote_copy(src_ref=src, dst_ref=dst, send_sem=self.sem.at[self.n], recv_sem=rsem, device_id=dev, device_id_type=MESH)
        self.n += 1
        if pred is None: c.start()
        else:
            @pl.when(pred)
            def _(): c.start()
        self.items.append((c,pred))
    def drain(self):
        for c,pred in self.items:
            if pred is None: c.wait_send()
            else:
                @pl.when(pred)
                def _(): c.wait_send()

def both(a,b):
    if a is None: return b
    if b is None: return a
    return jnp.logical_and(a,b)

def make_ag(spa=SPA):
    A=(0,spa); A1=(0,spa//2); A2=(spa//2,spa//2)
    nb=T-spa
    B=(spa,nb); B1=(spa,nb//2); B2=(spa+nb//2,nb//2)
    FULL=(0,T)
    def kernel(x_ref, out, ssem, lsem, zB, xB, yB, xBh, yBh, pA, zA, pown, pzB, pxB, pyB, pxBh, pyBh, ppA, pzA):
        b=lax.axis_index("batch"); f=lax.axis_index("frame")
        x=b%2; y=b//2; z=f//2; c=f%2
        bx=y*2+(1-x); by=(1-y)*2+x; bd=(1-y)*2+(1-x)
        X=(bx,f); Y=(by,f); Pn=(b,z*2+(1-c)); UP=(b,f+2); DN=(b,f-2)
        up=z<3; dn=z>0
        bar=pltpu.get_barrier_semaphore()
        for d,p in ((X,None),(Y,None),(Pn,None),(UP,up),(DN,dn)):
            if p is None: pl.semaphore_signal(bar,inc=1,device_id=d,device_id_type=MESH)
            else:
                @pl.when(p)
                def _(): pl.semaphore_signal(bar,inc=1,device_id=d,device_id_type=MESH)
        pl.semaphore_wait(bar, 4+(z*(3-z)+1)//3)
        S=Sends(ssem)
        def blk(bb,zz,part): return out.at[bb*8+zz*2+c, pl.ds(part[0],part[1])]
        def send(bb,zz,part,rsem,dev,pred=None,own=False):
            dst=blk(bb,zz,part)
            src=x_ref.at[pl.ds(part[0],part[1])] if own else dst
            S.go(src,dst,rsem,dev,pred)
        def wait(bb,zz,part,rsem):
            r=blk(bb,zz,part)
            pltpu.make_async_remote_copy(src_ref=r,dst_ref=r,send_sem=ssem.at[0],recv_sem=rsem,device_id=Pn,device_id_type=MESH).wait_recv()
        def waitp(pred,*a):
            if pred is None: wait(*a)
            else:
                @pl.when(pred)
                def _(): wait(*a)
        lc=pltpu.make_async_copy(x_ref, blk(b,z,FULL), lsem);
        send(b,z,A,pA.at[0],X,own=True); send(b,z,A,pA.at[1],Y,own=True)
        send(b,z,B,zB.at[z],UP,up,True); send(b,z,B,zB.at[z],DN,dn,True)
        send(b,z,B,xB.at[z],X,own=True); send(b,z,B,yB.at[z],Y,own=True)
        send(b,z,A,zA.at[z,0],UP,up,True); send(b,z,A,zA.at[z,0],DN,dn,True)
        send(b,z,FULL,pown.at[0],Pn,own=True)
        lc.start()
        pz=[]
        def pwait(*a): pz.append(a)
        pwait(None,b,z,FULL,pown.at[0])
        def zfwdA(bb,part,i,ps):
            send(bb,z,part,zA.at[z,i],UP,up); send(bb,z,part,zA.at[z,i],DN,dn)
            send(bb,z,part,ps,Pn); pwait(None,bb,z,part,ps)
        wait(bx,z,A,pA.at[0]); send(bx,z,A1,pA.at[2],Y); zfwdA(bx,A,1,ppA.at[0])
        wait(by,z,A,pA.at[1]); send(by,z,A2,pA.at[3],X); zfwdA(by,A,2,ppA.at[1])
        wait(bd,z,A1,pA.at[2]); zfwdA(bd,A1,3,ppA.at[2])
        wait(bd,z,A2,pA.at[3]); zfwdA(bd,A2,4,ppA.at[3])
        def xyB(zz,pred):
            waitp(pred,bx,zz,B,xB.at[zz]); send(bx,zz,B1,yBh.at[zz],Y,pred); send(bx,zz,B,pxB.at[zz],Pn,pred); pwait(pred,bx,zz,B,pxB.at[zz])
            waitp(pred,by,zz,B,yB.at[zz]); send(by,zz,B2,xBh.at[zz],X,pred); send(by,zz,B,pyB.at[zz],Pn,pred); pwait(pred,by,zz,B,pyB.at[zz])
        xyB(z,None)
        for d in (1,2,3):
            for s in (1,-1):
                zz=z+s*d
                pred=(zz<4) if s>0 else (zz>=0)
                nxt,np_=(DN,dn) if s>0 else (UP,up)
                waitp(pred,b,zz,B,zB.at[zz])
                send(b,zz,B,zB.at[zz],nxt,both(pred,np_))
                send(b,zz,B,xB.at[zz],X,pred); send(b,zz,B,yB.at[zz],Y,pred)
                send(b,zz,B,pzB.at[zz],Pn,pred); pwait(pred,b,zz,B,pzB.at[zz])
            for s in (1,-1):
                zz=z+s*d
                pred=(zz<4) if s>0 else (zz>=0)
                nxt,np_=(DN,dn) if s>0 else (UP,up)
                for i,(bb,part) in enumerate(((b,A),(bx,A),(by,A),(bd,A1),(bd,A2))):
                    waitp(pred,bb,zz,part,zA.at[zz,i]); send(bb,zz,part,zA.at[zz,i],nxt,both(pred,np_))
                    send(bb,zz,part,pzA.at[zz,i],Pn,pred); pwait(pred,bb,zz,part,pzA.at[zz,i])
            for s in (1,-1):
                zz=z+s*d
                pred=(zz<4) if s>0 else (zz>=0)
                xyB(zz,pred)
        for zz in range(4):
            wait(bd,zz,B1,yBh.at[zz]); send(bd,zz,B1,pyBh.at[zz],Pn); pwait(None,bd,zz,B1,pyBh.at[zz])
            wait(bd,zz,B2,xBh.at[zz]); send(bd,zz,B2,pxBh.at[zz],Pn); pwait(None,bd,zz,B2,pxBh.at[zz])
        for a in pz: waitp(*a)
        lc.wait()
        S.drain()
    D=pltpu.SemaphoreType.DMA
    def ag(xin, cid=0):
        return pl.pallas_call(kernel, out_shape=jax.ShapeDtypeStruct((32,T,16,128),jnp.bfloat16),
            in_specs=[pl.BlockSpec(memory_space=pltpu.VMEM)], out_specs=pl.BlockSpec(memory_space=pl.ANY),
            scratch_shapes=[D((160,)),D]+[D((4,))]*5+[D((4,)),D((4,5)),D((1,))]+[D((4,))]*5+[D((4,)),D((4,5))],
            compiler_params=pltpu.CompilerParams(collective_id=cid,has_side_effects=True))(xin)
    return ag


def make_rsx(spa=32):
    nb=T-spa
    A=(0,spa); A1=(0,spa//2); A2=(spa//2,spa//2)
    B=(spa,nb); B1=(spa,nb//2); B2=(spa+nb//2,nb//2)
    FULL=(0,T)
    def kernel(pix, h1, att, h2, act, dx0, dqkv, dattn, dpre, dmlp, tail, gout, nout,
               PS, R, h2T, LX, LY, LHX, LHY, LZB, LZA, LPA, out, C, CB_, CR_, NB, ssem, psem, stsem, csem, nsem, nsend, s_hx, s_hy, s_x, s_y, s_zb, s_za, s_pa):
        b=lax.axis_index("batch"); f=lax.axis_index("frame")
        x=b%2; y=b//2; z=f//2; c=f%2
        bx=y*2+(1-x); by=(1-y)*2+x; bd=(1-y)*2+(1-x)
        X=(bx,f); Y=(by,f); Pn=(b,z*2+(1-c)); UP=(b,f+2); DN=(b,f-2)
        up=z<3; dn=z>0
        t=z//2
        k=b*8+f
        def dev_of(kk): return (kk//8,kk%8)
        bar=pltpu.get_barrier_semaphore()
        def greet(d,_):
            pl.semaphore_signal(bar,inc=1,device_id=dev_of((k+d)%32),device_id_type=MESH); return 0
        lax.fori_loop(1,32,greet,0)
        zo=[3*(1-t), 2-t, (1-z)*(1-t)+(5-z)*t, z]
        order=[]
        for zz in zo: order += [(bd,zz)]
        for zz in zo: order += [(bx,zz),(by,zz)]
        for zz in zo: order += [(b,zz)]
        h2T[...]=h2[...].T
        TN_=(((0,),(0,)),((),()))
        def put(dst,r,m):
            rows=r.shape[0]
            r=r.astype(jnp.bfloat16)
            for s in range(rows//16):
                for j in range(m):
                    dst[s*m+j]=r[s*16:(s+1)*16,j*128:(j+1)*128]
        def col(a,i,n): return a[:,pl.ds(pl.multiple_of(i*n,128),n)]
        def comp(kk,dst):
            def mm(a,bb_,dims): return lax.dot_general(a,bb_,dims,preferred_element_type=jnp.float32)
            @pl.when(kk<4)
            def _(): put(dst,mm(col(pix,kk,384),dx0[...],TN_),6)
            @pl.when(jnp.logical_and(kk>=4,kk<10))
            def _(): put(dst,mm(col(h1,kk-4,128),dqkv[...],TN_),18)
            @pl.when(jnp.logical_and(kk>=10,kk<12))
            def _(): put(dst,mm(col(att,kk-10,384),dattn[...],TN_),6)
            @pl.when(jnp.logical_and(kk>=12,kk<20))
            def _(): put(dst,mm(h2T[pl.ds(pl.multiple_of((kk-12)*96,16),96)],dpre[...],(((1,),(0,)),((),()))),24)
            @pl.when(jnp.logical_and(kk>=20,kk<28))
            def _(): put(dst,mm(col(act,kk-20,384),dmlp[...],TN_),6)
            @pl.when(kk>=28)
            def _():
                def cp(i,_):
                    ds=pl.ds(i*8,8); dst[ds]=tail[kk-28,ds]; return 0
                lax.fori_loop(0,T//8,cp,0)
        def pick(i):
            g=jnp.where(i<4,i,jnp.where(i<12,(i-4)//2,i-12))
            zz=jnp.where(g==0,zo[0],jnp.where(g==1,zo[1],jnp.where(g==2,zo[2],zo[3])))
            bb=jnp.where(i<4,bd,jnp.where(i<12,jnp.where(i%2==0,bx,by),b))
            return bb,zz
        def pcopy(i):
            bb,zz=pick(i)
            return pltpu.make_async_remote_copy(src_ref=PS.at[16+i%4],dst_ref=R.at[bb,zz],send_sem=stsem.at[i%4],recv_sem=psem.at[bb,zz],device_id=Pn,device_id_type=MESH)
        def produce(h,_):
            i=h//2; own=h%2
            bb,zz=pick(i)
            @pl.when(own==0)
            def _():
                @pl.when(i>=4)
                def _(): pcopy(i-4).wait_send()
            kk=bb*8+zz*2+jnp.where(own==1,c,1-c)
            comp(kk,PS.at[jnp.where(own==1,bb*4+zz,16+i%4)])
            @pl.when(own==0)
            def _():
                @pl.when(i==0)
                def _(): pl.semaphore_wait(bar,31)
                pcopy(i).start()
            return 0
        lax.fori_loop(0,32,produce,0)
        S=Sends(ssem)
        def acc(dst, srcs, n, step=8):
            def body(i,_):
                ds=pl.ds(i*step,step)
                v=srcs[0][ds].astype(jnp.float32)
                for s in srcs[1:]: v=v+s[ds].astype(jnp.float32)
                dst[ds]=v.astype(dst.dtype)
                return 0
            lax.fori_loop(0,n//step,body,0)
        def sub(ref,part): return ref.at[pl.ds(part[0],part[1])]
        def ready(i):
            bb,zz=order[i]
            pltpu.make_async_remote_copy(src_ref=R.at[bb,zz],dst_ref=R.at[bb,zz],send_sem=ssem.at[0],recv_sem=psem.at[bb,zz],device_id=Pn,device_id_type=MESH).wait_recv()
        def wrecv(ref,sem):
            pltpu.make_async_remote_copy(src_ref=ref,dst_ref=ref,send_sem=ssem.at[0],recv_sem=sem,device_id=Pn,device_id_type=MESH).wait_recv()
        for i,zz in enumerate(zo):
            ready(i)
            acc(sub(PS.at[bd*4+zz],B), [sub(PS.at[bd*4+zz],B), sub(R.at[bd,zz],B)], nb)
            S.go(sub(PS.at[bd*4+zz],B1), LHY.at[zz], s_hy.at[zz], Y)
            S.go(sub(PS.at[bd*4+zz],B2), LHX.at[zz], s_hx.at[zz], X)
        def chainA(bi,bb):
            for d in (3,2,1):
                for s in (1,-1):
                    zz=z+s*d
                    pred=(zz<4) if s>0 else (zz>=0)
                    frm=dn if s>0 else up
                    dev=UP if s>0 else DN
                    di=0 if s>0 else 1
                    @pl.when(jnp.logical_and(pred,frm))
                    def _():
                        wrecv(LZA.at[di,zz,bi], s_za.at[di,zz,bi])
                        acc(sub(PS.at[bb*4+zz],A),[sub(PS.at[bb*4+zz],A),sub(R.at[bb,zz],A),LZA.at[di,zz,bi]],spa)
                    @pl.when(jnp.logical_and(pred,jnp.logical_not(frm)))
                    def _():
                        acc(sub(PS.at[bb*4+zz],A),[sub(PS.at[bb*4+zz],A),sub(R.at[bb,zz],A)],spa)
                    S.go(sub(PS.at[bb*4+zz],A), LZA.at[di,zz,bi], s_za.at[di,zz,bi], dev, pred)
        chainA(0,bd)
        for i,zz in enumerate(zo):
            ready(4+2*i); ready(5+2*i)
            wrecv(LHY.at[zz], s_hy.at[zz])
            acc(sub(PS.at[bx*4+zz],B1),[sub(PS.at[bx*4+zz],B1),sub(R.at[bx,zz],B1),LHY.at[zz]],nb//2)
            acc(sub(PS.at[bx*4+zz],B2),[sub(PS.at[bx*4+zz],B2),sub(R.at[bx,zz],B2)],nb//2)
            S.go(sub(PS.at[bx*4+zz],B), LX.at[zz], s_x.at[zz], X)
            wrecv(LHX.at[zz], s_hx.at[zz])
            acc(sub(PS.at[by*4+zz],B2),[sub(PS.at[by*4+zz],B2),sub(R.at[by,zz],B2),LHX.at[zz]],nb//2)
            acc(sub(PS.at[by*4+zz],B1),[sub(PS.at[by*4+zz],B1),sub(R.at[by,zz],B1)],nb//2)
            S.go(sub(PS.at[by*4+zz],B), LY.at[zz], s_y.at[zz], Y)
        chainA(1,bx); chainA(2,by)
        for i in range(4): ready(12+i)
        chainA(3,b)
        for i,zz in enumerate(zo[:3]):
            wrecv(LX.at[zz],s_x.at[zz]); wrecv(LY.at[zz],s_y.at[zz])
            isup=zz>z
            inc=jnp.logical_or(jnp.logical_and(isup,dn),jnp.logical_and(jnp.logical_not(isup),up))
            di=jnp.where(isup,0,1)
            base=[sub(PS.at[b*4+zz],B),sub(R.at[b,zz],B),LX.at[zz],LY.at[zz]]
            @pl.when(inc)
            def _():
                wrecv(LZB.at[di,zz],s_zb.at[di,zz])
                acc(sub(PS.at[b*4+zz],B),base+[LZB.at[di,zz]],nb)
            @pl.when(jnp.logical_not(inc))
            def _(): acc(sub(PS.at[b*4+zz],B),base,nb)
            S.go(sub(PS.at[b*4+zz],B),LZB.at[0,zz],s_zb.at[0,zz],UP,isup)
            S.go(sub(PS.at[b*4+zz],B),LZB.at[1,zz],s_zb.at[1,zz],DN,jnp.logical_not(isup))
        def totA(bi,bb,part,extra=(),dst=None):
            dst = dst if dst is not None else sub(PS.at[bb*4+z],part)
            srcs=[sub(PS.at[bb*4+z],part),sub(R.at[bb,z],part)]+list(extra)
            o=part[0]; n=part[1]
            l0=LZA.at[0,z,bi,pl.ds(o,n)]; l1=LZA.at[1,z,bi,pl.ds(o,n)]
            @pl.when(jnp.logical_and(up,dn))
            def _(): acc(dst,srcs+[l0,l1],n)
            @pl.when(jnp.logical_not(up))
            def _(): acc(dst,srcs+[l0],n)
            @pl.when(jnp.logical_not(dn))
            def _(): acc(dst,srcs+[l1],n)
        for bi in range(4):
            @pl.when(dn)
            def _(): wrecv(LZA.at[0,z,bi],s_za.at[0,z,bi])
            @pl.when(up)
            def _(): wrecv(LZA.at[1,z,bi],s_za.at[1,z,bi])
            if bi==0:
                totA(0,bd,A1); S.go(sub(PS.at[bd*4+z],A1),LPA.at[0,pl.ds(0,spa//2)],s_pa.at[0],Y)
                totA(0,bd,A2); S.go(sub(PS.at[bd*4+z],A2),LPA.at[1,pl.ds(0,spa//2)],s_pa.at[1],X)
            if bi==1:
                totA(1,bx,A2)
                wrecv(LPA.at[0,pl.ds(0,spa//2)],s_pa.at[0])
                totA(1,bx,A1,[LPA.at[0,pl.ds(0,spa//2)]])
                S.go(sub(PS.at[bx*4+z],A),LPA.at[2],s_pa.at[2],X)
            if bi==2:
                totA(2,by,A1)
                wrecv(LPA.at[1,pl.ds(0,spa//2)],s_pa.at[1])
                totA(2,by,A2,[LPA.at[1,pl.ds(0,spa//2)]])
                S.go(sub(PS.at[by*4+z],A),LPA.at[3],s_pa.at[3],Y)
        wrecv(LX.at[z],s_x.at[z]); wrecv(LY.at[z],s_y.at[z])
        base=[sub(PS.at[b*4+z],B),sub(R.at[b,z],B),LX.at[z],LY.at[z]]
        @pl.when(dn)
        def _(): wrecv(LZB.at[0,z],s_zb.at[0,z])
        @pl.when(up)
        def _(): wrecv(LZB.at[1,z],s_zb.at[1,z])
        @pl.when(jnp.logical_and(up,dn))
        def _(): acc(sub(out,B),base+[LZB.at[0,z],LZB.at[1,z]],nb)
        @pl.when(jnp.logical_not(up))
        def _(): acc(sub(out,B),base+[LZB.at[0,z]],nb)
        @pl.when(jnp.logical_not(dn))
        def _(): acc(sub(out,B),base+[LZB.at[1,z]],nb)
        wrecv(LPA.at[2],s_pa.at[2]); wrecv(LPA.at[3],s_pa.at[3])
        totA(3,b,A,[LPA.at[2],LPA.at[3]],dst=sub(out,A))
        def sq(i,a):
            v=out[i]; v=v*v
            return a+v[:8]+v[8:]
        NB[k]=lax.fori_loop(0,T,sq,jnp.zeros((8,128),jnp.float32))
        def ncopy(d):
            return pltpu.make_async_remote_copy(src_ref=NB.at[k],dst_ref=NB.at[k],send_sem=nsend.at[d],recv_sem=nsem.at[k],device_id=dev_of((k+d)%32),device_id_type=MESH)
        def nstart(d,_):
            ncopy(d).start(); return 0
        lax.fori_loop(1,32,nstart,0)
        CR=1440
        def untile(m,s0,n,t0):
            def body(s,_):
                for j in range(m):
                    C[pl.ds(CR+s0+s*16*m+j,16,stride=m),:]=out[t0+s*m+j]
                return 0
            lax.fori_loop(0,n,body,0)
        def plain(t0,n):
            def body(s,_):
                C[pl.ds(CR+(t0+s)*16,16),:]=out[t0+s]; return 0
            lax.fori_loop(0,n,body,0)
        def within(lo,hi): return jnp.logical_and(k>=lo,k<hi)
        @pl.when(jnp.logical_or(jnp.logical_or(within(0,4),within(10,12)),within(20,28)))
        def _(): untile(6,0,24,0)
        @pl.when(within(4,10))
        def _(): untile(18,0,8,0)
        @pl.when(within(12,20))
        def _(): untile(24,0,6,0)
        @pl.when(k==28)
        def _(): untile(4,0,36,0)
        @pl.when(k==29)
        def _():
            untile(4,0,12,0); plain(48,96)
        @pl.when(k>=30)
        def _(): plain(0,T)
        def carry(i,_):
            CB_[pl.ds(i*96,96)]=C[pl.ds(2304+i*96,96),:].astype(jnp.bfloat16); return 0
        lax.fori_loop(0,CR//96,carry,0)
        def cdesc(): return pltpu.make_async_remote_copy(src_ref=CB_,dst_ref=CR_,send_sem=csem.at[0],recv_sem=csem.at[1],device_id=dev_of((k+1)%32),device_id_type=MESH)
        @pl.when(k<31)
        def _(): cdesc().start()
        C[pl.ds(CR+2304,8),:]=jnp.zeros((8,128),jnp.float32)
        def nwait(d,_):
            kk=(k+d)%32
            wrecv_(NB.at[kk],nsem.at[kk],nsend.at[0],Pn); return 0
        lax.fori_loop(1,32,nwait,0)
        def nsum(i,a): return a+NB[i]
        nout[...]=lax.fori_loop(0,32,nsum,jnp.zeros((8,128),jnp.float32))
        @pl.when(k>0)
        def _():
            wrecv_(CR_,csem.at[1],csem.at[0],Pn)
            def uncarry(i,_):
                C[pl.ds(i*96,96),:]=CR_[pl.ds(i*96,96)].astype(jnp.float32); return 0
            lax.fori_loop(0,CR//96,uncarry,0)
        e=CR*128-(294912-289176)*k
        q=e//128; sh=e%128
        lane=lax.broadcasted_iota(jnp.int32,(96,128),1)
        def slide(i,_):
            r0=q+i*96
            a=pltpu.roll(C[pl.ds(r0,96),:],(128-sh)%128,1); b_=pltpu.roll(C[pl.ds(r0+1,96),:],(128-sh)%128,1)
            gout[pl.ds(i*96,96),:]=jnp.where(lane<128-sh,a,b_)
            return 0
        lax.fori_loop(0,24,slide,0)
        @pl.when(k<31)
        def _(): cdesc().wait_send()
        def ndone(d,_):
            ncopy(d).wait_send(); return 0
        lax.fori_loop(1,32,ndone,0)
        for i in range(12,16): pcopy(i).wait_send()
        S.drain()
    D=pltpu.SemaphoreType.DMA
    V=lambda *s: pltpu.VMEM(s+(16,128),jnp.bfloat16)
    VMs=pl.BlockSpec(memory_space=pltpu.VMEM)
    def rs(*args, cid=1):
        return pl.pallas_call(kernel, out_shape=(jax.ShapeDtypeStruct((2304,128),jnp.float32),jax.ShapeDtypeStruct((8,128),jnp.float32)),
            in_specs=[VMs]*11, out_specs=(VMs,VMs),
            scratch_shapes=[V(20,T),V(4,4,T),pltpu.VMEM((768,400),jnp.bfloat16),V(4,nb),V(4,nb),V(4,nb//2),V(4,nb//2),V(2,4,nb),V(2,4,4,spa),V(4,spa),
              pltpu.VMEM((T,16,128),jnp.float32),pltpu.VMEM((3752,128),jnp.float32),pltpu.VMEM((1440,128),jnp.bfloat16),pltpu.VMEM((1440,128),jnp.bfloat16),pltpu.VMEM((32,8,128),jnp.float32),
              D((80,)),D((4,4)),D((4,)),D((2,)),D((32,)),D((32,)),D((4,)),D((4,)),D((4,)),D((4,)),D((2,4)),D((2,4,4)),D((4,))],
            compiler_params=pltpu.CompilerParams(collective_id=cid,has_side_effects=True,vmem_limit_bytes=63*1024*1024))(*args)
    return rs

def wrecv_(ref,sem,ssem,dev):
    pltpu.make_async_remote_copy(src_ref=ref,dst_ref=ref,send_sem=ssem,recv_sem=sem,device_id=dev,device_id_type=MESH).wait_recv()


TOK=400; CB=208; NK=3200; NQ=1600; SUB=80; PADQ=512
ROWS={"q":0,"k":400,"v":800,"qc":1200,"kc":1408,"vc":1616}
NT=(((1,),(1,)),((),())); NN=(((1,),(0,)),((),())); TN=(((0,),(0,)),((),()))
f32=jnp.float32; bf16=jnp.bfloat16

def dot(a,b,dims): return lax.dot_general(a,b,dims,preferred_element_type=f32)

def mesh_pos():
    b=lax.axis_index("batch"); f=lax.axis_index("frame")
    return b,f//2,f%2

def zbarrier(b,z,c):
    bar=pltpu.get_barrier_semaphore()
    for d in (1,2,3):
        pl.semaphore_signal(bar,inc=1,device_id=(b,((z+d)%4)*2+c),device_id_type=MESH)
    pl.semaphore_signal(bar,inc=1,device_id=(b,z*2+1-c),device_id_type=MESH)
    pl.semaphore_wait(bar,4)

def wrecv(ref,sem,dev):
    pltpu.make_async_remote_copy(src_ref=ref,dst_ref=ref,send_sem=sem,recv_sem=sem,device_id=dev,device_id_type=MESH).wait_recv()

def others(z):
    return [((z+d)%4) for d in (2,1,3)]

def unpack_c(src, dst, row):
    v=src.astype(f32)
    lane=lax.broadcasted_iota(jnp.int32,(CB,128),1)
    lo=jnp.where(lane<64,v,0.0)
    hi=jnp.where(lane<64,pltpu.roll(v,64,1),0.0)
    dst[pl.ds(row,CB)]=lo.astype(bf16)
    dst[pl.ds(row+CB,TOK-CB)]=hi[:TOK-CB].astype(bf16)

def pack_c(lo, hi):
    hi=jnp.concatenate([hi,jnp.zeros((2*CB-TOK,128),f32)],0)
    lane=lax.broadcasted_iota(jnp.int32,(CB,128),1)
    return jnp.where(lane<64,lo,pltpu.roll(hi,64,1)).astype(bf16)

def fwd_kernel(sp, bias, og, Q, K, V, QC, KC, VC, OA, OC, LA, LC,
               QCp, KCp, VCp, OB, OCp, S, Pb, ssem, lsem, rq, rk, rv, rqc, rkc, rvc, pk, pv, pkc, pvc, ro, roc):
    b,z,c=mesh_pos()
    Pn=(b,z*2+1-c)
    dev=lambda zz:(b,zz*2+c)
    row=lambda zz: pl.multiple_of(zz*TOK,16)
    krow=lambda zz: pl.multiple_of((c*4+zz)*TOK,16)
    pkrow=lambda zz: pl.multiple_of(((1-c)*4+zz)*TOK,16)
    zbarrier(b,z,c)
    X=Sends(ssem)
    part=lambda g,n,ln: sp.at[g,pl.ds(ROWS[n],ln)]
    loc=[]
    def lcopy(src,dst):
        cp=pltpu.make_async_copy(src,dst,lsem.at[len(loc)]); cp.start(); loc.append(cp)
    for zz in others(z):
        X.go(part(zz,"k",TOK),K.at[pl.ds(krow(z),TOK)],rk.at[z],dev(zz))
        X.go(part(zz,"q",TOK),Q.at[pl.ds(row(z),TOK)],rq.at[z],dev(zz))
        X.go(part(zz,"v",TOK),V.at[pl.ds(krow(z),TOK)],rv.at[z],dev(zz))
    lcopy(part(z,"k",TOK),K.at[pl.ds(krow(z),TOK)])
    lcopy(part(z,"q",TOK),Q.at[pl.ds(row(z),TOK)])
    lcopy(part(z,"v",TOK),V.at[pl.ds(krow(z),TOK)])
    lcopy(part(z,"kc",CB),KCp.at[c*4+z]); lcopy(part(z,"qc",CB),QCp.at[z]); lcopy(part(z,"vc",CB),VCp.at[c*4+z])
    X.go(part(z,"k",TOK),K.at[pl.ds(krow(z),TOK)],pk.at[z],Pn)
    X.go(part(z,"v",TOK),V.at[pl.ds(krow(z),TOK)],pv.at[z],Pn)
    X.go(part(z,"kc",CB),KCp.at[c*4+z],pkc.at[z],Pn)
    X.go(part(z,"vc",CB),VCp.at[c*4+z],pvc.at[z],Pn)
    for zz in others(z):
        X.go(part(zz,"kc",CB),KCp.at[c*4+z],rkc.at[z],dev(zz))
        X.go(part(zz,"qc",CB),QCp.at[z],rqc.at[z],dev(zz))
        X.go(part(zz,"vc",CB),VCp.at[c*4+z],rvc.at[z],dev(zz))
    for zz in [((z+d)%4) for d in (1,3,2)]:
        kr=K.at[pl.ds(krow(zz),TOK)]; vr=V.at[pl.ds(krow(zz),TOK)]
        wrecv(kr,rk.at[zz],Pn); X.go(kr,kr,pk.at[zz],Pn)
        wrecv(vr,rv.at[zz],Pn); X.go(vr,vr,pv.at[zz],Pn)
    for zz in range(4):
        r=K.at[pl.ds(pkrow(zz),TOK)]; wrecv(r,pk.at[zz],Pn)
        r=V.at[pl.ds(pkrow(zz),TOK)]; wrecv(r,pv.at[zz],Pn)
    for zz in [((z+d)%4) for d in (1,2,3)]:
        wrecv(Q.at[pl.ds(row(zz),TOK)],rq.at[zz],Pn)
    for cp in loc: cp.wait()
    lane=lax.broadcasted_iota(jnp.int32,(TOK,128),1)
    lane8=lax.broadcasted_iota(jnp.int32,(SUB,128),1)
    def softmax(slot):
        def sub(i,carry):
            ds=pl.ds(pl.multiple_of(i*SUB,16),SUB)
            s=S[slot,ds,:]+bias[...]
            m=jnp.max(s,-1,keepdims=True)
            p=jnp.exp(s-m)
            l=jnp.sum(p,-1,keepdims=True)
            Pb[slot,ds,:]=p.astype(bf16)
            return m,l
        ms=[];ls=[]
        for i in range(TOK//SUB):
            m,l=sub(i,0); ms.append(m); ls.append(l)
        return jnp.concatenate(ms,0),jnp.concatenate(ls,0)
    def pairblock(i,_):
        ds=pl.ds(pl.multiple_of(i*TOK,16),TOK)
        q=Q[ds]
        zero=jnp.zeros_like(q)
        S[0]=dot(jnp.where(lane<64,q,zero),K[...],NT)
        S[1]=dot(jnp.where(lane<64,zero,q),K[...],NT)
        ma,la=softmax(0); mb,lb=softmax(1)
        oa=dot(Pb[0],V[...],NN)/la; ob=dot(Pb[1],V[...],NN)/lb
        o=jnp.where(lane<64,oa,ob)
        OA[ds]=o; OB[ds]=o.astype(bf16)
        LA[ds]=jnp.where(lane<64,ma+jnp.log(la),mb+jnp.log(lb))
        return 0
    lax.fori_loop(0,4,pairblock,0)
    for zz in [((z+d)%4) for d in (1,3,2)]:
        kr=KCp.at[c*4+zz]; vr=VCp.at[c*4+zz]
        wrecv(kr,rkc.at[zz],Pn); X.go(kr,kr,pkc.at[zz],Pn)
        wrecv(vr,rvc.at[zz],Pn); X.go(vr,vr,pvc.at[zz],Pn)
        wrecv(QCp.at[zz],rqc.at[zz],Pn)
    for zz in others(z):
        X.go(OB.at[pl.ds(row(zz),TOK)],og.at[z,pl.ds(0,TOK)],ro.at[z],dev(zz))
    lo=pltpu.make_async_copy(OB.at[pl.ds(row(z),TOK)],og.at[z,pl.ds(0,TOK)],lsem.at[6]); lo.start()
    for zz in range(4):
        wrecv(KCp.at[(1-c)*4+zz],pkc.at[zz],Pn); wrecv(VCp.at[(1-c)*4+zz],pvc.at[zz],Pn)
    def unp(i,_):
        r=pl.multiple_of(i*TOK,16)
        unpack_c(KCp[i],KC,r); unpack_c(VCp[i],VC,r)
        return 0
    lax.fori_loop(0,8,unp,0)
    def unq(i,_):
        unpack_c(QCp[i],QC,pl.multiple_of(i*TOK,16)); return 0
    lax.fori_loop(0,4,unq,0)
    def cblock(i,_):
        ds=pl.ds(pl.multiple_of(i*TOK,16),TOK)
        S[0]=dot(QC[ds],KC[...],NT)
        ma,la=softmax(0)
        o=dot(Pb[0],VC[...],NN)/la
        OC[ds]=o
        LC[ds]=jnp.broadcast_to(ma+jnp.log(la),(TOK,128))
        OCp[i]=pack_c(o[:CB],o[CB:])
        return 0
    lax.fori_loop(0,4,cblock,0)
    for zz in others(z):
        X.go(OCp.at[zz],og.at[z,pl.ds(TOK,CB)],roc.at[z],dev(zz))
    lc=pltpu.make_async_copy(OCp.at[z],og.at[z,pl.ds(TOK,CB)],lsem.at[7]); lc.start()
    for d in (1,2,3):
        zz=(z+d)%4
        wrecv(og.at[zz,pl.ds(0,TOK)],ro.at[zz],Pn)
        wrecv(og.at[zz,pl.ds(TOK,CB)],roc.at[zz],Pn)
    lo.wait(); lc.wait()
    X.drain()

D=pltpu.SemaphoreType.DMA
def vb(*s): return pltpu.VMEM(s,bf16)
def vf(*s): return pltpu.VMEM(s,f32)
VM=pl.BlockSpec(memory_space=pltpu.VMEM)
def sds(*s,d=bf16): return jax.ShapeDtypeStruct(s,d)

def attn_fwd(sp,bias,cid):
    return pl.pallas_call(fwd_kernel,
        out_shape=(sds(4,TOK+CB,128),sds(NQ,128),sds(NK,128),sds(NK,128),sds(NQ,128),sds(NK,128),sds(NK,128),
                   sds(NQ,128,d=f32),sds(NQ,128,d=f32),sds(NQ,128,d=f32),sds(NQ,128,d=f32)),
        in_specs=[VM,VM],out_specs=[VM]*11,
        scratch_shapes=[vb(4,CB,128),vb(8,CB,128),vb(8,CB,128),vb(NQ,128),vb(4,CB,128),vf(2,TOK,NK),vb(2,TOK,NK),
            D((48,)),D((8,))]+[D((4,))]*12,
        compiler_params=pltpu.CompilerParams(collective_id=cid,has_side_effects=True,vmem_limit_bytes=60*1024*1024))(sp,bias)

def bwd_kernel(dog, bias, Q, K, V, QC, KC, VC, OA, OC, LA, LC, dsp,
               DO, DOCp, DOC, S, P, DS, DKT, DVT, TT, DQ, DQC, XK, XV, YK, YV, SK, SV, HK, HV, XKC, XVC, YKC, YVC, HKC, HVC,
               ssem, lsem, rd, rdc, px, ho):
    b,z,c=mesh_pos()
    Pn=(b,z*2+1-c)
    dev=lambda zz:(b,zz*2+c)
    row=lambda zz: pl.multiple_of(zz*TOK,16)
    zbarrier(b,z,c)
    X=Sends(ssem)
    loc=[]
    def lcopy(src,dst):
        cp=pltpu.make_async_copy(src,dst,lsem.at[len(loc)]); cp.start(); loc.append(cp); return cp
    for zz in others(z):
        X.go(dog.at[zz,pl.ds(0,TOK)],DO.at[pl.ds(row(z),TOK)],rd.at[z],dev(zz))
    for zz in others(z):
        X.go(dog.at[zz,pl.ds(TOK,CB)],DOCp.at[z],rdc.at[z],dev(zz))
    l1=lcopy(dog.at[z,pl.ds(0,TOK)],DO.at[pl.ds(row(z),TOK)])
    l2=lcopy(dog.at[z,pl.ds(TOK,CB)],DOCp.at[z])
    l1.wait(); l2.wait()
    lane=lax.broadcasted_iota(jnp.int32,(TOK,128),1)
    def zero(ref):
        def bodyz(i,_):
            ref[:,pl.ds(pl.multiple_of(i*640,128),640)]=jnp.zeros((128,640),f32); return 0
        lax.fori_loop(0,NK//640,bodyz,0)
    def grads(q,k,v,do,lse,delta):
        S[0]=dot(q,k[...],NT)
        S[1]=dot(do,v[...],NT)
        for i in range(TOK//SUB):
            ds=pl.ds(i*SUB,SUB); sl=slice(i*SUB,(i+1)*SUB)
            p=jnp.exp(S[0,ds,:]+bias[...]-lse[sl])
            P[ds,:]=p.astype(bf16)
            DS[ds,:]=(p*(S[1,ds,:]-delta[sl])).astype(bf16)
        tail=jnp.zeros((PADQ-TOK,128),bf16)
        DKT[...]+=dot(jnp.concatenate([q,tail],0),DS[...],TN)
        DVT[...]+=dot(jnp.concatenate([do,tail],0),P[...],TN)
        return dot(DS[pl.ds(0,TOK)],k[...],NN)
    def home(src,r0,n,si):
        for zz in others(z):
            X.go(src(zz),dsp.at[z,pl.ds(r0,n)],ho.at[si,z],dev(zz))
        lcopy(src(z),dsp.at[z,pl.ds(r0,n)])
    mine=c*NQ; theirs=(1-c)*NQ
    def split(acc, x, own):
        def tr(i,_):
            TT[pl.ds(pl.multiple_of(i*640,16),640)]=acc[:,pl.ds(pl.multiple_of(i*640,128),640)].T
            return 0
        lax.fori_loop(0,NK//640,tr,0)
        def cut(i,_):
            r=pl.multiple_of(i*TOK,16)
            x[pl.ds(r,TOK)]=TT[pl.ds(pl.multiple_of(theirs+i*TOK,16),TOK)].astype(bf16)
            own[pl.ds(r,TOK)]=TT[pl.ds(pl.multiple_of(mine+i*TOK,16),TOK)]
            return 0
        lax.fori_loop(0,4,cut,0)
    P[pl.ds(TOK,PADQ-TOK)]=jnp.zeros((PADQ-TOK,NK),bf16)
    DS[pl.ds(TOK,PADQ-TOK)]=jnp.zeros((PADQ-TOK,NK),bf16)
    zero(DKT); zero(DVT)
    def pairblock(i,_):
        zz=(z+i)%4
        @pl.when(i>0)
        def _(): wrecv(DO.at[pl.ds(row(zz),TOK)],rd.at[zz],Pn)
        ds=pl.ds(row(zz),TOK)
        q=Q[ds]; do=DO[ds]; zero_=jnp.zeros_like(q)
        dof=do.astype(f32)*OA[ds]
        da=jnp.sum(jnp.where(lane<64,dof,0.0),-1,keepdims=True)
        db=jnp.sum(jnp.where(lane<64,0.0,dof),-1,keepdims=True)
        ga=grads(jnp.where(lane<64,q,zero_),K,V,jnp.where(lane<64,do,zero_),LA[ds,0:1],da)
        gb=grads(jnp.where(lane<64,zero_,q),K,V,jnp.where(lane<64,zero_,do),LA[ds,64:65],db)
        DQ[ds]=(jnp.where(lane<64,ga,gb)*0.125).astype(bf16)
        return 0
    lax.fori_loop(0,4,pairblock,0)
    home(lambda zz: DQ.at[pl.ds(row(zz),TOK)],0,TOK,0)
    split(DKT,XK,SK); X.go(XK,YK,px.at[0],Pn)
    split(DVT,XV,SV); X.go(XV,YV,px.at[1],Pn)
    zero(DKT); zero(DVT)
    def cblock(i,_):
        zz=(z+i)%4
        @pl.when(i>0)
        def _(): wrecv(DOCp.at[zz],rdc.at[zz],Pn)
        unpack_c(DOCp[zz],DOC,0)
        ds=pl.ds(row(zz),TOK)
        do=DOC[...]
        delta=jnp.sum(do.astype(f32)*OC[ds],-1,keepdims=True)
        g=grads(QC[ds],KC,VC,do,LC[ds,0:1],delta)*0.125
        DQC[zz]=pack_c(g[:CB],g[CB:])
        return 0
    lax.fori_loop(0,4,cblock,0)
    home(lambda zz: DQC.at[zz],ROWS["qc"],CB,1)
    wrecv(YK,px.at[0],Pn); wrecv(YV,px.at[1],Pn)
    def addp(i,_):
        ds=pl.ds(pl.multiple_of(i*TOK,16),TOK)
        HK[ds]=(SK[ds]+YK[ds].astype(f32)).astype(bf16)
        HV[ds]=(SV[ds]+YV[ds].astype(f32)).astype(bf16)
        return 0
    lax.fori_loop(0,4,addp,0)
    home(lambda zz: HK.at[pl.ds(row(zz),TOK)],ROWS["k"],TOK,2)
    home(lambda zz: HV.at[pl.ds(row(zz),TOK)],ROWS["v"],TOK,3)
    def splitc(acc, x, own):
        def tr(i,_):
            TT[pl.ds(pl.multiple_of(i*640,16),640)]=acc[:,pl.ds(pl.multiple_of(i*640,128),640)].T
            return 0
        lax.fori_loop(0,NK//640,tr,0)
        def cut(i,_):
            r=theirs+i*TOK
            x[i]=pack_c(TT[pl.ds(pl.multiple_of(r,16),CB)],TT[pl.ds(pl.multiple_of(r+CB,16),TOK-CB)])
            own[pl.ds(pl.multiple_of(i*TOK,16),TOK)]=TT[pl.ds(pl.multiple_of(mine+i*TOK,16),TOK)]
            return 0
        lax.fori_loop(0,4,cut,0)
    splitc(DKT,XKC,SK); X.go(XKC,YKC,px.at[2],Pn)
    splitc(DVT,XVC,SV); X.go(XVC,YVC,px.at[3],Pn)
    def addc(y,own,h):
        def body(i,_):
            unpack_c(y[i],DOC,0)
            r=i*TOK
            t=own[pl.ds(pl.multiple_of(r,16),TOK)]+DOC[...].astype(f32)
            h[i]=pack_c(t[:CB],t[CB:])
            return 0
        lax.fori_loop(0,4,body,0)
    wrecv(YKC,px.at[2],Pn); addc(YKC,SK,HKC)
    home(lambda zz: HKC.at[zz],ROWS["kc"],CB,4)
    wrecv(YVC,px.at[3],Pn); addc(YVC,SV,HVC)
    home(lambda zz: HVC.at[zz],ROWS["vc"],CB,5)
    for si,(r0,n) in enumerate(((0,TOK),(ROWS["qc"],CB),(ROWS["k"],TOK),(ROWS["v"],TOK),(ROWS["kc"],CB),(ROWS["vc"],CB))):
        for d in (1,2,3):
            zz=(z+d)%4
            wrecv(dsp.at[zz,pl.ds(r0,n)],ho.at[si,zz],Pn)
    for cp in loc[2:]: cp.wait()
    X.drain()

def attn_bwd(dog,bias,saved,cid):
    return pl.pallas_call(bwd_kernel,
        out_shape=sds(4,3*(TOK+CB),128),
        in_specs=[VM]*12,out_specs=VM,
        scratch_shapes=[vb(NQ,128),vb(4,CB,128),vb(TOK,128),vf(2,TOK,NK),vb(PADQ,NK),vb(PADQ,NK),vf(128,NK),vf(128,NK),vf(NK,128),
            vb(NQ,128),vb(4,CB,128)]+[vb(NQ,128)]*4+[vf(NQ,128)]*2+[vb(NQ,128)]*2+[vb(4,CB,128)]*6+[
            D((32,)),D((10,)),D((4,)),D((4,)),D((4,)),D((6,4))],
        compiler_params=pltpu.CompilerParams(collective_id=cid,has_side_effects=True,vmem_limit_bytes=60*1024*1024))(dog,bias,*saved)

PAIR=(0,256,384,640); CC=(128,192,512,576)
def pack_group(x,g):
    p=x[:,PAIR[g]:PAIR[g]+128]; ch=x[:,CC[g]:CC[g]+64]
    c=jnp.concatenate([ch[:CB],jnp.pad(ch[CB:],((0,2*CB-TOK),(0,0)))],1)
    return p,c
def pack_qkv(q,k,v):
    out=[]
    for g in range(4):
        qp,qc=pack_group(q,g); kp,kc=pack_group(k,g); vp,vc=pack_group(v,g)
        out.append(jnp.concatenate([qp,kp,vp,qc,kc,vc],0))
    return jnp.stack(out)
def unpack_group(p,c):
    ch=jnp.concatenate([c[:,:64],c[:TOK-CB,64:]],0)
    return p,ch
def unpack_x(ps,cs):
    u=[unpack_group(ps[g],cs[g])[1] for g in range(4)]
    return jnp.concatenate([ps[0],u[0],u[1],ps[1],ps[2],u[2],u[3],ps[3]],1)


SHARD = 289176
BLOCK = 294912
SLIDE = BLOCK - SHARD
CARRY = 32 * SLIDE
KEY_ORDER_C = 2


def to_tiles(matrix):
    rows, width = matrix.shape
    m = width // 128
    return matrix.reshape(rows // 16, 16, m, 128).transpose(0, 2, 1, 3).reshape(-1, 16, 128)


def from_tiles(tiles, width):
    m = width // 128
    return tiles.reshape(-1, m, 16, 128).transpose(0, 2, 1, 3).reshape(-1, width)


def block_to_tiles(flat, k):
    def of(width):
        return lambda v: to_tiles(v.reshape(-1, width))

    def split29(v):
        return jnp.concatenate([to_tiles(v[: 48 * 2048].reshape(-1, 512)), v[48 * 2048 :].reshape(-1, 16, 128)])

    branch = class_of(k)
    return lax.switch(branch, [of(768), of(2304), of(3072), of(512), split29, of(128)], flat)


def class_of(k):
    return jnp.where(
        k < 4, 0, jnp.where(k < 10, 1, jnp.where(k < 12, 0, jnp.where(k < 20, 2, jnp.where(k < 28, 0, jnp.where(k == 28, 3, jnp.where(k == 29, 4, 5))))))
    )


def tiles_to_block(tiles, k):
    def of(width):
        return lambda v: from_tiles(v, width).reshape(-1)

    def split29(v):
        return jnp.concatenate([from_tiles(v[:48], 512).reshape(-1), v[48:].reshape(-1)])

    return lax.switch(class_of(k), [of(768), of(2304), of(3072), of(512), split29, of(128)], tiles)


def local_4x8(
    pixels,
    res_class,
    valid_tubelet_count,
    positive,
    negatives,
    master,
    first_moment,
    second_moment,
    adam_step,
):
    D = HEAD_COUNT * HEAD_FEATURES
    both_axes = ("batch", "frame")
    bi = lax.axis_index("batch")
    fi = lax.axis_index("frame")
    k = bi * 8 + fi
    low = to_bfloat(master)
    nxt = lax.ppermute(low[:CARRY], both_axes, [(i + 1, i) for i in range(31)])
    block = lax.dynamic_slice(jnp.concatenate([low, nxt]), (SLIDE * k,), (BLOCK,))
    G = make_ag()(block_to_tiles(block, k), 0)
    w_embed = from_tiles(G[0:4].reshape(-1, 16, 128), D)
    w_qkv = from_tiles(G[4:10].reshape(-1, 16, 128), 3 * D)
    w_out = from_tiles(G[10:12].reshape(-1, 16, 128), D)
    w_up = from_tiles(G[12:20].reshape(-1, 16, 128), FFW)
    w_down = from_tiles(G[20:28].reshape(-1, 16, 128), D)
    rest = G[28:].reshape(-1, 16, 128)
    w_proj = from_tiles(rest[:192], EMB)
    tail = rest[192:].reshape(-1)
    w_map = tail[: D * NMAP].reshape(D, NMAP)
    off = D * NMAP
    pos_space = tail[off : off + 696 * D].reshape(696, D)
    off += 696 * D
    pos_time = tail[off : off + TMAX * D].reshape(TMAX, D)
    off += TMAX * D
    vec_f = tail[off : off + NVEC * D].reshape(NVEC, D).astype(jnp.float32)
    off += NVEC * D
    bias_up = tail[off : off + FFW]

    tubelets = lax.dynamic_slice_in_dim(valid_tubelet_count, bi, 1, 0)
    patches = jnp.where(res_class == 0, P0, jnp.where(res_class == 1, P1, PATCHES_THIRD_2)).astype(jnp.int32)
    start_rows = jnp.where(res_class == 0, 0, jnp.where(res_class == 1, P0, P0 + P1)).astype(jnp.int32)
    patch_pos = lax.dynamic_slice_in_dim(pos_space, start_rows[0], 400, 0).astype(jnp.float32)
    time_row = lax.dynamic_slice_in_dim(pos_time, fi, 1, 0).astype(jnp.float32)
    pix = pixels.reshape(400, TUBELET_PIXELS)
    first_in = jnp.dot(pix, w_embed, preferred_element_type=jnp.float32) + vec_f[8] + patch_pos + time_row
    h1, saved_one = norm_forward(first_in, vec_f[0], vec_f[1])
    h1 = to_bfloat(h1)
    qkv_bias = jnp.concatenate([vec_f[9], jnp.zeros_like(vec_f[9]), vec_f[10]])
    qkv = to_bfloat(jnp.dot(h1, w_qkv, preferred_element_type=jnp.float32) + qkv_bias)
    slot = jnp.arange(8, dtype=jnp.int32)
    slot_tubelet = (slot % 4) * 2 + slot // 4
    key_ok = (slot_tubelet[:, None] < tubelets[0]) & (jnp.arange(400, dtype=jnp.int32)[None] < patches[0])
    bias = jnp.where(key_ok.reshape(1, 3200), 0.0, -1e30).astype(jnp.float32)
    sp = pack_qkv((qkv[:, :D] * 0.125).astype(jnp.bfloat16), qkv[:, D : 2 * D], qkv[:, 2 * D :])
    og, *saved_attn = attn_fwd(sp, bias, 2)
    attended = unpack_x(og[:, :400], og[:, 400:])
    second_in = first_in + jnp.dot(attended, w_out, preferred_element_type=jnp.float32) + vec_f[11]
    h2, saved_two = norm_forward(second_in, vec_f[2], vec_f[3])
    h2 = to_bfloat(h2)
    hidden_pre = jnp.dot(h2, w_up, preferred_element_type=jnp.float32) + bias_up.astype(jnp.float32)
    hidden_act, gelu_pull = jax.vjp(partial(jax.nn.gelu, approximate=False), hidden_pre)
    hidden_low = to_bfloat(hidden_act)
    block_out = second_in + jnp.dot(hidden_low, w_down, preferred_element_type=jnp.float32) + vec_f[12]
    valid_patch = jnp.arange(400, dtype=jnp.int32) < patches[0]
    slot_weight = (fi < tubelets[0]).astype(jnp.float32)

    def learner(block_in, gain_row, shift_row, map_weight):
        normed, unused = norm_forward(block_in, gain_row, shift_row)
        logits = jnp.dot(normed, map_weight, precision=HIGH_ACCURACY)
        logits = jnp.where(valid_patch[:, None], logits, -1e30)
        token_maps = jax.nn.softmax(logits, axis=0)
        pooled_part = slot_weight * jnp.einsum("pm,pd->d", token_maps, block_in, precision=HIGH_ACCURACY)
        gram = jnp.einsum("pm,pn->mn", token_maps, token_maps, precision=HIGH_ACCURACY)
        return pooled_part, slot_weight * (jnp.sum(gram) - jnp.trace(gram))

    (pooled_part, correlation_part), learner_pull = jax.vjp(
        learner, block_out, vec_f[4], vec_f[5], w_map.astype(jnp.float32)
    )
    slots = jnp.zeros((4, D + 128), jnp.float32)
    mine = jnp.concatenate([pooled_part, jnp.full((128,), correlation_part)])
    totals = lax.psum(lax.dynamic_update_slice(slots, mine[None], (bi, 0)), both_axes)
    pooled_all, corr_all = totals[:, :D], totals[:, D]
    ids = lax.all_gather(jnp.concatenate([positive[:, None], negatives], axis=1).astype(jnp.float32), "batch", axis=0, tiled=True).astype(jnp.int32)
    total_count = jnp.sum(valid_tubelet_count).astype(jnp.float32)

    def head(pooled_in, gain_row, shift_row, proj_weight):
        pooled_mean = pooled_in / (NMAP * valid_tubelet_count).astype(jnp.float32)[:, None]
        normed, unused = norm_forward(pooled_mean, gain_row, shift_row)
        e = jnp.dot(normed, proj_weight, precision=HIGH_ACCURACY, preferred_element_type=jnp.float32)
        unit = e * lax.rsqrt(jnp.sum(e * e, -1, keepdims=True) + 1e-06)
        sim = jnp.einsum("yg,yeg->ye", unit, unit[ids], precision=HIGH_ACCURACY) / SOFTMAX_TEMPER
        return jnp.mean(jax.nn.logsumexp(sim, axis=1) - sim[:, 0])

    contrast, head_pull = jax.vjp(head, pooled_all, vec_f[6], vec_f[7], w_proj.astype(jnp.float32))
    d_pooled, g_final_gain, g_final_shift, g_proj = head_pull(jnp.ones_like(contrast))
    loss_value = contrast + DECAY_PENALTY * jnp.sum(corr_all) / total_count
    head_mask = (k == 0).astype(jnp.float32)
    d_mine = lax.dynamic_slice_in_dim(d_pooled, bi, 1, 0)[0]
    grad_block, g_learn_gain, g_learn_shift, g_map = learner_pull((d_mine, DECAY_PENALTY / total_count))
    g_mlp = to_bfloat(grad_block)
    g_down_bias = jnp.sum(g_mlp.astype(jnp.float32), 0)
    tn = (((0,), (0,)), ((), ()))
    nt = (((1,), (1,)), ((), ()))

    def mm(a, b_, dims):
        return lax.dot_general(a, b_, dims, preferred_element_type=jnp.float32)

    (g_pre,) = gelu_pull(mm(g_mlp, w_down, nt))
    g_pre = to_bfloat(g_pre)
    g_up_bias = jnp.sum(g_pre.astype(jnp.float32), 0)
    g_in_two, g_gain_two, g_shift_two = norm_backward(mm(g_pre, w_up, nt), vec_f[2], saved_two)
    g_second = grad_block + g_in_two
    g_attn = to_bfloat(g_second)
    g_out_bias = jnp.sum(g_attn.astype(jnp.float32), 0)
    g_att = to_bfloat(mm(g_attn, w_out, nt))
    dog = jnp.stack([jnp.concatenate(pack_group(g_att, g), 0) for g in range(4)])
    dsp = attn_bwd(dog, bias, saved_attn, 3)
    g_qkv = jnp.concatenate(
        [
            unpack_x(dsp[:, ROWS[a] : ROWS[a] + TOK], dsp[:, ROWS[c] : ROWS[c] + CB])
            for a, c in (("q", "qc"), ("k", "kc"), ("v", "vc"))
        ],
        1,
    )
    g_query_bias = jnp.sum(g_qkv[:, :D].astype(jnp.float32), 0)
    g_value_bias = jnp.sum(g_qkv[:, 2 * D :].astype(jnp.float32), 0)
    g_in_one, g_gain_one, g_shift_one = norm_backward(mm(g_qkv, w_qkv, nt), vec_f[0], saved_one)
    g_entry = g_second + g_in_one
    g_embed_bias = jnp.sum(g_entry, 0)
    g_pos = lax.dynamic_update_slice_in_dim(jnp.zeros((696, D), jnp.float32), g_entry, start_rows[0], 0)
    g_time = lax.dynamic_update_slice_in_dim(jnp.zeros((TMAX, D), jnp.float32), g_embed_bias[None], fi, 0)
    g_vec = jnp.stack(
        [g_gain_one, g_shift_one, g_gain_two, g_shift_two, g_learn_gain, g_learn_shift, g_final_gain * head_mask, g_final_shift * head_mask,
         g_embed_bias, g_query_bias, g_value_bias, g_out_bias, g_down_bias]
    )
    flat_tail = jnp.concatenate([v.reshape(-1).astype(jnp.bfloat16) for v in (g_map, g_pos, g_time, g_vec, g_up_bias)])
    flat_tail = jnp.pad(flat_tail, (0, 6144 * 128 - flat_tail.shape[0]))
    tail_tiles = jnp.concatenate([to_tiles((g_proj * head_mask).astype(jnp.bfloat16)), flat_tail.reshape(-1, 16, 128)])
    grad, squares = make_rsx()(
        pix, h1, attended, h2, hidden_low, to_bfloat(g_entry), g_qkv, g_attn, g_pre, g_mlp, tail_tiles.reshape(4, 144, 16, 128), cid=1
    )
    grad = grad.reshape(-1)[:SHARD]
    grad_norm = jnp.sqrt(jnp.sum(squares))
    clipped = grad * jnp.minimum(1.0, CLIP_AT / grad_norm)
    new_first = BETA_ONE * first_moment + (1.0 - BETA_ONE) * clipped
    new_second = BETA_TWO * second_moment + (1.0 - BETA_TWO) * clipped * clipped
    step = adam_step[0].astype(jnp.float32)
    update = new_first / (1.0 - BETA_ONE**step) / (jnp.sqrt(new_second / (1.0 - BETA_TWO**step)) + ADAM_EPS)
    new_master = master - RATE * (update + DECAY * master)
    return (new_master, new_first, new_second, to_bfloat(new_master), loss_value, grad_norm)


def solution(mesh):
    fast = dict(mesh.shape) == {"batch": 4, "frame": 8}
    return jax.shard_map(
        local_4x8 if fast else local_any_mesh,
        mesh=mesh,
        in_specs=(
            P("batch", "frame", None, None),
            P("batch"),
            P(),
            P("batch"),
            P("batch", None),
            P(("batch", "frame")),
            P(("batch", "frame")),
            P(("batch", "frame")),
            P(),
        ),
        out_specs=(
            P(("batch", "frame")),
            P(("batch", "frame")),
            P(("batch", "frame")),
            P(("batch", "frame")),
            P(),
            P(),
        ),
        check_vma=False,
    )
```

```python
from functools import partial
import math

import jax
import jax.numpy as jnp
from jax import lax
from jax.experimental import pallas as pl
from jax.experimental.pallas import tpu as pltpu
from jax.sharding import PartitionSpec as P

HEAD_COUNT = 12
HEAD_FEATURES = 64
FFW = 3072
TUBELET_PIXELS = 1536
EMB = 512
NMAP = 8
P0 = 100
P1 = 196
PATCHES_THIRD_2 = 400
TMAX = 64
NVEC = 13
CLIPS_PER_BATCH = 1


EPSILON = 1e-05
SOFTMAX_TEMPER = 0.02
DECAY_PENALTY = 1.0
CLIP_AT = 0.05
RATE = 0.03
DECAY = 0.05
BETA_ONE = 0.9
BETA_TWO = 0.999
ADAM_EPS = 1e-08
HIGH_ACCURACY = lax.Precision.HIGHEST


def to_bfloat(values):
    return values.astype(jnp.bfloat16)


def unpack_flat(flat_vector):
    width_of_model = HEAD_COUNT * HEAD_FEATURES
    dims_list = [
        (TUBELET_PIXELS, width_of_model),
        (width_of_model, 3 * width_of_model),
        (width_of_model, width_of_model),
        (width_of_model, FFW),
        (FFW, width_of_model),
        (width_of_model, EMB),
        (width_of_model, NMAP),
        (P0 + P1 + PATCHES_THIRD_2, width_of_model),
        (TMAX, width_of_model),
        (NVEC, width_of_model),
        (FFW,),
    ]
    pieces = []
    offset = 0
    for dims_of in dims_list:
        length = math.prod(dims_of)
        pieces.append(flat_vector[offset : offset + length].reshape(dims_of))
        offset += length
    return pieces


def norm_forward(inputs, gain_row, shift_row):
    center = inputs - jnp.mean(inputs, -1, keepdims=True)
    inverse = lax.rsqrt(jnp.mean(center * center, -1, keepdims=True) + EPSILON)
    normed = center * inverse
    return (normed * gain_row + shift_row, (normed, inverse))


def norm_backward(grad_out, gain_row, saved_parts):
    normed, inverse = saved_parts
    scaled = grad_out * gain_row
    grad_in = inverse * (
        scaled
        - jnp.mean(scaled, -1, keepdims=True)
        - normed * jnp.mean(scaled * normed, -1, keepdims=True)
    )
    lead_axes = tuple(range(grad_out.ndim - 1))
    return (grad_in, jnp.sum(grad_out * normed, lead_axes), jnp.sum(grad_out, lead_axes))


def block_plan(total_rows):
    shards = total_rows // PATCHES_THIRD_2
    group_size = 4
    return (shards // group_size, group_size * PATCHES_THIRD_2)


def local_any_mesh(
    pixels,
    res_class,
    valid_tubelet_count,
    positive,
    negatives,
    master,
    first_moment,
    second_moment,
    adam_step,
):
    width_of_model = HEAD_COUNT * HEAD_FEATURES
    score_scale = HEAD_FEATURES ** (-0.5)
    every_clip_rows = CLIPS_PER_BATCH * lax.axis_size("batch")
    index_of_batch = lax.axis_index("batch")
    frame_index = lax.axis_index("frame")
    gathered = lax.all_gather(to_bfloat(master), ("batch", "frame"), axis=0, tiled=True)
    w_embed, w_qkv, w_out, w_up, w_down, w_proj, w_map, pos_space, pos_time, vectors, bias_up = (
        unpack_flat(gathered)
    )
    vec_f = vectors.astype(jnp.float32)
    tubelet_stack = lax.dynamic_slice_in_dim(
        valid_tubelet_count, index_of_batch * CLIPS_PER_BATCH, CLIPS_PER_BATCH, 0
    )
    patches = jnp.where(res_class == 0, P0, jnp.where(res_class == 1, P1, PATCHES_THIRD_2)).astype(
        jnp.int32
    )
    start_rows = jnp.where(res_class == 0, 0, jnp.where(res_class == 1, P0, P0 + P1)).astype(
        jnp.int32
    )
    patch_pos = jnp.stack(
        [lax.dynamic_slice_in_dim(pos_space, start_rows[0], PATCHES_THIRD_2, 0)]
    ).astype(jnp.float32)
    time_row = lax.dynamic_slice_in_dim(pos_time, frame_index, 1, 0).astype(jnp.float32)
    rows_of_pixels = pixels.reshape(CLIPS_PER_BATCH * PATCHES_THIRD_2, TUBELET_PIXELS)
    embedded = jnp.dot(rows_of_pixels, w_embed, preferred_element_type=jnp.float32).reshape(
        CLIPS_PER_BATCH, PATCHES_THIRD_2, width_of_model
    )
    first_in = embedded + vec_f[8] + patch_pos + time_row
    normed_one, saved_one = norm_forward(first_in, vec_f[0], vec_f[1])
    normed_one = to_bfloat(normed_one)
    qkv_bias = jnp.concatenate([vec_f[9], jnp.zeros_like(vec_f[9]), vec_f[10]])
    projection_output = to_bfloat(
        jnp.einsum("cpd,de->cpe", normed_one, w_qkv, preferred_element_type=jnp.float32) + qkv_bias
    )
    query_matrix = projection_output[..., :width_of_model].reshape(
        CLIPS_PER_BATCH, PATCHES_THIRD_2, HEAD_COUNT, HEAD_FEATURES
    )
    kv_local = projection_output[..., width_of_model:]

    def key_mask(row_start, count_of_rows):
        row_ids = row_start + jnp.arange(count_of_rows, dtype=jnp.int32)
        return ((row_ids // PATCHES_THIRD_2)[None, :] < tubelet_stack[:, None]) & (
            (row_ids % PATCHES_THIRD_2)[None, :] < patches[:, None]
        )

    def block_scores(key_value_block, block_start):
        count_of_rows = key_value_block.shape[1]
        head_keys = key_value_block[..., :width_of_model].reshape(
            CLIPS_PER_BATCH, count_of_rows, HEAD_COUNT, HEAD_FEATURES
        )
        head_values = key_value_block[..., width_of_model:].reshape(
            CLIPS_PER_BATCH, count_of_rows, HEAD_COUNT, HEAD_FEATURES
        )
        key_ok = key_mask(block_start, count_of_rows)[:, None, None, :]
        scores = (
            jnp.einsum(
                "cqhd,ckhd->chqk", query_matrix, head_keys, preferred_element_type=jnp.float32
            )
            * score_scale
        )
        return (jnp.where(key_ok, scores, -1e30), key_ok, head_keys, head_values)

    forward_init = (
        jnp.full((CLIPS_PER_BATCH, HEAD_COUNT, PATCHES_THIRD_2), -1e30, jnp.float32),
        jnp.zeros((CLIPS_PER_BATCH, HEAD_COUNT, PATCHES_THIRD_2), jnp.float32),
        jnp.zeros((CLIPS_PER_BATCH, HEAD_COUNT, PATCHES_THIRD_2, HEAD_FEATURES), jnp.float32),
    )
    kv_piece = lax.all_gather(kv_local, "frame", axis=1, tiled=True)
    count_blocks, block_rows = block_plan(kv_piece.shape[1])

    def forward_one_block(block_index, running):
        run_max, run_sum, run_acc = running
        block_start = block_index * block_rows
        key_value_block = lax.dynamic_slice_in_dim(
            kv_piece, block_index * block_rows, block_rows, 1
        )
        scores, key_ok, head_keys, head_values = block_scores(key_value_block, block_start)
        new_max = jnp.maximum(run_max, jnp.max(scores, -1))
        factor = jnp.exp(run_max - new_max)
        prob_tile = jnp.where(key_ok, jnp.exp(scores - new_max[..., None]), 0.0)
        run_acc = run_acc * factor[..., None] + jnp.einsum(
            "chqk,ckhd->chqd", to_bfloat(prob_tile), head_values, preferred_element_type=jnp.float32
        )
        return (new_max, run_sum * factor + jnp.sum(prob_tile, -1), run_acc)

    run_max, run_sum, run_acc = lax.fori_loop(0, count_blocks, forward_one_block, forward_init)
    log_sum = run_max + jnp.log(run_sum)
    head_attended_rows = run_acc / run_sum[..., None]
    attended_reduced = to_bfloat(
        head_attended_rows.transpose(0, 2, 1, 3).reshape(
            CLIPS_PER_BATCH, PATCHES_THIRD_2, width_of_model
        )
    )
    second_in = (
        first_in
        + jnp.einsum("cpe,ed->cpd", attended_reduced, w_out, preferred_element_type=jnp.float32)
        + vec_f[11]
    )
    normed_two, saved_two = norm_forward(second_in, vec_f[2], vec_f[3])
    normed_two = to_bfloat(normed_two)
    hidden_pre = jnp.einsum(
        "cpd,df->cpf", normed_two, w_up, preferred_element_type=jnp.float32
    ) + bias_up.astype(jnp.float32)
    hidden_act, gelu_pull = jax.vjp(partial(jax.nn.gelu, approximate=False), hidden_pre)
    hidden_low = to_bfloat(hidden_act)
    block_out = (
        second_in
        + jnp.einsum("cpf,fd->cpd", hidden_low, w_down, preferred_element_type=jnp.float32)
        + vec_f[12]
    )
    valid_patch = jnp.arange(PATCHES_THIRD_2, dtype=jnp.int32)[None, :] < patches[:, None]
    slot_weight = (frame_index < tubelet_stack).astype(jnp.float32)

    def learner(block_in, gain_row, shift_row, map_weight):
        normed, unused = norm_forward(block_in, gain_row, shift_row)
        logits = jnp.einsum("cpd,dm->cpm", normed, map_weight, precision=HIGH_ACCURACY)
        logits = jnp.where(valid_patch[..., None], logits, -1e30)
        token_maps = jax.nn.softmax(logits, axis=1)
        pooled_part = jnp.einsum(
            "c,cpm,cpd->cd", slot_weight, token_maps, block_in, precision=HIGH_ACCURACY
        )
        gram_matrix = jnp.einsum("cpm,cpn->cmn", token_maps, token_maps, precision=HIGH_ACCURACY)
        correlation_part = slot_weight * (
            jnp.sum(gram_matrix, axis=(1, 2)) - jnp.trace(gram_matrix, axis1=1, axis2=2)
        )
        return (pooled_part, correlation_part)

    (pooled_part, correlation_part), learner_pull = jax.vjp(
        learner, block_out, vec_f[4], vec_f[5], w_map.astype(jnp.float32)
    )
    pooled_sum, correlation_sum = lax.psum((pooled_part, correlation_part), "frame")

    def head_map(pooled_in, gain_row, shift_row, proj_weight):
        pooled_mean = pooled_in / (NMAP * tubelet_stack).astype(jnp.float32)[:, None]
        normed, unused = norm_forward(pooled_mean, gain_row, shift_row)
        embedding = jnp.dot(
            normed, proj_weight, precision=HIGH_ACCURACY, preferred_element_type=jnp.float32
        )
        return embedding * lax.rsqrt(jnp.sum(embedding * embedding, -1, keepdims=True) + 1e-06)

    normalized_embedding, head_pull = jax.vjp(
        head_map, pooled_sum, vec_f[6], vec_f[7], w_proj.astype(jnp.float32)
    )
    embed_all, correlation_all = (
        lax.all_gather(normalized_embedding, "batch", axis=0, tiled=True),
        lax.all_gather(correlation_sum, "batch", axis=0, tiled=True),
    )
    selected_rows = jnp.concatenate([positive[:, None], negatives], axis=1)

    def contrast(embedding_input):
        local_row_set = lax.dynamic_slice_in_dim(
            embedding_input, index_of_batch * CLIPS_PER_BATCH, CLIPS_PER_BATCH, 0
        )
        similarity_matrix = (
            jnp.einsum(
                "yg,yeg->ye", local_row_set, embedding_input[selected_rows], precision=HIGH_ACCURACY
            )
            / SOFTMAX_TEMPER
        )
        return (
            jnp.sum(jax.nn.logsumexp(similarity_matrix, axis=1) - similarity_matrix[:, 0])
            / every_clip_rows
        )

    contrast_part, contrast_pull = jax.vjp(contrast, embed_all)
    (grad_embed_all,) = contrast_pull(jnp.ones_like(contrast_part))
    grad_unit = lax.psum_scatter(grad_embed_all, "batch", scatter_dimension=0, tiled=True)
    frame_total_count = jnp.sum(valid_tubelet_count).astype(jnp.float32)
    head_mask = (frame_index == 0).astype(jnp.float32)
    pooled_gradient, grad_final_gain, grad_final_shift, grad_proj = head_pull(grad_unit)
    grad_block, grad_learn_gain, grad_learn_shift, grad_map = learner_pull(
        (
            pooled_gradient,
            jnp.full((CLIPS_PER_BATCH,), DECAY_PENALTY / frame_total_count, jnp.float32),
        )
    )
    grad_mlp = to_bfloat(grad_block)
    grad_down_bias = jnp.sum(grad_mlp.astype(jnp.float32), (0, 1))
    grad_w_down = jnp.einsum(
        "cpf,cpd->fd", hidden_low, grad_mlp, preferred_element_type=jnp.float32
    )
    grad_hidden = jnp.einsum("cpd,fd->cpf", grad_mlp, w_down, preferred_element_type=jnp.float32)
    (grad_pre,) = gelu_pull(grad_hidden)
    grad_pre_low = to_bfloat(grad_pre)
    grad_up_bias = jnp.sum(grad_pre_low.astype(jnp.float32), (0, 1))
    grad_w_up = jnp.einsum(
        "cpd,cpf->df", normed_two, grad_pre_low, preferred_element_type=jnp.float32
    )
    grad_normed_two = jnp.einsum(
        "cpf,df->cpd", grad_pre_low, w_up, preferred_element_type=jnp.float32
    )
    grad_in_two, grad_gain_two, grad_shift_two = norm_backward(grad_normed_two, vec_f[2], saved_two)
    grad_second = grad_block + grad_in_two
    grad_attn = to_bfloat(grad_second)
    grad_out_bias = jnp.sum(grad_attn.astype(jnp.float32), (0, 1))
    grad_w_out = jnp.einsum(
        "cpe,cpd->ed", attended_reduced, grad_attn, preferred_element_type=jnp.float32
    )
    grad_attended = to_bfloat(
        jnp.einsum("cpd,ed->cpe", grad_attn, w_out, preferred_element_type=jnp.float32)
    ).reshape(CLIPS_PER_BATCH, PATCHES_THIRD_2, HEAD_COUNT, HEAD_FEATURES)
    row_delta = jnp.einsum("cqhd,chqd->chq", grad_attended.astype(jnp.float32), head_attended_rows)
    zeroed_query = jnp.zeros(
        (CLIPS_PER_BATCH, PATCHES_THIRD_2, HEAD_COUNT, HEAD_FEATURES), jnp.float32
    )
    query_kv_piece = lax.all_gather(kv_local, "frame", axis=1, tiled=True)
    count_blocks, query_block_rows = block_plan(query_kv_piece.shape[1])

    def query_one_block(block_index, query_gradient):
        block_start = block_index * query_block_rows
        key_value_block = lax.dynamic_slice_in_dim(
            query_kv_piece, block_index * query_block_rows, query_block_rows, 1
        )
        scores, key_ok, head_keys, head_values = block_scores(key_value_block, block_start)
        prob_tile = jnp.where(key_ok, jnp.exp(scores - log_sum[..., None]), 0.0)
        grad_prob = jnp.einsum(
            "cqhd,ckhd->chqk", grad_attended, head_values, preferred_element_type=jnp.float32
        )
        grad_score = to_bfloat(prob_tile * (grad_prob - row_delta[..., None]))
        return (
            query_gradient
            + jnp.einsum(
                "chqk,ckhd->cqhd", grad_score, head_keys, preferred_element_type=jnp.float32
            )
            * score_scale
        )

    query_gradient = lax.fori_loop(0, count_blocks, query_one_block, zeroed_query)
    own_keys = kv_local[..., :width_of_model].reshape(
        CLIPS_PER_BATCH, PATCHES_THIRD_2, HEAD_COUNT, HEAD_FEATURES
    )
    own_values = kv_local[..., width_of_model:].reshape(
        CLIPS_PER_BATCH, PATCHES_THIRD_2, HEAD_COUNT, HEAD_FEATURES
    )
    own_ok = key_mask(frame_index * PATCHES_THIRD_2, PATCHES_THIRD_2)[:, None, None, :]
    row_pieces = (
        query_matrix.astype(jnp.float32),
        grad_attended.astype(jnp.float32),
        log_sum.transpose(0, 2, 1),
        row_delta.transpose(0, 2, 1),
    )
    query_piece = lax.all_gather(
        row_pieces[0].astype(jnp.bfloat16), "frame", axis=1, tiled=True
    ).astype(jnp.float32)
    grad_out_piece = lax.all_gather(
        row_pieces[1].astype(jnp.bfloat16), "frame", axis=1, tiled=True
    ).astype(jnp.float32)
    lse_piece = lax.all_gather(
        row_pieces[2].astype(jnp.bfloat16), "frame", axis=1, tiled=True
    ).astype(jnp.float32)
    delta_piece = lax.all_gather(
        row_pieces[3].astype(jnp.bfloat16), "frame", axis=1, tiled=True
    ).astype(jnp.float32)
    count_blocks, own_block_rows = block_plan(query_piece.shape[1])

    def own_one_block(block_index, running):
        key_gradient, value_gradient = running
        offset = block_index * own_block_rows
        query_block = to_bfloat(lax.dynamic_slice_in_dim(query_piece, offset, own_block_rows, 1))
        grad_out_block = to_bfloat(
            lax.dynamic_slice_in_dim(grad_out_piece, offset, own_block_rows, 1)
        )
        lse_block = lax.dynamic_slice_in_dim(lse_piece, offset, own_block_rows, 1).transpose(
            0, 2, 1
        )
        delta_block = lax.dynamic_slice_in_dim(delta_piece, offset, own_block_rows, 1).transpose(
            0, 2, 1
        )
        scores = (
            jnp.einsum("cqhd,ckhd->chqk", query_block, own_keys, preferred_element_type=jnp.float32)
            * score_scale
        )
        scores = jnp.where(own_ok, scores, -1e30)
        prob_tile = jnp.where(own_ok, jnp.exp(scores - lse_block[..., None]), 0.0)
        grad_prob = jnp.einsum(
            "cqhd,ckhd->chqk", grad_out_block, own_values, preferred_element_type=jnp.float32
        )
        grad_score = to_bfloat(prob_tile * (grad_prob - delta_block[..., None]))
        key_gradient = (
            key_gradient
            + jnp.einsum(
                "chqk,cqhd->ckhd", grad_score, query_block, preferred_element_type=jnp.float32
            )
            * score_scale
        )
        value_gradient = value_gradient + jnp.einsum(
            "chqk,cqhd->ckhd",
            to_bfloat(prob_tile),
            grad_out_block,
            preferred_element_type=jnp.float32,
        )
        return (key_gradient, value_gradient)

    grad_key_own, grad_value_own = lax.fori_loop(
        0, count_blocks, own_one_block, (zeroed_query, zeroed_query)
    )
    gradient_key_value_local = to_bfloat(
        jnp.concatenate(
            [
                grad_key_own.reshape(CLIPS_PER_BATCH, PATCHES_THIRD_2, width_of_model),
                grad_value_own.reshape(CLIPS_PER_BATCH, PATCHES_THIRD_2, width_of_model),
            ],
            -1,
        )
    )
    gradient_query_key_value = jnp.concatenate(
        [
            to_bfloat(query_gradient).reshape(CLIPS_PER_BATCH, PATCHES_THIRD_2, width_of_model),
            gradient_key_value_local,
        ],
        -1,
    )
    grad_query_bias = jnp.sum(
        gradient_query_key_value[..., :width_of_model].astype(jnp.float32), (0, 1)
    )
    grad_value_bias = jnp.sum(
        gradient_query_key_value[..., 2 * width_of_model :].astype(jnp.float32), (0, 1)
    )
    grad_w_qkv = jnp.einsum(
        "cpd,cpe->de", normed_one, gradient_query_key_value, preferred_element_type=jnp.float32
    )
    grad_normed_one = jnp.einsum(
        "cpe,de->cpd", gradient_query_key_value, w_qkv, preferred_element_type=jnp.float32
    )
    grad_in_one, grad_gain_one, grad_shift_one = norm_backward(grad_normed_one, vec_f[0], saved_one)
    gradient_entry = grad_second + grad_in_one
    gradient_entry_low = to_bfloat(gradient_entry).reshape(
        CLIPS_PER_BATCH * PATCHES_THIRD_2, width_of_model
    )
    grad_w_embed = jnp.einsum(
        "rt,rd->td", rows_of_pixels, gradient_entry_low, preferred_element_type=jnp.float32
    )
    grad_embed_bias = jnp.sum(gradient_entry, (0, 1))
    grad_pos_space = jnp.zeros((P0 + P1 + PATCHES_THIRD_2, width_of_model), jnp.float32)
    current = lax.dynamic_slice_in_dim(grad_pos_space, start_rows[0], PATCHES_THIRD_2, 0)
    grad_pos_space = lax.dynamic_update_slice_in_dim(
        grad_pos_space, current + gradient_entry[0], start_rows[0], 0
    )
    grad_pos_time = lax.dynamic_update_slice_in_dim(
        jnp.zeros((TMAX, width_of_model), jnp.float32), grad_embed_bias[None], frame_index, 0
    )
    grad_vectors = jnp.stack(
        [
            grad_gain_one,
            grad_shift_one,
            grad_gain_two,
            grad_shift_two,
            grad_learn_gain,
            grad_learn_shift,
            grad_final_gain * head_mask,
            grad_final_shift * head_mask,
            grad_embed_bias,
            grad_query_bias,
            grad_value_bias,
            grad_out_bias,
            grad_down_bias,
        ]
    )
    flat_grad = jnp.concatenate(
        [
            piece_grad.reshape(-1)
            for piece_grad in (
                grad_w_embed,
                grad_w_qkv,
                grad_w_out,
                grad_w_up,
                grad_w_down,
                grad_proj * head_mask,
                grad_map,
                grad_pos_space,
                grad_pos_time,
                grad_vectors,
                grad_up_bias,
            )
        ]
    )
    grad_shard = lax.psum_scatter(flat_grad, ("batch", "frame"), scatter_dimension=0, tiled=True)
    contrast_keep = jnp.where(frame_index == 0, contrast_part, 0.0)
    square_sum, contrast_total = lax.psum(
        (jnp.sum(grad_shard * grad_shard), contrast_keep), ("batch", "frame")
    )
    grad_norm = jnp.sqrt(square_sum)
    loss_value = contrast_total + DECAY_PENALTY * jnp.sum(correlation_all) / frame_total_count
    clipped = grad_shard * jnp.minimum(1.0, CLIP_AT / grad_norm)
    new_first = BETA_ONE * first_moment + (1.0 - BETA_ONE) * clipped
    new_second = BETA_TWO * second_moment + (1.0 - BETA_TWO) * clipped * clipped
    step_count = adam_step[0].astype(jnp.float32)
    update = (
        new_first
        / (1.0 - BETA_ONE**step_count)
        / (jnp.sqrt(new_second / (1.0 - BETA_TWO**step_count)) + ADAM_EPS)
    )
    new_master = master - RATE * (update + DECAY * master)
    return (new_master, new_first, new_second, to_bfloat(new_master), loss_value, grad_norm)


MESH = pl.DeviceIdType.MESH
T=144
SPA=32

class Sends:
    def __init__(self, sem): self.sem=sem; self.n=0; self.items=[]
    def go(self, src, dst, rsem, dev, pred=None):
        c = pltpu.make_async_remote_copy(src_ref=src, dst_ref=dst, send_sem=self.sem.at[self.n], recv_sem=rsem, device_id=dev, device_id_type=MESH)
        self.n += 1
        if pred is None: c.start()
        else:
            @pl.when(pred)
            def _(): c.start()
        self.items.append((c,pred))
    def drain(self):
        for c,pred in self.items:
            if pred is None: c.wait_send()
            else:
                @pl.when(pred)
                def _(): c.wait_send()

def both(a,b):
    if a is None: return b
    if b is None: return a
    return jnp.logical_and(a,b)

def make_ag(spa=SPA):
    A=(0,spa); A1=(0,spa//2); A2=(spa//2,spa//2)
    nb=T-spa
    B=(spa,nb); B1=(spa,nb//2); B2=(spa+nb//2,nb//2)
    FULL=(0,T)
    def kernel(x_ref, out, ssem, lsem, zB, xB, yB, xBh, yBh, pA, zA, pown, pzB, pxB, pyB, pxBh, pyBh, ppA, pzA):
        b=lax.axis_index("batch"); f=lax.axis_index("frame")
        x=b%2; y=b//2; z=f//2; c=f%2
        bx=y*2+(1-x); by=(1-y)*2+x; bd=(1-y)*2+(1-x)
        X=(bx,f); Y=(by,f); Pn=(b,z*2+(1-c)); UP=(b,f+2); DN=(b,f-2)
        up=z<3; dn=z>0
        bar=pltpu.get_barrier_semaphore()
        for d,p in ((X,None),(Y,None),(Pn,None),(UP,up),(DN,dn)):
            if p is None: pl.semaphore_signal(bar,inc=1,device_id=d,device_id_type=MESH)
            else:
                @pl.when(p)
                def _(): pl.semaphore_signal(bar,inc=1,device_id=d,device_id_type=MESH)
        pl.semaphore_wait(bar, 4+(z*(3-z)+1)//3)
        S=Sends(ssem)
        def blk(bb,zz,part): return out.at[bb*8+zz*2+c, pl.ds(part[0],part[1])]
        def send(bb,zz,part,rsem,dev,pred=None,own=False):
            dst=blk(bb,zz,part)
            src=x_ref.at[pl.ds(part[0],part[1])] if own else dst
            S.go(src,dst,rsem,dev,pred)
        def wait(bb,zz,part,rsem):
            r=blk(bb,zz,part)
            pltpu.make_async_remote_copy(src_ref=r,dst_ref=r,send_sem=ssem.at[0],recv_sem=rsem,device_id=Pn,device_id_type=MESH).wait_recv()
        def waitp(pred,*a):
            if pred is None: wait(*a)
            else:
                @pl.when(pred)
                def _(): wait(*a)
        lc=pltpu.make_async_copy(x_ref, blk(b,z,FULL), lsem);
        send(b,z,A,pA.at[0],X,own=True); send(b,z,A,pA.at[1],Y,own=True)
        send(b,z,B,zB.at[z],UP,up,True); send(b,z,B,zB.at[z],DN,dn,True)
        send(b,z,B,xB.at[z],X,own=True); send(b,z,B,yB.at[z],Y,own=True)
        send(b,z,A,zA.at[z,0],UP,up,True); send(b,z,A,zA.at[z,0],DN,dn,True)
        send(b,z,FULL,pown.at[0],Pn,own=True)
        lc.start()
        pz=[]
        def pwait(*a): pz.append(a)
        pwait(None,b,z,FULL,pown.at[0])
        def zfwdA(bb,part,i,ps):
            send(bb,z,part,zA.at[z,i],UP,up); send(bb,z,part,zA.at[z,i],DN,dn)
            send(bb,z,part,ps,Pn); pwait(None,bb,z,part,ps)
        wait(bx,z,A,pA.at[0]); send(bx,z,A1,pA.at[2],Y); zfwdA(bx,A,1,ppA.at[0])
        wait(by,z,A,pA.at[1]); send(by,z,A2,pA.at[3],X); zfwdA(by,A,2,ppA.at[1])
        wait(bd,z,A1,pA.at[2]); zfwdA(bd,A1,3,ppA.at[2])
        wait(bd,z,A2,pA.at[3]); zfwdA(bd,A2,4,ppA.at[3])
        def xyB(zz,pred):
            waitp(pred,bx,zz,B,xB.at[zz]); send(bx,zz,B1,yBh.at[zz],Y,pred); send(bx,zz,B,pxB.at[zz],Pn,pred); pwait(pred,bx,zz,B,pxB.at[zz])
            waitp(pred,by,zz,B,yB.at[zz]); send(by,zz,B2,xBh.at[zz],X,pred); send(by,zz,B,pyB.at[zz],Pn,pred); pwait(pred,by,zz,B,pyB.at[zz])
        xyB(z,None)
        for d in (1,2,3):
            for s in (1,-1):
                zz=z+s*d
                pred=(zz<4) if s>0 else (zz>=0)
                nxt,np_=(DN,dn) if s>0 else (UP,up)
                waitp(pred,b,zz,B,zB.at[zz])
                send(b,zz,B,zB.at[zz],nxt,both(pred,np_))
                send(b,zz,B,xB.at[zz],X,pred); send(b,zz,B,yB.at[zz],Y,pred)
                send(b,zz,B,pzB.at[zz],Pn,pred); pwait(pred,b,zz,B,pzB.at[zz])
            for s in (1,-1):
                zz=z+s*d
                pred=(zz<4) if s>0 else (zz>=0)
                nxt,np_=(DN,dn) if s>0 else (UP,up)
                for i,(bb,part) in enumerate(((b,A),(bx,A),(by,A),(bd,A1),(bd,A2))):
                    waitp(pred,bb,zz,part,zA.at[zz,i]); send(bb,zz,part,zA.at[zz,i],nxt,both(pred,np_))
                    send(bb,zz,part,pzA.at[zz,i],Pn,pred); pwait(pred,bb,zz,part,pzA.at[zz,i])
            for s in (1,-1):
                zz=z+s*d
                pred=(zz<4) if s>0 else (zz>=0)
                xyB(zz,pred)
        for zz in range(4):
            wait(bd,zz,B1,yBh.at[zz]); send(bd,zz,B1,pyBh.at[zz],Pn); pwait(None,bd,zz,B1,pyBh.at[zz])
            wait(bd,zz,B2,xBh.at[zz]); send(bd,zz,B2,pxBh.at[zz],Pn); pwait(None,bd,zz,B2,pxBh.at[zz])
        for a in pz: waitp(*a)
        lc.wait()
        S.drain()
    D=pltpu.SemaphoreType.DMA
    def ag(xin, cid=0):
        return pl.pallas_call(kernel, out_shape=jax.ShapeDtypeStruct((32,T,16,128),jnp.bfloat16),
            in_specs=[pl.BlockSpec(memory_space=pltpu.VMEM)], out_specs=pl.BlockSpec(memory_space=pl.ANY),
            scratch_shapes=[D((160,)),D]+[D((4,))]*5+[D((4,)),D((4,5)),D((1,))]+[D((4,))]*5+[D((4,)),D((4,5))],
            compiler_params=pltpu.CompilerParams(collective_id=cid,has_side_effects=True))(xin)
    return ag


def make_rsx(spa=32):
    nb=T-spa
    A=(0,spa); A1=(0,spa//2); A2=(spa//2,spa//2)
    B=(spa,nb); B1=(spa,nb//2); B2=(spa+nb//2,nb//2)
    FULL=(0,T)
    def kernel(pix, h1, att, h2, act, dx0, dqkv, dattn, dpre, dmlp, tail, gout, nout,
               PS, R, h2T, LX, LY, LHX, LHY, LZB, LZA, LPA, out, C, CB_, CR_, NB, ssem, psem, stsem, csem, nsem, nsend, s_hx, s_hy, s_x, s_y, s_zb, s_za, s_pa):
        b=lax.axis_index("batch"); f=lax.axis_index("frame")
        x=b%2; y=b//2; z=f//2; c=f%2
        bx=y*2+(1-x); by=(1-y)*2+x; bd=(1-y)*2+(1-x)
        X=(bx,f); Y=(by,f); Pn=(b,z*2+(1-c)); UP=(b,f+2); DN=(b,f-2)
        up=z<3; dn=z>0
        t=z//2
        k=b*8+f
        def dev_of(kk): return (kk//8,kk%8)
        bar=pltpu.get_barrier_semaphore()
        def greet(d,_):
            pl.semaphore_signal(bar,inc=1,device_id=dev_of((k+d)%32),device_id_type=MESH); return 0
        lax.fori_loop(1,32,greet,0)
        zo=[3*(1-t), 2-t, (1-z)*(1-t)+(5-z)*t, z]
        order=[]
        for zz in zo: order += [(bd,zz)]
        for zz in zo: order += [(bx,zz),(by,zz)]
        for zz in zo: order += [(b,zz)]
        h2T[...]=h2[...].T
        TN_=(((0,),(0,)),((),()))
        def put(dst,r,m):
            rows=r.shape[0]
            r=r.astype(jnp.bfloat16)
            for s in range(rows//16):
                for j in range(m):
                    dst[s*m+j]=r[s*16:(s+1)*16,j*128:(j+1)*128]
        def col(a,i,n): return a[:,pl.ds(pl.multiple_of(i*n,128),n)]
        def comp(kk,dst):
            def mm(a,bb_,dims): return lax.dot_general(a,bb_,dims,preferred_element_type=jnp.float32)
            @pl.when(kk<4)
            def _(): put(dst,mm(col(pix,kk,384),dx0[...],TN_),6)
            @pl.when(jnp.logical_and(kk>=4,kk<10))
            def _(): put(dst,mm(col(h1,kk-4,128),dqkv[...],TN_),18)
            @pl.when(jnp.logical_and(kk>=10,kk<12))
            def _(): put(dst,mm(col(att,kk-10,384),dattn[...],TN_),6)
            @pl.when(jnp.logical_and(kk>=12,kk<20))
            def _(): put(dst,mm(h2T[pl.ds(pl.multiple_of((kk-12)*96,16),96)],dpre[...],(((1,),(0,)),((),()))),24)
            @pl.when(jnp.logical_and(kk>=20,kk<28))
            def _(): put(dst,mm(col(act,kk-20,384),dmlp[...],TN_),6)
            @pl.when(kk>=28)
            def _():
                def cp(i,_):
                    ds=pl.ds(i*8,8); dst[ds]=tail[kk-28,ds]; return 0
                lax.fori_loop(0,T//8,cp,0)
        def pick(i):
            g=jnp.where(i<4,i,jnp.where(i<12,(i-4)//2,i-12))
            zz=jnp.where(g==0,zo[0],jnp.where(g==1,zo[1],jnp.where(g==2,zo[2],zo[3])))
            bb=jnp.where(i<4,bd,jnp.where(i<12,jnp.where(i%2==0,bx,by),b))
            return bb,zz
        def pcopy(i):
            bb,zz=pick(i)
            return pltpu.make_async_remote_copy(src_ref=PS.at[16+i%4],dst_ref=R.at[bb,zz],send_sem=stsem.at[i%4],recv_sem=psem.at[bb,zz],device_id=Pn,device_id_type=MESH)
        def produce(h,_):
            i=h//2; own=h%2
            bb,zz=pick(i)
            @pl.when(own==0)
            def _():
                @pl.when(i>=4)
                def _(): pcopy(i-4).wait_send()
            kk=bb*8+zz*2+jnp.where(own==1,c,1-c)
            comp(kk,PS.at[jnp.where(own==1,bb*4+zz,16+i%4)])
            @pl.when(own==0)
            def _():
                @pl.when(i==0)
                def _(): pl.semaphore_wait(bar,31)
                pcopy(i).start()
            return 0
        lax.fori_loop(0,32,produce,0)
        S=Sends(ssem)
        def acc(dst, srcs, n, step=8):
            def body(i,_):
                ds=pl.ds(i*step,step)
                v=srcs[0][ds].astype(jnp.float32)
                for s in srcs[1:]: v=v+s[ds].astype(jnp.float32)
                dst[ds]=v.astype(dst.dtype)
                return 0
            lax.fori_loop(0,n//step,body,0)
        def sub(ref,part): return ref.at[pl.ds(part[0],part[1])]
        def ready(i):
            bb,zz=order[i]
            pltpu.make_async_remote_copy(src_ref=R.at[bb,zz],dst_ref=R.at[bb,zz],send_sem=ssem.at[0],recv_sem=psem.at[bb,zz],device_id=Pn,device_id_type=MESH).wait_recv()
        def wrecv(ref,sem):
            pltpu.make_async_remote_copy(src_ref=ref,dst_ref=ref,send_sem=ssem.at[0],recv_sem=sem,device_id=Pn,device_id_type=MESH).wait_recv()
        for i,zz in enumerate(zo):
            ready(i)
            acc(sub(PS.at[bd*4+zz],B), [sub(PS.at[bd*4+zz],B), sub(R.at[bd,zz],B)], nb)
            S.go(sub(PS.at[bd*4+zz],B1), LHY.at[zz], s_hy.at[zz], Y)
            S.go(sub(PS.at[bd*4+zz],B2), LHX.at[zz], s_hx.at[zz], X)
        def chainA(bi,bb):
            for d in (3,2,1):
                for s in (1,-1):
                    zz=z+s*d
                    pred=(zz<4) if s>0 else (zz>=0)
                    frm=dn if s>0 else up
                    dev=UP if s>0 else DN
                    di=0 if s>0 else 1
                    @pl.when(jnp.logical_and(pred,frm))
                    def _():
                        wrecv(LZA.at[di,zz,bi], s_za.at[di,zz,bi])
                        acc(sub(PS.at[bb*4+zz],A),[sub(PS.at[bb*4+zz],A),sub(R.at[bb,zz],A),LZA.at[di,zz,bi]],spa)
                    @pl.when(jnp.logical_and(pred,jnp.logical_not(frm)))
                    def _():
                        acc(sub(PS.at[bb*4+zz],A),[sub(PS.at[bb*4+zz],A),sub(R.at[bb,zz],A)],spa)
                    S.go(sub(PS.at[bb*4+zz],A), LZA.at[di,zz,bi], s_za.at[di,zz,bi], dev, pred)
        chainA(0,bd)
        for i,zz in enumerate(zo):
            ready(4+2*i); ready(5+2*i)
            wrecv(LHY.at[zz], s_hy.at[zz])
            acc(sub(PS.at[bx*4+zz],B1),[sub(PS.at[bx*4+zz],B1),sub(R.at[bx,zz],B1),LHY.at[zz]],nb//2)
            acc(sub(PS.at[bx*4+zz],B2),[sub(PS.at[bx*4+zz],B2),sub(R.at[bx,zz],B2)],nb//2)
            S.go(sub(PS.at[bx*4+zz],B), LX.at[zz], s_x.at[zz], X)
            wrecv(LHX.at[zz], s_hx.at[zz])
            acc(sub(PS.at[by*4+zz],B2),[sub(PS.at[by*4+zz],B2),sub(R.at[by,zz],B2),LHX.at[zz]],nb//2)
            acc(sub(PS.at[by*4+zz],B1),[sub(PS.at[by*4+zz],B1),sub(R.at[by,zz],B1)],nb//2)
            S.go(sub(PS.at[by*4+zz],B), LY.at[zz], s_y.at[zz], Y)
        chainA(1,bx); chainA(2,by)
        for i in range(4): ready(12+i)
        chainA(3,b)
        for i,zz in enumerate(zo[:3]):
            wrecv(LX.at[zz],s_x.at[zz]); wrecv(LY.at[zz],s_y.at[zz])
            isup=zz>z
            inc=jnp.logical_or(jnp.logical_and(isup,dn),jnp.logical_and(jnp.logical_not(isup),up))
            di=jnp.where(isup,0,1)
            base=[sub(PS.at[b*4+zz],B),sub(R.at[b,zz],B),LX.at[zz],LY.at[zz]]
            @pl.when(inc)
            def _():
                wrecv(LZB.at[di,zz],s_zb.at[di,zz])
                acc(sub(PS.at[b*4+zz],B),base+[LZB.at[di,zz]],nb)
            @pl.when(jnp.logical_not(inc))
            def _(): acc(sub(PS.at[b*4+zz],B),base,nb)
            S.go(sub(PS.at[b*4+zz],B),LZB.at[0,zz],s_zb.at[0,zz],UP,isup)
            S.go(sub(PS.at[b*4+zz],B),LZB.at[1,zz],s_zb.at[1,zz],DN,jnp.logical_not(isup))
        def totA(bi,bb,part,extra=(),dst=None):
            dst = dst if dst is not None else sub(PS.at[bb*4+z],part)
            srcs=[sub(PS.at[bb*4+z],part),sub(R.at[bb,z],part)]+list(extra)
            o=part[0]; n=part[1]
            l0=LZA.at[0,z,bi,pl.ds(o,n)]; l1=LZA.at[1,z,bi,pl.ds(o,n)]
            @pl.when(jnp.logical_and(up,dn))
            def _(): acc(dst,srcs+[l0,l1],n)
            @pl.when(jnp.logical_not(up))
            def _(): acc(dst,srcs+[l0],n)
            @pl.when(jnp.logical_not(dn))
            def _(): acc(dst,srcs+[l1],n)
        for bi in range(4):
            @pl.when(dn)
            def _(): wrecv(LZA.at[0,z,bi],s_za.at[0,z,bi])
            @pl.when(up)
            def _(): wrecv(LZA.at[1,z,bi],s_za.at[1,z,bi])
            if bi==0:
                totA(0,bd,A1); S.go(sub(PS.at[bd*4+z],A1),LPA.at[0,pl.ds(0,spa//2)],s_pa.at[0],Y)
                totA(0,bd,A2); S.go(sub(PS.at[bd*4+z],A2),LPA.at[1,pl.ds(0,spa//2)],s_pa.at[1],X)
            if bi==1:
                totA(1,bx,A2)
                wrecv(LPA.at[0,pl.ds(0,spa//2)],s_pa.at[0])
                totA(1,bx,A1,[LPA.at[0,pl.ds(0,spa//2)]])
                S.go(sub(PS.at[bx*4+z],A),LPA.at[2],s_pa.at[2],X)
            if bi==2:
                totA(2,by,A1)
                wrecv(LPA.at[1,pl.ds(0,spa//2)],s_pa.at[1])
                totA(2,by,A2,[LPA.at[1,pl.ds(0,spa//2)]])
                S.go(sub(PS.at[by*4+z],A),LPA.at[3],s_pa.at[3],Y)
        wrecv(LX.at[z],s_x.at[z]); wrecv(LY.at[z],s_y.at[z])
        base=[sub(PS.at[b*4+z],B),sub(R.at[b,z],B),LX.at[z],LY.at[z]]
        @pl.when(dn)
        def _(): wrecv(LZB.at[0,z],s_zb.at[0,z])
        @pl.when(up)
        def _(): wrecv(LZB.at[1,z],s_zb.at[1,z])
        @pl.when(jnp.logical_and(up,dn))
        def _(): acc(sub(out,B),base+[LZB.at[0,z],LZB.at[1,z]],nb)
        @pl.when(jnp.logical_not(up))
        def _(): acc(sub(out,B),base+[LZB.at[0,z]],nb)
        @pl.when(jnp.logical_not(dn))
        def _(): acc(sub(out,B),base+[LZB.at[1,z]],nb)
        wrecv(LPA.at[2],s_pa.at[2]); wrecv(LPA.at[3],s_pa.at[3])
        totA(3,b,A,[LPA.at[2],LPA.at[3]],dst=sub(out,A))
        def sq(i,a):
            v=out[i]; v=v*v
            return a+v[:8]+v[8:]
        NB[k]=lax.fori_loop(0,T,sq,jnp.zeros((8,128),jnp.float32))
        def ncopy(d):
            return pltpu.make_async_remote_copy(src_ref=NB.at[k],dst_ref=NB.at[k],send_sem=nsend.at[d],recv_sem=nsem.at[k],device_id=dev_of((k+d)%32),device_id_type=MESH)
        def nstart(d,_):
            ncopy(d).start(); return 0
        lax.fori_loop(1,32,nstart,0)
        CR=1440
        def untile(m,s0,n,t0):
            def body(s,_):
                for j in range(m):
                    C[pl.ds(CR+s0+s*16*m+j,16,stride=m),:]=out[t0+s*m+j]
                return 0
            lax.fori_loop(0,n,body,0)
        def plain(t0,n):
            def body(s,_):
                C[pl.ds(CR+(t0+s)*16,16),:]=out[t0+s]; return 0
            lax.fori_loop(0,n,body,0)
        def within(lo,hi): return jnp.logical_and(k>=lo,k<hi)
        @pl.when(jnp.logical_or(jnp.logical_or(within(0,4),within(10,12)),within(20,28)))
        def _(): untile(6,0,24,0)
        @pl.when(within(4,10))
        def _(): untile(18,0,8,0)
        @pl.when(within(12,20))
        def _(): untile(24,0,6,0)
        @pl.when(k==28)
        def _(): untile(4,0,36,0)
        @pl.when(k==29)
        def _():
            untile(4,0,12,0); plain(48,96)
        @pl.when(k>=30)
        def _(): plain(0,T)
        def carry(i,_):
            CB_[pl.ds(i*96,96)]=C[pl.ds(2304+i*96,96),:].astype(jnp.bfloat16); return 0
        lax.fori_loop(0,CR//96,carry,0)
        def cdesc(): return pltpu.make_async_remote_copy(src_ref=CB_,dst_ref=CR_,send_sem=csem.at[0],recv_sem=csem.at[1],device_id=dev_of((k+1)%32),device_id_type=MESH)
        @pl.when(k<31)
        def _(): cdesc().start()
        C[pl.ds(CR+2304,8),:]=jnp.zeros((8,128),jnp.float32)
        def nwait(d,_):
            kk=(k+d)%32
            wrecv_(NB.at[kk],nsem.at[kk],nsend.at[0],Pn); return 0
        lax.fori_loop(1,32,nwait,0)
        def nsum(i,a): return a+NB[i]
        nout[...]=lax.fori_loop(0,32,nsum,jnp.zeros((8,128),jnp.float32))
        @pl.when(k>0)
        def _():
            wrecv_(CR_,csem.at[1],csem.at[0],Pn)
            def uncarry(i,_):
                C[pl.ds(i*96,96),:]=CR_[pl.ds(i*96,96)].astype(jnp.float32); return 0
            lax.fori_loop(0,CR//96,uncarry,0)
        e=CR*128-(294912-289176)*k
        q=e//128; sh=e%128
        lane=lax.broadcasted_iota(jnp.int32,(96,128),1)
        def slide(i,_):
            r0=q+i*96
            a=pltpu.roll(C[pl.ds(r0,96),:],(128-sh)%128,1); b_=pltpu.roll(C[pl.ds(r0+1,96),:],(128-sh)%128,1)
            gout[pl.ds(i*96,96),:]=jnp.where(lane<128-sh,a,b_)
            return 0
        lax.fori_loop(0,24,slide,0)
        @pl.when(k<31)
        def _(): cdesc().wait_send()
        def ndone(d,_):
            ncopy(d).wait_send(); return 0
        lax.fori_loop(1,32,ndone,0)
        for i in range(12,16): pcopy(i).wait_send()
        S.drain()
    D=pltpu.SemaphoreType.DMA
    V=lambda *s: pltpu.VMEM(s+(16,128),jnp.bfloat16)
    VMs=pl.BlockSpec(memory_space=pltpu.VMEM)
    def rs(*args, cid=1):
        return pl.pallas_call(kernel, out_shape=(jax.ShapeDtypeStruct((2304,128),jnp.float32),jax.ShapeDtypeStruct((8,128),jnp.float32)),
            in_specs=[VMs]*11, out_specs=(VMs,VMs),
            scratch_shapes=[V(20,T),V(4,4,T),pltpu.VMEM((768,400),jnp.bfloat16),V(4,nb),V(4,nb),V(4,nb//2),V(4,nb//2),V(2,4,nb),V(2,4,4,spa),V(4,spa),
              pltpu.VMEM((T,16,128),jnp.float32),pltpu.VMEM((3752,128),jnp.float32),pltpu.VMEM((1440,128),jnp.bfloat16),pltpu.VMEM((1440,128),jnp.bfloat16),pltpu.VMEM((32,8,128),jnp.float32),
              D((80,)),D((4,4)),D((4,)),D((2,)),D((32,)),D((32,)),D((4,)),D((4,)),D((4,)),D((4,)),D((2,4)),D((2,4,4)),D((4,))],
            compiler_params=pltpu.CompilerParams(collective_id=cid,has_side_effects=True,vmem_limit_bytes=63*1024*1024))(*args)
    return rs

def wrecv_(ref,sem,ssem,dev):
    pltpu.make_async_remote_copy(src_ref=ref,dst_ref=ref,send_sem=ssem,recv_sem=sem,device_id=dev,device_id_type=MESH).wait_recv()


TOK=400; CB=208; NK=3200; NQ=1600; SUB=80; PADQ=512
ROWS={"q":0,"k":400,"v":800,"qc":1200,"kc":1408,"vc":1616}
NT=(((1,),(1,)),((),())); NN=(((1,),(0,)),((),())); TN=(((0,),(0,)),((),()))
f32=jnp.float32; bf16=jnp.bfloat16

def dot(a,b,dims): return lax.dot_general(a,b,dims,preferred_element_type=f32)

def mesh_pos():
    b=lax.axis_index("batch"); f=lax.axis_index("frame")
    return b,f//2,f%2

def zbarrier(b,z,c):
    bar=pltpu.get_barrier_semaphore()
    for d in (1,2,3):
        pl.semaphore_signal(bar,inc=1,device_id=(b,((z+d)%4)*2+c),device_id_type=MESH)
    pl.semaphore_signal(bar,inc=1,device_id=(b,z*2+1-c),device_id_type=MESH)
    pl.semaphore_wait(bar,4)

def wrecv(ref,sem,dev):
    pltpu.make_async_remote_copy(src_ref=ref,dst_ref=ref,send_sem=sem,recv_sem=sem,device_id=dev,device_id_type=MESH).wait_recv()

def others(z):
    return [((z+d)%4) for d in (2,1,3)]

def unpack_c(src, dst, row):
    v=src.astype(f32)
    lane=lax.broadcasted_iota(jnp.int32,(CB,128),1)
    lo=jnp.where(lane<64,v,0.0)
    hi=jnp.where(lane<64,pltpu.roll(v,64,1),0.0)
    dst[pl.ds(row,CB)]=lo.astype(bf16)
    dst[pl.ds(row+CB,TOK-CB)]=hi[:TOK-CB].astype(bf16)

def pack_c(lo, hi):
    hi=jnp.concatenate([hi,jnp.zeros((2*CB-TOK,128),f32)],0)
    lane=lax.broadcasted_iota(jnp.int32,(CB,128),1)
    return jnp.where(lane<64,lo,pltpu.roll(hi,64,1)).astype(bf16)

def fwd_kernel(sp, bias, og, Q, K, V, QC, KC, VC, OA, OC, LA, LC,
               QCp, KCp, VCp, OB, OCp, S, Pb, ssem, lsem, rq, rk, rv, rqc, rkc, rvc, pk, pv, pkc, pvc, ro, roc):
    b,z,c=mesh_pos()
    Pn=(b,z*2+1-c)
    dev=lambda zz:(b,zz*2+c)
    row=lambda zz: pl.multiple_of(zz*TOK,16)
    krow=lambda zz: pl.multiple_of((c*4+zz)*TOK,16)
    pkrow=lambda zz: pl.multiple_of(((1-c)*4+zz)*TOK,16)
    zbarrier(b,z,c)
    X=Sends(ssem)
    part=lambda g,n,ln: sp.at[g,pl.ds(ROWS[n],ln)]
    loc=[]
    def lcopy(src,dst):
        cp=pltpu.make_async_copy(src,dst,lsem.at[len(loc)]); cp.start(); loc.append(cp)
    for zz in others(z):
        X.go(part(zz,"k",TOK),K.at[pl.ds(krow(z),TOK)],rk.at[z],dev(zz))
        X.go(part(zz,"q",TOK),Q.at[pl.ds(row(z),TOK)],rq.at[z],dev(zz))
        X.go(part(zz,"v",TOK),V.at[pl.ds(krow(z),TOK)],rv.at[z],dev(zz))
    lcopy(part(z,"k",TOK),K.at[pl.ds(krow(z),TOK)])
    lcopy(part(z,"q",TOK),Q.at[pl.ds(row(z),TOK)])
    lcopy(part(z,"v",TOK),V.at[pl.ds(krow(z),TOK)])
    lcopy(part(z,"kc",CB),KCp.at[c*4+z]); lcopy(part(z,"qc",CB),QCp.at[z]); lcopy(part(z,"vc",CB),VCp.at[c*4+z])
    X.go(part(z,"k",TOK),K.at[pl.ds(krow(z),TOK)],pk.at[z],Pn)
    X.go(part(z,"v",TOK),V.at[pl.ds(krow(z),TOK)],pv.at[z],Pn)
    X.go(part(z,"kc",CB),KCp.at[c*4+z],pkc.at[z],Pn)
    X.go(part(z,"vc",CB),VCp.at[c*4+z],pvc.at[z],Pn)
    for zz in others(z):
        X.go(part(zz,"kc",CB),KCp.at[c*4+z],rkc.at[z],dev(zz))
        X.go(part(zz,"qc",CB),QCp.at[z],rqc.at[z],dev(zz))
        X.go(part(zz,"vc",CB),VCp.at[c*4+z],rvc.at[z],dev(zz))
    for zz in [((z+d)%4) for d in (1,3,2)]:
        kr=K.at[pl.ds(krow(zz),TOK)]; vr=V.at[pl.ds(krow(zz),TOK)]
        wrecv(kr,rk.at[zz],Pn); X.go(kr,kr,pk.at[zz],Pn)
        wrecv(vr,rv.at[zz],Pn); X.go(vr,vr,pv.at[zz],Pn)
    for zz in range(4):
        r=K.at[pl.ds(pkrow(zz),TOK)]; wrecv(r,pk.at[zz],Pn)
        r=V.at[pl.ds(pkrow(zz),TOK)]; wrecv(r,pv.at[zz],Pn)
    for zz in [((z+d)%4) for d in (1,2,3)]:
        wrecv(Q.at[pl.ds(row(zz),TOK)],rq.at[zz],Pn)
    for cp in loc: cp.wait()
    lane=lax.broadcasted_iota(jnp.int32,(TOK,128),1)
    lane8=lax.broadcasted_iota(jnp.int32,(SUB,128),1)
    def softmax(slot):
        def sub(i,carry):
            ds=pl.ds(pl.multiple_of(i*SUB,16),SUB)
            s=S[slot,ds,:]+bias[...]
            m=jnp.max(s,-1,keepdims=True)
            p=jnp.exp(s-m)
            l=jnp.sum(p,-1,keepdims=True)
            Pb[slot,ds,:]=p.astype(bf16)
            return m,l
        ms=[];ls=[]
        for i in range(TOK//SUB):
            m,l=sub(i,0); ms.append(m); ls.append(l)
        return jnp.concatenate(ms,0),jnp.concatenate(ls,0)
    def pairblock(i,_):
        ds=pl.ds(pl.multiple_of(i*TOK,16),TOK)
        q=Q[ds]
        zero=jnp.zeros_like(q)
        S[0]=dot(jnp.where(lane<64,q,zero),K[...],NT)
        S[1]=dot(jnp.where(lane<64,zero,q),K[...],NT)
        ma,la=softmax(0); mb,lb=softmax(1)
        oa=dot(Pb[0],V[...],NN)/la; ob=dot(Pb[1],V[...],NN)/lb
        o=jnp.where(lane<64,oa,ob)
        OA[ds]=o; OB[ds]=o.astype(bf16)
        LA[ds]=jnp.where(lane<64,ma+jnp.log(la),mb+jnp.log(lb))
        return 0
    lax.fori_loop(0,4,pairblock,0)
    for zz in [((z+d)%4) for d in (1,3,2)]:
        kr=KCp.at[c*4+zz]; vr=VCp.at[c*4+zz]
        wrecv(kr,rkc.at[zz],Pn); X.go(kr,kr,pkc.at[zz],Pn)
        wrecv(vr,rvc.at[zz],Pn); X.go(vr,vr,pvc.at[zz],Pn)
        wrecv(QCp.at[zz],rqc.at[zz],Pn)
    for zz in others(z):
        X.go(OB.at[pl.ds(row(zz),TOK)],og.at[z,pl.ds(0,TOK)],ro.at[z],dev(zz))
    lo=pltpu.make_async_copy(OB.at[pl.ds(row(z),TOK)],og.at[z,pl.ds(0,TOK)],lsem.at[6]); lo.start()
    for zz in range(4):
        wrecv(KCp.at[(1-c)*4+zz],pkc.at[zz],Pn); wrecv(VCp.at[(1-c)*4+zz],pvc.at[zz],Pn)
    def unp(i,_):
        r=pl.multiple_of(i*TOK,16)
        unpack_c(KCp[i],KC,r); unpack_c(VCp[i],VC,r)
        return 0
    lax.fori_loop(0,8,unp,0)
    def unq(i,_):
        unpack_c(QCp[i],QC,pl.multiple_of(i*TOK,16)); return 0
    lax.fori_loop(0,4,unq,0)
    def cblock(i,_):
        ds=pl.ds(pl.multiple_of(i*TOK,16),TOK)
        S[0]=dot(QC[ds],KC[...],NT)
        ma,la=softmax(0)
        o=dot(Pb[0],VC[...],NN)/la
        OC[ds]=o
        LC[ds]=jnp.broadcast_to(ma+jnp.log(la),(TOK,128))
        OCp[i]=pack_c(o[:CB],o[CB:])
        return 0
    lax.fori_loop(0,4,cblock,0)
    for zz in others(z):
        X.go(OCp.at[zz],og.at[z,pl.ds(TOK,CB)],roc.at[z],dev(zz))
    lc=pltpu.make_async_copy(OCp.at[z],og.at[z,pl.ds(TOK,CB)],lsem.at[7]); lc.start()
    for d in (1,2,3):
        zz=(z+d)%4
        wrecv(og.at[zz,pl.ds(0,TOK)],ro.at[zz],Pn)
        wrecv(og.at[zz,pl.ds(TOK,CB)],roc.at[zz],Pn)
    lo.wait(); lc.wait()
    X.drain()

D=pltpu.SemaphoreType.DMA
def vb(*s): return pltpu.VMEM(s,bf16)
def vf(*s): return pltpu.VMEM(s,f32)
VM=pl.BlockSpec(memory_space=pltpu.VMEM)
def sds(*s,d=bf16): return jax.ShapeDtypeStruct(s,d)

def attn_fwd(sp,bias,cid):
    return pl.pallas_call(fwd_kernel,
        out_shape=(sds(4,TOK+CB,128),sds(NQ,128),sds(NK,128),sds(NK,128),sds(NQ,128),sds(NK,128),sds(NK,128),
                   sds(NQ,128,d=f32),sds(NQ,128,d=f32),sds(NQ,128,d=f32),sds(NQ,128,d=f32)),
        in_specs=[VM,VM],out_specs=[VM]*11,
        scratch_shapes=[vb(4,CB,128),vb(8,CB,128),vb(8,CB,128),vb(NQ,128),vb(4,CB,128),vf(2,TOK,NK),vb(2,TOK,NK),
            D((48,)),D((8,))]+[D((4,))]*12,
        compiler_params=pltpu.CompilerParams(collective_id=cid,has_side_effects=True,vmem_limit_bytes=60*1024*1024))(sp,bias)

def bwd_kernel(dog, bias, Q, K, V, QC, KC, VC, OA, OC, LA, LC, dsp,
               DO, DOCp, DOC, S, P, DS, DKT, DVT, TT, DQ, DQC, XK, XV, YK, YV, SK, SV, HK, HV, XKC, XVC, YKC, YVC, HKC, HVC,
               ssem, lsem, rd, rdc, px, ho):
    b,z,c=mesh_pos()
    Pn=(b,z*2+1-c)
    dev=lambda zz:(b,zz*2+c)
    row=lambda zz: pl.multiple_of(zz*TOK,16)
    zbarrier(b,z,c)
    X=Sends(ssem)
    loc=[]
    def lcopy(src,dst):
        cp=pltpu.make_async_copy(src,dst,lsem.at[len(loc)]); cp.start(); loc.append(cp); return cp
    for zz in others(z):
        X.go(dog.at[zz,pl.ds(0,TOK)],DO.at[pl.ds(row(z),TOK)],rd.at[z],dev(zz))
    for zz in others(z):
        X.go(dog.at[zz,pl.ds(TOK,CB)],DOCp.at[z],rdc.at[z],dev(zz))
    l1=lcopy(dog.at[z,pl.ds(0,TOK)],DO.at[pl.ds(row(z),TOK)])
    l2=lcopy(dog.at[z,pl.ds(TOK,CB)],DOCp.at[z])
    l1.wait(); l2.wait()
    lane=lax.broadcasted_iota(jnp.int32,(TOK,128),1)
    def zero(ref):
        def bodyz(i,_):
            ref[:,pl.ds(pl.multiple_of(i*640,128),640)]=jnp.zeros((128,640),f32); return 0
        lax.fori_loop(0,NK//640,bodyz,0)
    def grads(q,k,v,do,lse,delta):
        S[0]=dot(q,k[...],NT)
        S[1]=dot(do,v[...],NT)
        for i in range(TOK//SUB):
            ds=pl.ds(i*SUB,SUB); sl=slice(i*SUB,(i+1)*SUB)
            p=jnp.exp(S[0,ds,:]+bias[...]-lse[sl])
            P[ds,:]=p.astype(bf16)
            DS[ds,:]=(p*(S[1,ds,:]-delta[sl])).astype(bf16)
        tail=jnp.zeros((PADQ-TOK,128),bf16)
        DKT[...]+=dot(jnp.concatenate([q,tail],0),DS[...],TN)
        DVT[...]+=dot(jnp.concatenate([do,tail],0),P[...],TN)
        return dot(DS[pl.ds(0,TOK)],k[...],NN)
    def home(src,r0,n,si):
        for zz in others(z):
            X.go(src(zz),dsp.at[z,pl.ds(r0,n)],ho.at[si,z],dev(zz))
        lcopy(src(z),dsp.at[z,pl.ds(r0,n)])
    mine=c*NQ; theirs=(1-c)*NQ
    def split(acc, x, own):
        def tr(i,_):
            TT[pl.ds(pl.multiple_of(i*640,16),640)]=acc[:,pl.ds(pl.multiple_of(i*640,128),640)].T
            return 0
        lax.fori_loop(0,NK//640,tr,0)
        def cut(i,_):
            r=pl.multiple_of(i*TOK,16)
            x[pl.ds(r,TOK)]=TT[pl.ds(pl.multiple_of(theirs+i*TOK,16),TOK)].astype(bf16)
            own[pl.ds(r,TOK)]=TT[pl.ds(pl.multiple_of(mine+i*TOK,16),TOK)]
            return 0
        lax.fori_loop(0,4,cut,0)
    P[pl.ds(TOK,PADQ-TOK)]=jnp.zeros((PADQ-TOK,NK),bf16)
    DS[pl.ds(TOK,PADQ-TOK)]=jnp.zeros((PADQ-TOK,NK),bf16)
    zero(DKT); zero(DVT)
    def pairblock(i,_):
        zz=(z+i)%4
        @pl.when(i>0)
        def _(): wrecv(DO.at[pl.ds(row(zz),TOK)],rd.at[zz],Pn)
        ds=pl.ds(row(zz),TOK)
        q=Q[ds]; do=DO[ds]; zero_=jnp.zeros_like(q)
        dof=do.astype(f32)*OA[ds]
        da=jnp.sum(jnp.where(lane<64,dof,0.0),-1,keepdims=True)
        db=jnp.sum(jnp.where(lane<64,0.0,dof),-1,keepdims=True)
        ga=grads(jnp.where(lane<64,q,zero_),K,V,jnp.where(lane<64,do,zero_),LA[ds,0:1],da)
        gb=grads(jnp.where(lane<64,zero_,q),K,V,jnp.where(lane<64,zero_,do),LA[ds,64:65],db)
        DQ[ds]=(jnp.where(lane<64,ga,gb)*0.125).astype(bf16)
        return 0
    lax.fori_loop(0,4,pairblock,0)
    home(lambda zz: DQ.at[pl.ds(row(zz),TOK)],0,TOK,0)
    split(DKT,XK,SK); X.go(XK,YK,px.at[0],Pn)
    split(DVT,XV,SV); X.go(XV,YV,px.at[1],Pn)
    zero(DKT); zero(DVT)
    def cblock(i,_):
        zz=(z+i)%4
        @pl.when(i>0)
        def _(): wrecv(DOCp.at[zz],rdc.at[zz],Pn)
        unpack_c(DOCp[zz],DOC,0)
        ds=pl.ds(row(zz),TOK)
        do=DOC[...]
        delta=jnp.sum(do.astype(f32)*OC[ds],-1,keepdims=True)
        g=grads(QC[ds],KC,VC,do,LC[ds,0:1],delta)*0.125
        DQC[zz]=pack_c(g[:CB],g[CB:])
        return 0
    lax.fori_loop(0,4,cblock,0)
    home(lambda zz: DQC.at[zz],ROWS["qc"],CB,1)
    wrecv(YK,px.at[0],Pn); wrecv(YV,px.at[1],Pn)
    def addp(i,_):
        ds=pl.ds(pl.multiple_of(i*TOK,16),TOK)
        HK[ds]=(SK[ds]+YK[ds].astype(f32)).astype(bf16)
        HV[ds]=(SV[ds]+YV[ds].astype(f32)).astype(bf16)
        return 0
    lax.fori_loop(0,4,addp,0)
    home(lambda zz: HK.at[pl.ds(row(zz),TOK)],ROWS["k"],TOK,2)
    home(lambda zz: HV.at[pl.ds(row(zz),TOK)],ROWS["v"],TOK,3)
    def splitc(acc, x, own):
        def tr(i,_):
            TT[pl.ds(pl.multiple_of(i*640,16),640)]=acc[:,pl.ds(pl.multiple_of(i*640,128),640)].T
            return 0
        lax.fori_loop(0,NK//640,tr,0)
        def cut(i,_):
            r=theirs+i*TOK
            x[i]=pack_c(TT[pl.ds(pl.multiple_of(r,16),CB)],TT[pl.ds(pl.multiple_of(r+CB,16),TOK-CB)])
            own[pl.ds(pl.multiple_of(i*TOK,16),TOK)]=TT[pl.ds(pl.multiple_of(mine+i*TOK,16),TOK)]
            return 0
        lax.fori_loop(0,4,cut,0)
    splitc(DKT,XKC,SK); X.go(XKC,YKC,px.at[2],Pn)
    splitc(DVT,XVC,SV); X.go(XVC,YVC,px.at[3],Pn)
    def addc(y,own,h):
        def body(i,_):
            unpack_c(y[i],DOC,0)
            r=i*TOK
            t=own[pl.ds(pl.multiple_of(r,16),TOK)]+DOC[...].astype(f32)
            h[i]=pack_c(t[:CB],t[CB:])
            return 0
        lax.fori_loop(0,4,body,0)
    wrecv(YKC,px.at[2],Pn); addc(YKC,SK,HKC)
    home(lambda zz: HKC.at[zz],ROWS["kc"],CB,4)
    wrecv(YVC,px.at[3],Pn); addc(YVC,SV,HVC)
    home(lambda zz: HVC.at[zz],ROWS["vc"],CB,5)
    for si,(r0,n) in enumerate(((0,TOK),(ROWS["qc"],CB),(ROWS["k"],TOK),(ROWS["v"],TOK),(ROWS["kc"],CB),(ROWS["vc"],CB))):
        for d in (1,2,3):
            zz=(z+d)%4
            wrecv(dsp.at[zz,pl.ds(r0,n)],ho.at[si,zz],Pn)
    for cp in loc[2:]: cp.wait()
    X.drain()

def attn_bwd(dog,bias,saved,cid):
    return pl.pallas_call(bwd_kernel,
        out_shape=sds(4,3*(TOK+CB),128),
        in_specs=[VM]*12,out_specs=VM,
        scratch_shapes=[vb(NQ,128),vb(4,CB,128),vb(TOK,128),vf(2,TOK,NK),vb(PADQ,NK),vb(PADQ,NK),vf(128,NK),vf(128,NK),vf(NK,128),
            vb(NQ,128),vb(4,CB,128)]+[vb(NQ,128)]*4+[vf(NQ,128)]*2+[vb(NQ,128)]*2+[vb(4,CB,128)]*6+[
            D((32,)),D((10,)),D((4,)),D((4,)),D((4,)),D((6,4))],
        compiler_params=pltpu.CompilerParams(collective_id=cid,has_side_effects=True,vmem_limit_bytes=60*1024*1024))(dog,bias,*saved)


HI=lax.Precision.HIGHEST
DM=768
MTILES=(0,None,1,2,None,3)

def spread(pair, packed):
    lane=lax.broadcasted_iota(jnp.int32,(CB,128),1)
    def mid(g0,g1):
        a=packed(g0).astype(f32); b=packed(g1).astype(f32)
        top=jnp.where(lane<64,a,pltpu.roll(b,64,1))
        low=jnp.where(lane<64,pltpu.roll(a,64,1),b)
        return jnp.concatenate([top,low[:TOK-CB]],0).astype(bf16)
    return [pair(0),mid(0,1),pair(1),pair(2),mid(2,3),pair(3)]

def gather_groups(tiles):
    out=[]
    for g in range(4):
        p=tiles[(0,2,3,5)[g]]
        t=tiles[(1,1,4,4)[g]]
        if g%2: t=pltpu.roll(t,64,1)
        out.append((p.astype(bf16),pack_c(t[:CB],t[CB:])))
    return out

def wcols(W,j,n):
    S=W.shape[0]
    return jnp.concatenate([W[:,j+i].reshape(S*16,128) for i in range(n)],1)

def lnorm(x):
    c=x-jnp.mean(x,-1,keepdims=True)
    inv=lax.rsqrt(jnp.mean(c*c,-1,keepdims=True)+EPSILON)
    return c*inv,inv

def lnorm_back(dy,gain,n,inv):
    g=dy*gain
    return inv*(g-jnp.mean(g,-1,keepdims=True)-n*jnp.mean(g*n,-1,keepdims=True))

def vrow(V,i):
    return jnp.concatenate([V[6*i+j:6*i+j+1,:] for j in range(6)],1)

def colsum(x): return jnp.sum(x,0,keepdims=True)

def front_kernel(start, fidx, pix, G, x0o, h1o, sp, We, Wq, PO, POf, TI, VE, V, TIf, sems):
    cps=[pltpu.make_async_copy(G.at[pl.ds(0,576)],We,sems.at[0]),
         pltpu.make_async_copy(G.at[pl.ds(4224+(48+6*start[0])//16,151)],PO,sems.at[1]),
         pltpu.make_async_copy(G.at[pl.ds(4224+264,3)],TI,sems.at[2]),
         pltpu.make_async_copy(G.at[pl.ds(4512,7)],VE,sems.at[3]),
         pltpu.make_async_copy(G.at[pl.ds(576,864)],Wq,sems.at[4])]
    for cp in cps: cp.start()
    for cp in cps[:4]: cp.wait()
    for i in range(7): V[pl.ds(i*16,16),:]=VE[i].astype(f32)
    for i in range(3): TIf[pl.ds(i*16,16),:]=TI[i].astype(f32)
    def cv(i,_):
        POf[pl.ds(i*16,16),:]=PO[i].astype(f32); return 0
    lax.fori_loop(0,151,cv,0)
    rem=(6*start[0])%16
    W4=We.reshape(96,6,16,128)
    for j in range(3):
        e=dot(pix[...],wcols(W4,2*j,2),NN)
        p=jnp.concatenate([POf[pl.ds(rem+2*j+i,TOK,stride=6),:] for i in range(2)],1)
        tm=jnp.concatenate([TIf[pl.ds(6*fidx[0]+2*j+i,1),:] for i in range(2)],1)
        bb=jnp.concatenate([V[48+2*j+i:49+2*j+i,:] for i in range(2)],1)
        x0o[:,j*256:(j+1)*256]=e+bb+p+tm
    n,inv=lnorm(x0o[...])
    h1=(n*vrow(V,0)+vrow(V,1)).astype(bf16)
    h1o[...]=h1
    cps[4].wait()
    W4=Wq.reshape(48,18,16,128)
    for part in range(3):
        tiles=[]
        for j in range(3):
            r=dot(h1,wcols(W4,part*6+2*j,2),NN)
            if part!=1:
                o=54 if part==0 else 60
                r=r+jnp.concatenate([V[o+2*j+i:o+1+2*j+i,:] for i in range(2)],1)
            r=r.astype(bf16).astype(f32)
            if part==0: r=r*0.125
            tiles+=[r[:,:128],r[:,128:]]
        for g,(p,c) in enumerate(gather_groups(tiles)):
            sp[g,pl.ds(part*TOK,TOK)]=p
            sp[g,pl.ds(3*TOK+part*CB,CB)]=c

SM=pl.BlockSpec(memory_space=pltpu.SMEM)
ANYS=pl.BlockSpec(memory_space=pl.ANY)
def front(start,fidx,pix,G):
    return pl.pallas_call(front_kernel,
        out_shape=(sds(TOK,DM,d=f32),sds(TOK,DM),sds(4,3*(TOK+CB),128)),
        in_specs=[SM,SM,VM,ANYS],out_specs=(VM,)*3,
        scratch_shapes=[vb(576,16,128),vb(864,16,128),vb(151,16,128),vf(2416,128),vb(3,16,128),vb(7,16,128),vf(112,128),vf(48,128),D((5,))],
        compiler_params=pltpu.CompilerParams(vmem_limit_bytes=60*1024*1024))(start,fidx,pix,G)

def mid_kernel(og, x0, G, wmap, vmask, scal, counts, sel,
               atto, h2o, acto, dpreo, dmlpo, dattno, dsec, dog, vgo, ubo, gmapo, gprojo, losso,
               Wo, Wu, Wd, Wp, VE, V, A2, GP, SLOT, x1s, x2s, sems, ssem, rsem):
    b=lax.axis_index("batch"); f=lax.axis_index("frame"); k=b*8+f
    def dev_of(kk): return (kk//8,kk%8)
    bar=pltpu.get_barrier_semaphore()
    def greet(d,_):
        pl.semaphore_signal(bar,inc=1,device_id=dev_of((k+d)%32),device_id_type=MESH); return 0
    lax.fori_loop(1,32,greet,0)
    cps=[pltpu.make_async_copy(G.at[pl.ds(10*144,288)],Wo,sems.at[0]),
         pltpu.make_async_copy(G.at[pl.ds(4512,7)],VE,sems.at[1]),
         pltpu.make_async_copy(G.at[pl.ds(12*144,1152)],Wu,sems.at[2]),
         pltpu.make_async_copy(G.at[pl.ds(20*144,1152)],Wd,sems.at[3]),
         pltpu.make_async_copy(G.at[pl.ds(28*144,192)],Wp,sems.at[4])]
    for cp in cps: cp.start()
    for j,t in enumerate(spread(lambda g: og[g,pl.ds(0,TOK)],lambda g: og[g,pl.ds(TOK,CB)])):
        atto[:,j*128:(j+1)*128]=t
    cps[0].wait(); cps[1].wait()
    for i in range(7): V[pl.ds(i*16,16),:]=VE[i].astype(f32)
    Wo4=Wo.reshape(48,6,16,128); Wu4=Wu.reshape(48,24,16,128); Wd4=Wd.reshape(192,6,16,128); Wp4=Wp.reshape(48,4,16,128)
    att=atto[...]
    for j in range(3):
        bb=jnp.concatenate([V[66+2*j+i:67+2*j+i,:] for i in range(2)],1)
        x1s[:,j*256:(j+1)*256]=x0[:,j*256:(j+1)*256]+(dot(att,wcols(Wo4,2*j,2),NN)+bb)
    n2,inv2=lnorm(x1s[...])
    h2=(n2*vrow(V,2)+vrow(V,3)).astype(bf16)
    h2o[...]=h2
    x2s[...]=x1s[...]+vrow(V,12)
    cps[2].wait(); cps[3].wait()
    def hid(j,_):
        w=jnp.concatenate([Wu4[:,2*j+i].reshape(768,128) for i in range(2)],1)
        bb=jnp.concatenate([V[pl.ds(78+2*j+i,1),:] for i in range(2)],1)
        u=dot(h2o[...],w,NN)+bb
        phi=0.5*(1.0+lax.erf(u*(0.5**0.5)))
        a=(u*phi).astype(bf16)
        cs=pl.ds(pl.multiple_of(j*256,256),256)
        GP[:,cs]=phi+u*(jnp.exp(-0.5*u*u)*0.3989422804014327)
        acto[:,cs]=a
        wd=Wd4[pl.ds(j*16,16)]
        x2s[...]+=dot(a,jnp.concatenate([wd[:,t].reshape(256,128) for t in range(6)],1),NN)
        return 0
    lax.fori_loop(0,12,hid,0)
    x2=x2s[...]
    nm,invm=lnorm(x2)
    nmap=nm*vrow(V,4)+vrow(V,5)
    lg=lax.dot_general(nmap,wmap[...],NN,precision=HI,preferred_element_type=f32)
    ok=vmask[...]>0.0
    lg=jnp.where(ok,lg,-1e30)
    ex=jnp.where(ok,jnp.exp(lg-jnp.max(lg,0,keepdims=True)),0.0)
    lane8=lax.broadcasted_iota(jnp.int32,(TOK,128),1)<NMAP
    maps=jnp.where(lane8,ex/jnp.sum(ex,0,keepdims=True),0.0)
    r=jnp.sum(maps,-1,keepdims=True)
    sw=scal[0:1,0:1]; inv_total=scal[1:2,0:1]
    pooled=sw*colsum(r*x2)
    corr=sw*colsum(r*r-jnp.sum(maps*maps,-1,keepdims=True))
    slot=[pooled[:,j*128:(j+1)*128] for j in range(6)]+[jnp.broadcast_to(corr,(1,128)),jnp.zeros((1,128),f32)]
    SLOT[k,pl.ds(0,8)]=jnp.concatenate(slot,0)
    SLOT[k,pl.ds(8,8)]=sel[...]
    def xcopy(d):
        return pltpu.make_async_remote_copy(src_ref=SLOT.at[k],dst_ref=SLOT.at[k],send_sem=ssem.at[d],recv_sem=rsem.at[k],device_id=dev_of((k+d)%32),device_id_type=MESH)
    pl.semaphore_wait(bar,31)
    def xs(d,_):
        xcopy(d).start(); return 0
    lax.fori_loop(1,32,xs,0)
    cps[4].wait()
    def xw(d,_):
        kk=(k+d)%32
        wrecv(SLOT.at[kk],rsem.at[kk],(b,f)); return 0
    lax.fori_loop(1,32,xw,0)
    tot=[]
    for cl in range(4):
        t=SLOT[cl*8,pl.ds(0,8)]
        for ff in range(1,8): t=t+SLOT[cl*8+ff,pl.ds(0,8)]
        tot.append(t)
    corr_total=(tot[0]+tot[1]+tot[2]+tot[3])[6:7,0:1]
    pm=jnp.concatenate([jnp.concatenate([t[j:j+1,:] for j in range(6)],1) for t in tot]+[jnp.zeros((4,DM),f32)],0)/counts[:,0:1]
    nf,invf=lnorm(pm)
    hf=nf*vrow(V,6)+vrow(V,7)
    rows=lax.broadcasted_iota(jnp.int32,(8,1),0)
    live=rows<4
    wp=jnp.concatenate([Wp4[:,t].reshape(768,128) for t in range(4)],1).astype(f32)
    e=lax.dot_general(hf,wp,NN,precision=HI,preferred_element_type=f32)
    rn=lax.rsqrt(jnp.sum(e*e,-1,keepdims=True)+1e-06)
    unit=e*rn
    lanes=lax.broadcasted_iota(jnp.int32,(8,128),1)
    gm=jnp.zeros((8,128),f32)
    for j in range(4):
        gm=gm+jnp.where(lanes==j,jnp.sum(unit*unit[j:j+1,:],-1,keepdims=True),0.0)
    selk=[jnp.concatenate([SLOT[cl*8,pl.ds(8+kk,1)] for cl in range(4)]+[jnp.zeros((4,128),f32)],0) for kk in range(5)]
    S=[jnp.sum(s*gm,-1,keepdims=True)/SOFTMAX_TEMPER for s in selk]
    mx=S[0]
    for s in S[1:]: mx=jnp.maximum(mx,s)
    es=[jnp.exp(s-mx) for s in S]
    se=es[0]+es[1]+es[2]+es[3]+es[4]
    contrast=jnp.sum(jnp.where(live,mx+jnp.log(se)-S[0],0.0),0,keepdims=True)*0.25
    losso[...]=jnp.broadcast_to(contrast+DECAY_PENALTY*corr_total*inv_total,(8,128))
    dgm=jnp.zeros((8,128),f32)
    for kk in range(5):
        w=es[kk]/se-(1.0 if kk==0 else 0.0)
        dgm=dgm+jnp.where(live,w,0.0)*selk[kk]
    dgm=dgm*(0.25/SOFTMAX_TEMPER)
    du=jnp.zeros((8,EMB),f32)
    for j in range(4):
        cj=dgm[:,j:j+1]
        du=du+cj*unit[j:j+1,:]
        du=du+jnp.where(rows==j,colsum(cj*unit),0.0)
    de=rn*du-e*(rn*rn*rn)*jnp.sum(e*du,-1,keepdims=True)
    de=jnp.where(live,de,0.0)
    dhf=lax.dot_general(de,wp,NT,precision=HI,preferred_element_type=f32)
    head=jnp.where(k==0,1.0,0.0)
    gp=lax.dot_general(hf,de,TN,precision=HI,preferred_element_type=f32)*head
    gpb=gp.astype(bf16)
    for s in range(48):
        for t in range(4): gprojo[s*4+t]=gpb[s*16:(s+1)*16,t*128:(t+1)*128]
    vgo[6:7,:]=colsum(dhf*nf)*head
    vgo[7:8,:]=colsum(dhf)*head
    dpm=lnorm_back(dhf,vrow(V,6),nf,invf)/counts[:,0:1]
    dpool=colsum(jnp.where(rows==b,dpm,0.0))
    cdec=DECAY_PENALTY*inv_total*sw
    dm=sw*jnp.sum(x2*dpool,-1,keepdims=True)+2.0*cdec*(r-maps)
    dm=jnp.where(lane8,dm,0.0)
    dl=maps*(dm-colsum(maps*dm))
    gmapo[...]=lax.dot_general(nmap,dl,TN,precision=HI,preferred_element_type=f32)
    dnm=lax.dot_general(dl,wmap[...],NT,precision=HI,preferred_element_type=f32)
    vgo[4:5,:]=colsum(dnm*nm)
    vgo[5:6,:]=colsum(dnm)
    dx2=(sw*r)*dpool+lnorm_back(dnm,vrow(V,4),nm,invm)
    dmlp=dx2.astype(bf16)
    dmlpo[...]=dmlp
    vgo[12:13,:]=colsum(dmlp.astype(f32))
    x2s[...]=jnp.zeros((TOK,DM),f32)
    dsec[...]=dx2
    def hidb(j,_):
        cs=pl.ds(pl.multiple_of(j*256,256),256)
        wd=Wd4[pl.ds(j*16,16)]
        da=dot(dmlpo[...],jnp.concatenate([wd[:,t].reshape(256,128) for t in range(6)],1),NT)
        dp=(da*GP[:,cs]).astype(bf16)
        dpreo[:,cs]=dp
        ubo[:,cs]=colsum(dp.astype(f32))
        w=jnp.concatenate([Wu4[:,2*j+i].reshape(768,128) for i in range(2)],1)
        x2s[...]+=dot(dp,w,NT)
        return 0
    lax.fori_loop(0,12,hidb,0)
    dh2=x2s[...]
    n2,inv2=lnorm(x1s[...])
    vgo[2:3,:]=colsum(dh2*n2)
    vgo[3:4,:]=colsum(dh2)
    dx1=dsec[...]+lnorm_back(dh2,vrow(V,2),n2,inv2)
    dsec[...]=dx1
    da_=dx1.astype(bf16)
    dattno[...]=da_
    vgo[11:12,:]=colsum(da_.astype(f32))
    tiles=[]
    for j in range(6):
        w=jnp.concatenate([Wo4[8*j:8*j+8,t].reshape(128,128) for t in range(6)],1)
        tiles.append(dot(da_,w,NT).astype(bf16).astype(f32))
    for g,(p,c) in enumerate(gather_groups(tiles)):
        dog[g,pl.ds(0,TOK)]=p
        dog[g,pl.ds(TOK,CB)]=c
    def xd(d,_):
        xcopy(d).wait_send(); return 0
    lax.fori_loop(1,32,xd,0)

def middle(og,x0,G,wmap,vmask,scal,counts,sel,cid):
    return pl.pallas_call(mid_kernel,
        out_shape=(sds(TOK,DM),sds(TOK,DM),sds(TOK,FFW),sds(TOK,FFW),sds(TOK,DM),sds(TOK,DM),sds(TOK,DM,d=f32),sds(4,TOK+CB,128),
                   sds(16,DM,d=f32),sds(1,FFW,d=f32),sds(DM,128,d=f32),sds(192,16,128),sds(8,128,d=f32)),
        in_specs=[VM,VM,ANYS]+[VM]*5,out_specs=(VM,)*13,
        scratch_shapes=[vb(288,16,128),vb(1152,16,128),vb(1152,16,128),vb(192,16,128),vb(7,16,128),vf(112,128),vf(8,128),vf(TOK,FFW),vf(32,16,128),
            vf(TOK,DM),vf(TOK,DM),D((5,)),D((32,)),D((32,))],
        compiler_params=pltpu.CompilerParams(collective_id=cid,has_side_effects=True,vmem_limit_bytes=63*1024*1024))(og,x0,G,wmap,vmask,scal,counts,sel)

def back_kernel(start, fidx, dsp, G, x0, dsec, vg, ub, gmap, gproj, dqkv, dx0o, tailo, Wq, VE, V, TL, sems):
    cps=[pltpu.make_async_copy(G.at[pl.ds(576,864)],Wq,sems.at[0]),pltpu.make_async_copy(G.at[pl.ds(4512,7)],VE,sems.at[1])]
    for cp in cps: cp.start()
    for part in range(3):
        for j,t in enumerate(spread(lambda g: dsp[g,pl.ds(part*TOK,TOK)],lambda g: dsp[g,pl.ds(3*TOK+part*CB,CB)])):
            dqkv[:,(part*6+j)*128:(part*6+j+1)*128]=t
    def z(i,_):
        TL[pl.ds(i*64,64),:]=jnp.zeros((64,128),f32); return 0
    lax.fori_loop(0,96,z,0)
    for cp in cps: cp.wait()
    for i in range(7): V[pl.ds(i*16,16),:]=VE[i].astype(f32)
    W4=Wq.reshape(48,18,16,128)
    acc=jnp.zeros((TOK,DM),f32)
    for j in range(9):
        acc=acc+dot(dqkv[:,j*256:(j+1)*256],wcols(W4,2*j,2),NT)
    n,inv=lnorm(x0[...])
    ent=dsec[...]+lnorm_back(acc,vrow(V,0),n,inv)
    dx0o[...]=ent.astype(bf16)
    eb=colsum(ent)
    def rowput(i,v):
        for j in range(6): TL[pl.ds(i+j,1),:]=v[:,j*128:(j+1)*128]
    TL[0:48,:]=gmap[...]
    for j in range(6):
        TL[pl.ds(48+6*start[0]+j,TOK,stride=6),:]=ent[:,j*128:(j+1)*128]
    rowput(4224+6*fidx[0],eb)
    vec={0:colsum(acc*n),1:colsum(acc),8:eb,9:colsum(dqkv[:,0:DM].astype(f32)),10:colsum(dqkv[:,2*DM:].astype(f32))}
    for i in range(13):
        rowput(4608+6*i, vec[i] if i in vec else vg[i:i+1,:])
    for j in range(24): TL[4608+78+j:4608+79+j,:]=ub[:,j*128:(j+1)*128]
    def cg(i,_):
        tailo[pl.ds(i*8,8)]=gproj[pl.ds(i*8,8)]; return 0
    lax.fori_loop(0,24,cg,0)
    def ct(i,_):
        tailo[192+i]=TL[pl.ds(pl.multiple_of(i*16,16),16),:].astype(bf16); return 0
    lax.fori_loop(0,384,ct,0)

def back(start,fidx,dsp,G,x0,dsec,vg,ub,gmap,gproj):
    return pl.pallas_call(back_kernel,
        out_shape=(sds(TOK,3*DM),sds(TOK,DM),sds(576,16,128)),
        in_specs=[SM,SM,VM,ANYS]+[VM]*6,out_specs=(VM,)*3,
        scratch_shapes=[vb(864,16,128),vb(7,16,128),vf(112,128),vf(6144,128),D((2,))],
        compiler_params=pltpu.CompilerParams(vmem_limit_bytes=60*1024*1024))(start,fidx,dsp,G,x0,dsec,vg,ub,gmap,gproj)


SHARD = 289176
BLOCK = 294912
SLIDE = BLOCK - SHARD
CARRY = 32 * SLIDE
KEY_ORDER_C = 2


def to_tiles(matrix):
    rows, width = matrix.shape
    m = width // 128
    return matrix.reshape(rows // 16, 16, m, 128).transpose(0, 2, 1, 3).reshape(-1, 16, 128)


def block_to_tiles(flat, k):
    def of(width):
        return lambda v: to_tiles(v.reshape(-1, width))

    def split29(v):
        return jnp.concatenate([to_tiles(v[: 48 * 2048].reshape(-1, 512)), v[48 * 2048 :].reshape(-1, 16, 128)])

    branch = class_of(k)
    return lax.switch(branch, [of(768), of(2304), of(3072), of(512), split29, of(128)], flat)


def class_of(k):
    return jnp.where(
        k < 4, 0, jnp.where(k < 10, 1, jnp.where(k < 12, 0, jnp.where(k < 20, 2, jnp.where(k < 28, 0, jnp.where(k == 28, 3, jnp.where(k == 29, 4, 5))))))
    )


def local_4x8(
    pixels,
    res_class,
    valid_tubelet_count,
    positive,
    negatives,
    master,
    first_moment,
    second_moment,
    adam_step,
):
    D = HEAD_COUNT * HEAD_FEATURES
    both_axes = ("batch", "frame")
    bi = lax.axis_index("batch")
    fi = lax.axis_index("frame")
    k = bi * 8 + fi
    low = to_bfloat(master)
    nxt = lax.ppermute(low[:CARRY], both_axes, [(i + 1, i) for i in range(31)])
    block = lax.dynamic_slice(jnp.concatenate([low, nxt]), (SLIDE * k,), (BLOCK,))
    G = make_ag()(block_to_tiles(block, k), 0)
    flat_tiles = G.reshape(32 * 144, 16, 128)
    w_map = G[29, 48:51].reshape(D, NMAP).astype(jnp.float32)
    w_map = jnp.pad(w_map, ((0, 0), (0, 128 - NMAP)))
    tubelets = lax.dynamic_slice_in_dim(valid_tubelet_count, bi, 1, 0)
    patches = jnp.where(res_class == 0, P0, jnp.where(res_class == 1, P1, PATCHES_THIRD_2)).astype(jnp.int32)
    start_rows = jnp.where(res_class == 0, 0, jnp.where(res_class == 1, P0, P0 + P1)).astype(jnp.int32)
    frame = jnp.full((1,), fi, jnp.int32)
    pix = pixels.reshape(400, TUBELET_PIXELS)
    first_in, h1, sp = front(start_rows, frame, pix, flat_tiles)
    slot = jnp.arange(8, dtype=jnp.int32)
    slot_tubelet = (slot % 4) * 2 + slot // 4
    key_ok = (slot_tubelet[:, None] < tubelets[0]) & (jnp.arange(400, dtype=jnp.int32)[None] < patches[0])
    bias = jnp.where(key_ok.reshape(1, 3200), 0.0, -1e30).astype(jnp.float32)
    og, *saved_attn = attn_fwd(sp, bias, 2)
    total_count = jnp.sum(valid_tubelet_count).astype(jnp.float32)
    patch_mask = jnp.broadcast_to((jnp.arange(400, dtype=jnp.int32)[:, None] < patches[0]).astype(jnp.float32), (400, 128))
    slot_weight = (fi < tubelets[0]).astype(jnp.float32)
    scal = jnp.broadcast_to(
        jnp.concatenate([slot_weight[None], 1.0 / total_count[None], jnp.zeros((6,), jnp.float32)])[:, None], (8, 128)
    )
    counts = jnp.broadcast_to(
        jnp.concatenate([(NMAP * valid_tubelet_count).astype(jnp.float32), jnp.ones((4,), jnp.float32)])[:, None], (8, 128)
    )
    ids = jnp.concatenate([positive, negatives[0], jnp.full((3,), -1, jnp.int32)])
    chosen = (ids[:, None] == jnp.arange(128, dtype=jnp.int32)[None]).astype(jnp.float32)
    (attended, h2, hidden_low, g_pre, g_mlp, g_attn, g_second, dog, g_vec, g_up_bias, g_map, g_proj, loss_rows) = middle(
        og, first_in, flat_tiles, w_map, patch_mask, scal, counts, chosen, 4
    )
    loss_value = loss_rows[0, 0]
    dsp = attn_bwd(dog, bias, saved_attn, 3)
    g_qkv, g_entry, tail_tiles = back(
        start_rows, frame, dsp, flat_tiles, first_in, g_second, g_vec, g_up_bias, g_map[:, :NMAP].reshape(48, 128), g_proj
    )
    grad, squares = make_rsx()(
        pix, h1, attended, h2, hidden_low, g_entry, g_qkv, g_attn, g_pre, g_mlp, tail_tiles.reshape(4, 144, 16, 128), cid=1
    )
    grad = grad.reshape(-1)[:SHARD]
    grad_norm = jnp.sqrt(jnp.sum(squares))
    clipped = grad * jnp.minimum(1.0, CLIP_AT / grad_norm)
    new_first = BETA_ONE * first_moment + (1.0 - BETA_ONE) * clipped
    new_second = BETA_TWO * second_moment + (1.0 - BETA_TWO) * clipped * clipped
    step = adam_step[0].astype(jnp.float32)
    update = new_first / (1.0 - BETA_ONE**step) / (jnp.sqrt(new_second / (1.0 - BETA_TWO**step)) + ADAM_EPS)
    new_master = master - RATE * (update + DECAY * master)
    return (new_master, new_first, new_second, to_bfloat(new_master), loss_value, grad_norm)


def solution(mesh):
    fast = dict(mesh.shape) == {"batch": 4, "frame": 8}
    return jax.shard_map(
        local_4x8 if fast else local_any_mesh,
        mesh=mesh,
        in_specs=(
            P("batch", "frame", None, None),
            P("batch"),
            P(),
            P("batch"),
            P("batch", None),
            P(("batch", "frame")),
            P(("batch", "frame")),
            P(("batch", "frame")),
            P(),
        ),
        out_specs=(
            P(("batch", "frame")),
            P(("batch", "frame")),
            P(("batch", "frame")),
            P(("batch", "frame")),
            P(),
            P(),
        ),
        check_vma=False,
    )
```

```python
from functools import partial
import math

import jax
import jax.numpy as jnp
from jax import lax
from jax.experimental import pallas as pl
from jax.experimental.pallas import tpu as pltpu
from jax.sharding import PartitionSpec as P

HEAD_COUNT = 12
HEAD_FEATURES = 64
FFW = 3072
TUBELET_PIXELS = 1536
EMB = 512
NMAP = 8
P0 = 100
P1 = 196
PATCHES_THIRD_2 = 400
TMAX = 64
NVEC = 13
CLIPS_PER_BATCH = 1


EPSILON = 1e-05
SOFTMAX_TEMPER = 0.02
DECAY_PENALTY = 1.0
CLIP_AT = 0.05
RATE = 0.03
DECAY = 0.05
BETA_ONE = 0.9
BETA_TWO = 0.999
ADAM_EPS = 1e-08
HIGH_ACCURACY = lax.Precision.HIGHEST


def to_bfloat(values):
    return values.astype(jnp.bfloat16)


def unpack_flat(flat_vector):
    width_of_model = HEAD_COUNT * HEAD_FEATURES
    dims_list = [
        (TUBELET_PIXELS, width_of_model),
        (width_of_model, 3 * width_of_model),
        (width_of_model, width_of_model),
        (width_of_model, FFW),
        (FFW, width_of_model),
        (width_of_model, EMB),
        (width_of_model, NMAP),
        (P0 + P1 + PATCHES_THIRD_2, width_of_model),
        (TMAX, width_of_model),
        (NVEC, width_of_model),
        (FFW,),
    ]
    pieces = []
    offset = 0
    for dims_of in dims_list:
        length = math.prod(dims_of)
        pieces.append(flat_vector[offset : offset + length].reshape(dims_of))
        offset += length
    return pieces


def norm_forward(inputs, gain_row, shift_row):
    center = inputs - jnp.mean(inputs, -1, keepdims=True)
    inverse = lax.rsqrt(jnp.mean(center * center, -1, keepdims=True) + EPSILON)
    normed = center * inverse
    return (normed * gain_row + shift_row, (normed, inverse))


def norm_backward(grad_out, gain_row, saved_parts):
    normed, inverse = saved_parts
    scaled = grad_out * gain_row
    grad_in = inverse * (
        scaled
        - jnp.mean(scaled, -1, keepdims=True)
        - normed * jnp.mean(scaled * normed, -1, keepdims=True)
    )
    lead_axes = tuple(range(grad_out.ndim - 1))
    return (grad_in, jnp.sum(grad_out * normed, lead_axes), jnp.sum(grad_out, lead_axes))


def block_plan(total_rows):
    shards = total_rows // PATCHES_THIRD_2
    group_size = 4
    return (shards // group_size, group_size * PATCHES_THIRD_2)


def local_any_mesh(
    pixels,
    res_class,
    valid_tubelet_count,
    positive,
    negatives,
    master,
    first_moment,
    second_moment,
    adam_step,
):
    width_of_model = HEAD_COUNT * HEAD_FEATURES
    score_scale = HEAD_FEATURES ** (-0.5)
    every_clip_rows = CLIPS_PER_BATCH * lax.axis_size("batch")
    index_of_batch = lax.axis_index("batch")
    frame_index = lax.axis_index("frame")
    gathered = lax.all_gather(to_bfloat(master), ("batch", "frame"), axis=0, tiled=True)
    w_embed, w_qkv, w_out, w_up, w_down, w_proj, w_map, pos_space, pos_time, vectors, bias_up = (
        unpack_flat(gathered)
    )
    vec_f = vectors.astype(jnp.float32)
    tubelet_stack = lax.dynamic_slice_in_dim(
        valid_tubelet_count, index_of_batch * CLIPS_PER_BATCH, CLIPS_PER_BATCH, 0
    )
    patches = jnp.where(res_class == 0, P0, jnp.where(res_class == 1, P1, PATCHES_THIRD_2)).astype(
        jnp.int32
    )
    start_rows = jnp.where(res_class == 0, 0, jnp.where(res_class == 1, P0, P0 + P1)).astype(
        jnp.int32
    )
    patch_pos = jnp.stack(
        [lax.dynamic_slice_in_dim(pos_space, start_rows[0], PATCHES_THIRD_2, 0)]
    ).astype(jnp.float32)
    time_row = lax.dynamic_slice_in_dim(pos_time, frame_index, 1, 0).astype(jnp.float32)
    rows_of_pixels = pixels.reshape(CLIPS_PER_BATCH * PATCHES_THIRD_2, TUBELET_PIXELS)
    embedded = jnp.dot(rows_of_pixels, w_embed, preferred_element_type=jnp.float32).reshape(
        CLIPS_PER_BATCH, PATCHES_THIRD_2, width_of_model
    )
    first_in = embedded + vec_f[8] + patch_pos + time_row
    normed_one, saved_one = norm_forward(first_in, vec_f[0], vec_f[1])
    normed_one = to_bfloat(normed_one)
    qkv_bias = jnp.concatenate([vec_f[9], jnp.zeros_like(vec_f[9]), vec_f[10]])
    projection_output = to_bfloat(
        jnp.einsum("cpd,de->cpe", normed_one, w_qkv, preferred_element_type=jnp.float32) + qkv_bias
    )
    query_matrix = projection_output[..., :width_of_model].reshape(
        CLIPS_PER_BATCH, PATCHES_THIRD_2, HEAD_COUNT, HEAD_FEATURES
    )
    kv_local = projection_output[..., width_of_model:]

    def key_mask(row_start, count_of_rows):
        row_ids = row_start + jnp.arange(count_of_rows, dtype=jnp.int32)
        return ((row_ids // PATCHES_THIRD_2)[None, :] < tubelet_stack[:, None]) & (
            (row_ids % PATCHES_THIRD_2)[None, :] < patches[:, None]
        )

    def block_scores(key_value_block, block_start):
        count_of_rows = key_value_block.shape[1]
        head_keys = key_value_block[..., :width_of_model].reshape(
            CLIPS_PER_BATCH, count_of_rows, HEAD_COUNT, HEAD_FEATURES
        )
        head_values = key_value_block[..., width_of_model:].reshape(
            CLIPS_PER_BATCH, count_of_rows, HEAD_COUNT, HEAD_FEATURES
        )
        key_ok = key_mask(block_start, count_of_rows)[:, None, None, :]
        scores = (
            jnp.einsum(
                "cqhd,ckhd->chqk", query_matrix, head_keys, preferred_element_type=jnp.float32
            )
            * score_scale
        )
        return (jnp.where(key_ok, scores, -1e30), key_ok, head_keys, head_values)

    forward_init = (
        jnp.full((CLIPS_PER_BATCH, HEAD_COUNT, PATCHES_THIRD_2), -1e30, jnp.float32),
        jnp.zeros((CLIPS_PER_BATCH, HEAD_COUNT, PATCHES_THIRD_2), jnp.float32),
        jnp.zeros((CLIPS_PER_BATCH, HEAD_COUNT, PATCHES_THIRD_2, HEAD_FEATURES), jnp.float32),
    )
    kv_piece = lax.all_gather(kv_local, "frame", axis=1, tiled=True)
    count_blocks, block_rows = block_plan(kv_piece.shape[1])

    def forward_one_block(block_index, running):
        run_max, run_sum, run_acc = running
        block_start = block_index * block_rows
        key_value_block = lax.dynamic_slice_in_dim(
            kv_piece, block_index * block_rows, block_rows, 1
        )
        scores, key_ok, head_keys, head_values = block_scores(key_value_block, block_start)
        new_max = jnp.maximum(run_max, jnp.max(scores, -1))
        factor = jnp.exp(run_max - new_max)
        prob_tile = jnp.where(key_ok, jnp.exp(scores - new_max[..., None]), 0.0)
        run_acc = run_acc * factor[..., None] + jnp.einsum(
            "chqk,ckhd->chqd", to_bfloat(prob_tile), head_values, preferred_element_type=jnp.float32
        )
        return (new_max, run_sum * factor + jnp.sum(prob_tile, -1), run_acc)

    run_max, run_sum, run_acc = lax.fori_loop(0, count_blocks, forward_one_block, forward_init)
    log_sum = run_max + jnp.log(run_sum)
    head_attended_rows = run_acc / run_sum[..., None]
    attended_reduced = to_bfloat(
        head_attended_rows.transpose(0, 2, 1, 3).reshape(
            CLIPS_PER_BATCH, PATCHES_THIRD_2, width_of_model
        )
    )
    second_in = (
        first_in
        + jnp.einsum("cpe,ed->cpd", attended_reduced, w_out, preferred_element_type=jnp.float32)
        + vec_f[11]
    )
    normed_two, saved_two = norm_forward(second_in, vec_f[2], vec_f[3])
    normed_two = to_bfloat(normed_two)
    hidden_pre = jnp.einsum(
        "cpd,df->cpf", normed_two, w_up, preferred_element_type=jnp.float32
    ) + bias_up.astype(jnp.float32)
    hidden_act, gelu_pull = jax.vjp(partial(jax.nn.gelu, approximate=False), hidden_pre)
    hidden_low = to_bfloat(hidden_act)
    block_out = (
        second_in
        + jnp.einsum("cpf,fd->cpd", hidden_low, w_down, preferred_element_type=jnp.float32)
        + vec_f[12]
    )
    valid_patch = jnp.arange(PATCHES_THIRD_2, dtype=jnp.int32)[None, :] < patches[:, None]
    slot_weight = (frame_index < tubelet_stack).astype(jnp.float32)

    def learner(block_in, gain_row, shift_row, map_weight):
        normed, unused = norm_forward(block_in, gain_row, shift_row)
        logits = jnp.einsum("cpd,dm->cpm", normed, map_weight, precision=HIGH_ACCURACY)
        logits = jnp.where(valid_patch[..., None], logits, -1e30)
        token_maps = jax.nn.softmax(logits, axis=1)
        pooled_part = jnp.einsum(
            "c,cpm,cpd->cd", slot_weight, token_maps, block_in, precision=HIGH_ACCURACY
        )
        gram_matrix = jnp.einsum("cpm,cpn->cmn", token_maps, token_maps, precision=HIGH_ACCURACY)
        correlation_part = slot_weight * (
            jnp.sum(gram_matrix, axis=(1, 2)) - jnp.trace(gram_matrix, axis1=1, axis2=2)
        )
        return (pooled_part, correlation_part)

    (pooled_part, correlation_part), learner_pull = jax.vjp(
        learner, block_out, vec_f[4], vec_f[5], w_map.astype(jnp.float32)
    )
    pooled_sum, correlation_sum = lax.psum((pooled_part, correlation_part), "frame")

    def head_map(pooled_in, gain_row, shift_row, proj_weight):
        pooled_mean = pooled_in / (NMAP * tubelet_stack).astype(jnp.float32)[:, None]
        normed, unused = norm_forward(pooled_mean, gain_row, shift_row)
        embedding = jnp.dot(
            normed, proj_weight, precision=HIGH_ACCURACY, preferred_element_type=jnp.float32
        )
        return embedding * lax.rsqrt(jnp.sum(embedding * embedding, -1, keepdims=True) + 1e-06)

    normalized_embedding, head_pull = jax.vjp(
        head_map, pooled_sum, vec_f[6], vec_f[7], w_proj.astype(jnp.float32)
    )
    embed_all, correlation_all = (
        lax.all_gather(normalized_embedding, "batch", axis=0, tiled=True),
        lax.all_gather(correlation_sum, "batch", axis=0, tiled=True),
    )
    selected_rows = jnp.concatenate([positive[:, None], negatives], axis=1)

    def contrast(embedding_input):
        local_row_set = lax.dynamic_slice_in_dim(
            embedding_input, index_of_batch * CLIPS_PER_BATCH, CLIPS_PER_BATCH, 0
        )
        similarity_matrix = (
            jnp.einsum(
                "yg,yeg->ye", local_row_set, embedding_input[selected_rows], precision=HIGH_ACCURACY
            )
            / SOFTMAX_TEMPER
        )
        return (
            jnp.sum(jax.nn.logsumexp(similarity_matrix, axis=1) - similarity_matrix[:, 0])
            / every_clip_rows
        )

    contrast_part, contrast_pull = jax.vjp(contrast, embed_all)
    (grad_embed_all,) = contrast_pull(jnp.ones_like(contrast_part))
    grad_unit = lax.psum_scatter(grad_embed_all, "batch", scatter_dimension=0, tiled=True)
    frame_total_count = jnp.sum(valid_tubelet_count).astype(jnp.float32)
    head_mask = (frame_index == 0).astype(jnp.float32)
    pooled_gradient, grad_final_gain, grad_final_shift, grad_proj = head_pull(grad_unit)
    grad_block, grad_learn_gain, grad_learn_shift, grad_map = learner_pull(
        (
            pooled_gradient,
            jnp.full((CLIPS_PER_BATCH,), DECAY_PENALTY / frame_total_count, jnp.float32),
        )
    )
    grad_mlp = to_bfloat(grad_block)
    grad_down_bias = jnp.sum(grad_mlp.astype(jnp.float32), (0, 1))
    grad_w_down = jnp.einsum(
        "cpf,cpd->fd", hidden_low, grad_mlp, preferred_element_type=jnp.float32
    )
    grad_hidden = jnp.einsum("cpd,fd->cpf", grad_mlp, w_down, preferred_element_type=jnp.float32)
    (grad_pre,) = gelu_pull(grad_hidden)
    grad_pre_low = to_bfloat(grad_pre)
    grad_up_bias = jnp.sum(grad_pre_low.astype(jnp.float32), (0, 1))
    grad_w_up = jnp.einsum(
        "cpd,cpf->df", normed_two, grad_pre_low, preferred_element_type=jnp.float32
    )
    grad_normed_two = jnp.einsum(
        "cpf,df->cpd", grad_pre_low, w_up, preferred_element_type=jnp.float32
    )
    grad_in_two, grad_gain_two, grad_shift_two = norm_backward(grad_normed_two, vec_f[2], saved_two)
    grad_second = grad_block + grad_in_two
    grad_attn = to_bfloat(grad_second)
    grad_out_bias = jnp.sum(grad_attn.astype(jnp.float32), (0, 1))
    grad_w_out = jnp.einsum(
        "cpe,cpd->ed", attended_reduced, grad_attn, preferred_element_type=jnp.float32
    )
    grad_attended = to_bfloat(
        jnp.einsum("cpd,ed->cpe", grad_attn, w_out, preferred_element_type=jnp.float32)
    ).reshape(CLIPS_PER_BATCH, PATCHES_THIRD_2, HEAD_COUNT, HEAD_FEATURES)
    row_delta = jnp.einsum("cqhd,chqd->chq", grad_attended.astype(jnp.float32), head_attended_rows)
    zeroed_query = jnp.zeros(
        (CLIPS_PER_BATCH, PATCHES_THIRD_2, HEAD_COUNT, HEAD_FEATURES), jnp.float32
    )
    query_kv_piece = lax.all_gather(kv_local, "frame", axis=1, tiled=True)
    count_blocks, query_block_rows = block_plan(query_kv_piece.shape[1])

    def query_one_block(block_index, query_gradient):
        block_start = block_index * query_block_rows
        key_value_block = lax.dynamic_slice_in_dim(
            query_kv_piece, block_index * query_block_rows, query_block_rows, 1
        )
        scores, key_ok, head_keys, head_values = block_scores(key_value_block, block_start)
        prob_tile = jnp.where(key_ok, jnp.exp(scores - log_sum[..., None]), 0.0)
        grad_prob = jnp.einsum(
            "cqhd,ckhd->chqk", grad_attended, head_values, preferred_element_type=jnp.float32
        )
        grad_score = to_bfloat(prob_tile * (grad_prob - row_delta[..., None]))
        return (
            query_gradient
            + jnp.einsum(
                "chqk,ckhd->cqhd", grad_score, head_keys, preferred_element_type=jnp.float32
            )
            * score_scale
        )

    query_gradient = lax.fori_loop(0, count_blocks, query_one_block, zeroed_query)
    own_keys = kv_local[..., :width_of_model].reshape(
        CLIPS_PER_BATCH, PATCHES_THIRD_2, HEAD_COUNT, HEAD_FEATURES
    )
    own_values = kv_local[..., width_of_model:].reshape(
        CLIPS_PER_BATCH, PATCHES_THIRD_2, HEAD_COUNT, HEAD_FEATURES
    )
    own_ok = key_mask(frame_index * PATCHES_THIRD_2, PATCHES_THIRD_2)[:, None, None, :]
    row_pieces = (
        query_matrix.astype(jnp.float32),
        grad_attended.astype(jnp.float32),
        log_sum.transpose(0, 2, 1),
        row_delta.transpose(0, 2, 1),
    )
    query_piece = lax.all_gather(
        row_pieces[0].astype(jnp.bfloat16), "frame", axis=1, tiled=True
    ).astype(jnp.float32)
    grad_out_piece = lax.all_gather(
        row_pieces[1].astype(jnp.bfloat16), "frame", axis=1, tiled=True
    ).astype(jnp.float32)
    lse_piece = lax.all_gather(
        row_pieces[2].astype(jnp.bfloat16), "frame", axis=1, tiled=True
    ).astype(jnp.float32)
    delta_piece = lax.all_gather(
        row_pieces[3].astype(jnp.bfloat16), "frame", axis=1, tiled=True
    ).astype(jnp.float32)
    count_blocks, own_block_rows = block_plan(query_piece.shape[1])

    def own_one_block(block_index, running):
        key_gradient, value_gradient = running
        offset = block_index * own_block_rows
        query_block = to_bfloat(lax.dynamic_slice_in_dim(query_piece, offset, own_block_rows, 1))
        grad_out_block = to_bfloat(
            lax.dynamic_slice_in_dim(grad_out_piece, offset, own_block_rows, 1)
        )
        lse_block = lax.dynamic_slice_in_dim(lse_piece, offset, own_block_rows, 1).transpose(
            0, 2, 1
        )
        delta_block = lax.dynamic_slice_in_dim(delta_piece, offset, own_block_rows, 1).transpose(
            0, 2, 1
        )
        scores = (
            jnp.einsum("cqhd,ckhd->chqk", query_block, own_keys, preferred_element_type=jnp.float32)
            * score_scale
        )
        scores = jnp.where(own_ok, scores, -1e30)
        prob_tile = jnp.where(own_ok, jnp.exp(scores - lse_block[..., None]), 0.0)
        grad_prob = jnp.einsum(
            "cqhd,ckhd->chqk", grad_out_block, own_values, preferred_element_type=jnp.float32
        )
        grad_score = to_bfloat(prob_tile * (grad_prob - delta_block[..., None]))
        key_gradient = (
            key_gradient
            + jnp.einsum(
                "chqk,cqhd->ckhd", grad_score, query_block, preferred_element_type=jnp.float32
            )
            * score_scale
        )
        value_gradient = value_gradient + jnp.einsum(
            "chqk,cqhd->ckhd",
            to_bfloat(prob_tile),
            grad_out_block,
            preferred_element_type=jnp.float32,
        )
        return (key_gradient, value_gradient)

    grad_key_own, grad_value_own = lax.fori_loop(
        0, count_blocks, own_one_block, (zeroed_query, zeroed_query)
    )
    gradient_key_value_local = to_bfloat(
        jnp.concatenate(
            [
                grad_key_own.reshape(CLIPS_PER_BATCH, PATCHES_THIRD_2, width_of_model),
                grad_value_own.reshape(CLIPS_PER_BATCH, PATCHES_THIRD_2, width_of_model),
            ],
            -1,
        )
    )
    gradient_query_key_value = jnp.concatenate(
        [
            to_bfloat(query_gradient).reshape(CLIPS_PER_BATCH, PATCHES_THIRD_2, width_of_model),
            gradient_key_value_local,
        ],
        -1,
    )
    grad_query_bias = jnp.sum(
        gradient_query_key_value[..., :width_of_model].astype(jnp.float32), (0, 1)
    )
    grad_value_bias = jnp.sum(
        gradient_query_key_value[..., 2 * width_of_model :].astype(jnp.float32), (0, 1)
    )
    grad_w_qkv = jnp.einsum(
        "cpd,cpe->de", normed_one, gradient_query_key_value, preferred_element_type=jnp.float32
    )
    grad_normed_one = jnp.einsum(
        "cpe,de->cpd", gradient_query_key_value, w_qkv, preferred_element_type=jnp.float32
    )
    grad_in_one, grad_gain_one, grad_shift_one = norm_backward(grad_normed_one, vec_f[0], saved_one)
    gradient_entry = grad_second + grad_in_one
    gradient_entry_low = to_bfloat(gradient_entry).reshape(
        CLIPS_PER_BATCH * PATCHES_THIRD_2, width_of_model
    )
    grad_w_embed = jnp.einsum(
        "rt,rd->td", rows_of_pixels, gradient_entry_low, preferred_element_type=jnp.float32
    )
    grad_embed_bias = jnp.sum(gradient_entry, (0, 1))
    grad_pos_space = jnp.zeros((P0 + P1 + PATCHES_THIRD_2, width_of_model), jnp.float32)
    current = lax.dynamic_slice_in_dim(grad_pos_space, start_rows[0], PATCHES_THIRD_2, 0)
    grad_pos_space = lax.dynamic_update_slice_in_dim(
        grad_pos_space, current + gradient_entry[0], start_rows[0], 0
    )
    grad_pos_time = lax.dynamic_update_slice_in_dim(
        jnp.zeros((TMAX, width_of_model), jnp.float32), grad_embed_bias[None], frame_index, 0
    )
    grad_vectors = jnp.stack(
        [
            grad_gain_one,
            grad_shift_one,
            grad_gain_two,
            grad_shift_two,
            grad_learn_gain,
            grad_learn_shift,
            grad_final_gain * head_mask,
            grad_final_shift * head_mask,
            grad_embed_bias,
            grad_query_bias,
            grad_value_bias,
            grad_out_bias,
            grad_down_bias,
        ]
    )
    flat_grad = jnp.concatenate(
        [
            piece_grad.reshape(-1)
            for piece_grad in (
                grad_w_embed,
                grad_w_qkv,
                grad_w_out,
                grad_w_up,
                grad_w_down,
                grad_proj * head_mask,
                grad_map,
                grad_pos_space,
                grad_pos_time,
                grad_vectors,
                grad_up_bias,
            )
        ]
    )
    grad_shard = lax.psum_scatter(flat_grad, ("batch", "frame"), scatter_dimension=0, tiled=True)
    contrast_keep = jnp.where(frame_index == 0, contrast_part, 0.0)
    square_sum, contrast_total = lax.psum(
        (jnp.sum(grad_shard * grad_shard), contrast_keep), ("batch", "frame")
    )
    grad_norm = jnp.sqrt(square_sum)
    loss_value = contrast_total + DECAY_PENALTY * jnp.sum(correlation_all) / frame_total_count
    clipped = grad_shard * jnp.minimum(1.0, CLIP_AT / grad_norm)
    new_first = BETA_ONE * first_moment + (1.0 - BETA_ONE) * clipped
    new_second = BETA_TWO * second_moment + (1.0 - BETA_TWO) * clipped * clipped
    step_count = adam_step[0].astype(jnp.float32)
    update = (
        new_first
        / (1.0 - BETA_ONE**step_count)
        / (jnp.sqrt(new_second / (1.0 - BETA_TWO**step_count)) + ADAM_EPS)
    )
    new_master = master - RATE * (update + DECAY * master)
    return (new_master, new_first, new_second, to_bfloat(new_master), loss_value, grad_norm)


MESH = pl.DeviceIdType.MESH
T=144
SPA=32

class Sends:
    def __init__(self, sem): self.sem=sem; self.n=0; self.items=[]
    def go(self, src, dst, rsem, dev, pred=None):
        c = pltpu.make_async_remote_copy(src_ref=src, dst_ref=dst, send_sem=self.sem.at[self.n], recv_sem=rsem, device_id=dev, device_id_type=MESH)
        self.n += 1
        if pred is None: c.start()
        else:
            @pl.when(pred)
            def _(): c.start()
        self.items.append((c,pred))
    def prep(self, src, dst, rsem, dev, pred=None):
        c = pltpu.make_async_remote_copy(src_ref=src, dst_ref=dst, send_sem=self.sem.at[self.n], recv_sem=rsem, device_id=dev, device_id_type=MESH)
        self.n += 1
        self.items.append((c,pred))
        def fire():
            if pred is None: c.start()
            else:
                @pl.when(pred)
                def _(): c.start()
        return fire
    def drain(self):
        for c,pred in self.items:
            if pred is None: c.wait_send()
            else:
                @pl.when(pred)
                def _(): c.wait_send()

def both(a,b):
    if a is None: return b
    if b is None: return a
    return jnp.logical_and(a,b)

def make_ag(spa=SPA):
    A=(0,spa); A1=(0,spa//2); A2=(spa//2,spa//2)
    nb=T-spa
    B=(spa,nb); B1=(spa,nb//2); B2=(spa+nb//2,nb//2)
    FULL=(0,T)
    def kernel(x_ref, out, ssem, lsem, zB, xB, yB, xBh, yBh, pA, zA, pown, pzB, pxB, pyB, pxBh, pyBh, ppA, pzA):
        b=lax.axis_index("batch"); f=lax.axis_index("frame")
        x=b%2; y=b//2; z=f//2; c=f%2
        bx=y*2+(1-x); by=(1-y)*2+x; bd=(1-y)*2+(1-x)
        X=(bx,f); Y=(by,f); Pn=(b,z*2+(1-c)); UP=(b,f+2); DN=(b,f-2)
        up=z<3; dn=z>0
        bar=pltpu.get_barrier_semaphore()
        for d,p in ((X,None),(Y,None),(Pn,None),(UP,up),(DN,dn)):
            if p is None: pl.semaphore_signal(bar,inc=1,device_id=d,device_id_type=MESH)
            else:
                @pl.when(p)
                def _(): pl.semaphore_signal(bar,inc=1,device_id=d,device_id_type=MESH)
        pl.semaphore_wait(bar, 4+(z*(3-z)+1)//3)
        S=Sends(ssem)
        def blk(bb,zz,part): return out.at[bb*8+zz*2+c, pl.ds(part[0],part[1])]
        def send(bb,zz,part,rsem,dev,pred=None,own=False):
            dst=blk(bb,zz,part)
            src=x_ref.at[pl.ds(part[0],part[1])] if own else dst
            S.go(src,dst,rsem,dev,pred)
        def wait(bb,zz,part,rsem):
            r=blk(bb,zz,part)
            pltpu.make_async_remote_copy(src_ref=r,dst_ref=r,send_sem=ssem.at[0],recv_sem=rsem,device_id=Pn,device_id_type=MESH).wait_recv()
        def waitp(pred,*a):
            if pred is None: wait(*a)
            else:
                @pl.when(pred)
                def _(): wait(*a)
        lc=pltpu.make_async_copy(x_ref, blk(b,z,FULL), lsem);
        send(b,z,A,pA.at[0],X,own=True); send(b,z,A,pA.at[1],Y,own=True)
        send(b,z,B,zB.at[z],UP,up,True); send(b,z,B,zB.at[z],DN,dn,True)
        send(b,z,B,xB.at[z],X,own=True); send(b,z,B,yB.at[z],Y,own=True)
        send(b,z,A,zA.at[z,0],UP,up,True); send(b,z,A,zA.at[z,0],DN,dn,True)
        send(b,z,FULL,pown.at[0],Pn,own=True)
        lc.start()
        pz=[]
        def pwait(*a): pz.append(a)
        pwait(None,b,z,FULL,pown.at[0])
        def zfwdA(bb,part,i,ps):
            send(bb,z,part,zA.at[z,i],UP,up); send(bb,z,part,zA.at[z,i],DN,dn)
            send(bb,z,part,ps,Pn); pwait(None,bb,z,part,ps)
        wait(bx,z,A,pA.at[0]); send(bx,z,A1,pA.at[2],Y); zfwdA(bx,A,1,ppA.at[0])
        wait(by,z,A,pA.at[1]); send(by,z,A2,pA.at[3],X); zfwdA(by,A,2,ppA.at[1])
        wait(bd,z,A1,pA.at[2]); zfwdA(bd,A1,3,ppA.at[2])
        wait(bd,z,A2,pA.at[3]); zfwdA(bd,A2,4,ppA.at[3])
        def xyB(zz,pred):
            waitp(pred,bx,zz,B,xB.at[zz]); send(bx,zz,B1,yBh.at[zz],Y,pred); send(bx,zz,B,pxB.at[zz],Pn,pred); pwait(pred,bx,zz,B,pxB.at[zz])
            waitp(pred,by,zz,B,yB.at[zz]); send(by,zz,B2,xBh.at[zz],X,pred); send(by,zz,B,pyB.at[zz],Pn,pred); pwait(pred,by,zz,B,pyB.at[zz])
        xyB(z,None)
        for d in (1,2,3):
            for s in (1,-1):
                zz=z+s*d
                pred=(zz<4) if s>0 else (zz>=0)
                nxt,np_=(DN,dn) if s>0 else (UP,up)
                waitp(pred,b,zz,B,zB.at[zz])
                send(b,zz,B,zB.at[zz],nxt,both(pred,np_))
                send(b,zz,B,xB.at[zz],X,pred); send(b,zz,B,yB.at[zz],Y,pred)
                send(b,zz,B,pzB.at[zz],Pn,pred); pwait(pred,b,zz,B,pzB.at[zz])
            for s in (1,-1):
                zz=z+s*d
                pred=(zz<4) if s>0 else (zz>=0)
                nxt,np_=(DN,dn) if s>0 else (UP,up)
                for i,(bb,part) in enumerate(((b,A),(bx,A),(by,A),(bd,A1),(bd,A2))):
                    waitp(pred,bb,zz,part,zA.at[zz,i]); send(bb,zz,part,zA.at[zz,i],nxt,both(pred,np_))
                    send(bb,zz,part,pzA.at[zz,i],Pn,pred); pwait(pred,bb,zz,part,pzA.at[zz,i])
            for s in (1,-1):
                zz=z+s*d
                pred=(zz<4) if s>0 else (zz>=0)
                xyB(zz,pred)
        for zz in range(4):
            wait(bd,zz,B1,yBh.at[zz]); send(bd,zz,B1,pyBh.at[zz],Pn); pwait(None,bd,zz,B1,pyBh.at[zz])
            wait(bd,zz,B2,xBh.at[zz]); send(bd,zz,B2,pxBh.at[zz],Pn); pwait(None,bd,zz,B2,pxBh.at[zz])
        for a in pz: waitp(*a)
        lc.wait()
        S.drain()
    D=pltpu.SemaphoreType.DMA
    def ag(xin, cid=0):
        return pl.pallas_call(kernel, out_shape=jax.ShapeDtypeStruct((32,T,16,128),jnp.bfloat16),
            in_specs=[pl.BlockSpec(memory_space=pltpu.VMEM)], out_specs=pl.BlockSpec(memory_space=pl.ANY),
            scratch_shapes=[D((160,)),D]+[D((4,))]*5+[D((4,)),D((4,5)),D((1,))]+[D((4,))]*5+[D((4,)),D((4,5))],
            compiler_params=pltpu.CompilerParams(collective_id=cid,has_side_effects=True))(xin)
    return ag


def make_rsx(spa=32):
    nb=T-spa
    A=(0,spa); A1=(0,spa//2); A2=(spa//2,spa//2)
    B=(spa,nb); B1=(spa,nb//2); B2=(spa+nb//2,nb//2)
    FULL=(0,T)
    def kernel(pix, h1, att, h2, act, dx0, dqkv, dattn, dpre, dmlp, tail, gout, nout,
               PS, R, h2T, LX, LY, LHX, LHY, LZB, LZA, LPA, out, C, CB_, CR_, NB, ssem, psem, stsem, csem, nsem, nsend, s_hx, s_hy, s_x, s_y, s_zb, s_za, s_pa):
        b=lax.axis_index("batch"); f=lax.axis_index("frame")
        x=b%2; y=b//2; z=f//2; c=f%2
        bx=y*2+(1-x); by=(1-y)*2+x; bd=(1-y)*2+(1-x)
        X=(bx,f); Y=(by,f); Pn=(b,z*2+(1-c)); UP=(b,f+2); DN=(b,f-2)
        up=z<3; dn=z>0
        t=z//2
        k=b*8+f
        def dev_of(kk): return (kk//8,kk%8)
        bar=pltpu.get_barrier_semaphore()
        def greet(d,_):
            pl.semaphore_signal(bar,inc=1,device_id=dev_of((k+d)%32),device_id_type=MESH); return 0
        lax.fori_loop(1,32,greet,0)
        zo=[3*(1-t), 2-t, (1-z)*(1-t)+(5-z)*t, z]
        order=[]
        for zz in zo: order += [(bd,zz)]
        for zz in zo: order += [(bx,zz),(by,zz)]
        for zz in zo: order += [(b,zz)]
        h2T[...]=h2[...].T
        TN_=(((0,),(0,)),((),()))
        def put(dst,r,m):
            rows=r.shape[0]
            r=r.astype(jnp.bfloat16)
            for s in range(rows//16):
                for j in range(m):
                    dst[s*m+j]=r[s*16:(s+1)*16,j*128:(j+1)*128]
        def col(a,i,n): return a[:,pl.ds(pl.multiple_of(i*n,128),n)]
        def comp(kk,dst):
            def mm(a,bb_,dims): return lax.dot_general(a,bb_,dims,preferred_element_type=jnp.float32)
            @pl.when(kk<4)
            def _(): put(dst,mm(col(pix,kk,384),dx0[...],TN_),6)
            @pl.when(jnp.logical_and(kk>=4,kk<10))
            def _(): put(dst,mm(col(h1,kk-4,128),dqkv[...],TN_),18)
            @pl.when(jnp.logical_and(kk>=10,kk<12))
            def _(): put(dst,mm(col(att,kk-10,384),dattn[...],TN_),6)
            @pl.when(jnp.logical_and(kk>=12,kk<20))
            def _(): put(dst,mm(h2T[pl.ds(pl.multiple_of((kk-12)*96,16),96)],dpre[...],(((1,),(0,)),((),()))),24)
            @pl.when(jnp.logical_and(kk>=20,kk<28))
            def _(): put(dst,mm(col(act,kk-20,384),dmlp[...],TN_),6)
            @pl.when(kk>=28)
            def _():
                def cp(i,_):
                    ds=pl.ds(i*8,8); dst[ds]=tail[kk-28,ds]; return 0
                lax.fori_loop(0,T//8,cp,0)
        def pick(i):
            g=jnp.where(i<4,i,jnp.where(i<12,(i-4)//2,i-12))
            zz=jnp.where(g==0,zo[0],jnp.where(g==1,zo[1],jnp.where(g==2,zo[2],zo[3])))
            bb=jnp.where(i<4,bd,jnp.where(i<12,jnp.where(i%2==0,bx,by),b))
            return bb,zz
        def pcopy(i):
            bb,zz=pick(i)
            return pltpu.make_async_remote_copy(src_ref=PS.at[16+i%4],dst_ref=R.at[bb,zz],send_sem=stsem.at[i%4],recv_sem=psem.at[bb,zz],device_id=Pn,device_id_type=MESH)
        S=Sends(ssem)
        def acc(dst, srcs, n, step=8):
            def body(i,_):
                ds=pl.ds(i*step,step)
                v=srcs[0][ds].astype(jnp.float32)
                for s in srcs[1:]: v=v+s[ds].astype(jnp.float32)
                dst[ds]=v.astype(dst.dtype)
                return 0
            lax.fori_loop(0,n//step,body,0)
        def sub(ref,part): return ref.at[pl.ds(part[0],part[1])]
        def ready(i):
            bb,zz=order[i]
            pltpu.make_async_remote_copy(src_ref=R.at[bb,zz],dst_ref=R.at[bb,zz],send_sem=ssem.at[0],recv_sem=psem.at[bb,zz],device_id=Pn,device_id_type=MESH).wait_recv()
        def wrecv(ref,sem):
            pltpu.make_async_remote_copy(src_ref=ref,dst_ref=ref,send_sem=ssem.at[0],recv_sem=sem,device_id=Pn,device_id_type=MESH).wait_recv()
        plan={}
        def at(h,fn): plan.setdefault(h,[]).append(fn)
        def diag(i,zz):
            f1=S.prep(sub(PS.at[bd*4+zz],B1), LHY.at[zz], s_hy.at[zz], Y)
            f2=S.prep(sub(PS.at[bd*4+zz],B2), LHX.at[zz], s_hx.at[zz], X)
            def fn():
                ready(i)
                acc(sub(PS.at[bd*4+zz],B), [sub(PS.at[bd*4+zz],B), sub(R.at[bd,zz],B)], nb)
                f1(); f2()
            return fn
        def chainA(bi,bb,ds=(3,2,1)):
            fns=[]
            for d in ds:
                for s in (1,-1):
                    zz=z+s*d
                    pred=(zz<4) if s>0 else (zz>=0)
                    frm=dn if s>0 else up
                    dev=UP if s>0 else DN
                    di=0 if s>0 else 1
                    fire=S.prep(sub(PS.at[bb*4+zz],A), LZA.at[di,zz,bi], s_za.at[di,zz,bi], dev, pred)
                    def fn(zz=zz,pred=pred,frm=frm,di=di,fire=fire):
                        @pl.when(jnp.logical_and(pred,frm))
                        def _():
                            wrecv(LZA.at[di,zz,bi], s_za.at[di,zz,bi])
                            acc(sub(PS.at[bb*4+zz],A),[sub(PS.at[bb*4+zz],A),sub(R.at[bb,zz],A),LZA.at[di,zz,bi]],spa)
                        @pl.when(jnp.logical_and(pred,jnp.logical_not(frm)))
                        def _():
                            acc(sub(PS.at[bb*4+zz],A),[sub(PS.at[bb*4+zz],A),sub(R.at[bb,zz],A)],spa)
                        fire()
                    fns.append(fn)
            return fns
        def sides(i,zz):
            fx=S.prep(sub(PS.at[bx*4+zz],B), LX.at[zz], s_x.at[zz], X)
            fy=S.prep(sub(PS.at[by*4+zz],B), LY.at[zz], s_y.at[zz], Y)
            def fn():
                ready(4+2*i); ready(5+2*i)
                wrecv(LHY.at[zz], s_hy.at[zz])
                acc(sub(PS.at[bx*4+zz],B1),[sub(PS.at[bx*4+zz],B1),sub(R.at[bx,zz],B1),LHY.at[zz]],nb//2)
                acc(sub(PS.at[bx*4+zz],B2),[sub(PS.at[bx*4+zz],B2),sub(R.at[bx,zz],B2)],nb//2)
                fx()
                wrecv(LHX.at[zz], s_hx.at[zz])
                acc(sub(PS.at[by*4+zz],B2),[sub(PS.at[by*4+zz],B2),sub(R.at[by,zz],B2),LHX.at[zz]],nb//2)
                acc(sub(PS.at[by*4+zz],B1),[sub(PS.at[by*4+zz],B1),sub(R.at[by,zz],B1)],nb//2)
                fy()
            return fn
        for i,zz in enumerate(zo): at(2*i+3,diag(i,zz))
        for j,d in enumerate((3,2,1)):
            for fn in chainA(0,bd,(d,)): at(10+2*j,fn)
        for i,zz in enumerate(zo): at(13+4*i,sides(i,zz))
        for bi,bb in ((1,bx),(2,by)):
            for j,d in enumerate((3,2,1)):
                for fn in chainA(bi,bb,(d,)): at(26+2*j,fn)
        def produce(h,_):
            i=h//2; own=h%2
            bb,zz=pick(i)
            @pl.when(own==0)
            def _():
                @pl.when(i>=4)
                def _(): pcopy(i-4).wait_send()
            kk=bb*8+zz*2+jnp.where(own==1,c,1-c)
            comp(kk,PS.at[jnp.where(own==1,bb*4+zz,16+i%4)])
            @pl.when(own==0)
            def _():
                @pl.when(i==0)
                def _(): pl.semaphore_wait(bar,31)
                pcopy(i).start()
            for hh,fns in sorted(plan.items()):
                @pl.when(h==hh)
                def _():
                    for fn in fns: fn()
            return 0
        lax.fori_loop(0,32,produce,0)
        for i in range(4): ready(12+i)
        for fn in chainA(3,b): fn()
        for i,zz in enumerate(zo[:3]):
            wrecv(LX.at[zz],s_x.at[zz]); wrecv(LY.at[zz],s_y.at[zz])
            isup=zz>z
            inc=jnp.logical_or(jnp.logical_and(isup,dn),jnp.logical_and(jnp.logical_not(isup),up))
            di=jnp.where(isup,0,1)
            base=[sub(PS.at[b*4+zz],B),sub(R.at[b,zz],B),LX.at[zz],LY.at[zz]]
            @pl.when(inc)
            def _():
                wrecv(LZB.at[di,zz],s_zb.at[di,zz])
                acc(sub(PS.at[b*4+zz],B),base+[LZB.at[di,zz]],nb)
            @pl.when(jnp.logical_not(inc))
            def _(): acc(sub(PS.at[b*4+zz],B),base,nb)
            S.go(sub(PS.at[b*4+zz],B),LZB.at[0,zz],s_zb.at[0,zz],UP,isup)
            S.go(sub(PS.at[b*4+zz],B),LZB.at[1,zz],s_zb.at[1,zz],DN,jnp.logical_not(isup))
        def totA(bi,bb,part,extra=(),dst=None):
            dst = dst if dst is not None else sub(PS.at[bb*4+z],part)
            srcs=[sub(PS.at[bb*4+z],part),sub(R.at[bb,z],part)]+list(extra)
            o=part[0]; n=part[1]
            l0=LZA.at[0,z,bi,pl.ds(o,n)]; l1=LZA.at[1,z,bi,pl.ds(o,n)]
            @pl.when(jnp.logical_and(up,dn))
            def _(): acc(dst,srcs+[l0,l1],n)
            @pl.when(jnp.logical_not(up))
            def _(): acc(dst,srcs+[l0],n)
            @pl.when(jnp.logical_not(dn))
            def _(): acc(dst,srcs+[l1],n)
        for bi in range(4):
            @pl.when(dn)
            def _(): wrecv(LZA.at[0,z,bi],s_za.at[0,z,bi])
            @pl.when(up)
            def _(): wrecv(LZA.at[1,z,bi],s_za.at[1,z,bi])
            if bi==0:
                totA(0,bd,A1); S.go(sub(PS.at[bd*4+z],A1),LPA.at[0,pl.ds(0,spa//2)],s_pa.at[0],Y)
                totA(0,bd,A2); S.go(sub(PS.at[bd*4+z],A2),LPA.at[1,pl.ds(0,spa//2)],s_pa.at[1],X)
            if bi==1:
                totA(1,bx,A2)
                wrecv(LPA.at[0,pl.ds(0,spa//2)],s_pa.at[0])
                totA(1,bx,A1,[LPA.at[0,pl.ds(0,spa//2)]])
                S.go(sub(PS.at[bx*4+z],A),LPA.at[2],s_pa.at[2],X)
            if bi==2:
                totA(2,by,A1)
                wrecv(LPA.at[1,pl.ds(0,spa//2)],s_pa.at[1])
                totA(2,by,A2,[LPA.at[1,pl.ds(0,spa//2)]])
                S.go(sub(PS.at[by*4+z],A),LPA.at[3],s_pa.at[3],Y)
        wrecv(LX.at[z],s_x.at[z]); wrecv(LY.at[z],s_y.at[z])
        base=[sub(PS.at[b*4+z],B),sub(R.at[b,z],B),LX.at[z],LY.at[z]]
        @pl.when(dn)
        def _(): wrecv(LZB.at[0,z],s_zb.at[0,z])
        @pl.when(up)
        def _(): wrecv(LZB.at[1,z],s_zb.at[1,z])
        @pl.when(jnp.logical_and(up,dn))
        def _(): acc(sub(out,B),base+[LZB.at[0,z],LZB.at[1,z]],nb)
        @pl.when(jnp.logical_not(up))
        def _(): acc(sub(out,B),base+[LZB.at[0,z]],nb)
        @pl.when(jnp.logical_not(dn))
        def _(): acc(sub(out,B),base+[LZB.at[1,z]],nb)
        wrecv(LPA.at[2],s_pa.at[2]); wrecv(LPA.at[3],s_pa.at[3])
        totA(3,b,A,[LPA.at[2],LPA.at[3]],dst=sub(out,A))
        def sq(i,a):
            v=out[i]; v=v*v
            return a+v[:8]+v[8:]
        NB[k]=lax.fori_loop(0,T,sq,jnp.zeros((8,128),jnp.float32))
        def ncopy(d):
            return pltpu.make_async_remote_copy(src_ref=NB.at[k],dst_ref=NB.at[k],send_sem=nsend.at[d],recv_sem=nsem.at[k],device_id=dev_of((k+d)%32),device_id_type=MESH)
        def nstart(d,_):
            ncopy(d).start(); return 0
        lax.fori_loop(1,32,nstart,0)
        CR=1440
        def untile(m,s0,n,t0):
            def body(s,_):
                for j in range(m):
                    C[pl.ds(CR+s0+s*16*m+j,16,stride=m),:]=out[t0+s*m+j]
                return 0
            lax.fori_loop(0,n,body,0)
        def plain(t0,n):
            def body(s,_):
                C[pl.ds(CR+(t0+s)*16,16),:]=out[t0+s]; return 0
            lax.fori_loop(0,n,body,0)
        def within(lo,hi): return jnp.logical_and(k>=lo,k<hi)
        @pl.when(jnp.logical_or(jnp.logical_or(within(0,4),within(10,12)),within(20,28)))
        def _(): untile(6,0,24,0)
        @pl.when(within(4,10))
        def _(): untile(18,0,8,0)
        @pl.when(within(12,20))
        def _(): untile(24,0,6,0)
        @pl.when(k==28)
        def _(): untile(4,0,36,0)
        @pl.when(k==29)
        def _():
            untile(4,0,12,0); plain(48,96)
        @pl.when(k>=30)
        def _(): plain(0,T)
        def carry(i,_):
            CB_[pl.ds(i*96,96)]=C[pl.ds(2304+i*96,96),:].astype(jnp.bfloat16); return 0
        lax.fori_loop(0,CR//96,carry,0)
        def cdesc(): return pltpu.make_async_remote_copy(src_ref=CB_,dst_ref=CR_,send_sem=csem.at[0],recv_sem=csem.at[1],device_id=dev_of((k+1)%32),device_id_type=MESH)
        @pl.when(k<31)
        def _(): cdesc().start()
        C[pl.ds(CR+2304,8),:]=jnp.zeros((8,128),jnp.float32)
        def nwait(d,_):
            kk=(k+d)%32
            wrecv_(NB.at[kk],nsem.at[kk],nsend.at[0],Pn); return 0
        lax.fori_loop(1,32,nwait,0)
        def nsum(i,a): return a+NB[i]
        nout[...]=lax.fori_loop(0,32,nsum,jnp.zeros((8,128),jnp.float32))
        @pl.when(k>0)
        def _():
            wrecv_(CR_,csem.at[1],csem.at[0],Pn)
            def uncarry(i,_):
                C[pl.ds(i*96,96),:]=CR_[pl.ds(i*96,96)].astype(jnp.float32); return 0
            lax.fori_loop(0,CR//96,uncarry,0)
        e=CR*128-(294912-289176)*k
        q=e//128; sh=e%128
        lane=lax.broadcasted_iota(jnp.int32,(96,128),1)
        def slide(i,_):
            r0=q+i*96
            a=pltpu.roll(C[pl.ds(r0,96),:],(128-sh)%128,1); b_=pltpu.roll(C[pl.ds(r0+1,96),:],(128-sh)%128,1)
            gout[pl.ds(i*96,96),:]=jnp.where(lane<128-sh,a,b_)
            return 0
        lax.fori_loop(0,24,slide,0)
        @pl.when(k<31)
        def _(): cdesc().wait_send()
        def ndone(d,_):
            ncopy(d).wait_send(); return 0
        lax.fori_loop(1,32,ndone,0)
        for i in range(12,16): pcopy(i).wait_send()
        S.drain()
    D=pltpu.SemaphoreType.DMA
    V=lambda *s: pltpu.VMEM(s+(16,128),jnp.bfloat16)
    VMs=pl.BlockSpec(memory_space=pltpu.VMEM)
    def rs(*args, cid=1):
        return pl.pallas_call(kernel, out_shape=(jax.ShapeDtypeStruct((2304,128),jnp.float32),jax.ShapeDtypeStruct((8,128),jnp.float32)),
            in_specs=[VMs]*11, out_specs=(VMs,VMs),
            scratch_shapes=[V(20,T),V(4,4,T),pltpu.VMEM((768,400),jnp.bfloat16),V(4,nb),V(4,nb),V(4,nb//2),V(4,nb//2),V(2,4,nb),V(2,4,4,spa),V(4,spa),
              pltpu.VMEM((T,16,128),jnp.float32),pltpu.VMEM((3752,128),jnp.float32),pltpu.VMEM((1440,128),jnp.bfloat16),pltpu.VMEM((1440,128),jnp.bfloat16),pltpu.VMEM((32,8,128),jnp.float32),
              D((80,)),D((4,4)),D((4,)),D((2,)),D((32,)),D((32,)),D((4,)),D((4,)),D((4,)),D((4,)),D((2,4)),D((2,4,4)),D((4,))],
            compiler_params=pltpu.CompilerParams(collective_id=cid,has_side_effects=True,vmem_limit_bytes=63*1024*1024))(*args)
    return rs

def wrecv_(ref,sem,ssem,dev):
    pltpu.make_async_remote_copy(src_ref=ref,dst_ref=ref,send_sem=ssem,recv_sem=sem,device_id=dev,device_id_type=MESH).wait_recv()


TOK=400; CB=208; NK=3200; NQ=1600; SUB=80; PADQ=512
ROWS={"q":0,"k":400,"v":800,"qc":1200,"kc":1408,"vc":1616}
NT=(((1,),(1,)),((),())); NN=(((1,),(0,)),((),())); TN=(((0,),(0,)),((),()))
f32=jnp.float32; bf16=jnp.bfloat16

def dot(a,b,dims): return lax.dot_general(a,b,dims,preferred_element_type=f32)

def mesh_pos():
    b=lax.axis_index("batch"); f=lax.axis_index("frame")
    return b,f//2,f%2

def zbarrier(b,z,c):
    bar=pltpu.get_barrier_semaphore()
    for d in (1,2,3):
        pl.semaphore_signal(bar,inc=1,device_id=(b,((z+d)%4)*2+c),device_id_type=MESH)
    pl.semaphore_signal(bar,inc=1,device_id=(b,z*2+1-c),device_id_type=MESH)
    pl.semaphore_wait(bar,4)

def wrecv(ref,sem,dev):
    pltpu.make_async_remote_copy(src_ref=ref,dst_ref=ref,send_sem=sem,recv_sem=sem,device_id=dev,device_id_type=MESH).wait_recv()

def others(z):
    return [((z+d)%4) for d in (2,1,3)]

def unpack_c(src, dst, row):
    v=src.astype(f32)
    lane=lax.broadcasted_iota(jnp.int32,(CB,128),1)
    lo=jnp.where(lane<64,v,0.0)
    hi=jnp.where(lane<64,pltpu.roll(v,64,1),0.0)
    dst[pl.ds(row,CB)]=lo.astype(bf16)
    dst[pl.ds(row+CB,TOK-CB)]=hi[:TOK-CB].astype(bf16)

def pack_c(lo, hi):
    hi=jnp.concatenate([hi,jnp.zeros((2*CB-TOK,128),f32)],0)
    lane=lax.broadcasted_iota(jnp.int32,(CB,128),1)
    return jnp.where(lane<64,lo,pltpu.roll(hi,64,1)).astype(bf16)

def fwd_kernel(sp, bias, og, Q, K, V, QC, KC, VC, OA, OC, LA, LC,
               QCp, KCp, VCp, OB, OCp, S, Pb, ssem, lsem, rq, rk, rv, rqc, rkc, rvc, pk, pv, pkc, pvc, ro, roc):
    b,z,c=mesh_pos()
    Pn=(b,z*2+1-c)
    dev=lambda zz:(b,zz*2+c)
    row=lambda zz: pl.multiple_of(zz*TOK,16)
    krow=lambda zz: pl.multiple_of((c*4+zz)*TOK,16)
    pkrow=lambda zz: pl.multiple_of(((1-c)*4+zz)*TOK,16)
    zbarrier(b,z,c)
    X=Sends(ssem)
    part=lambda g,n,ln: sp.at[g,pl.ds(ROWS[n],ln)]
    loc=[]
    def lcopy(src,dst):
        cp=pltpu.make_async_copy(src,dst,lsem.at[len(loc)]); cp.start(); loc.append(cp)
    for zz in others(z):
        X.go(part(zz,"k",TOK),K.at[pl.ds(krow(z),TOK)],rk.at[z],dev(zz))
        X.go(part(zz,"q",TOK),Q.at[pl.ds(row(z),TOK)],rq.at[z],dev(zz))
        X.go(part(zz,"v",TOK),V.at[pl.ds(krow(z),TOK)],rv.at[z],dev(zz))
    lcopy(part(z,"k",TOK),K.at[pl.ds(krow(z),TOK)])
    lcopy(part(z,"q",TOK),Q.at[pl.ds(row(z),TOK)])
    lcopy(part(z,"v",TOK),V.at[pl.ds(krow(z),TOK)])
    lcopy(part(z,"kc",CB),KCp.at[c*4+z]); lcopy(part(z,"qc",CB),QCp.at[z]); lcopy(part(z,"vc",CB),VCp.at[c*4+z])
    X.go(part(z,"k",TOK),K.at[pl.ds(krow(z),TOK)],pk.at[z],Pn)
    X.go(part(z,"v",TOK),V.at[pl.ds(krow(z),TOK)],pv.at[z],Pn)
    X.go(part(z,"kc",CB),KCp.at[c*4+z],pkc.at[z],Pn)
    X.go(part(z,"vc",CB),VCp.at[c*4+z],pvc.at[z],Pn)
    for zz in others(z):
        X.go(part(zz,"kc",CB),KCp.at[c*4+z],rkc.at[z],dev(zz))
        X.go(part(zz,"qc",CB),QCp.at[z],rqc.at[z],dev(zz))
        X.go(part(zz,"vc",CB),VCp.at[c*4+z],rvc.at[z],dev(zz))
    for zz in [((z+d)%4) for d in (1,3,2)]:
        kr=K.at[pl.ds(krow(zz),TOK)]; vr=V.at[pl.ds(krow(zz),TOK)]
        wrecv(kr,rk.at[zz],Pn); X.go(kr,kr,pk.at[zz],Pn)
        wrecv(vr,rv.at[zz],Pn); X.go(vr,vr,pv.at[zz],Pn)
    for zz in range(4):
        r=K.at[pl.ds(pkrow(zz),TOK)]; wrecv(r,pk.at[zz],Pn)
        r=V.at[pl.ds(pkrow(zz),TOK)]; wrecv(r,pv.at[zz],Pn)
    for zz in [((z+d)%4) for d in (1,2,3)]:
        wrecv(Q.at[pl.ds(row(zz),TOK)],rq.at[zz],Pn)
    for cp in loc: cp.wait()
    lane=lax.broadcasted_iota(jnp.int32,(TOK,128),1)
    lane8=lax.broadcasted_iota(jnp.int32,(SUB,128),1)
    def softmax(slot):
        def sub(i,carry):
            ds=pl.ds(pl.multiple_of(i*SUB,16),SUB)
            s=S[slot,ds,:]+bias[...]
            m=jnp.max(s,-1,keepdims=True)
            p=jnp.exp(s-m)
            l=jnp.sum(p,-1,keepdims=True)
            Pb[slot,ds,:]=p.astype(bf16)
            return m,l
        ms=[];ls=[]
        for i in range(TOK//SUB):
            m,l=sub(i,0); ms.append(m); ls.append(l)
        return jnp.concatenate(ms,0),jnp.concatenate(ls,0)
    def pairblock(i,_):
        ds=pl.ds(pl.multiple_of(i*TOK,16),TOK)
        q=Q[ds]
        zero=jnp.zeros_like(q)
        S[0]=dot(jnp.where(lane<64,q,zero),K[...],NT)
        S[1]=dot(jnp.where(lane<64,zero,q),K[...],NT)
        ma,la=softmax(0); mb,lb=softmax(1)
        oa=dot(Pb[0],V[...],NN)/la; ob=dot(Pb[1],V[...],NN)/lb
        o=jnp.where(lane<64,oa,ob)
        OA[ds]=o; OB[ds]=o.astype(bf16)
        LA[ds]=jnp.where(lane<64,ma+jnp.log(la),mb+jnp.log(lb))
        return 0
    lax.fori_loop(0,4,pairblock,0)
    for zz in [((z+d)%4) for d in (1,3,2)]:
        kr=KCp.at[c*4+zz]; vr=VCp.at[c*4+zz]
        wrecv(kr,rkc.at[zz],Pn); X.go(kr,kr,pkc.at[zz],Pn)
        wrecv(vr,rvc.at[zz],Pn); X.go(vr,vr,pvc.at[zz],Pn)
        wrecv(QCp.at[zz],rqc.at[zz],Pn)
    for zz in others(z):
        X.go(OB.at[pl.ds(row(zz),TOK)],og.at[z,pl.ds(0,TOK)],ro.at[z],dev(zz))
    lo=pltpu.make_async_copy(OB.at[pl.ds(row(z),TOK)],og.at[z,pl.ds(0,TOK)],lsem.at[6]); lo.start()
    for zz in range(4):
        wrecv(KCp.at[(1-c)*4+zz],pkc.at[zz],Pn); wrecv(VCp.at[(1-c)*4+zz],pvc.at[zz],Pn)
    def unp(i,_):
        r=pl.multiple_of(i*TOK,16)
        unpack_c(KCp[i],KC,r); unpack_c(VCp[i],VC,r)
        return 0
    lax.fori_loop(0,8,unp,0)
    def unq(i,_):
        unpack_c(QCp[i],QC,pl.multiple_of(i*TOK,16)); return 0
    lax.fori_loop(0,4,unq,0)
    def cblock(i,_):
        ds=pl.ds(pl.multiple_of(i*TOK,16),TOK)
        S[0]=dot(QC[ds],KC[...],NT)
        ma,la=softmax(0)
        o=dot(Pb[0],VC[...],NN)/la
        OC[ds]=o
        LC[ds]=jnp.broadcast_to(ma+jnp.log(la),(TOK,128))
        OCp[i]=pack_c(o[:CB],o[CB:])
        return 0
    lax.fori_loop(0,4,cblock,0)
    for zz in others(z):
        X.go(OCp.at[zz],og.at[z,pl.ds(TOK,CB)],roc.at[z],dev(zz))
    lc=pltpu.make_async_copy(OCp.at[z],og.at[z,pl.ds(TOK,CB)],lsem.at[7]); lc.start()
    for d in (1,2,3):
        zz=(z+d)%4
        wrecv(og.at[zz,pl.ds(0,TOK)],ro.at[zz],Pn)
        wrecv(og.at[zz,pl.ds(TOK,CB)],roc.at[zz],Pn)
    lo.wait(); lc.wait()
    X.drain()

D=pltpu.SemaphoreType.DMA
def vb(*s): return pltpu.VMEM(s,bf16)
def vf(*s): return pltpu.VMEM(s,f32)
VM=pl.BlockSpec(memory_space=pltpu.VMEM)
def sds(*s,d=bf16): return jax.ShapeDtypeStruct(s,d)

def attn_fwd(sp,bias,cid):
    return pl.pallas_call(fwd_kernel,
        out_shape=(sds(4,TOK+CB,128),sds(NQ,128),sds(NK,128),sds(NK,128),sds(NQ,128),sds(NK,128),sds(NK,128),
                   sds(NQ,128,d=f32),sds(NQ,128,d=f32),sds(NQ,128,d=f32),sds(NQ,128,d=f32)),
        in_specs=[VM,VM],out_specs=[VM]*11,
        scratch_shapes=[vb(4,CB,128),vb(8,CB,128),vb(8,CB,128),vb(NQ,128),vb(4,CB,128),vf(2,TOK,NK),vb(2,TOK,NK),
            D((48,)),D((8,))]+[D((4,))]*12,
        compiler_params=pltpu.CompilerParams(collective_id=cid,has_side_effects=True,vmem_limit_bytes=60*1024*1024))(sp,bias)

def bwd_kernel(dog, bias, Q, K, V, QC, KC, VC, OA, OC, LA, LC, dsp,
               DO, DOCp, DOC, S, P, DS, DKT, DVT, TT, DQ, DQC, XK, XV, YK, YV, SK, SV, HK, HV, XKC, XVC, YKC, YVC, HKC, HVC,
               ssem, lsem, rd, rdc, px, ho):
    b,z,c=mesh_pos()
    Pn=(b,z*2+1-c)
    dev=lambda zz:(b,zz*2+c)
    row=lambda zz: pl.multiple_of(zz*TOK,16)
    zbarrier(b,z,c)
    X=Sends(ssem)
    loc=[]
    def lcopy(src,dst):
        cp=pltpu.make_async_copy(src,dst,lsem.at[len(loc)]); cp.start(); loc.append(cp); return cp
    for zz in others(z):
        X.go(dog.at[zz,pl.ds(0,TOK)],DO.at[pl.ds(row(z),TOK)],rd.at[z],dev(zz))
    for zz in others(z):
        X.go(dog.at[zz,pl.ds(TOK,CB)],DOCp.at[z],rdc.at[z],dev(zz))
    l1=lcopy(dog.at[z,pl.ds(0,TOK)],DO.at[pl.ds(row(z),TOK)])
    l2=lcopy(dog.at[z,pl.ds(TOK,CB)],DOCp.at[z])
    l1.wait(); l2.wait()
    lane=lax.broadcasted_iota(jnp.int32,(TOK,128),1)
    def zero(ref):
        def bodyz(i,_):
            ref[:,pl.ds(pl.multiple_of(i*640,128),640)]=jnp.zeros((128,640),f32); return 0
        lax.fori_loop(0,NK//640,bodyz,0)
    def grads(q,k,v,do,lse,delta):
        S[0]=dot(q,k[...],NT)
        S[1]=dot(do,v[...],NT)
        for i in range(TOK//SUB):
            ds=pl.ds(i*SUB,SUB); sl=slice(i*SUB,(i+1)*SUB)
            p=jnp.exp(S[0,ds,:]+bias[...]-lse[sl])
            P[ds,:]=p.astype(bf16)
            DS[ds,:]=(p*(S[1,ds,:]-delta[sl])).astype(bf16)
        tail=jnp.zeros((PADQ-TOK,128),bf16)
        DKT[...]+=dot(jnp.concatenate([q,tail],0),DS[...],TN)
        DVT[...]+=dot(jnp.concatenate([do,tail],0),P[...],TN)
        return dot(DS[pl.ds(0,TOK)],k[...],NN)
    def home(src,r0,n,si):
        for zz in others(z):
            X.go(src(zz),dsp.at[z,pl.ds(r0,n)],ho.at[si,z],dev(zz))
        lcopy(src(z),dsp.at[z,pl.ds(r0,n)])
    mine=c*NQ; theirs=(1-c)*NQ
    def split(acc, x, own):
        def tr(i,_):
            TT[pl.ds(pl.multiple_of(i*640,16),640)]=acc[:,pl.ds(pl.multiple_of(i*640,128),640)].T
            return 0
        lax.fori_loop(0,NK//640,tr,0)
        def cut(i,_):
            r=pl.multiple_of(i*TOK,16)
            x[pl.ds(r,TOK)]=TT[pl.ds(pl.multiple_of(theirs+i*TOK,16),TOK)].astype(bf16)
            own[pl.ds(r,TOK)]=TT[pl.ds(pl.multiple_of(mine+i*TOK,16),TOK)]
            return 0
        lax.fori_loop(0,4,cut,0)
    P[pl.ds(TOK,PADQ-TOK)]=jnp.zeros((PADQ-TOK,NK),bf16)
    DS[pl.ds(TOK,PADQ-TOK)]=jnp.zeros((PADQ-TOK,NK),bf16)
    zero(DKT); zero(DVT)
    def pairblock(i,_):
        zz=(z+i)%4
        @pl.when(i>0)
        def _(): wrecv(DO.at[pl.ds(row(zz),TOK)],rd.at[zz],Pn)
        ds=pl.ds(row(zz),TOK)
        q=Q[ds]; do=DO[ds]; zero_=jnp.zeros_like(q)
        dof=do.astype(f32)*OA[ds]
        da=jnp.sum(jnp.where(lane<64,dof,0.0),-1,keepdims=True)
        db=jnp.sum(jnp.where(lane<64,0.0,dof),-1,keepdims=True)
        ga=grads(jnp.where(lane<64,q,zero_),K,V,jnp.where(lane<64,do,zero_),LA[ds,0:1],da)
        gb=grads(jnp.where(lane<64,zero_,q),K,V,jnp.where(lane<64,zero_,do),LA[ds,64:65],db)
        DQ[ds]=(jnp.where(lane<64,ga,gb)*0.125).astype(bf16)
        return 0
    lax.fori_loop(0,4,pairblock,0)
    home(lambda zz: DQ.at[pl.ds(row(zz),TOK)],0,TOK,0)
    split(DKT,XK,SK); X.go(XK,YK,px.at[0],Pn)
    split(DVT,XV,SV); X.go(XV,YV,px.at[1],Pn)
    zero(DKT); zero(DVT)
    def cblock(i,_):
        zz=(z+i)%4
        @pl.when(i>0)
        def _(): wrecv(DOCp.at[zz],rdc.at[zz],Pn)
        unpack_c(DOCp[zz],DOC,0)
        ds=pl.ds(row(zz),TOK)
        do=DOC[...]
        delta=jnp.sum(do.astype(f32)*OC[ds],-1,keepdims=True)
        g=grads(QC[ds],KC,VC,do,LC[ds,0:1],delta)*0.125
        DQC[zz]=pack_c(g[:CB],g[CB:])
        return 0
    lax.fori_loop(0,4,cblock,0)
    home(lambda zz: DQC.at[zz],ROWS["qc"],CB,1)
    wrecv(YK,px.at[0],Pn); wrecv(YV,px.at[1],Pn)
    def addp(i,_):
        ds=pl.ds(pl.multiple_of(i*TOK,16),TOK)
        HK[ds]=(SK[ds]+YK[ds].astype(f32)).astype(bf16)
        HV[ds]=(SV[ds]+YV[ds].astype(f32)).astype(bf16)
        return 0
    lax.fori_loop(0,4,addp,0)
    home(lambda zz: HK.at[pl.ds(row(zz),TOK)],ROWS["k"],TOK,2)
    home(lambda zz: HV.at[pl.ds(row(zz),TOK)],ROWS["v"],TOK,3)
    def splitc(acc, x, own):
        def tr(i,_):
            TT[pl.ds(pl.multiple_of(i*640,16),640)]=acc[:,pl.ds(pl.multiple_of(i*640,128),640)].T
            return 0
        lax.fori_loop(0,NK//640,tr,0)
        def cut(i,_):
            r=theirs+i*TOK
            x[i]=pack_c(TT[pl.ds(pl.multiple_of(r,16),CB)],TT[pl.ds(pl.multiple_of(r+CB,16),TOK-CB)])
            own[pl.ds(pl.multiple_of(i*TOK,16),TOK)]=TT[pl.ds(pl.multiple_of(mine+i*TOK,16),TOK)]
            return 0
        lax.fori_loop(0,4,cut,0)
    splitc(DKT,XKC,SK); X.go(XKC,YKC,px.at[2],Pn)
    splitc(DVT,XVC,SV); X.go(XVC,YVC,px.at[3],Pn)
    def addc(y,own,h):
        def body(i,_):
            unpack_c(y[i],DOC,0)
            r=i*TOK
            t=own[pl.ds(pl.multiple_of(r,16),TOK)]+DOC[...].astype(f32)
            h[i]=pack_c(t[:CB],t[CB:])
            return 0
        lax.fori_loop(0,4,body,0)
    wrecv(YKC,px.at[2],Pn); addc(YKC,SK,HKC)
    home(lambda zz: HKC.at[zz],ROWS["kc"],CB,4)
    wrecv(YVC,px.at[3],Pn); addc(YVC,SV,HVC)
    home(lambda zz: HVC.at[zz],ROWS["vc"],CB,5)
    for si,(r0,n) in enumerate(((0,TOK),(ROWS["qc"],CB),(ROWS["k"],TOK),(ROWS["v"],TOK),(ROWS["kc"],CB),(ROWS["vc"],CB))):
        for d in (1,2,3):
            zz=(z+d)%4
            wrecv(dsp.at[zz,pl.ds(r0,n)],ho.at[si,zz],Pn)
    for cp in loc[2:]: cp.wait()
    X.drain()

def attn_bwd(dog,bias,saved,cid):
    return pl.pallas_call(bwd_kernel,
        out_shape=sds(4,3*(TOK+CB),128),
        in_specs=[VM]*12,out_specs=VM,
        scratch_shapes=[vb(NQ,128),vb(4,CB,128),vb(TOK,128),vf(2,TOK,NK),vb(PADQ,NK),vb(PADQ,NK),vf(128,NK),vf(128,NK),vf(NK,128),
            vb(NQ,128),vb(4,CB,128)]+[vb(NQ,128)]*4+[vf(NQ,128)]*2+[vb(NQ,128)]*2+[vb(4,CB,128)]*6+[
            D((32,)),D((10,)),D((4,)),D((4,)),D((4,)),D((6,4))],
        compiler_params=pltpu.CompilerParams(collective_id=cid,has_side_effects=True,vmem_limit_bytes=60*1024*1024))(dog,bias,*saved)


HI=lax.Precision.HIGHEST
DM=768
MTILES=(0,None,1,2,None,3)

def spread(pair, packed):
    lane=lax.broadcasted_iota(jnp.int32,(CB,128),1)
    def mid(g0,g1):
        a=packed(g0).astype(f32); b=packed(g1).astype(f32)
        top=jnp.where(lane<64,a,pltpu.roll(b,64,1))
        low=jnp.where(lane<64,pltpu.roll(a,64,1),b)
        return jnp.concatenate([top,low[:TOK-CB]],0).astype(bf16)
    return [pair(0),mid(0,1),pair(1),pair(2),mid(2,3),pair(3)]

def gather_groups(tiles):
    out=[]
    for g in range(4):
        p=tiles[(0,2,3,5)[g]]
        t=tiles[(1,1,4,4)[g]]
        if g%2: t=pltpu.roll(t,64,1)
        out.append((p.astype(bf16),pack_c(t[:CB],t[CB:])))
    return out

def wcols(W,j,n):
    S=W.shape[0]
    return jnp.concatenate([W[:,j+i].reshape(S*16,128) for i in range(n)],1)

def lnorm(x):
    c=x-jnp.mean(x,-1,keepdims=True)
    inv=lax.rsqrt(jnp.mean(c*c,-1,keepdims=True)+EPSILON)
    return c*inv,inv

def lnorm_back(dy,gain,n,inv):
    g=dy*gain
    return inv*(g-jnp.mean(g,-1,keepdims=True)-n*jnp.mean(g*n,-1,keepdims=True))

def vrow(V,i):
    return jnp.concatenate([V[6*i+j:6*i+j+1,:] for j in range(6)],1)

def colsum(x): return jnp.sum(x,0,keepdims=True)

def front_kernel(start, fidx, pix, G, x0o, h1o, sp, We, Wq, PO, POf, TI, VE, V, TIf, sems):
    cps=[pltpu.make_async_copy(G.at[pl.ds(0,576)],We,sems.at[0]),
         pltpu.make_async_copy(G.at[pl.ds(4224+(48+6*start[0])//16,151)],PO,sems.at[1]),
         pltpu.make_async_copy(G.at[pl.ds(4224+264,3)],TI,sems.at[2]),
         pltpu.make_async_copy(G.at[pl.ds(4512,7)],VE,sems.at[3]),
         pltpu.make_async_copy(G.at[pl.ds(576,864)],Wq,sems.at[4])]
    for cp in cps: cp.start()
    for cp in cps[:4]: cp.wait()
    for i in range(7): V[pl.ds(i*16,16),:]=VE[i].astype(f32)
    for i in range(3): TIf[pl.ds(i*16,16),:]=TI[i].astype(f32)
    def cv(i,_):
        POf[pl.ds(i*16,16),:]=PO[i].astype(f32); return 0
    lax.fori_loop(0,151,cv,0)
    rem=(6*start[0])%16
    W4=We.reshape(96,6,16,128)
    for j in range(3):
        e=dot(pix[...],wcols(W4,2*j,2),NN)
        p=jnp.concatenate([POf[pl.ds(rem+2*j+i,TOK,stride=6),:] for i in range(2)],1)
        tm=jnp.concatenate([TIf[pl.ds(6*fidx[0]+2*j+i,1),:] for i in range(2)],1)
        bb=jnp.concatenate([V[48+2*j+i:49+2*j+i,:] for i in range(2)],1)
        x0o[:,j*256:(j+1)*256]=e+bb+p+tm
    n,inv=lnorm(x0o[...])
    h1=(n*vrow(V,0)+vrow(V,1)).astype(bf16)
    h1o[...]=h1
    cps[4].wait()
    W4=Wq.reshape(48,18,16,128)
    for part in range(3):
        tiles=[]
        for j in range(3):
            r=dot(h1,wcols(W4,part*6+2*j,2),NN)
            if part!=1:
                o=54 if part==0 else 60
                r=r+jnp.concatenate([V[o+2*j+i:o+1+2*j+i,:] for i in range(2)],1)
            r=r.astype(bf16).astype(f32)
            if part==0: r=r*0.125
            tiles+=[r[:,:128],r[:,128:]]
        for g,(p,c) in enumerate(gather_groups(tiles)):
            sp[g,pl.ds(part*TOK,TOK)]=p
            sp[g,pl.ds(3*TOK+part*CB,CB)]=c

SM=pl.BlockSpec(memory_space=pltpu.SMEM)
ANYS=pl.BlockSpec(memory_space=pl.ANY)
def front(start,fidx,pix,G):
    return pl.pallas_call(front_kernel,
        out_shape=(sds(TOK,DM,d=f32),sds(TOK,DM),sds(4,3*(TOK+CB),128)),
        in_specs=[SM,SM,VM,ANYS],out_specs=(VM,)*3,
        scratch_shapes=[vb(576,16,128),vb(864,16,128),vb(151,16,128),vf(2416,128),vb(3,16,128),vb(7,16,128),vf(112,128),vf(48,128),D((5,))],
        compiler_params=pltpu.CompilerParams(vmem_limit_bytes=60*1024*1024))(start,fidx,pix,G)

def mid_kernel(og, x0, G, wmap, vmask, scal, counts, sel,
               atto, h2o, acto, dpreo, dmlpo, dattno, dsec, dog, vgo, ubo, gmapo, gprojo, losso,
               Wo, Wu, Wd, Wp, VE, V, A2, GP, SLOT, x1s, x2s, sems, ssem, rsem):
    b=lax.axis_index("batch"); f=lax.axis_index("frame"); k=b*8+f
    def dev_of(kk): return (kk//8,kk%8)
    bar=pltpu.get_barrier_semaphore()
    def greet(d,_):
        pl.semaphore_signal(bar,inc=1,device_id=dev_of((k+d)%32),device_id_type=MESH); return 0
    lax.fori_loop(1,32,greet,0)
    cps=[pltpu.make_async_copy(G.at[pl.ds(10*144,288)],Wo,sems.at[0]),
         pltpu.make_async_copy(G.at[pl.ds(4512,7)],VE,sems.at[1]),
         pltpu.make_async_copy(G.at[pl.ds(12*144,1152)],Wu,sems.at[2]),
         pltpu.make_async_copy(G.at[pl.ds(20*144,1152)],Wd,sems.at[3]),
         pltpu.make_async_copy(G.at[pl.ds(28*144,192)],Wp,sems.at[4])]
    for cp in cps: cp.start()
    for j,t in enumerate(spread(lambda g: og[g,pl.ds(0,TOK)],lambda g: og[g,pl.ds(TOK,CB)])):
        atto[:,j*128:(j+1)*128]=t
    cps[0].wait(); cps[1].wait()
    for i in range(7): V[pl.ds(i*16,16),:]=VE[i].astype(f32)
    Wo4=Wo.reshape(48,6,16,128); Wu4=Wu.reshape(48,24,16,128); Wd4=Wd.reshape(192,6,16,128); Wp4=Wp.reshape(48,4,16,128)
    att=atto[...]
    for j in range(3):
        bb=jnp.concatenate([V[66+2*j+i:67+2*j+i,:] for i in range(2)],1)
        x1s[:,j*256:(j+1)*256]=x0[:,j*256:(j+1)*256]+(dot(att,wcols(Wo4,2*j,2),NN)+bb)
    n2,inv2=lnorm(x1s[...])
    h2=(n2*vrow(V,2)+vrow(V,3)).astype(bf16)
    h2o[...]=h2
    x2s[...]=x1s[...]+vrow(V,12)
    cps[2].wait(); cps[3].wait()
    def hid(j,_):
        w=jnp.concatenate([Wu4[:,2*j+i].reshape(768,128) for i in range(2)],1)
        bb=jnp.concatenate([V[pl.ds(78+2*j+i,1),:] for i in range(2)],1)
        u=dot(h2o[...],w,NN)+bb
        phi=0.5*(1.0+lax.erf(u*(0.5**0.5)))
        a=(u*phi).astype(bf16)
        cs=pl.ds(pl.multiple_of(j*256,256),256)
        GP[:,cs]=phi+u*(jnp.exp(-0.5*u*u)*0.3989422804014327)
        acto[:,cs]=a
        wd=Wd4[pl.ds(j*16,16)]
        x2s[...]+=dot(a,jnp.concatenate([wd[:,t].reshape(256,128) for t in range(6)],1),NN)
        return 0
    lax.fori_loop(0,12,hid,0)
    x2=x2s[...]
    nm,invm=lnorm(x2)
    nmap=nm*vrow(V,4)+vrow(V,5)
    lg=lax.dot_general(nmap,wmap[...],NN,precision=HI,preferred_element_type=f32)
    ok=vmask[...]>0.0
    lg=jnp.where(ok,lg,-1e30)
    ex=jnp.where(ok,jnp.exp(lg-jnp.max(lg,0,keepdims=True)),0.0)
    lane8=lax.broadcasted_iota(jnp.int32,(TOK,128),1)<NMAP
    maps=jnp.where(lane8,ex/jnp.sum(ex,0,keepdims=True),0.0)
    r=jnp.sum(maps,-1,keepdims=True)
    sw=scal[0:1,0:1]; inv_total=scal[1:2,0:1]
    pooled=sw*colsum(r*x2)
    corr=sw*colsum(r*r-jnp.sum(maps*maps,-1,keepdims=True))
    slot=[pooled[:,j*128:(j+1)*128] for j in range(6)]+[jnp.broadcast_to(corr,(1,128)),jnp.zeros((1,128),f32)]
    SLOT[k,pl.ds(0,8)]=jnp.concatenate(slot,0)
    SLOT[k,pl.ds(8,8)]=sel[...]
    def xcopy(d):
        return pltpu.make_async_remote_copy(src_ref=SLOT.at[k],dst_ref=SLOT.at[k],send_sem=ssem.at[d],recv_sem=rsem.at[k],device_id=dev_of((k+d)%32),device_id_type=MESH)
    pl.semaphore_wait(bar,31)
    def xs(d,_):
        xcopy(d).start(); return 0
    lax.fori_loop(1,32,xs,0)
    cps[4].wait()
    def xw(d,_):
        kk=(k+d)%32
        wrecv(SLOT.at[kk],rsem.at[kk],(b,f)); return 0
    lax.fori_loop(1,32,xw,0)
    tot=[]
    for cl in range(4):
        t=SLOT[cl*8,pl.ds(0,8)]
        for ff in range(1,8): t=t+SLOT[cl*8+ff,pl.ds(0,8)]
        tot.append(t)
    corr_total=(tot[0]+tot[1]+tot[2]+tot[3])[6:7,0:1]
    pm=jnp.concatenate([jnp.concatenate([t[j:j+1,:] for j in range(6)],1) for t in tot]+[jnp.zeros((4,DM),f32)],0)/counts[:,0:1]
    nf,invf=lnorm(pm)
    hf=nf*vrow(V,6)+vrow(V,7)
    rows=lax.broadcasted_iota(jnp.int32,(8,1),0)
    live=rows<4
    wp=jnp.concatenate([Wp4[:,t].reshape(768,128) for t in range(4)],1).astype(f32)
    e=lax.dot_general(hf,wp,NN,precision=HI,preferred_element_type=f32)
    rn=lax.rsqrt(jnp.sum(e*e,-1,keepdims=True)+1e-06)
    unit=e*rn
    lanes=lax.broadcasted_iota(jnp.int32,(8,128),1)
    gm=jnp.zeros((8,128),f32)
    for j in range(4):
        gm=gm+jnp.where(lanes==j,jnp.sum(unit*unit[j:j+1,:],-1,keepdims=True),0.0)
    selk=[jnp.concatenate([SLOT[cl*8,pl.ds(8+kk,1)] for cl in range(4)]+[jnp.zeros((4,128),f32)],0) for kk in range(5)]
    S=[jnp.sum(s*gm,-1,keepdims=True)/SOFTMAX_TEMPER for s in selk]
    mx=S[0]
    for s in S[1:]: mx=jnp.maximum(mx,s)
    es=[jnp.exp(s-mx) for s in S]
    se=es[0]+es[1]+es[2]+es[3]+es[4]
    contrast=jnp.sum(jnp.where(live,mx+jnp.log(se)-S[0],0.0),0,keepdims=True)*0.25
    losso[...]=jnp.broadcast_to(contrast+DECAY_PENALTY*corr_total*inv_total,(8,128))
    dgm=jnp.zeros((8,128),f32)
    for kk in range(5):
        w=es[kk]/se-(1.0 if kk==0 else 0.0)
        dgm=dgm+jnp.where(live,w,0.0)*selk[kk]
    dgm=dgm*(0.25/SOFTMAX_TEMPER)
    du=jnp.zeros((8,EMB),f32)
    for j in range(4):
        cj=dgm[:,j:j+1]
        du=du+cj*unit[j:j+1,:]
        du=du+jnp.where(rows==j,colsum(cj*unit),0.0)
    de=rn*du-e*(rn*rn*rn)*jnp.sum(e*du,-1,keepdims=True)
    de=jnp.where(live,de,0.0)
    dhf=lax.dot_general(de,wp,NT,precision=HI,preferred_element_type=f32)
    head=jnp.where(k==0,1.0,0.0)
    gp=lax.dot_general(hf,de,TN,precision=HI,preferred_element_type=f32)*head
    gpb=gp.astype(bf16)
    for s in range(48):
        for t in range(4): gprojo[s*4+t]=gpb[s*16:(s+1)*16,t*128:(t+1)*128]
    vgo[6:7,:]=colsum(dhf*nf)*head
    vgo[7:8,:]=colsum(dhf)*head
    dpm=lnorm_back(dhf,vrow(V,6),nf,invf)/counts[:,0:1]
    dpool=colsum(jnp.where(rows==b,dpm,0.0))
    cdec=DECAY_PENALTY*inv_total*sw
    dm=sw*jnp.sum(x2*dpool,-1,keepdims=True)+2.0*cdec*(r-maps)
    dm=jnp.where(lane8,dm,0.0)
    dl=maps*(dm-colsum(maps*dm))
    gmapo[...]=lax.dot_general(nmap,dl,TN,precision=HI,preferred_element_type=f32)
    dnm=lax.dot_general(dl,wmap[...],NT,precision=HI,preferred_element_type=f32)
    vgo[4:5,:]=colsum(dnm*nm)
    vgo[5:6,:]=colsum(dnm)
    dx2=(sw*r)*dpool+lnorm_back(dnm,vrow(V,4),nm,invm)
    dmlp=dx2.astype(bf16)
    dmlpo[...]=dmlp
    vgo[12:13,:]=colsum(dmlp.astype(f32))
    x2s[...]=jnp.zeros((TOK,DM),f32)
    dsec[...]=dx2
    def hidb(j,_):
        cs=pl.ds(pl.multiple_of(j*256,256),256)
        wd=Wd4[pl.ds(j*16,16)]
        da=dot(dmlpo[...],jnp.concatenate([wd[:,t].reshape(256,128) for t in range(6)],1),NT)
        dp=(da*GP[:,cs]).astype(bf16)
        dpreo[:,cs]=dp
        ubo[:,cs]=colsum(dp.astype(f32))
        w=jnp.concatenate([Wu4[:,2*j+i].reshape(768,128) for i in range(2)],1)
        x2s[...]+=dot(dp,w,NT)
        return 0
    lax.fori_loop(0,12,hidb,0)
    dh2=x2s[...]
    n2,inv2=lnorm(x1s[...])
    vgo[2:3,:]=colsum(dh2*n2)
    vgo[3:4,:]=colsum(dh2)
    dx1=dsec[...]+lnorm_back(dh2,vrow(V,2),n2,inv2)
    dsec[...]=dx1
    da_=dx1.astype(bf16)
    dattno[...]=da_
    vgo[11:12,:]=colsum(da_.astype(f32))
    tiles=[]
    for j in range(6):
        w=jnp.concatenate([Wo4[8*j:8*j+8,t].reshape(128,128) for t in range(6)],1)
        tiles.append(dot(da_,w,NT).astype(bf16).astype(f32))
    for g,(p,c) in enumerate(gather_groups(tiles)):
        dog[g,pl.ds(0,TOK)]=p
        dog[g,pl.ds(TOK,CB)]=c
    def xd(d,_):
        xcopy(d).wait_send(); return 0
    lax.fori_loop(1,32,xd,0)

def middle(og,x0,G,wmap,vmask,scal,counts,sel,cid):
    return pl.pallas_call(mid_kernel,
        out_shape=(sds(TOK,DM),sds(TOK,DM),sds(TOK,FFW),sds(TOK,FFW),sds(TOK,DM),sds(TOK,DM),sds(TOK,DM,d=f32),sds(4,TOK+CB,128),
                   sds(16,DM,d=f32),sds(1,FFW,d=f32),sds(DM,128,d=f32),sds(192,16,128),sds(8,128,d=f32)),
        in_specs=[VM,VM,ANYS]+[VM]*5,out_specs=(VM,)*13,
        scratch_shapes=[vb(288,16,128),vb(1152,16,128),vb(1152,16,128),vb(192,16,128),vb(7,16,128),vf(112,128),vf(8,128),vf(TOK,FFW),vf(32,16,128),
            vf(TOK,DM),vf(TOK,DM),D((5,)),D((32,)),D((32,))],
        compiler_params=pltpu.CompilerParams(collective_id=cid,has_side_effects=True,vmem_limit_bytes=63*1024*1024))(og,x0,G,wmap,vmask,scal,counts,sel)

def back_kernel(start, fidx, dsp, G, x0, dsec, vg, ub, gmap, gproj, dqkv, dx0o, tailo, Wq, VE, V, TL, sems):
    cps=[pltpu.make_async_copy(G.at[pl.ds(576,864)],Wq,sems.at[0]),pltpu.make_async_copy(G.at[pl.ds(4512,7)],VE,sems.at[1])]
    for cp in cps: cp.start()
    for part in range(3):
        for j,t in enumerate(spread(lambda g: dsp[g,pl.ds(part*TOK,TOK)],lambda g: dsp[g,pl.ds(3*TOK+part*CB,CB)])):
            dqkv[:,(part*6+j)*128:(part*6+j+1)*128]=t
    def z(i,_):
        TL[pl.ds(i*64,64),:]=jnp.zeros((64,128),f32); return 0
    lax.fori_loop(0,96,z,0)
    for cp in cps: cp.wait()
    for i in range(7): V[pl.ds(i*16,16),:]=VE[i].astype(f32)
    W4=Wq.reshape(48,18,16,128)
    acc=jnp.zeros((TOK,DM),f32)
    for j in range(9):
        acc=acc+dot(dqkv[:,j*256:(j+1)*256],wcols(W4,2*j,2),NT)
    n,inv=lnorm(x0[...])
    ent=dsec[...]+lnorm_back(acc,vrow(V,0),n,inv)
    dx0o[...]=ent.astype(bf16)
    eb=colsum(ent)
    def rowput(i,v):
        for j in range(6): TL[pl.ds(i+j,1),:]=v[:,j*128:(j+1)*128]
    TL[0:48,:]=gmap[...]
    for j in range(6):
        TL[pl.ds(48+6*start[0]+j,TOK,stride=6),:]=ent[:,j*128:(j+1)*128]
    rowput(4224+6*fidx[0],eb)
    vec={0:colsum(acc*n),1:colsum(acc),8:eb,9:colsum(dqkv[:,0:DM].astype(f32)),10:colsum(dqkv[:,2*DM:].astype(f32))}
    for i in range(13):
        rowput(4608+6*i, vec[i] if i in vec else vg[i:i+1,:])
    for j in range(24): TL[4608+78+j:4608+79+j,:]=ub[:,j*128:(j+1)*128]
    def cg(i,_):
        tailo[pl.ds(i*8,8)]=gproj[pl.ds(i*8,8)]; return 0
    lax.fori_loop(0,24,cg,0)
    def ct(i,_):
        tailo[192+i]=TL[pl.ds(pl.multiple_of(i*16,16),16),:].astype(bf16); return 0
    lax.fori_loop(0,384,ct,0)

def back(start,fidx,dsp,G,x0,dsec,vg,ub,gmap,gproj):
    return pl.pallas_call(back_kernel,
        out_shape=(sds(TOK,3*DM),sds(TOK,DM),sds(576,16,128)),
        in_specs=[SM,SM,VM,ANYS]+[VM]*6,out_specs=(VM,)*3,
        scratch_shapes=[vb(864,16,128),vb(7,16,128),vf(112,128),vf(6144,128),D((2,))],
        compiler_params=pltpu.CompilerParams(vmem_limit_bytes=60*1024*1024))(start,fidx,dsp,G,x0,dsec,vg,ub,gmap,gproj)


SHARD = 289176
BLOCK = 294912
SLIDE = BLOCK - SHARD
CARRY = 32 * SLIDE
KEY_ORDER_C = 2


def to_tiles(matrix):
    rows, width = matrix.shape
    m = width // 128
    return matrix.reshape(rows // 16, 16, m, 128).transpose(0, 2, 1, 3).reshape(-1, 16, 128)


def block_to_tiles(flat, k):
    def of(width):
        return lambda v: to_tiles(v.reshape(-1, width))

    def split29(v):
        return jnp.concatenate([to_tiles(v[: 48 * 2048].reshape(-1, 512)), v[48 * 2048 :].reshape(-1, 16, 128)])

    branch = class_of(k)
    return lax.switch(branch, [of(768), of(2304), of(3072), of(512), split29, of(128)], flat)


def class_of(k):
    return jnp.where(
        k < 4, 0, jnp.where(k < 10, 1, jnp.where(k < 12, 0, jnp.where(k < 20, 2, jnp.where(k < 28, 0, jnp.where(k == 28, 3, jnp.where(k == 29, 4, 5))))))
    )


def local_4x8(
    pixels,
    res_class,
    valid_tubelet_count,
    positive,
    negatives,
    master,
    first_moment,
    second_moment,
    adam_step,
):
    D = HEAD_COUNT * HEAD_FEATURES
    both_axes = ("batch", "frame")
    bi = lax.axis_index("batch")
    fi = lax.axis_index("frame")
    k = bi * 8 + fi
    low = to_bfloat(master)
    nxt = lax.ppermute(low[:CARRY], both_axes, [(i + 1, i) for i in range(31)])
    block = lax.dynamic_slice(jnp.concatenate([low, nxt]), (SLIDE * k,), (BLOCK,))
    G = make_ag()(block_to_tiles(block, k), 0)
    flat_tiles = G.reshape(32 * 144, 16, 128)
    w_map = G[29, 48:51].reshape(D, NMAP).astype(jnp.float32)
    w_map = jnp.pad(w_map, ((0, 0), (0, 128 - NMAP)))
    tubelets = lax.dynamic_slice_in_dim(valid_tubelet_count, bi, 1, 0)
    patches = jnp.where(res_class == 0, P0, jnp.where(res_class == 1, P1, PATCHES_THIRD_2)).astype(jnp.int32)
    start_rows = jnp.where(res_class == 0, 0, jnp.where(res_class == 1, P0, P0 + P1)).astype(jnp.int32)
    frame = jnp.full((1,), fi, jnp.int32)
    pix = pixels.reshape(400, TUBELET_PIXELS)
    first_in, h1, sp = front(start_rows, frame, pix, flat_tiles)
    slot = jnp.arange(8, dtype=jnp.int32)
    slot_tubelet = (slot % 4) * 2 + slot // 4
    key_ok = (slot_tubelet[:, None] < tubelets[0]) & (jnp.arange(400, dtype=jnp.int32)[None] < patches[0])
    bias = jnp.where(key_ok.reshape(1, 3200), 0.0, -1e30).astype(jnp.float32)
    og, *saved_attn = attn_fwd(sp, bias, 2)
    total_count = jnp.sum(valid_tubelet_count).astype(jnp.float32)
    patch_mask = jnp.broadcast_to((jnp.arange(400, dtype=jnp.int32)[:, None] < patches[0]).astype(jnp.float32), (400, 128))
    slot_weight = (fi < tubelets[0]).astype(jnp.float32)
    scal = jnp.broadcast_to(
        jnp.concatenate([slot_weight[None], 1.0 / total_count[None], jnp.zeros((6,), jnp.float32)])[:, None], (8, 128)
    )
    counts = jnp.broadcast_to(
        jnp.concatenate([(NMAP * valid_tubelet_count).astype(jnp.float32), jnp.ones((4,), jnp.float32)])[:, None], (8, 128)
    )
    ids = jnp.concatenate([positive, negatives[0], jnp.full((3,), -1, jnp.int32)])
    chosen = (ids[:, None] == jnp.arange(128, dtype=jnp.int32)[None]).astype(jnp.float32)
    (attended, h2, hidden_low, g_pre, g_mlp, g_attn, g_second, dog, g_vec, g_up_bias, g_map, g_proj, loss_rows) = middle(
        og, first_in, flat_tiles, w_map, patch_mask, scal, counts, chosen, 4
    )
    loss_value = loss_rows[0, 0]
    dsp = attn_bwd(dog, bias, saved_attn, 3)
    g_qkv, g_entry, tail_tiles = back(
        start_rows, frame, dsp, flat_tiles, first_in, g_second, g_vec, g_up_bias, g_map[:, :NMAP].reshape(48, 128), g_proj
    )
    grad, squares = make_rsx()(
        pix, h1, attended, h2, hidden_low, g_entry, g_qkv, g_attn, g_pre, g_mlp, tail_tiles.reshape(4, 144, 16, 128), cid=1
    )
    grad = grad.reshape(-1)[:SHARD]
    grad_norm = jnp.sqrt(jnp.sum(squares))
    clipped = grad * jnp.minimum(1.0, CLIP_AT / grad_norm)
    new_first = BETA_ONE * first_moment + (1.0 - BETA_ONE) * clipped
    new_second = BETA_TWO * second_moment + (1.0 - BETA_TWO) * clipped * clipped
    step = adam_step[0].astype(jnp.float32)
    update = new_first / (1.0 - BETA_ONE**step) / (jnp.sqrt(new_second / (1.0 - BETA_TWO**step)) + ADAM_EPS)
    new_master = master - RATE * (update + DECAY * master)
    return (new_master, new_first, new_second, to_bfloat(new_master), loss_value, grad_norm)


def solution(mesh):
    fast = dict(mesh.shape) == {"batch": 4, "frame": 8}
    return jax.shard_map(
        local_4x8 if fast else local_any_mesh,
        mesh=mesh,
        in_specs=(
            P("batch", "frame", None, None),
            P("batch"),
            P(),
            P("batch"),
            P("batch", None),
            P(("batch", "frame")),
            P(("batch", "frame")),
            P(("batch", "frame")),
            P(),
        ),
        out_specs=(
            P(("batch", "frame")),
            P(("batch", "frame")),
            P(("batch", "frame")),
            P(("batch", "frame")),
            P(),
            P(),
        ),
        check_vma=False,
    )
```

```python
from functools import partial
import math

import jax
import jax.numpy as jnp
from jax import lax
from jax.experimental import pallas as pl
from jax.experimental.pallas import tpu as pltpu
from jax.sharding import PartitionSpec as P

HEAD_COUNT = 12
HEAD_FEATURES = 64
FFW = 3072
TUBELET_PIXELS = 1536
EMB = 512
NMAP = 8
P0 = 100
P1 = 196
PATCHES_THIRD_2 = 400
TMAX = 64
NVEC = 13
CLIPS_PER_BATCH = 1


EPSILON = 1e-05
SOFTMAX_TEMPER = 0.02
DECAY_PENALTY = 1.0
CLIP_AT = 0.05
RATE = 0.03
DECAY = 0.05
BETA_ONE = 0.9
BETA_TWO = 0.999
ADAM_EPS = 1e-08
HIGH_ACCURACY = lax.Precision.HIGHEST


def to_bfloat(values):
    return values.astype(jnp.bfloat16)


def unpack_flat(flat_vector):
    width_of_model = HEAD_COUNT * HEAD_FEATURES
    dims_list = [
        (TUBELET_PIXELS, width_of_model),
        (width_of_model, 3 * width_of_model),
        (width_of_model, width_of_model),
        (width_of_model, FFW),
        (FFW, width_of_model),
        (width_of_model, EMB),
        (width_of_model, NMAP),
        (P0 + P1 + PATCHES_THIRD_2, width_of_model),
        (TMAX, width_of_model),
        (NVEC, width_of_model),
        (FFW,),
    ]
    pieces = []
    offset = 0
    for dims_of in dims_list:
        length = math.prod(dims_of)
        pieces.append(flat_vector[offset : offset + length].reshape(dims_of))
        offset += length
    return pieces


def norm_forward(inputs, gain_row, shift_row):
    center = inputs - jnp.mean(inputs, -1, keepdims=True)
    inverse = lax.rsqrt(jnp.mean(center * center, -1, keepdims=True) + EPSILON)
    normed = center * inverse
    return (normed * gain_row + shift_row, (normed, inverse))


def norm_backward(grad_out, gain_row, saved_parts):
    normed, inverse = saved_parts
    scaled = grad_out * gain_row
    grad_in = inverse * (
        scaled
        - jnp.mean(scaled, -1, keepdims=True)
        - normed * jnp.mean(scaled * normed, -1, keepdims=True)
    )
    lead_axes = tuple(range(grad_out.ndim - 1))
    return (grad_in, jnp.sum(grad_out * normed, lead_axes), jnp.sum(grad_out, lead_axes))


def block_plan(total_rows):
    shards = total_rows // PATCHES_THIRD_2
    group_size = 4
    return (shards // group_size, group_size * PATCHES_THIRD_2)


def local_any_mesh(
    pixels,
    res_class,
    valid_tubelet_count,
    positive,
    negatives,
    master,
    first_moment,
    second_moment,
    adam_step,
):
    width_of_model = HEAD_COUNT * HEAD_FEATURES
    score_scale = HEAD_FEATURES ** (-0.5)
    every_clip_rows = CLIPS_PER_BATCH * lax.axis_size("batch")
    index_of_batch = lax.axis_index("batch")
    frame_index = lax.axis_index("frame")
    gathered = lax.all_gather(to_bfloat(master), ("batch", "frame"), axis=0, tiled=True)
    w_embed, w_qkv, w_out, w_up, w_down, w_proj, w_map, pos_space, pos_time, vectors, bias_up = (
        unpack_flat(gathered)
    )
    vec_f = vectors.astype(jnp.float32)
    tubelet_stack = lax.dynamic_slice_in_dim(
        valid_tubelet_count, index_of_batch * CLIPS_PER_BATCH, CLIPS_PER_BATCH, 0
    )
    patches = jnp.where(res_class == 0, P0, jnp.where(res_class == 1, P1, PATCHES_THIRD_2)).astype(
        jnp.int32
    )
    start_rows = jnp.where(res_class == 0, 0, jnp.where(res_class == 1, P0, P0 + P1)).astype(
        jnp.int32
    )
    patch_pos = jnp.stack(
        [lax.dynamic_slice_in_dim(pos_space, start_rows[0], PATCHES_THIRD_2, 0)]
    ).astype(jnp.float32)
    time_row = lax.dynamic_slice_in_dim(pos_time, frame_index, 1, 0).astype(jnp.float32)
    rows_of_pixels = pixels.reshape(CLIPS_PER_BATCH * PATCHES_THIRD_2, TUBELET_PIXELS)
    embedded = jnp.dot(rows_of_pixels, w_embed, preferred_element_type=jnp.float32).reshape(
        CLIPS_PER_BATCH, PATCHES_THIRD_2, width_of_model
    )
    first_in = embedded + vec_f[8] + patch_pos + time_row
    normed_one, saved_one = norm_forward(first_in, vec_f[0], vec_f[1])
    normed_one = to_bfloat(normed_one)
    qkv_bias = jnp.concatenate([vec_f[9], jnp.zeros_like(vec_f[9]), vec_f[10]])
    projection_output = to_bfloat(
        jnp.einsum("cpd,de->cpe", normed_one, w_qkv, preferred_element_type=jnp.float32) + qkv_bias
    )
    query_matrix = projection_output[..., :width_of_model].reshape(
        CLIPS_PER_BATCH, PATCHES_THIRD_2, HEAD_COUNT, HEAD_FEATURES
    )
    kv_local = projection_output[..., width_of_model:]

    def key_mask(row_start, count_of_rows):
        row_ids = row_start + jnp.arange(count_of_rows, dtype=jnp.int32)
        return ((row_ids // PATCHES_THIRD_2)[None, :] < tubelet_stack[:, None]) & (
            (row_ids % PATCHES_THIRD_2)[None, :] < patches[:, None]
        )

    def block_scores(key_value_block, block_start):
        count_of_rows = key_value_block.shape[1]
        head_keys = key_value_block[..., :width_of_model].reshape(
            CLIPS_PER_BATCH, count_of_rows, HEAD_COUNT, HEAD_FEATURES
        )
        head_values = key_value_block[..., width_of_model:].reshape(
            CLIPS_PER_BATCH, count_of_rows, HEAD_COUNT, HEAD_FEATURES
        )
        key_ok = key_mask(block_start, count_of_rows)[:, None, None, :]
        scores = (
            jnp.einsum(
                "cqhd,ckhd->chqk", query_matrix, head_keys, preferred_element_type=jnp.float32
            )
            * score_scale
        )
        return (jnp.where(key_ok, scores, -1e30), key_ok, head_keys, head_values)

    forward_init = (
        jnp.full((CLIPS_PER_BATCH, HEAD_COUNT, PATCHES_THIRD_2), -1e30, jnp.float32),
        jnp.zeros((CLIPS_PER_BATCH, HEAD_COUNT, PATCHES_THIRD_2), jnp.float32),
        jnp.zeros((CLIPS_PER_BATCH, HEAD_COUNT, PATCHES_THIRD_2, HEAD_FEATURES), jnp.float32),
    )
    kv_piece = lax.all_gather(kv_local, "frame", axis=1, tiled=True)
    count_blocks, block_rows = block_plan(kv_piece.shape[1])

    def forward_one_block(block_index, running):
        run_max, run_sum, run_acc = running
        block_start = block_index * block_rows
        key_value_block = lax.dynamic_slice_in_dim(
            kv_piece, block_index * block_rows, block_rows, 1
        )
        scores, key_ok, head_keys, head_values = block_scores(key_value_block, block_start)
        new_max = jnp.maximum(run_max, jnp.max(scores, -1))
        factor = jnp.exp(run_max - new_max)
        prob_tile = jnp.where(key_ok, jnp.exp(scores - new_max[..., None]), 0.0)
        run_acc = run_acc * factor[..., None] + jnp.einsum(
            "chqk,ckhd->chqd", to_bfloat(prob_tile), head_values, preferred_element_type=jnp.float32
        )
        return (new_max, run_sum * factor + jnp.sum(prob_tile, -1), run_acc)

    run_max, run_sum, run_acc = lax.fori_loop(0, count_blocks, forward_one_block, forward_init)
    log_sum = run_max + jnp.log(run_sum)
    head_attended_rows = run_acc / run_sum[..., None]
    attended_reduced = to_bfloat(
        head_attended_rows.transpose(0, 2, 1, 3).reshape(
            CLIPS_PER_BATCH, PATCHES_THIRD_2, width_of_model
        )
    )
    second_in = (
        first_in
        + jnp.einsum("cpe,ed->cpd", attended_reduced, w_out, preferred_element_type=jnp.float32)
        + vec_f[11]
    )
    normed_two, saved_two = norm_forward(second_in, vec_f[2], vec_f[3])
    normed_two = to_bfloat(normed_two)
    hidden_pre = jnp.einsum(
        "cpd,df->cpf", normed_two, w_up, preferred_element_type=jnp.float32
    ) + bias_up.astype(jnp.float32)
    hidden_act, gelu_pull = jax.vjp(partial(jax.nn.gelu, approximate=False), hidden_pre)
    hidden_low = to_bfloat(hidden_act)
    block_out = (
        second_in
        + jnp.einsum("cpf,fd->cpd", hidden_low, w_down, preferred_element_type=jnp.float32)
        + vec_f[12]
    )
    valid_patch = jnp.arange(PATCHES_THIRD_2, dtype=jnp.int32)[None, :] < patches[:, None]
    slot_weight = (frame_index < tubelet_stack).astype(jnp.float32)

    def learner(block_in, gain_row, shift_row, map_weight):
        normed, unused = norm_forward(block_in, gain_row, shift_row)
        logits = jnp.einsum("cpd,dm->cpm", normed, map_weight, precision=HIGH_ACCURACY)
        logits = jnp.where(valid_patch[..., None], logits, -1e30)
        token_maps = jax.nn.softmax(logits, axis=1)
        pooled_part = jnp.einsum(
            "c,cpm,cpd->cd", slot_weight, token_maps, block_in, precision=HIGH_ACCURACY
        )
        gram_matrix = jnp.einsum("cpm,cpn->cmn", token_maps, token_maps, precision=HIGH_ACCURACY)
        correlation_part = slot_weight * (
            jnp.sum(gram_matrix, axis=(1, 2)) - jnp.trace(gram_matrix, axis1=1, axis2=2)
        )
        return (pooled_part, correlation_part)

    (pooled_part, correlation_part), learner_pull = jax.vjp(
        learner, block_out, vec_f[4], vec_f[5], w_map.astype(jnp.float32)
    )
    pooled_sum, correlation_sum = lax.psum((pooled_part, correlation_part), "frame")

    def head_map(pooled_in, gain_row, shift_row, proj_weight):
        pooled_mean = pooled_in / (NMAP * tubelet_stack).astype(jnp.float32)[:, None]
        normed, unused = norm_forward(pooled_mean, gain_row, shift_row)
        embedding = jnp.dot(
            normed, proj_weight, precision=HIGH_ACCURACY, preferred_element_type=jnp.float32
        )
        return embedding * lax.rsqrt(jnp.sum(embedding * embedding, -1, keepdims=True) + 1e-06)

    normalized_embedding, head_pull = jax.vjp(
        head_map, pooled_sum, vec_f[6], vec_f[7], w_proj.astype(jnp.float32)
    )
    embed_all, correlation_all = (
        lax.all_gather(normalized_embedding, "batch", axis=0, tiled=True),
        lax.all_gather(correlation_sum, "batch", axis=0, tiled=True),
    )
    selected_rows = jnp.concatenate([positive[:, None], negatives], axis=1)

    def contrast(embedding_input):
        local_row_set = lax.dynamic_slice_in_dim(
            embedding_input, index_of_batch * CLIPS_PER_BATCH, CLIPS_PER_BATCH, 0
        )
        similarity_matrix = (
            jnp.einsum(
                "yg,yeg->ye", local_row_set, embedding_input[selected_rows], precision=HIGH_ACCURACY
            )
            / SOFTMAX_TEMPER
        )
        return (
            jnp.sum(jax.nn.logsumexp(similarity_matrix, axis=1) - similarity_matrix[:, 0])
            / every_clip_rows
        )

    contrast_part, contrast_pull = jax.vjp(contrast, embed_all)
    (grad_embed_all,) = contrast_pull(jnp.ones_like(contrast_part))
    grad_unit = lax.psum_scatter(grad_embed_all, "batch", scatter_dimension=0, tiled=True)
    frame_total_count = jnp.sum(valid_tubelet_count).astype(jnp.float32)
    head_mask = (frame_index == 0).astype(jnp.float32)
    pooled_gradient, grad_final_gain, grad_final_shift, grad_proj = head_pull(grad_unit)
    grad_block, grad_learn_gain, grad_learn_shift, grad_map = learner_pull(
        (
            pooled_gradient,
            jnp.full((CLIPS_PER_BATCH,), DECAY_PENALTY / frame_total_count, jnp.float32),
        )
    )
    grad_mlp = to_bfloat(grad_block)
    grad_down_bias = jnp.sum(grad_mlp.astype(jnp.float32), (0, 1))
    grad_w_down = jnp.einsum(
        "cpf,cpd->fd", hidden_low, grad_mlp, preferred_element_type=jnp.float32
    )
    grad_hidden = jnp.einsum("cpd,fd->cpf", grad_mlp, w_down, preferred_element_type=jnp.float32)
    (grad_pre,) = gelu_pull(grad_hidden)
    grad_pre_low = to_bfloat(grad_pre)
    grad_up_bias = jnp.sum(grad_pre_low.astype(jnp.float32), (0, 1))
    grad_w_up = jnp.einsum(
        "cpd,cpf->df", normed_two, grad_pre_low, preferred_element_type=jnp.float32
    )
    grad_normed_two = jnp.einsum(
        "cpf,df->cpd", grad_pre_low, w_up, preferred_element_type=jnp.float32
    )
    grad_in_two, grad_gain_two, grad_shift_two = norm_backward(grad_normed_two, vec_f[2], saved_two)
    grad_second = grad_block + grad_in_two
    grad_attn = to_bfloat(grad_second)
    grad_out_bias = jnp.sum(grad_attn.astype(jnp.float32), (0, 1))
    grad_w_out = jnp.einsum(
        "cpe,cpd->ed", attended_reduced, grad_attn, preferred_element_type=jnp.float32
    )
    grad_attended = to_bfloat(
        jnp.einsum("cpd,ed->cpe", grad_attn, w_out, preferred_element_type=jnp.float32)
    ).reshape(CLIPS_PER_BATCH, PATCHES_THIRD_2, HEAD_COUNT, HEAD_FEATURES)
    row_delta = jnp.einsum("cqhd,chqd->chq", grad_attended.astype(jnp.float32), head_attended_rows)
    zeroed_query = jnp.zeros(
        (CLIPS_PER_BATCH, PATCHES_THIRD_2, HEAD_COUNT, HEAD_FEATURES), jnp.float32
    )
    query_kv_piece = lax.all_gather(kv_local, "frame", axis=1, tiled=True)
    count_blocks, query_block_rows = block_plan(query_kv_piece.shape[1])

    def query_one_block(block_index, query_gradient):
        block_start = block_index * query_block_rows
        key_value_block = lax.dynamic_slice_in_dim(
            query_kv_piece, block_index * query_block_rows, query_block_rows, 1
        )
        scores, key_ok, head_keys, head_values = block_scores(key_value_block, block_start)
        prob_tile = jnp.where(key_ok, jnp.exp(scores - log_sum[..., None]), 0.0)
        grad_prob = jnp.einsum(
            "cqhd,ckhd->chqk", grad_attended, head_values, preferred_element_type=jnp.float32
        )
        grad_score = to_bfloat(prob_tile * (grad_prob - row_delta[..., None]))
        return (
            query_gradient
            + jnp.einsum(
                "chqk,ckhd->cqhd", grad_score, head_keys, preferred_element_type=jnp.float32
            )
            * score_scale
        )

    query_gradient = lax.fori_loop(0, count_blocks, query_one_block, zeroed_query)
    own_keys = kv_local[..., :width_of_model].reshape(
        CLIPS_PER_BATCH, PATCHES_THIRD_2, HEAD_COUNT, HEAD_FEATURES
    )
    own_values = kv_local[..., width_of_model:].reshape(
        CLIPS_PER_BATCH, PATCHES_THIRD_2, HEAD_COUNT, HEAD_FEATURES
    )
    own_ok = key_mask(frame_index * PATCHES_THIRD_2, PATCHES_THIRD_2)[:, None, None, :]
    row_pieces = (
        query_matrix.astype(jnp.float32),
        grad_attended.astype(jnp.float32),
        log_sum.transpose(0, 2, 1),
        row_delta.transpose(0, 2, 1),
    )
    query_piece = lax.all_gather(
        row_pieces[0].astype(jnp.bfloat16), "frame", axis=1, tiled=True
    ).astype(jnp.float32)
    grad_out_piece = lax.all_gather(
        row_pieces[1].astype(jnp.bfloat16), "frame", axis=1, tiled=True
    ).astype(jnp.float32)
    lse_piece = lax.all_gather(
        row_pieces[2].astype(jnp.bfloat16), "frame", axis=1, tiled=True
    ).astype(jnp.float32)
    delta_piece = lax.all_gather(
        row_pieces[3].astype(jnp.bfloat16), "frame", axis=1, tiled=True
    ).astype(jnp.float32)
    count_blocks, own_block_rows = block_plan(query_piece.shape[1])

    def own_one_block(block_index, running):
        key_gradient, value_gradient = running
        offset = block_index * own_block_rows
        query_block = to_bfloat(lax.dynamic_slice_in_dim(query_piece, offset, own_block_rows, 1))
        grad_out_block = to_bfloat(
            lax.dynamic_slice_in_dim(grad_out_piece, offset, own_block_rows, 1)
        )
        lse_block = lax.dynamic_slice_in_dim(lse_piece, offset, own_block_rows, 1).transpose(
            0, 2, 1
        )
        delta_block = lax.dynamic_slice_in_dim(delta_piece, offset, own_block_rows, 1).transpose(
            0, 2, 1
        )
        scores = (
            jnp.einsum("cqhd,ckhd->chqk", query_block, own_keys, preferred_element_type=jnp.float32)
            * score_scale
        )
        scores = jnp.where(own_ok, scores, -1e30)
        prob_tile = jnp.where(own_ok, jnp.exp(scores - lse_block[..., None]), 0.0)
        grad_prob = jnp.einsum(
            "cqhd,ckhd->chqk", grad_out_block, own_values, preferred_element_type=jnp.float32
        )
        grad_score = to_bfloat(prob_tile * (grad_prob - delta_block[..., None]))
        key_gradient = (
            key_gradient
            + jnp.einsum(
                "chqk,cqhd->ckhd", grad_score, query_block, preferred_element_type=jnp.float32
            )
            * score_scale
        )
        value_gradient = value_gradient + jnp.einsum(
            "chqk,cqhd->ckhd",
            to_bfloat(prob_tile),
            grad_out_block,
            preferred_element_type=jnp.float32,
        )
        return (key_gradient, value_gradient)

    grad_key_own, grad_value_own = lax.fori_loop(
        0, count_blocks, own_one_block, (zeroed_query, zeroed_query)
    )
    gradient_key_value_local = to_bfloat(
        jnp.concatenate(
            [
                grad_key_own.reshape(CLIPS_PER_BATCH, PATCHES_THIRD_2, width_of_model),
                grad_value_own.reshape(CLIPS_PER_BATCH, PATCHES_THIRD_2, width_of_model),
            ],
            -1,
        )
    )
    gradient_query_key_value = jnp.concatenate(
        [
            to_bfloat(query_gradient).reshape(CLIPS_PER_BATCH, PATCHES_THIRD_2, width_of_model),
            gradient_key_value_local,
        ],
        -1,
    )
    grad_query_bias = jnp.sum(
        gradient_query_key_value[..., :width_of_model].astype(jnp.float32), (0, 1)
    )
    grad_value_bias = jnp.sum(
        gradient_query_key_value[..., 2 * width_of_model :].astype(jnp.float32), (0, 1)
    )
    grad_w_qkv = jnp.einsum(
        "cpd,cpe->de", normed_one, gradient_query_key_value, preferred_element_type=jnp.float32
    )
    grad_normed_one = jnp.einsum(
        "cpe,de->cpd", gradient_query_key_value, w_qkv, preferred_element_type=jnp.float32
    )
    grad_in_one, grad_gain_one, grad_shift_one = norm_backward(grad_normed_one, vec_f[0], saved_one)
    gradient_entry = grad_second + grad_in_one
    gradient_entry_low = to_bfloat(gradient_entry).reshape(
        CLIPS_PER_BATCH * PATCHES_THIRD_2, width_of_model
    )
    grad_w_embed = jnp.einsum(
        "rt,rd->td", rows_of_pixels, gradient_entry_low, preferred_element_type=jnp.float32
    )
    grad_embed_bias = jnp.sum(gradient_entry, (0, 1))
    grad_pos_space = jnp.zeros((P0 + P1 + PATCHES_THIRD_2, width_of_model), jnp.float32)
    current = lax.dynamic_slice_in_dim(grad_pos_space, start_rows[0], PATCHES_THIRD_2, 0)
    grad_pos_space = lax.dynamic_update_slice_in_dim(
        grad_pos_space, current + gradient_entry[0], start_rows[0], 0
    )
    grad_pos_time = lax.dynamic_update_slice_in_dim(
        jnp.zeros((TMAX, width_of_model), jnp.float32), grad_embed_bias[None], frame_index, 0
    )
    grad_vectors = jnp.stack(
        [
            grad_gain_one,
            grad_shift_one,
            grad_gain_two,
            grad_shift_two,
            grad_learn_gain,
            grad_learn_shift,
            grad_final_gain * head_mask,
            grad_final_shift * head_mask,
            grad_embed_bias,
            grad_query_bias,
            grad_value_bias,
            grad_out_bias,
            grad_down_bias,
        ]
    )
    flat_grad = jnp.concatenate(
        [
            piece_grad.reshape(-1)
            for piece_grad in (
                grad_w_embed,
                grad_w_qkv,
                grad_w_out,
                grad_w_up,
                grad_w_down,
                grad_proj * head_mask,
                grad_map,
                grad_pos_space,
                grad_pos_time,
                grad_vectors,
                grad_up_bias,
            )
        ]
    )
    grad_shard = lax.psum_scatter(flat_grad, ("batch", "frame"), scatter_dimension=0, tiled=True)
    contrast_keep = jnp.where(frame_index == 0, contrast_part, 0.0)
    square_sum, contrast_total = lax.psum(
        (jnp.sum(grad_shard * grad_shard), contrast_keep), ("batch", "frame")
    )
    grad_norm = jnp.sqrt(square_sum)
    loss_value = contrast_total + DECAY_PENALTY * jnp.sum(correlation_all) / frame_total_count
    clipped = grad_shard * jnp.minimum(1.0, CLIP_AT / grad_norm)
    new_first = BETA_ONE * first_moment + (1.0 - BETA_ONE) * clipped
    new_second = BETA_TWO * second_moment + (1.0 - BETA_TWO) * clipped * clipped
    step_count = adam_step[0].astype(jnp.float32)
    update = (
        new_first
        / (1.0 - BETA_ONE**step_count)
        / (jnp.sqrt(new_second / (1.0 - BETA_TWO**step_count)) + ADAM_EPS)
    )
    new_master = master - RATE * (update + DECAY * master)
    return (new_master, new_first, new_second, to_bfloat(new_master), loss_value, grad_norm)


MESH = pl.DeviceIdType.MESH
T=144
SPA=32

class Sends:
    def __init__(self, sem): self.sem=sem; self.n=0; self.items=[]
    def go(self, src, dst, rsem, dev, pred=None):
        c = pltpu.make_async_remote_copy(src_ref=src, dst_ref=dst, send_sem=self.sem.at[self.n], recv_sem=rsem, device_id=dev, device_id_type=MESH)
        self.n += 1
        if pred is None: c.start()
        else:
            @pl.when(pred)
            def _(): c.start()
        self.items.append((c,pred))
    def prep(self, src, dst, rsem, dev, pred=None):
        c = pltpu.make_async_remote_copy(src_ref=src, dst_ref=dst, send_sem=self.sem.at[self.n], recv_sem=rsem, device_id=dev, device_id_type=MESH)
        self.n += 1
        self.items.append((c,pred))
        def fire():
            if pred is None: c.start()
            else:
                @pl.when(pred)
                def _(): c.start()
        return fire
    def drain(self):
        for c,pred in self.items:
            if pred is None: c.wait_send()
            else:
                @pl.when(pred)
                def _(): c.wait_send()

def both(a,b):
    if a is None: return b
    if b is None: return a
    return jnp.logical_and(a,b)

def make_ag(spa=SPA):
    A=(0,spa); A1=(0,spa//2); A2=(spa//2,spa//2)
    nb=T-spa
    B=(spa,nb); B1=(spa,nb//2); B2=(spa+nb//2,nb//2)
    FULL=(0,T)
    def kernel(x_ref, out, ssem, lsem, zB, xB, yB, xBh, yBh, pA, zA, pown, pzB, pxB, pyB, pxBh, pyBh, ppA, pzA):
        b=lax.axis_index("batch"); f=lax.axis_index("frame")
        x=b%2; y=b//2; z=f//2; c=f%2
        bx=y*2+(1-x); by=(1-y)*2+x; bd=(1-y)*2+(1-x)
        X=(bx,f); Y=(by,f); Pn=(b,z*2+(1-c)); UP=(b,f+2); DN=(b,f-2)
        up=z<3; dn=z>0
        bar=pltpu.get_barrier_semaphore()
        for d,p in ((X,None),(Y,None),(Pn,None),(UP,up),(DN,dn)):
            if p is None: pl.semaphore_signal(bar,inc=1,device_id=d,device_id_type=MESH)
            else:
                @pl.when(p)
                def _(): pl.semaphore_signal(bar,inc=1,device_id=d,device_id_type=MESH)
        pl.semaphore_wait(bar, 4+(z*(3-z)+1)//3)
        S=Sends(ssem)
        def blk(bb,zz,part): return out.at[bb*8+zz*2+c, pl.ds(part[0],part[1])]
        def send(bb,zz,part,rsem,dev,pred=None,own=False):
            dst=blk(bb,zz,part)
            src=x_ref.at[pl.ds(part[0],part[1])] if own else dst
            S.go(src,dst,rsem,dev,pred)
        def wait(bb,zz,part,rsem):
            r=blk(bb,zz,part)
            pltpu.make_async_remote_copy(src_ref=r,dst_ref=r,send_sem=ssem.at[0],recv_sem=rsem,device_id=Pn,device_id_type=MESH).wait_recv()
        def waitp(pred,*a):
            if pred is None: wait(*a)
            else:
                @pl.when(pred)
                def _(): wait(*a)
        lc=pltpu.make_async_copy(x_ref, blk(b,z,FULL), lsem);
        send(b,z,A,pA.at[0],X,own=True); send(b,z,A,pA.at[1],Y,own=True)
        send(b,z,B,zB.at[z],UP,up,True); send(b,z,B,zB.at[z],DN,dn,True)
        send(b,z,B,xB.at[z],X,own=True); send(b,z,B,yB.at[z],Y,own=True)
        send(b,z,A,zA.at[z,0],UP,up,True); send(b,z,A,zA.at[z,0],DN,dn,True)
        send(b,z,FULL,pown.at[0],Pn,own=True)
        lc.start()
        pz=[]
        def pwait(*a): pz.append(a)
        pwait(None,b,z,FULL,pown.at[0])
        def zfwdA(bb,part,i,ps):
            send(bb,z,part,zA.at[z,i],UP,up); send(bb,z,part,zA.at[z,i],DN,dn)
            send(bb,z,part,ps,Pn); pwait(None,bb,z,part,ps)
        wait(bx,z,A,pA.at[0]); send(bx,z,A1,pA.at[2],Y); zfwdA(bx,A,1,ppA.at[0])
        wait(by,z,A,pA.at[1]); send(by,z,A2,pA.at[3],X); zfwdA(by,A,2,ppA.at[1])
        wait(bd,z,A1,pA.at[2]); zfwdA(bd,A1,3,ppA.at[2])
        wait(bd,z,A2,pA.at[3]); zfwdA(bd,A2,4,ppA.at[3])
        def xyB(zz,pred):
            waitp(pred,bx,zz,B,xB.at[zz]); send(bx,zz,B1,yBh.at[zz],Y,pred); send(bx,zz,B,pxB.at[zz],Pn,pred); pwait(pred,bx,zz,B,pxB.at[zz])
            waitp(pred,by,zz,B,yB.at[zz]); send(by,zz,B2,xBh.at[zz],X,pred); send(by,zz,B,pyB.at[zz],Pn,pred); pwait(pred,by,zz,B,pyB.at[zz])
        xyB(z,None)
        for d in (1,2,3):
            for s in (1,-1):
                zz=z+s*d
                pred=(zz<4) if s>0 else (zz>=0)
                nxt,np_=(DN,dn) if s>0 else (UP,up)
                waitp(pred,b,zz,B,zB.at[zz])
                send(b,zz,B,zB.at[zz],nxt,both(pred,np_))
                send(b,zz,B,xB.at[zz],X,pred); send(b,zz,B,yB.at[zz],Y,pred)
                send(b,zz,B,pzB.at[zz],Pn,pred); pwait(pred,b,zz,B,pzB.at[zz])
            for s in (1,-1):
                zz=z+s*d
                pred=(zz<4) if s>0 else (zz>=0)
                nxt,np_=(DN,dn) if s>0 else (UP,up)
                for i,(bb,part) in enumerate(((b,A),(bx,A),(by,A),(bd,A1),(bd,A2))):
                    waitp(pred,bb,zz,part,zA.at[zz,i]); send(bb,zz,part,zA.at[zz,i],nxt,both(pred,np_))
                    send(bb,zz,part,pzA.at[zz,i],Pn,pred); pwait(pred,bb,zz,part,pzA.at[zz,i])
            for s in (1,-1):
                zz=z+s*d
                pred=(zz<4) if s>0 else (zz>=0)
                xyB(zz,pred)
        for zz in range(4):
            wait(bd,zz,B1,yBh.at[zz]); send(bd,zz,B1,pyBh.at[zz],Pn); pwait(None,bd,zz,B1,pyBh.at[zz])
            wait(bd,zz,B2,xBh.at[zz]); send(bd,zz,B2,pxBh.at[zz],Pn); pwait(None,bd,zz,B2,pxBh.at[zz])
        for a in pz: waitp(*a)
        lc.wait()
        S.drain()
    D=pltpu.SemaphoreType.DMA
    def ag(xin, cid=0):
        return pl.pallas_call(kernel, out_shape=jax.ShapeDtypeStruct((32,T,16,128),jnp.bfloat16),
            in_specs=[pl.BlockSpec(memory_space=pltpu.VMEM)], out_specs=pl.BlockSpec(memory_space=pl.ANY),
            scratch_shapes=[D((160,)),D]+[D((4,))]*5+[D((4,)),D((4,5)),D((1,))]+[D((4,))]*5+[D((4,)),D((4,5))],
            compiler_params=pltpu.CompilerParams(collective_id=cid,has_side_effects=True))(xin)
    return ag


def make_rsx(spa=16):
    nb=T-spa
    A=(0,spa); A1=(0,spa//2); A2=(spa//2,spa//2)
    B=(spa,nb); B1=(spa,nb//2); B2=(spa+nb//2,nb//2)
    FULL=(0,T)
    def kernel(pix, h1, att, h2, act, dx0, dqkv, dattn, dpre, dmlp, tail, gout, nout,
               PS, R, h2T, LX, LY, LHX, LHY, LZB, LZA, LPA, out, C, CB_, CR_, NB, ssem, psem, stsem, csem, nsem, nsend, s_hx, s_hy, s_x, s_y, s_zb, s_za, s_pa):
        b=lax.axis_index("batch"); f=lax.axis_index("frame")
        x=b%2; y=b//2; z=f//2; c=f%2
        bx=y*2+(1-x); by=(1-y)*2+x; bd=(1-y)*2+(1-x)
        X=(bx,f); Y=(by,f); Pn=(b,z*2+(1-c)); UP=(b,f+2); DN=(b,f-2)
        up=z<3; dn=z>0
        t=z//2
        k=b*8+f
        def dev_of(kk): return (kk//8,kk%8)
        bar=pltpu.get_barrier_semaphore()
        def greet(d,_):
            pl.semaphore_signal(bar,inc=1,device_id=dev_of((k+d)%32),device_id_type=MESH); return 0
        lax.fori_loop(1,32,greet,0)
        zo=[3*(1-t), 2-t, (1-z)*(1-t)+(5-z)*t, z]
        order=[]
        for zz in zo: order += [(bd,zz)]
        for zz in zo: order += [(bx,zz),(by,zz)]
        for zz in zo: order += [(b,zz)]
        h2T[...]=h2[...].T
        TN_=(((0,),(0,)),((),()))
        def put(dst,r,m):
            rows=r.shape[0]
            r=r.astype(jnp.bfloat16)
            for s in range(rows//16):
                for j in range(m):
                    dst[s*m+j]=r[s*16:(s+1)*16,j*128:(j+1)*128]
        def col(a,i,n): return a[:,pl.ds(pl.multiple_of(i*n,128),n)]
        def comp(kk,dst):
            def mm(a,bb_,dims): return lax.dot_general(a,bb_,dims,preferred_element_type=jnp.float32)
            @pl.when(kk<4)
            def _(): put(dst,mm(col(pix,kk,384),dx0[...],TN_),6)
            @pl.when(jnp.logical_and(kk>=4,kk<10))
            def _(): put(dst,mm(col(h1,kk-4,128),dqkv[...],TN_),18)
            @pl.when(jnp.logical_and(kk>=10,kk<12))
            def _(): put(dst,mm(col(att,kk-10,384),dattn[...],TN_),6)
            @pl.when(jnp.logical_and(kk>=12,kk<20))
            def _(): put(dst,mm(h2T[pl.ds(pl.multiple_of((kk-12)*96,16),96)],dpre[...],(((1,),(0,)),((),()))),24)
            @pl.when(jnp.logical_and(kk>=20,kk<28))
            def _(): put(dst,mm(col(act,kk-20,384),dmlp[...],TN_),6)
            @pl.when(kk>=28)
            def _():
                def cp(i,_):
                    ds=pl.ds(i*8,8); dst[ds]=tail[kk-28,ds]; return 0
                lax.fori_loop(0,T//8,cp,0)
        def pick(i):
            g=jnp.where(i<4,i,jnp.where(i<12,(i-4)//2,i-12))
            zz=jnp.where(g==0,zo[0],jnp.where(g==1,zo[1],jnp.where(g==2,zo[2],zo[3])))
            bb=jnp.where(i<4,bd,jnp.where(i<12,jnp.where(i%2==0,bx,by),b))
            return bb,zz
        def pcopy(i):
            bb,zz=pick(i)
            return pltpu.make_async_remote_copy(src_ref=PS.at[16+i%4],dst_ref=R.at[bb,zz],send_sem=stsem.at[i%4],recv_sem=psem.at[bb,zz],device_id=Pn,device_id_type=MESH)
        S=Sends(ssem)
        def acc(dst, srcs, n, step=8):
            def body(i,_):
                ds=pl.ds(i*step,step)
                v=srcs[0][ds].astype(jnp.float32)
                for s in srcs[1:]: v=v+s[ds].astype(jnp.float32)
                dst[ds]=v.astype(dst.dtype)
                return 0
            lax.fori_loop(0,n//step,body,0)
        def sub(ref,part): return ref.at[pl.ds(part[0],part[1])]
        def ready(i):
            bb,zz=order[i]
            pltpu.make_async_remote_copy(src_ref=R.at[bb,zz],dst_ref=R.at[bb,zz],send_sem=ssem.at[0],recv_sem=psem.at[bb,zz],device_id=Pn,device_id_type=MESH).wait_recv()
        def wrecv(ref,sem):
            pltpu.make_async_remote_copy(src_ref=ref,dst_ref=ref,send_sem=ssem.at[0],recv_sem=sem,device_id=Pn,device_id_type=MESH).wait_recv()
        plan={}
        def at(h,fn): plan.setdefault(h,[]).append(fn)
        def diag(i,zz):
            f1=S.prep(sub(PS.at[bd*4+zz],B1), LHY.at[zz], s_hy.at[zz], Y)
            f2=S.prep(sub(PS.at[bd*4+zz],B2), LHX.at[zz], s_hx.at[zz], X)
            def fn():
                ready(i)
                acc(sub(PS.at[bd*4+zz],B), [sub(PS.at[bd*4+zz],B), sub(R.at[bd,zz],B)], nb)
                f1(); f2()
            return fn
        def chainA(bi,bb,ds=(3,2,1)):
            fns=[]
            for d in ds:
                for s in (1,-1):
                    zz=z+s*d
                    pred=(zz<4) if s>0 else (zz>=0)
                    frm=dn if s>0 else up
                    dev=UP if s>0 else DN
                    di=0 if s>0 else 1
                    fire=S.prep(sub(PS.at[bb*4+zz],A), LZA.at[di,zz,bi], s_za.at[di,zz,bi], dev, pred)
                    def fn(zz=zz,pred=pred,frm=frm,di=di,fire=fire):
                        @pl.when(jnp.logical_and(pred,frm))
                        def _():
                            wrecv(LZA.at[di,zz,bi], s_za.at[di,zz,bi])
                            acc(sub(PS.at[bb*4+zz],A),[sub(PS.at[bb*4+zz],A),sub(R.at[bb,zz],A),LZA.at[di,zz,bi]],spa)
                        @pl.when(jnp.logical_and(pred,jnp.logical_not(frm)))
                        def _():
                            acc(sub(PS.at[bb*4+zz],A),[sub(PS.at[bb*4+zz],A),sub(R.at[bb,zz],A)],spa)
                        fire()
                    fns.append(fn)
            return fns
        def sides(i,zz):
            fx=S.prep(sub(PS.at[bx*4+zz],B), LX.at[zz], s_x.at[zz], X)
            fy=S.prep(sub(PS.at[by*4+zz],B), LY.at[zz], s_y.at[zz], Y)
            def fn():
                ready(4+2*i); ready(5+2*i)
                wrecv(LHY.at[zz], s_hy.at[zz])
                acc(sub(PS.at[bx*4+zz],B1),[sub(PS.at[bx*4+zz],B1),sub(R.at[bx,zz],B1),LHY.at[zz]],nb//2)
                acc(sub(PS.at[bx*4+zz],B2),[sub(PS.at[bx*4+zz],B2),sub(R.at[bx,zz],B2)],nb//2)
                fx()
                wrecv(LHX.at[zz], s_hx.at[zz])
                acc(sub(PS.at[by*4+zz],B2),[sub(PS.at[by*4+zz],B2),sub(R.at[by,zz],B2),LHX.at[zz]],nb//2)
                acc(sub(PS.at[by*4+zz],B1),[sub(PS.at[by*4+zz],B1),sub(R.at[by,zz],B1)],nb//2)
                fy()
            return fn
        for i,zz in enumerate(zo): at(2*i+3,diag(i,zz))
        for j,d in enumerate((3,2,1)):
            for fn in chainA(0,bd,(d,)): at(10+2*j,fn)
        for i,zz in enumerate(zo): at(13+4*i,sides(i,zz))
        for bi,bb in ((1,bx),(2,by)):
            for j,d in enumerate((3,2,1)):
                for fn in chainA(bi,bb,(d,)): at(26+2*j,fn)
        def produce(h,_):
            i=h//2; own=h%2
            bb,zz=pick(i)
            @pl.when(own==0)
            def _():
                @pl.when(i>=4)
                def _(): pcopy(i-4).wait_send()
            kk=bb*8+zz*2+jnp.where(own==1,c,1-c)
            comp(kk,PS.at[jnp.where(own==1,bb*4+zz,16+i%4)])
            @pl.when(own==0)
            def _():
                @pl.when(i==0)
                def _(): pl.semaphore_wait(bar,31)
                pcopy(i).start()
            for hh,fns in sorted(plan.items()):
                @pl.when(h==hh)
                def _():
                    for fn in fns: fn()
            return 0
        lax.fori_loop(0,32,produce,0)
        for i in range(4): ready(12+i)
        for fn in chainA(3,b): fn()
        for i,zz in enumerate(zo[:3]):
            wrecv(LX.at[zz],s_x.at[zz]); wrecv(LY.at[zz],s_y.at[zz])
            isup=zz>z
            inc=jnp.logical_or(jnp.logical_and(isup,dn),jnp.logical_and(jnp.logical_not(isup),up))
            di=jnp.where(isup,0,1)
            base=[sub(PS.at[b*4+zz],B),sub(R.at[b,zz],B),LX.at[zz],LY.at[zz]]
            @pl.when(inc)
            def _():
                wrecv(LZB.at[di,zz],s_zb.at[di,zz])
                acc(sub(PS.at[b*4+zz],B),base+[LZB.at[di,zz]],nb)
            @pl.when(jnp.logical_not(inc))
            def _(): acc(sub(PS.at[b*4+zz],B),base,nb)
            S.go(sub(PS.at[b*4+zz],B),LZB.at[0,zz],s_zb.at[0,zz],UP,isup)
            S.go(sub(PS.at[b*4+zz],B),LZB.at[1,zz],s_zb.at[1,zz],DN,jnp.logical_not(isup))
        def totA(bi,bb,part,extra=(),dst=None):
            dst = dst if dst is not None else sub(PS.at[bb*4+z],part)
            srcs=[sub(PS.at[bb*4+z],part),sub(R.at[bb,z],part)]+list(extra)
            o=part[0]; n=part[1]
            l0=LZA.at[0,z,bi,pl.ds(o,n)]; l1=LZA.at[1,z,bi,pl.ds(o,n)]
            @pl.when(jnp.logical_and(up,dn))
            def _(): acc(dst,srcs+[l0,l1],n)
            @pl.when(jnp.logical_not(up))
            def _(): acc(dst,srcs+[l0],n)
            @pl.when(jnp.logical_not(dn))
            def _(): acc(dst,srcs+[l1],n)
        for bi in range(4):
            @pl.when(dn)
            def _(): wrecv(LZA.at[0,z,bi],s_za.at[0,z,bi])
            @pl.when(up)
            def _(): wrecv(LZA.at[1,z,bi],s_za.at[1,z,bi])
            if bi==0:
                totA(0,bd,A1); S.go(sub(PS.at[bd*4+z],A1),LPA.at[0,pl.ds(0,spa//2)],s_pa.at[0],Y)
                totA(0,bd,A2); S.go(sub(PS.at[bd*4+z],A2),LPA.at[1,pl.ds(0,spa//2)],s_pa.at[1],X)
            if bi==1:
                totA(1,bx,A2)
                wrecv(LPA.at[0,pl.ds(0,spa//2)],s_pa.at[0])
                totA(1,bx,A1,[LPA.at[0,pl.ds(0,spa//2)]])
                S.go(sub(PS.at[bx*4+z],A),LPA.at[2],s_pa.at[2],X)
            if bi==2:
                totA(2,by,A1)
                wrecv(LPA.at[1,pl.ds(0,spa//2)],s_pa.at[1])
                totA(2,by,A2,[LPA.at[1,pl.ds(0,spa//2)]])
                S.go(sub(PS.at[by*4+z],A),LPA.at[3],s_pa.at[3],Y)
        wrecv(LX.at[z],s_x.at[z]); wrecv(LY.at[z],s_y.at[z])
        base=[sub(PS.at[b*4+z],B),sub(R.at[b,z],B),LX.at[z],LY.at[z]]
        @pl.when(dn)
        def _(): wrecv(LZB.at[0,z],s_zb.at[0,z])
        @pl.when(up)
        def _(): wrecv(LZB.at[1,z],s_zb.at[1,z])
        @pl.when(jnp.logical_and(up,dn))
        def _(): acc(sub(out,B),base+[LZB.at[0,z],LZB.at[1,z]],nb)
        @pl.when(jnp.logical_not(up))
        def _(): acc(sub(out,B),base+[LZB.at[0,z]],nb)
        @pl.when(jnp.logical_not(dn))
        def _(): acc(sub(out,B),base+[LZB.at[1,z]],nb)
        wrecv(LPA.at[2],s_pa.at[2]); wrecv(LPA.at[3],s_pa.at[3])
        totA(3,b,A,[LPA.at[2],LPA.at[3]],dst=sub(out,A))
        def sq(i,a):
            v=out[i]; v=v*v
            return a+v[:8]+v[8:]
        NB[k]=lax.fori_loop(0,T,sq,jnp.zeros((8,128),jnp.float32))
        def ncopy(d):
            return pltpu.make_async_remote_copy(src_ref=NB.at[k],dst_ref=NB.at[k],send_sem=nsend.at[d],recv_sem=nsem.at[k],device_id=dev_of((k+d)%32),device_id_type=MESH)
        def nstart(d,_):
            ncopy(d).start(); return 0
        lax.fori_loop(1,32,nstart,0)
        CR=1440
        def untile(m,s0,n,t0):
            def body(s,_):
                for j in range(m):
                    C[pl.ds(CR+s0+s*16*m+j,16,stride=m),:]=out[t0+s*m+j]
                return 0
            lax.fori_loop(0,n,body,0)
        def plain(t0,n):
            def body(s,_):
                C[pl.ds(CR+(t0+s)*16,16),:]=out[t0+s]; return 0
            lax.fori_loop(0,n,body,0)
        def within(lo,hi): return jnp.logical_and(k>=lo,k<hi)
        @pl.when(jnp.logical_or(jnp.logical_or(within(0,4),within(10,12)),within(20,28)))
        def _(): untile(6,0,24,0)
        @pl.when(within(4,10))
        def _(): untile(18,0,8,0)
        @pl.when(within(12,20))
        def _(): untile(24,0,6,0)
        @pl.when(k==28)
        def _(): untile(4,0,36,0)
        @pl.when(k==29)
        def _():
            untile(4,0,12,0); plain(48,96)
        @pl.when(k>=30)
        def _(): plain(0,T)
        def carry(i,_):
            CB_[pl.ds(i*96,96)]=C[pl.ds(2304+i*96,96),:].astype(jnp.bfloat16); return 0
        lax.fori_loop(0,CR//96,carry,0)
        def cdesc(): return pltpu.make_async_remote_copy(src_ref=CB_,dst_ref=CR_,send_sem=csem.at[0],recv_sem=csem.at[1],device_id=dev_of((k+1)%32),device_id_type=MESH)
        @pl.when(k<31)
        def _(): cdesc().start()
        C[pl.ds(CR+2304,8),:]=jnp.zeros((8,128),jnp.float32)
        def nwait(d,_):
            kk=(k+d)%32
            wrecv_(NB.at[kk],nsem.at[kk],nsend.at[0],Pn); return 0
        lax.fori_loop(1,32,nwait,0)
        def nsum(i,a): return a+NB[i]
        nout[...]=lax.fori_loop(0,32,nsum,jnp.zeros((8,128),jnp.float32))
        @pl.when(k>0)
        def _():
            wrecv_(CR_,csem.at[1],csem.at[0],Pn)
            def uncarry(i,_):
                C[pl.ds(i*96,96),:]=CR_[pl.ds(i*96,96)].astype(jnp.float32); return 0
            lax.fori_loop(0,CR//96,uncarry,0)
        e=CR*128-(294912-289176)*k
        q=e//128; sh=e%128
        lane=lax.broadcasted_iota(jnp.int32,(96,128),1)
        def slide(i,_):
            r0=q+i*96
            a=pltpu.roll(C[pl.ds(r0,96),:],(128-sh)%128,1); b_=pltpu.roll(C[pl.ds(r0+1,96),:],(128-sh)%128,1)
            gout[pl.ds(i*96,96),:]=jnp.where(lane<128-sh,a,b_)
            return 0
        lax.fori_loop(0,24,slide,0)
        @pl.when(k<31)
        def _(): cdesc().wait_send()
        def ndone(d,_):
            ncopy(d).wait_send(); return 0
        lax.fori_loop(1,32,ndone,0)
        for i in range(12,16): pcopy(i).wait_send()
        S.drain()
    D=pltpu.SemaphoreType.DMA
    V=lambda *s: pltpu.VMEM(s+(16,128),jnp.bfloat16)
    VMs=pl.BlockSpec(memory_space=pltpu.VMEM)
    def rs(*args, cid=1):
        return pl.pallas_call(kernel, out_shape=(jax.ShapeDtypeStruct((2304,128),jnp.float32),jax.ShapeDtypeStruct((8,128),jnp.float32)),
            in_specs=[VMs]*11, out_specs=(VMs,VMs),
            scratch_shapes=[V(20,T),V(4,4,T),pltpu.VMEM((768,400),jnp.bfloat16),V(4,nb),V(4,nb),V(4,nb//2),V(4,nb//2),V(2,4,nb),V(2,4,4,spa),V(4,spa),
              pltpu.VMEM((T,16,128),jnp.float32),pltpu.VMEM((3752,128),jnp.float32),pltpu.VMEM((1440,128),jnp.bfloat16),pltpu.VMEM((1440,128),jnp.bfloat16),pltpu.VMEM((32,8,128),jnp.float32),
              D((80,)),D((4,4)),D((4,)),D((2,)),D((32,)),D((32,)),D((4,)),D((4,)),D((4,)),D((4,)),D((2,4)),D((2,4,4)),D((4,))],
            compiler_params=pltpu.CompilerParams(collective_id=cid,has_side_effects=True,vmem_limit_bytes=63*1024*1024))(*args)
    return rs

def wrecv_(ref,sem,ssem,dev):
    pltpu.make_async_remote_copy(src_ref=ref,dst_ref=ref,send_sem=ssem,recv_sem=sem,device_id=dev,device_id_type=MESH).wait_recv()


TOK=400; CB=208; NK=3200; NQ=1600; SUB=80; PADQ=512
ROWS={"q":0,"k":400,"v":800,"qc":1200,"kc":1408,"vc":1616}
NT=(((1,),(1,)),((),())); NN=(((1,),(0,)),((),())); TN=(((0,),(0,)),((),()))
f32=jnp.float32; bf16=jnp.bfloat16

def dot(a,b,dims): return lax.dot_general(a,b,dims,preferred_element_type=f32)

def mesh_pos():
    b=lax.axis_index("batch"); f=lax.axis_index("frame")
    return b,f//2,f%2

def zbarrier(b,z,c):
    bar=pltpu.get_barrier_semaphore()
    for d in (1,2,3):
        pl.semaphore_signal(bar,inc=1,device_id=(b,((z+d)%4)*2+c),device_id_type=MESH)
    pl.semaphore_signal(bar,inc=1,device_id=(b,z*2+1-c),device_id_type=MESH)
    pl.semaphore_wait(bar,4)

def wrecv(ref,sem,dev):
    pltpu.make_async_remote_copy(src_ref=ref,dst_ref=ref,send_sem=sem,recv_sem=sem,device_id=dev,device_id_type=MESH).wait_recv()

def others(z):
    return [((z+d)%4) for d in (2,1,3)]

def unpack_c(src, dst, row):
    v=src.astype(f32)
    lane=lax.broadcasted_iota(jnp.int32,(CB,128),1)
    lo=jnp.where(lane<64,v,0.0)
    hi=jnp.where(lane<64,pltpu.roll(v,64,1),0.0)
    dst[pl.ds(row,CB)]=lo.astype(bf16)
    dst[pl.ds(row+CB,TOK-CB)]=hi[:TOK-CB].astype(bf16)

def pack_c(lo, hi):
    hi=jnp.concatenate([hi,jnp.zeros((2*CB-TOK,128),f32)],0)
    lane=lax.broadcasted_iota(jnp.int32,(CB,128),1)
    return jnp.where(lane<64,lo,pltpu.roll(hi,64,1)).astype(bf16)

def key_lanes(v, free, ok):
    e=lax.broadcasted_iota(jnp.int32,v.shape,1)-free
    v=jnp.where(jnp.logical_and(e>=1,e<4),1.0,v)
    return jnp.where(e==0,jnp.where(ok,0.0,-1e30),v)

def value_lanes(v, free):
    e=lax.broadcasted_iota(jnp.int32,v.shape,1)-free
    return jnp.where(jnp.logical_and(e>=0,e<3),1.0,v)

def three_lanes(v, free, col):
    hi=col.astype(bf16).astype(f32); mid=(col-hi).astype(bf16).astype(f32); lo=col-hi-mid
    e=lax.broadcasted_iota(jnp.int32,v.shape,1)-free
    return jnp.where(e==0,hi,jnp.where(e==1,mid,jnp.where(e==2,lo,v)))

def one_lane(v, free):
    e=lax.broadcasted_iota(jnp.int32,v.shape,1)-free
    return jnp.where(e==0,1.0,v)

def fwd_kernel(lims, sp, og, Q, KA, KB, VA, VB, QC, KC, VC, OA, OC, LA, LC,
               K, V, QCp, KCp, VCp, OB, OCp, S, Pb, ssem, lsem, rq, rk, rv, rqc, rkc, rvc, pk, pv, pkc, pvc, ro, roc):
    b,z,c=mesh_pos()
    Pn=(b,z*2+1-c)
    dev=lambda zz:(b,zz*2+c)
    row=lambda zz: pl.multiple_of(zz*TOK,16)
    krow=lambda zz: pl.multiple_of((c*4+zz)*TOK,16)
    pkrow=lambda zz: pl.multiple_of(((1-c)*4+zz)*TOK,16)
    zbarrier(b,z,c)
    X=Sends(ssem)
    part=lambda g,n,ln: sp.at[g,pl.ds(ROWS[n],ln)]
    loc=[]
    def lcopy(src,dst):
        cp=pltpu.make_async_copy(src,dst,lsem.at[len(loc)]); cp.start(); loc.append(cp)
    for zz in others(z):
        X.go(part(zz,"k",TOK),K.at[pl.ds(krow(z),TOK)],rk.at[z],dev(zz))
        X.go(part(zz,"q",TOK),Q.at[pl.ds(row(z),TOK)],rq.at[z],dev(zz))
        X.go(part(zz,"v",TOK),V.at[pl.ds(krow(z),TOK)],rv.at[z],dev(zz))
    lcopy(part(z,"k",TOK),K.at[pl.ds(krow(z),TOK)])
    lcopy(part(z,"q",TOK),Q.at[pl.ds(row(z),TOK)])
    lcopy(part(z,"v",TOK),V.at[pl.ds(krow(z),TOK)])
    lcopy(part(z,"kc",CB),KCp.at[c*4+z]); lcopy(part(z,"qc",CB),QCp.at[z]); lcopy(part(z,"vc",CB),VCp.at[c*4+z])
    X.go(part(z,"k",TOK),K.at[pl.ds(krow(z),TOK)],pk.at[z],Pn)
    X.go(part(z,"v",TOK),V.at[pl.ds(krow(z),TOK)],pv.at[z],Pn)
    X.go(part(z,"kc",CB),KCp.at[c*4+z],pkc.at[z],Pn)
    X.go(part(z,"vc",CB),VCp.at[c*4+z],pvc.at[z],Pn)
    for zz in others(z):
        X.go(part(zz,"kc",CB),KCp.at[c*4+z],rkc.at[z],dev(zz))
        X.go(part(zz,"qc",CB),QCp.at[z],rqc.at[z],dev(zz))
        X.go(part(zz,"vc",CB),VCp.at[c*4+z],rvc.at[z],dev(zz))
    for zz in [((z+d)%4) for d in (1,3,2)]:
        kr=K.at[pl.ds(krow(zz),TOK)]; vr=V.at[pl.ds(krow(zz),TOK)]
        wrecv(kr,rk.at[zz],Pn); X.go(kr,kr,pk.at[zz],Pn)
        wrecv(vr,rv.at[zz],Pn); X.go(vr,vr,pv.at[zz],Pn)
    for zz in range(4):
        r=K.at[pl.ds(pkrow(zz),TOK)]; wrecv(r,pk.at[zz],Pn)
        r=V.at[pl.ds(pkrow(zz),TOK)]; wrecv(r,pv.at[zz],Pn)
    for zz in [((z+d)%4) for d in (1,2,3)]:
        wrecv(Q.at[pl.ds(row(zz),TOK)],rq.at[zz],Pn)
    for cp in loc: cp.wait()
    lane=lax.broadcasted_iota(jnp.int32,(TOK,128),1)
    patch=lax.broadcasted_iota(jnp.int32,(TOK,128),0)
    def key_ok(i):
        return patch<jnp.where((i%4)*2+i//4<lims[1],lims[0],0)
    def widen(i,_):
        ds=pl.ds(pl.multiple_of(i*TOK,16),TOK)
        ok=key_ok(i)
        kk=K[ds].astype(f32); vv=V[ds].astype(f32)
        ka=jnp.where(lane<64,kk,0.0); va=jnp.where(lane<64,vv,0.0)
        KA[ds]=key_lanes(ka,64,ok).astype(bf16); KB[ds]=key_lanes(kk-ka,0,ok).astype(bf16)
        VA[ds]=value_lanes(va,64).astype(bf16); VB[ds]=value_lanes(vv-va,0).astype(bf16)
        return 0
    lax.fori_loop(0,8,widen,0)
    def softmax(slot):
        def sub(i,carry):
            ds=pl.ds(pl.multiple_of(i*SUB,16),SUB)
            m=jnp.max(S[slot,ds,:],-1,keepdims=True)
            Pb[slot,ds,:]=jnp.exp(S[slot,ds,:]-m).astype(bf16)
            return m
        return jnp.concatenate([sub(i,0) for i in range(TOK//SUB)],0)
    def pairblock(i,_):
        ds=pl.ds(pl.multiple_of(i*TOK,16),TOK)
        q=Q[ds].astype(f32)
        qa=jnp.where(lane<64,q,0.0)
        S[0]=dot(one_lane(qa,64).astype(bf16),KA[...],NT)
        S[1]=dot(one_lane(q-qa,0).astype(bf16),KB[...],NT)
        ma=softmax(0); mb=softmax(1)
        oa=dot(Pb[0],VA[...],NN); ob=dot(Pb[1],VB[...],NN)
        la=oa[:,64:65]; lb=ob[:,0:1]
        o=jnp.where(lane<64,oa/la,ob/lb)
        OA[ds]=o; OB[ds]=o.astype(bf16)
        LA[ds]=jnp.where(lane<64,ma+jnp.log(la),mb+jnp.log(lb))
        return 0
    lax.fori_loop(0,4,pairblock,0)
    for zz in [((z+d)%4) for d in (1,3,2)]:
        kr=KCp.at[c*4+zz]; vr=VCp.at[c*4+zz]
        wrecv(kr,rkc.at[zz],Pn); X.go(kr,kr,pkc.at[zz],Pn)
        wrecv(vr,rvc.at[zz],Pn); X.go(vr,vr,pvc.at[zz],Pn)
        wrecv(QCp.at[zz],rqc.at[zz],Pn)
    for zz in others(z):
        X.go(OB.at[pl.ds(row(zz),TOK)],og.at[z,pl.ds(0,TOK)],ro.at[z],dev(zz))
    lo=pltpu.make_async_copy(OB.at[pl.ds(row(z),TOK)],og.at[z,pl.ds(0,TOK)],lsem.at[6]); lo.start()
    for zz in range(4):
        wrecv(KCp.at[(1-c)*4+zz],pkc.at[zz],Pn); wrecv(VCp.at[(1-c)*4+zz],pvc.at[zz],Pn)
    def unp(i,_):
        r=pl.multiple_of(i*TOK,16)
        unpack_c(KCp[i],KC,r); unpack_c(VCp[i],VC,r)
        ds=pl.ds(r,TOK)
        KC[ds]=key_lanes(KC[ds].astype(f32),64,key_ok(i)).astype(bf16)
        VC[ds]=value_lanes(VC[ds].astype(f32),64).astype(bf16)
        return 0
    lax.fori_loop(0,8,unp,0)
    def unq(i,_):
        unpack_c(QCp[i],QC,pl.multiple_of(i*TOK,16)); return 0
    lax.fori_loop(0,4,unq,0)
    def cblock(i,_):
        ds=pl.ds(pl.multiple_of(i*TOK,16),TOK)
        S[0]=dot(one_lane(QC[ds].astype(f32),64).astype(bf16),KC[...],NT)
        ma=softmax(0)
        o=dot(Pb[0],VC[...],NN)
        la=o[:,64:65]
        o=o/la
        OC[ds]=o
        LC[ds]=jnp.broadcast_to(ma+jnp.log(la),(TOK,128))
        OCp[i]=pack_c(o[:CB],o[CB:])
        return 0
    lax.fori_loop(0,4,cblock,0)
    for zz in others(z):
        X.go(OCp.at[zz],og.at[z,pl.ds(TOK,CB)],roc.at[z],dev(zz))
    lc=pltpu.make_async_copy(OCp.at[z],og.at[z,pl.ds(TOK,CB)],lsem.at[7]); lc.start()
    for d in (1,2,3):
        zz=(z+d)%4
        wrecv(og.at[zz,pl.ds(0,TOK)],ro.at[zz],Pn)
        wrecv(og.at[zz,pl.ds(TOK,CB)],roc.at[zz],Pn)
    lo.wait(); lc.wait()
    X.drain()

D=pltpu.SemaphoreType.DMA
def vb(*s): return pltpu.VMEM(s,bf16)
def vf(*s): return pltpu.VMEM(s,f32)
VM=pl.BlockSpec(memory_space=pltpu.VMEM)
SM=pl.BlockSpec(memory_space=pltpu.SMEM)
def sds(*s,d=bf16): return jax.ShapeDtypeStruct(s,d)

def attn_fwd(sp,lims,cid):
    return pl.pallas_call(fwd_kernel,
        out_shape=(sds(4,TOK+CB,128),sds(NQ,128),sds(NK,128),sds(NK,128),sds(NK,128),sds(NK,128),sds(NQ,128),sds(NK,128),sds(NK,128),
                   sds(NQ,128,d=f32),sds(NQ,128,d=f32),sds(NQ,128,d=f32),sds(NQ,128,d=f32)),
        in_specs=[SM,VM],out_specs=[VM]*13,
        scratch_shapes=[vb(NK,128),vb(NK,128),vb(4,CB,128),vb(8,CB,128),vb(8,CB,128),vb(NQ,128),vb(4,CB,128),vf(2,TOK,NK),vb(2,TOK,NK),
            D((48,)),D((8,))]+[D((4,))]*12,
        compiler_params=pltpu.CompilerParams(collective_id=cid,has_side_effects=True,vmem_limit_bytes=60*1024*1024))(lims,sp)

def bwd_kernel(dog, Q, KA, KB, VA, VB, QC, KC, VC, OA, OC, LA, LC, dsp,
               DO, DOCp, DOC, S, P, DS, DKT, DVT, TT, DQ, DQC, XK, XV, YK, YV, SK, SV, HK, HV, XKC, XVC, YKC, YVC, HKC, HVC,
               ssem, lsem, rd, rdc, px, ho):
    b,z,c=mesh_pos()
    Pn=(b,z*2+1-c)
    dev=lambda zz:(b,zz*2+c)
    row=lambda zz: pl.multiple_of(zz*TOK,16)
    zbarrier(b,z,c)
    X=Sends(ssem)
    loc=[]
    def lcopy(src,dst):
        cp=pltpu.make_async_copy(src,dst,lsem.at[len(loc)]); cp.start(); loc.append(cp); return cp
    for zz in others(z):
        X.go(dog.at[zz,pl.ds(0,TOK)],DO.at[pl.ds(row(z),TOK)],rd.at[z],dev(zz))
    for zz in others(z):
        X.go(dog.at[zz,pl.ds(TOK,CB)],DOCp.at[z],rdc.at[z],dev(zz))
    l1=lcopy(dog.at[z,pl.ds(0,TOK)],DO.at[pl.ds(row(z),TOK)])
    l2=lcopy(dog.at[z,pl.ds(TOK,CB)],DOCp.at[z])
    l1.wait(); l2.wait()
    lane=lax.broadcasted_iota(jnp.int32,(TOK,128),1)
    def zero(ref):
        def bodyz(i,_):
            ref[:,pl.ds(pl.multiple_of(i*640,128),640)]=jnp.zeros((128,640),f32); return 0
        lax.fori_loop(0,NK//640,bodyz,0)
    def grads(q,k,v,do,lse,delta,free):
        S[0]=dot(three_lanes(one_lane(q,free),free+1,-lse).astype(bf16),k[...],NT)
        S[1]=dot(three_lanes(do,free,-delta).astype(bf16),v[...],NT)
        q=q.astype(bf16); do=do.astype(bf16)
        for i in range(TOK//SUB):
            ds=pl.ds(i*SUB,SUB)
            p=jnp.exp(S[0,ds,:])
            P[ds,:]=p.astype(bf16)
            DS[ds,:]=(p*S[1,ds,:]).astype(bf16)
        tail=jnp.zeros((PADQ-TOK,128),bf16)
        DKT[...]+=dot(jnp.concatenate([q,tail],0),DS[...],TN)
        DVT[...]+=dot(jnp.concatenate([do,tail],0),P[...],TN)
        return dot(DS[pl.ds(0,TOK)],k[...],NN)
    def home(src,r0,n,si):
        for zz in others(z):
            X.go(src(zz),dsp.at[z,pl.ds(r0,n)],ho.at[si,z],dev(zz))
        lcopy(src(z),dsp.at[z,pl.ds(r0,n)])
    mine=c*NQ; theirs=(1-c)*NQ
    def split(acc, x, own):
        def tr(i,_):
            TT[pl.ds(pl.multiple_of(i*640,16),640)]=acc[:,pl.ds(pl.multiple_of(i*640,128),640)].T
            return 0
        lax.fori_loop(0,NK//640,tr,0)
        def cut(i,_):
            r=pl.multiple_of(i*TOK,16)
            x[pl.ds(r,TOK)]=TT[pl.ds(pl.multiple_of(theirs+i*TOK,16),TOK)].astype(bf16)
            own[pl.ds(r,TOK)]=TT[pl.ds(pl.multiple_of(mine+i*TOK,16),TOK)]
            return 0
        lax.fori_loop(0,4,cut,0)
    P[pl.ds(TOK,PADQ-TOK)]=jnp.zeros((PADQ-TOK,NK),bf16)
    DS[pl.ds(TOK,PADQ-TOK)]=jnp.zeros((PADQ-TOK,NK),bf16)
    zero(DKT); zero(DVT)
    def pairblock(i,_):
        zz=(z+i)%4
        @pl.when(i>0)
        def _(): wrecv(DO.at[pl.ds(row(zz),TOK)],rd.at[zz],Pn)
        ds=pl.ds(row(zz),TOK)
        q=Q[ds].astype(f32); do=DO[ds].astype(f32)
        dof=do*OA[ds]
        da=jnp.sum(jnp.where(lane<64,dof,0.0),-1,keepdims=True)
        db=jnp.sum(jnp.where(lane<64,0.0,dof),-1,keepdims=True)
        qa=jnp.where(lane<64,q,0.0); doa=jnp.where(lane<64,do,0.0)
        ga=grads(qa,KA,VA,doa,LA[ds,0:1],da,64)
        gb=grads(q-qa,KB,VB,do-doa,LA[ds,64:65],db,0)
        DQ[ds]=(jnp.where(lane<64,ga,gb)*0.125).astype(bf16)
        return 0
    lax.fori_loop(0,4,pairblock,0)
    home(lambda zz: DQ.at[pl.ds(row(zz),TOK)],0,TOK,0)
    split(DKT,XK,SK); X.go(XK,YK,px.at[0],Pn)
    split(DVT,XV,SV); X.go(XV,YV,px.at[1],Pn)
    zero(DKT); zero(DVT)
    def cblock(i,_):
        zz=(z+i)%4
        @pl.when(i>0)
        def _(): wrecv(DOCp.at[zz],rdc.at[zz],Pn)
        unpack_c(DOCp[zz],DOC,0)
        ds=pl.ds(row(zz),TOK)
        do=DOC[...].astype(f32)
        delta=jnp.sum(do*OC[ds],-1,keepdims=True)
        g=grads(QC[ds].astype(f32),KC,VC,do,LC[ds,0:1],delta,64)*0.125
        DQC[zz]=pack_c(g[:CB],g[CB:])
        return 0
    lax.fori_loop(0,4,cblock,0)
    home(lambda zz: DQC.at[zz],ROWS["qc"],CB,1)
    wrecv(YK,px.at[0],Pn); wrecv(YV,px.at[1],Pn)
    def addp(i,_):
        ds=pl.ds(pl.multiple_of(i*TOK,16),TOK)
        HK[ds]=(SK[ds]+YK[ds].astype(f32)).astype(bf16)
        HV[ds]=(SV[ds]+YV[ds].astype(f32)).astype(bf16)
        return 0
    lax.fori_loop(0,4,addp,0)
    home(lambda zz: HK.at[pl.ds(row(zz),TOK)],ROWS["k"],TOK,2)
    home(lambda zz: HV.at[pl.ds(row(zz),TOK)],ROWS["v"],TOK,3)
    def splitc(acc, x, own):
        def tr(i,_):
            TT[pl.ds(pl.multiple_of(i*640,16),640)]=acc[:,pl.ds(pl.multiple_of(i*640,128),640)].T
            return 0
        lax.fori_loop(0,NK//640,tr,0)
        def cut(i,_):
            r=theirs+i*TOK
            x[i]=pack_c(TT[pl.ds(pl.multiple_of(r,16),CB)],TT[pl.ds(pl.multiple_of(r+CB,16),TOK-CB)])
            own[pl.ds(pl.multiple_of(i*TOK,16),TOK)]=TT[pl.ds(pl.multiple_of(mine+i*TOK,16),TOK)]
            return 0
        lax.fori_loop(0,4,cut,0)
    splitc(DKT,XKC,SK); X.go(XKC,YKC,px.at[2],Pn)
    splitc(DVT,XVC,SV); X.go(XVC,YVC,px.at[3],Pn)
    def addc(y,own,h):
        def body(i,_):
            unpack_c(y[i],DOC,0)
            r=i*TOK
            t=own[pl.ds(pl.multiple_of(r,16),TOK)]+DOC[...].astype(f32)
            h[i]=pack_c(t[:CB],t[CB:])
            return 0
        lax.fori_loop(0,4,body,0)
    wrecv(YKC,px.at[2],Pn); addc(YKC,SK,HKC)
    home(lambda zz: HKC.at[zz],ROWS["kc"],CB,4)
    wrecv(YVC,px.at[3],Pn); addc(YVC,SV,HVC)
    home(lambda zz: HVC.at[zz],ROWS["vc"],CB,5)
    for si,(r0,n) in enumerate(((0,TOK),(ROWS["qc"],CB),(ROWS["k"],TOK),(ROWS["v"],TOK),(ROWS["kc"],CB),(ROWS["vc"],CB))):
        for d in (1,2,3):
            zz=(z+d)%4
            wrecv(dsp.at[zz,pl.ds(r0,n)],ho.at[si,zz],Pn)
    for cp in loc[2:]: cp.wait()
    X.drain()

def attn_bwd(dog,saved,cid):
    return pl.pallas_call(bwd_kernel,
        out_shape=sds(4,3*(TOK+CB),128),
        in_specs=[VM]*13,out_specs=VM,
        scratch_shapes=[vb(NQ,128),vb(4,CB,128),vb(TOK,128),vf(2,TOK,NK),vb(PADQ,NK),vb(PADQ,NK),vf(128,NK),vf(128,NK),vf(NK,128),
            vb(NQ,128),vb(4,CB,128)]+[vb(NQ,128)]*4+[vf(NQ,128)]*2+[vb(NQ,128)]*2+[vb(4,CB,128)]*6+[
            D((32,)),D((10,)),D((4,)),D((4,)),D((4,)),D((6,4))],
        compiler_params=pltpu.CompilerParams(collective_id=cid,has_side_effects=True,vmem_limit_bytes=60*1024*1024))(dog,*saved)


HI=lax.Precision.HIGHEST
DM=768
MTILES=(0,None,1,2,None,3)

def spread(pair, packed):
    lane=lax.broadcasted_iota(jnp.int32,(CB,128),1)
    def mid(g0,g1):
        a=packed(g0).astype(f32); b=packed(g1).astype(f32)
        top=jnp.where(lane<64,a,pltpu.roll(b,64,1))
        low=jnp.where(lane<64,pltpu.roll(a,64,1),b)
        return jnp.concatenate([top,low[:TOK-CB]],0).astype(bf16)
    return [pair(0),mid(0,1),pair(1),pair(2),mid(2,3),pair(3)]

def gather_groups(tiles):
    out=[]
    for g in range(4):
        p=tiles[(0,2,3,5)[g]]
        t=tiles[(1,1,4,4)[g]]
        if g%2: t=pltpu.roll(t,64,1)
        out.append((p.astype(bf16),pack_c(t[:CB],t[CB:])))
    return out

def wcols(W,j,n):
    S=W.shape[0]
    return jnp.concatenate([W[:,j+i].reshape(S*16,128) for i in range(n)],1)

def lnorm(x):
    c=x-jnp.mean(x,-1,keepdims=True)
    inv=lax.rsqrt(jnp.mean(c*c,-1,keepdims=True)+EPSILON)
    return c*inv,inv

def lnorm_back(dy,gain,n,inv):
    g=dy*gain
    return inv*(g-jnp.mean(g,-1,keepdims=True)-n*jnp.mean(g*n,-1,keepdims=True))

def vrow(V,i):
    return jnp.concatenate([V[6*i+j:6*i+j+1,:] for j in range(6)],1)

def colsum(x): return jnp.sum(x,0,keepdims=True)

def front_kernel(start, fidx, pix, G, x0o, h1o, sp, We, Wq, PO, POf, TI, VE, V, TIf, sems):
    cps=[pltpu.make_async_copy(G.at[pl.ds(0,576)],We,sems.at[0]),
         pltpu.make_async_copy(G.at[pl.ds(4224+(48+6*start[0])//16,151)],PO,sems.at[1]),
         pltpu.make_async_copy(G.at[pl.ds(4224+264,3)],TI,sems.at[2]),
         pltpu.make_async_copy(G.at[pl.ds(4512,7)],VE,sems.at[3]),
         pltpu.make_async_copy(G.at[pl.ds(576,864)],Wq,sems.at[4])]
    for cp in cps: cp.start()
    for cp in cps[:4]: cp.wait()
    for i in range(7): V[pl.ds(i*16,16),:]=VE[i].astype(f32)
    for i in range(3): TIf[pl.ds(i*16,16),:]=TI[i].astype(f32)
    def cv(i,_):
        POf[pl.ds(i*16,16),:]=PO[i].astype(f32); return 0
    lax.fori_loop(0,151,cv,0)
    rem=(6*start[0])%16
    W4=We.reshape(96,6,16,128)
    for j in range(3):
        e=dot(pix[...],wcols(W4,2*j,2),NN)
        p=jnp.concatenate([POf[pl.ds(rem+2*j+i,TOK,stride=6),:] for i in range(2)],1)
        tm=jnp.concatenate([TIf[pl.ds(6*fidx[0]+2*j+i,1),:] for i in range(2)],1)
        bb=jnp.concatenate([V[48+2*j+i:49+2*j+i,:] for i in range(2)],1)
        x0o[:,j*256:(j+1)*256]=e+bb+p+tm
    n,inv=lnorm(x0o[...])
    h1=(n*vrow(V,0)+vrow(V,1)).astype(bf16)
    h1o[...]=h1
    cps[4].wait()
    W4=Wq.reshape(48,18,16,128)
    for part in range(3):
        tiles=[]
        for j in range(3):
            r=dot(h1,wcols(W4,part*6+2*j,2),NN)
            if part!=1:
                o=54 if part==0 else 60
                r=r+jnp.concatenate([V[o+2*j+i:o+1+2*j+i,:] for i in range(2)],1)
            r=r.astype(bf16).astype(f32)
            if part==0: r=r*0.125
            tiles+=[r[:,:128],r[:,128:]]
        for g,(p,c) in enumerate(gather_groups(tiles)):
            sp[g,pl.ds(part*TOK,TOK)]=p
            sp[g,pl.ds(3*TOK+part*CB,CB)]=c

ANYS=pl.BlockSpec(memory_space=pl.ANY)
def front(start,fidx,pix,G):
    return pl.pallas_call(front_kernel,
        out_shape=(sds(TOK,DM,d=f32),sds(TOK,DM),sds(4,3*(TOK+CB),128)),
        in_specs=[SM,SM,VM,ANYS],out_specs=(VM,)*3,
        scratch_shapes=[vb(576,16,128),vb(864,16,128),vb(151,16,128),vf(2416,128),vb(3,16,128),vb(7,16,128),vf(112,128),vf(48,128),D((5,))],
        compiler_params=pltpu.CompilerParams(vmem_limit_bytes=60*1024*1024))(start,fidx,pix,G)

def mid_kernel(og, x0, G, wmap, vmask, scal, counts, sel,
               atto, h2o, acto, dpreo, dmlpo, dattno, dsec, dog, vgo, ubo, gmapo, gprojo, losso,
               Wo, Wu, Wd, Wp, VE, V, A2, GP, SLOT, x1s, x2s, sems, ssem, rsem):
    b=lax.axis_index("batch"); f=lax.axis_index("frame"); k=b*8+f
    def dev_of(kk): return (kk//8,kk%8)
    bar=pltpu.get_barrier_semaphore()
    def greet(d,_):
        pl.semaphore_signal(bar,inc=1,device_id=dev_of((k+d)%32),device_id_type=MESH); return 0
    lax.fori_loop(1,32,greet,0)
    cps=[pltpu.make_async_copy(G.at[pl.ds(10*144,288)],Wo,sems.at[0]),
         pltpu.make_async_copy(G.at[pl.ds(4512,7)],VE,sems.at[1]),
         pltpu.make_async_copy(G.at[pl.ds(12*144,1152)],Wu,sems.at[2]),
         pltpu.make_async_copy(G.at[pl.ds(20*144,1152)],Wd,sems.at[3]),
         pltpu.make_async_copy(G.at[pl.ds(28*144,192)],Wp,sems.at[4])]
    for cp in cps: cp.start()
    for j,t in enumerate(spread(lambda g: og[g,pl.ds(0,TOK)],lambda g: og[g,pl.ds(TOK,CB)])):
        atto[:,j*128:(j+1)*128]=t
    cps[0].wait(); cps[1].wait()
    for i in range(7): V[pl.ds(i*16,16),:]=VE[i].astype(f32)
    Wo4=Wo.reshape(48,6,16,128); Wu4=Wu.reshape(48,24,16,128); Wd4=Wd.reshape(192,6,16,128); Wp4=Wp.reshape(48,4,16,128)
    att=atto[...]
    for j in range(3):
        bb=jnp.concatenate([V[66+2*j+i:67+2*j+i,:] for i in range(2)],1)
        x1s[:,j*256:(j+1)*256]=x0[:,j*256:(j+1)*256]+(dot(att,wcols(Wo4,2*j,2),NN)+bb)
    n2,inv2=lnorm(x1s[...])
    h2=(n2*vrow(V,2)+vrow(V,3)).astype(bf16)
    h2o[...]=h2
    x2s[...]=x1s[...]+vrow(V,12)
    cps[2].wait(); cps[3].wait()
    def hid(j,_):
        w=jnp.concatenate([Wu4[:,2*j+i].reshape(768,128) for i in range(2)],1)
        bb=jnp.concatenate([V[pl.ds(78+2*j+i,1),:] for i in range(2)],1)
        u=dot(h2o[...],w,NN)+bb
        phi=0.5*(1.0+lax.erf(u*(0.5**0.5)))
        a=(u*phi).astype(bf16)
        cs=pl.ds(pl.multiple_of(j*256,256),256)
        GP[:,cs]=phi+u*(jnp.exp(-0.5*u*u)*0.3989422804014327)
        acto[:,cs]=a
        wd=Wd4[pl.ds(j*16,16)]
        x2s[...]+=dot(a,jnp.concatenate([wd[:,t].reshape(256,128) for t in range(6)],1),NN)
        return 0
    lax.fori_loop(0,12,hid,0)
    x2=x2s[...]
    nm,invm=lnorm(x2)
    nmap=nm*vrow(V,4)+vrow(V,5)
    lg=lax.dot_general(nmap,wmap[...],NN,precision=HI,preferred_element_type=f32)
    ok=vmask[...]>0.0
    lg=jnp.where(ok,lg,-1e30)
    ex=jnp.where(ok,jnp.exp(lg-jnp.max(lg,0,keepdims=True)),0.0)
    lane8=lax.broadcasted_iota(jnp.int32,(TOK,128),1)<NMAP
    maps=jnp.where(lane8,ex/jnp.sum(ex,0,keepdims=True),0.0)
    r=jnp.sum(maps,-1,keepdims=True)
    sw=scal[0:1,0:1]; inv_total=scal[1:2,0:1]
    pooled=sw*colsum(r*x2)
    corr=sw*colsum(r*r-jnp.sum(maps*maps,-1,keepdims=True))
    slot=[pooled[:,j*128:(j+1)*128] for j in range(6)]+[jnp.broadcast_to(corr,(1,128)),jnp.zeros((1,128),f32)]
    SLOT[k,pl.ds(0,8)]=jnp.concatenate(slot,0)
    SLOT[k,pl.ds(8,8)]=sel[...]
    def xcopy(d):
        return pltpu.make_async_remote_copy(src_ref=SLOT.at[k],dst_ref=SLOT.at[k],send_sem=ssem.at[d],recv_sem=rsem.at[k],device_id=dev_of((k+d)%32),device_id_type=MESH)
    pl.semaphore_wait(bar,31)
    def xs(d,_):
        xcopy(d).start(); return 0
    lax.fori_loop(1,32,xs,0)
    cps[4].wait()
    def xw(d,_):
        kk=(k+d)%32
        wrecv(SLOT.at[kk],rsem.at[kk],(b,f)); return 0
    lax.fori_loop(1,32,xw,0)
    tot=[]
    for cl in range(4):
        t=SLOT[cl*8,pl.ds(0,8)]
        for ff in range(1,8): t=t+SLOT[cl*8+ff,pl.ds(0,8)]
        tot.append(t)
    corr_total=(tot[0]+tot[1]+tot[2]+tot[3])[6:7,0:1]
    pm=jnp.concatenate([jnp.concatenate([t[j:j+1,:] for j in range(6)],1) for t in tot]+[jnp.zeros((4,DM),f32)],0)/counts[:,0:1]
    nf,invf=lnorm(pm)
    hf=nf*vrow(V,6)+vrow(V,7)
    rows=lax.broadcasted_iota(jnp.int32,(8,1),0)
    live=rows<4
    wp=jnp.concatenate([Wp4[:,t].reshape(768,128) for t in range(4)],1).astype(f32)
    e=lax.dot_general(hf,wp,NN,precision=HI,preferred_element_type=f32)
    rn=lax.rsqrt(jnp.sum(e*e,-1,keepdims=True)+1e-06)
    unit=e*rn
    lanes=lax.broadcasted_iota(jnp.int32,(8,128),1)
    gm=jnp.zeros((8,128),f32)
    for j in range(4):
        gm=gm+jnp.where(lanes==j,jnp.sum(unit*unit[j:j+1,:],-1,keepdims=True),0.0)
    selk=[jnp.concatenate([SLOT[cl*8,pl.ds(8+kk,1)] for cl in range(4)]+[jnp.zeros((4,128),f32)],0) for kk in range(5)]
    S=[jnp.sum(s*gm,-1,keepdims=True)/SOFTMAX_TEMPER for s in selk]
    mx=S[0]
    for s in S[1:]: mx=jnp.maximum(mx,s)
    es=[jnp.exp(s-mx) for s in S]
    se=es[0]+es[1]+es[2]+es[3]+es[4]
    contrast=jnp.sum(jnp.where(live,mx+jnp.log(se)-S[0],0.0),0,keepdims=True)*0.25
    losso[...]=jnp.broadcast_to(contrast+DECAY_PENALTY*corr_total*inv_total,(8,128))
    dgm=jnp.zeros((8,128),f32)
    for kk in range(5):
        w=es[kk]/se-(1.0 if kk==0 else 0.0)
        dgm=dgm+jnp.where(live,w,0.0)*selk[kk]
    dgm=dgm*(0.25/SOFTMAX_TEMPER)
    du=jnp.zeros((8,EMB),f32)
    for j in range(4):
        cj=dgm[:,j:j+1]
        du=du+cj*unit[j:j+1,:]
        du=du+jnp.where(rows==j,colsum(cj*unit),0.0)
    de=rn*du-e*(rn*rn*rn)*jnp.sum(e*du,-1,keepdims=True)
    de=jnp.where(live,de,0.0)
    dhf=lax.dot_general(de,wp,NT,precision=HI,preferred_element_type=f32)
    head=jnp.where(k==0,1.0,0.0)
    gp=lax.dot_general(hf,de,TN,precision=HI,preferred_element_type=f32)*head
    gpb=gp.astype(bf16)
    for s in range(48):
        for t in range(4): gprojo[s*4+t]=gpb[s*16:(s+1)*16,t*128:(t+1)*128]
    vgo[6:7,:]=colsum(dhf*nf)*head
    vgo[7:8,:]=colsum(dhf)*head
    dpm=lnorm_back(dhf,vrow(V,6),nf,invf)/counts[:,0:1]
    dpool=colsum(jnp.where(rows==b,dpm,0.0))
    cdec=DECAY_PENALTY*inv_total*sw
    dm=sw*jnp.sum(x2*dpool,-1,keepdims=True)+2.0*cdec*(r-maps)
    dm=jnp.where(lane8,dm,0.0)
    dl=maps*(dm-colsum(maps*dm))
    gmapo[...]=lax.dot_general(nmap,dl,TN,precision=HI,preferred_element_type=f32)
    dnm=lax.dot_general(dl,wmap[...],NT,precision=HI,preferred_element_type=f32)
    vgo[4:5,:]=colsum(dnm*nm)
    vgo[5:6,:]=colsum(dnm)
    dx2=(sw*r)*dpool+lnorm_back(dnm,vrow(V,4),nm,invm)
    dmlp=dx2.astype(bf16)
    dmlpo[...]=dmlp
    vgo[12:13,:]=colsum(dmlp.astype(f32))
    x2s[...]=jnp.zeros((TOK,DM),f32)
    dsec[...]=dx2
    def hidb(j,_):
        cs=pl.ds(pl.multiple_of(j*256,256),256)
        wd=Wd4[pl.ds(j*16,16)]
        da=dot(dmlpo[...],jnp.concatenate([wd[:,t].reshape(256,128) for t in range(6)],1),NT)
        dp=(da*GP[:,cs]).astype(bf16)
        dpreo[:,cs]=dp
        ubo[:,cs]=colsum(dp.astype(f32))
        w=jnp.concatenate([Wu4[:,2*j+i].reshape(768,128) for i in range(2)],1)
        x2s[...]+=dot(dp,w,NT)
        return 0
    lax.fori_loop(0,12,hidb,0)
    dh2=x2s[...]
    n2,inv2=lnorm(x1s[...])
    vgo[2:3,:]=colsum(dh2*n2)
    vgo[3:4,:]=colsum(dh2)
    dx1=dsec[...]+lnorm_back(dh2,vrow(V,2),n2,inv2)
    dsec[...]=dx1
    da_=dx1.astype(bf16)
    dattno[...]=da_
    vgo[11:12,:]=colsum(da_.astype(f32))
    tiles=[]
    for j in range(6):
        w=jnp.concatenate([Wo4[8*j:8*j+8,t].reshape(128,128) for t in range(6)],1)
        tiles.append(dot(da_,w,NT).astype(bf16).astype(f32))
    for g,(p,c) in enumerate(gather_groups(tiles)):
        dog[g,pl.ds(0,TOK)]=p
        dog[g,pl.ds(TOK,CB)]=c
    def xd(d,_):
        xcopy(d).wait_send(); return 0
    lax.fori_loop(1,32,xd,0)

def middle(og,x0,G,wmap,vmask,scal,counts,sel,cid):
    return pl.pallas_call(mid_kernel,
        out_shape=(sds(TOK,DM),sds(TOK,DM),sds(TOK,FFW),sds(TOK,FFW),sds(TOK,DM),sds(TOK,DM),sds(TOK,DM,d=f32),sds(4,TOK+CB,128),
                   sds(16,DM,d=f32),sds(1,FFW,d=f32),sds(DM,128,d=f32),sds(192,16,128),sds(8,128,d=f32)),
        in_specs=[VM,VM,ANYS]+[VM]*5,out_specs=(VM,)*13,
        scratch_shapes=[vb(288,16,128),vb(1152,16,128),vb(1152,16,128),vb(192,16,128),vb(7,16,128),vf(112,128),vf(8,128),vf(TOK,FFW),vf(32,16,128),
            vf(TOK,DM),vf(TOK,DM),D((5,)),D((32,)),D((32,))],
        compiler_params=pltpu.CompilerParams(collective_id=cid,has_side_effects=True,vmem_limit_bytes=63*1024*1024))(og,x0,G,wmap,vmask,scal,counts,sel)

def back_kernel(start, fidx, dsp, G, x0, dsec, vg, ub, gmap, gproj, dqkv, dx0o, tailo, Wq, VE, V, TL, sems):
    cps=[pltpu.make_async_copy(G.at[pl.ds(576,864)],Wq,sems.at[0]),pltpu.make_async_copy(G.at[pl.ds(4512,7)],VE,sems.at[1])]
    for cp in cps: cp.start()
    for part in range(3):
        for j,t in enumerate(spread(lambda g: dsp[g,pl.ds(part*TOK,TOK)],lambda g: dsp[g,pl.ds(3*TOK+part*CB,CB)])):
            dqkv[:,(part*6+j)*128:(part*6+j+1)*128]=t
    def z(i,_):
        TL[pl.ds(i*64,64),:]=jnp.zeros((64,128),f32); return 0
    lax.fori_loop(0,96,z,0)
    for cp in cps: cp.wait()
    for i in range(7): V[pl.ds(i*16,16),:]=VE[i].astype(f32)
    W4=Wq.reshape(48,18,16,128)
    acc=jnp.zeros((TOK,DM),f32)
    for j in range(9):
        acc=acc+dot(dqkv[:,j*256:(j+1)*256],wcols(W4,2*j,2),NT)
    n,inv=lnorm(x0[...])
    ent=dsec[...]+lnorm_back(acc,vrow(V,0),n,inv)
    dx0o[...]=ent.astype(bf16)
    eb=colsum(ent)
    def rowput(i,v):
        for j in range(6): TL[pl.ds(i+j,1),:]=v[:,j*128:(j+1)*128]
    TL[0:48,:]=gmap[...]
    for j in range(6):
        TL[pl.ds(48+6*start[0]+j,TOK,stride=6),:]=ent[:,j*128:(j+1)*128]
    rowput(4224+6*fidx[0],eb)
    vec={0:colsum(acc*n),1:colsum(acc),8:eb,9:colsum(dqkv[:,0:DM].astype(f32)),10:colsum(dqkv[:,2*DM:].astype(f32))}
    for i in range(13):
        rowput(4608+6*i, vec[i] if i in vec else vg[i:i+1,:])
    for j in range(24): TL[4608+78+j:4608+79+j,:]=ub[:,j*128:(j+1)*128]
    def cg(i,_):
        tailo[pl.ds(i*8,8)]=gproj[pl.ds(i*8,8)]; return 0
    lax.fori_loop(0,24,cg,0)
    def ct(i,_):
        tailo[192+i]=TL[pl.ds(pl.multiple_of(i*16,16),16),:].astype(bf16); return 0
    lax.fori_loop(0,384,ct,0)

def back(start,fidx,dsp,G,x0,dsec,vg,ub,gmap,gproj):
    return pl.pallas_call(back_kernel,
        out_shape=(sds(TOK,3*DM),sds(TOK,DM),sds(576,16,128)),
        in_specs=[SM,SM,VM,ANYS]+[VM]*6,out_specs=(VM,)*3,
        scratch_shapes=[vb(864,16,128),vb(7,16,128),vf(112,128),vf(6144,128),D((2,))],
        compiler_params=pltpu.CompilerParams(vmem_limit_bytes=60*1024*1024))(start,fidx,dsp,G,x0,dsec,vg,ub,gmap,gproj)


SHARD = 289176
BLOCK = 294912
SLIDE = BLOCK - SHARD
CARRY = 32 * SLIDE
KEY_ORDER_C = 2


def to_tiles(matrix):
    rows, width = matrix.shape
    m = width // 128
    return matrix.reshape(rows // 16, 16, m, 128).transpose(0, 2, 1, 3).reshape(-1, 16, 128)


def block_to_tiles(flat, k):
    def of(width):
        return lambda v: to_tiles(v.reshape(-1, width))

    def split29(v):
        return jnp.concatenate([to_tiles(v[: 48 * 2048].reshape(-1, 512)), v[48 * 2048 :].reshape(-1, 16, 128)])

    branch = class_of(k)
    return lax.switch(branch, [of(768), of(2304), of(3072), of(512), split29, of(128)], flat)


def class_of(k):
    return jnp.where(
        k < 4, 0, jnp.where(k < 10, 1, jnp.where(k < 12, 0, jnp.where(k < 20, 2, jnp.where(k < 28, 0, jnp.where(k == 28, 3, jnp.where(k == 29, 4, 5))))))
    )


def local_4x8(
    pixels,
    res_class,
    valid_tubelet_count,
    positive,
    negatives,
    master,
    first_moment,
    second_moment,
    adam_step,
):
    D = HEAD_COUNT * HEAD_FEATURES
    both_axes = ("batch", "frame")
    bi = lax.axis_index("batch")
    fi = lax.axis_index("frame")
    k = bi * 8 + fi
    low = to_bfloat(master)
    nxt = lax.ppermute(low[:CARRY], both_axes, [(i + 1, i) for i in range(31)])
    block = lax.dynamic_slice(jnp.concatenate([low, nxt]), (SLIDE * k,), (BLOCK,))
    G = make_ag()(block_to_tiles(block, k), 0)
    flat_tiles = G.reshape(32 * 144, 16, 128)
    w_map = G[29, 48:51].reshape(D, NMAP).astype(jnp.float32)
    w_map = jnp.pad(w_map, ((0, 0), (0, 128 - NMAP)))
    tubelets = lax.dynamic_slice_in_dim(valid_tubelet_count, bi, 1, 0)
    patches = jnp.where(res_class == 0, P0, jnp.where(res_class == 1, P1, PATCHES_THIRD_2)).astype(jnp.int32)
    start_rows = jnp.where(res_class == 0, 0, jnp.where(res_class == 1, P0, P0 + P1)).astype(jnp.int32)
    frame = jnp.full((1,), fi, jnp.int32)
    pix = pixels.reshape(400, TUBELET_PIXELS)
    first_in, h1, sp = front(start_rows, frame, pix, flat_tiles)
    lims = jnp.concatenate([patches, tubelets])
    og, *saved_attn = attn_fwd(sp, lims, 2)
    total_count = jnp.sum(valid_tubelet_count).astype(jnp.float32)
    patch_mask = jnp.broadcast_to((jnp.arange(400, dtype=jnp.int32)[:, None] < patches[0]).astype(jnp.float32), (400, 128))
    slot_weight = (fi < tubelets[0]).astype(jnp.float32)
    scal = jnp.broadcast_to(
        jnp.concatenate([slot_weight[None], 1.0 / total_count[None], jnp.zeros((6,), jnp.float32)])[:, None], (8, 128)
    )
    counts = jnp.broadcast_to(
        jnp.concatenate([(NMAP * valid_tubelet_count).astype(jnp.float32), jnp.ones((4,), jnp.float32)])[:, None], (8, 128)
    )
    ids = jnp.concatenate([positive, negatives[0], jnp.full((3,), -1, jnp.int32)])
    chosen = (ids[:, None] == jnp.arange(128, dtype=jnp.int32)[None]).astype(jnp.float32)
    (attended, h2, hidden_low, g_pre, g_mlp, g_attn, g_second, dog, g_vec, g_up_bias, g_map, g_proj, loss_rows) = middle(
        og, first_in, flat_tiles, w_map, patch_mask, scal, counts, chosen, 4
    )
    loss_value = loss_rows[0, 0]
    dsp = attn_bwd(dog, saved_attn, 3)
    g_qkv, g_entry, tail_tiles = back(
        start_rows, frame, dsp, flat_tiles, first_in, g_second, g_vec, g_up_bias, g_map[:, :NMAP].reshape(48, 128), g_proj
    )
    grad, squares = make_rsx()(
        pix, h1, attended, h2, hidden_low, g_entry, g_qkv, g_attn, g_pre, g_mlp, tail_tiles.reshape(4, 144, 16, 128), cid=1
    )
    grad = grad.reshape(-1)[:SHARD]
    grad_norm = jnp.sqrt(jnp.sum(squares))
    clipped = grad * jnp.minimum(1.0, CLIP_AT / grad_norm)
    new_first = BETA_ONE * first_moment + (1.0 - BETA_ONE) * clipped
    new_second = BETA_TWO * second_moment + (1.0 - BETA_TWO) * clipped * clipped
    step = adam_step[0].astype(jnp.float32)
    update = new_first / (1.0 - BETA_ONE**step) / (jnp.sqrt(new_second / (1.0 - BETA_TWO**step)) + ADAM_EPS)
    new_master = master - RATE * (update + DECAY * master)
    return (new_master, new_first, new_second, to_bfloat(new_master), loss_value, grad_norm)


def solution(mesh):
    fast = dict(mesh.shape) == {"batch": 4, "frame": 8}
    return jax.shard_map(
        local_4x8 if fast else local_any_mesh,
        mesh=mesh,
        in_specs=(
            P("batch", "frame", None, None),
            P("batch"),
            P(),
            P("batch"),
            P("batch", None),
            P(("batch", "frame")),
            P(("batch", "frame")),
            P(("batch", "frame")),
            P(),
        ),
        out_specs=(
            P(("batch", "frame")),
            P(("batch", "frame")),
            P(("batch", "frame")),
            P(("batch", "frame")),
            P(),
            P(),
        ),
        check_vma=False,
    )
```

```python
from functools import partial
import math

import jax
import jax.numpy as jnp
from jax import lax
from jax.experimental import pallas as pl
from jax.experimental.pallas import tpu as pltpu
from jax.sharding import PartitionSpec as P

HEAD_COUNT = 12
HEAD_FEATURES = 64
FFW = 3072
TUBELET_PIXELS = 1536
EMB = 512
NMAP = 8
P0 = 100
P1 = 196
PATCHES_THIRD_2 = 400
TMAX = 64
NVEC = 13
CLIPS_PER_BATCH = 1


EPSILON = 1e-05
SOFTMAX_TEMPER = 0.02
DECAY_PENALTY = 1.0
CLIP_AT = 0.05
RATE = 0.03
DECAY = 0.05
BETA_ONE = 0.9
BETA_TWO = 0.999
ADAM_EPS = 1e-08
HIGH_ACCURACY = lax.Precision.HIGHEST


def to_bfloat(values):
    return values.astype(jnp.bfloat16)


def unpack_flat(flat_vector):
    width_of_model = HEAD_COUNT * HEAD_FEATURES
    dims_list = [
        (TUBELET_PIXELS, width_of_model),
        (width_of_model, 3 * width_of_model),
        (width_of_model, width_of_model),
        (width_of_model, FFW),
        (FFW, width_of_model),
        (width_of_model, EMB),
        (width_of_model, NMAP),
        (P0 + P1 + PATCHES_THIRD_2, width_of_model),
        (TMAX, width_of_model),
        (NVEC, width_of_model),
        (FFW,),
    ]
    pieces = []
    offset = 0
    for dims_of in dims_list:
        length = math.prod(dims_of)
        pieces.append(flat_vector[offset : offset + length].reshape(dims_of))
        offset += length
    return pieces


def norm_forward(inputs, gain_row, shift_row):
    center = inputs - jnp.mean(inputs, -1, keepdims=True)
    inverse = lax.rsqrt(jnp.mean(center * center, -1, keepdims=True) + EPSILON)
    normed = center * inverse
    return (normed * gain_row + shift_row, (normed, inverse))


def norm_backward(grad_out, gain_row, saved_parts):
    normed, inverse = saved_parts
    scaled = grad_out * gain_row
    grad_in = inverse * (
        scaled
        - jnp.mean(scaled, -1, keepdims=True)
        - normed * jnp.mean(scaled * normed, -1, keepdims=True)
    )
    lead_axes = tuple(range(grad_out.ndim - 1))
    return (grad_in, jnp.sum(grad_out * normed, lead_axes), jnp.sum(grad_out, lead_axes))


def block_plan(total_rows):
    shards = total_rows // PATCHES_THIRD_2
    group_size = 4
    return (shards // group_size, group_size * PATCHES_THIRD_2)


def local_any_mesh(
    pixels,
    res_class,
    valid_tubelet_count,
    positive,
    negatives,
    master,
    first_moment,
    second_moment,
    adam_step,
):
    width_of_model = HEAD_COUNT * HEAD_FEATURES
    score_scale = HEAD_FEATURES ** (-0.5)
    every_clip_rows = CLIPS_PER_BATCH * lax.axis_size("batch")
    index_of_batch = lax.axis_index("batch")
    frame_index = lax.axis_index("frame")
    gathered = lax.all_gather(to_bfloat(master), ("batch", "frame"), axis=0, tiled=True)
    w_embed, w_qkv, w_out, w_up, w_down, w_proj, w_map, pos_space, pos_time, vectors, bias_up = (
        unpack_flat(gathered)
    )
    vec_f = vectors.astype(jnp.float32)
    tubelet_stack = lax.dynamic_slice_in_dim(
        valid_tubelet_count, index_of_batch * CLIPS_PER_BATCH, CLIPS_PER_BATCH, 0
    )
    patches = jnp.where(res_class == 0, P0, jnp.where(res_class == 1, P1, PATCHES_THIRD_2)).astype(
        jnp.int32
    )
    start_rows = jnp.where(res_class == 0, 0, jnp.where(res_class == 1, P0, P0 + P1)).astype(
        jnp.int32
    )
    patch_pos = jnp.stack(
        [lax.dynamic_slice_in_dim(pos_space, start_rows[0], PATCHES_THIRD_2, 0)]
    ).astype(jnp.float32)
    time_row = lax.dynamic_slice_in_dim(pos_time, frame_index, 1, 0).astype(jnp.float32)
    rows_of_pixels = pixels.reshape(CLIPS_PER_BATCH * PATCHES_THIRD_2, TUBELET_PIXELS)
    embedded = jnp.dot(rows_of_pixels, w_embed, preferred_element_type=jnp.float32).reshape(
        CLIPS_PER_BATCH, PATCHES_THIRD_2, width_of_model
    )
    first_in = embedded + vec_f[8] + patch_pos + time_row
    normed_one, saved_one = norm_forward(first_in, vec_f[0], vec_f[1])
    normed_one = to_bfloat(normed_one)
    qkv_bias = jnp.concatenate([vec_f[9], jnp.zeros_like(vec_f[9]), vec_f[10]])
    projection_output = to_bfloat(
        jnp.einsum("cpd,de->cpe", normed_one, w_qkv, preferred_element_type=jnp.float32) + qkv_bias
    )
    query_matrix = projection_output[..., :width_of_model].reshape(
        CLIPS_PER_BATCH, PATCHES_THIRD_2, HEAD_COUNT, HEAD_FEATURES
    )
    kv_local = projection_output[..., width_of_model:]

    def key_mask(row_start, count_of_rows):
        row_ids = row_start + jnp.arange(count_of_rows, dtype=jnp.int32)
        return ((row_ids // PATCHES_THIRD_2)[None, :] < tubelet_stack[:, None]) & (
            (row_ids % PATCHES_THIRD_2)[None, :] < patches[:, None]
        )

    def block_scores(key_value_block, block_start):
        count_of_rows = key_value_block.shape[1]
        head_keys = key_value_block[..., :width_of_model].reshape(
            CLIPS_PER_BATCH, count_of_rows, HEAD_COUNT, HEAD_FEATURES
        )
        head_values = key_value_block[..., width_of_model:].reshape(
            CLIPS_PER_BATCH, count_of_rows, HEAD_COUNT, HEAD_FEATURES
        )
        key_ok = key_mask(block_start, count_of_rows)[:, None, None, :]
        scores = (
            jnp.einsum(
                "cqhd,ckhd->chqk", query_matrix, head_keys, preferred_element_type=jnp.float32
            )
            * score_scale
        )
        return (jnp.where(key_ok, scores, -1e30), key_ok, head_keys, head_values)

    forward_init = (
        jnp.full((CLIPS_PER_BATCH, HEAD_COUNT, PATCHES_THIRD_2), -1e30, jnp.float32),
        jnp.zeros((CLIPS_PER_BATCH, HEAD_COUNT, PATCHES_THIRD_2), jnp.float32),
        jnp.zeros((CLIPS_PER_BATCH, HEAD_COUNT, PATCHES_THIRD_2, HEAD_FEATURES), jnp.float32),
    )
    kv_piece = lax.all_gather(kv_local, "frame", axis=1, tiled=True)
    count_blocks, block_rows = block_plan(kv_piece.shape[1])

    def forward_one_block(block_index, running):
        run_max, run_sum, run_acc = running
        block_start = block_index * block_rows
        key_value_block = lax.dynamic_slice_in_dim(
            kv_piece, block_index * block_rows, block_rows, 1
        )
        scores, key_ok, head_keys, head_values = block_scores(key_value_block, block_start)
        new_max = jnp.maximum(run_max, jnp.max(scores, -1))
        factor = jnp.exp(run_max - new_max)
        prob_tile = jnp.where(key_ok, jnp.exp(scores - new_max[..., None]), 0.0)
        run_acc = run_acc * factor[..., None] + jnp.einsum(
            "chqk,ckhd->chqd", to_bfloat(prob_tile), head_values, preferred_element_type=jnp.float32
        )
        return (new_max, run_sum * factor + jnp.sum(prob_tile, -1), run_acc)

    run_max, run_sum, run_acc = lax.fori_loop(0, count_blocks, forward_one_block, forward_init)
    log_sum = run_max + jnp.log(run_sum)
    head_attended_rows = run_acc / run_sum[..., None]
    attended_reduced = to_bfloat(
        head_attended_rows.transpose(0, 2, 1, 3).reshape(
            CLIPS_PER_BATCH, PATCHES_THIRD_2, width_of_model
        )
    )
    second_in = (
        first_in
        + jnp.einsum("cpe,ed->cpd", attended_reduced, w_out, preferred_element_type=jnp.float32)
        + vec_f[11]
    )
    normed_two, saved_two = norm_forward(second_in, vec_f[2], vec_f[3])
    normed_two = to_bfloat(normed_two)
    hidden_pre = jnp.einsum(
        "cpd,df->cpf", normed_two, w_up, preferred_element_type=jnp.float32
    ) + bias_up.astype(jnp.float32)
    hidden_act, gelu_pull = jax.vjp(partial(jax.nn.gelu, approximate=False), hidden_pre)
    hidden_low = to_bfloat(hidden_act)
    block_out = (
        second_in
        + jnp.einsum("cpf,fd->cpd", hidden_low, w_down, preferred_element_type=jnp.float32)
        + vec_f[12]
    )
    valid_patch = jnp.arange(PATCHES_THIRD_2, dtype=jnp.int32)[None, :] < patches[:, None]
    slot_weight = (frame_index < tubelet_stack).astype(jnp.float32)

    def learner(block_in, gain_row, shift_row, map_weight):
        normed, unused = norm_forward(block_in, gain_row, shift_row)
        logits = jnp.einsum("cpd,dm->cpm", normed, map_weight, precision=HIGH_ACCURACY)
        logits = jnp.where(valid_patch[..., None], logits, -1e30)
        token_maps = jax.nn.softmax(logits, axis=1)
        pooled_part = jnp.einsum(
            "c,cpm,cpd->cd", slot_weight, token_maps, block_in, precision=HIGH_ACCURACY
        )
        gram_matrix = jnp.einsum("cpm,cpn->cmn", token_maps, token_maps, precision=HIGH_ACCURACY)
        correlation_part = slot_weight * (
            jnp.sum(gram_matrix, axis=(1, 2)) - jnp.trace(gram_matrix, axis1=1, axis2=2)
        )
        return (pooled_part, correlation_part)

    (pooled_part, correlation_part), learner_pull = jax.vjp(
        learner, block_out, vec_f[4], vec_f[5], w_map.astype(jnp.float32)
    )
    pooled_sum, correlation_sum = lax.psum((pooled_part, correlation_part), "frame")

    def head_map(pooled_in, gain_row, shift_row, proj_weight):
        pooled_mean = pooled_in / (NMAP * tubelet_stack).astype(jnp.float32)[:, None]
        normed, unused = norm_forward(pooled_mean, gain_row, shift_row)
        embedding = jnp.dot(
            normed, proj_weight, precision=HIGH_ACCURACY, preferred_element_type=jnp.float32
        )
        return embedding * lax.rsqrt(jnp.sum(embedding * embedding, -1, keepdims=True) + 1e-06)

    normalized_embedding, head_pull = jax.vjp(
        head_map, pooled_sum, vec_f[6], vec_f[7], w_proj.astype(jnp.float32)
    )
    embed_all, correlation_all = (
        lax.all_gather(normalized_embedding, "batch", axis=0, tiled=True),
        lax.all_gather(correlation_sum, "batch", axis=0, tiled=True),
    )
    selected_rows = jnp.concatenate([positive[:, None], negatives], axis=1)

    def contrast(embedding_input):
        local_row_set = lax.dynamic_slice_in_dim(
            embedding_input, index_of_batch * CLIPS_PER_BATCH, CLIPS_PER_BATCH, 0
        )
        similarity_matrix = (
            jnp.einsum(
                "yg,yeg->ye", local_row_set, embedding_input[selected_rows], precision=HIGH_ACCURACY
            )
            / SOFTMAX_TEMPER
        )
        return (
            jnp.sum(jax.nn.logsumexp(similarity_matrix, axis=1) - similarity_matrix[:, 0])
            / every_clip_rows
        )

    contrast_part, contrast_pull = jax.vjp(contrast, embed_all)
    (grad_embed_all,) = contrast_pull(jnp.ones_like(contrast_part))
    grad_unit = lax.psum_scatter(grad_embed_all, "batch", scatter_dimension=0, tiled=True)
    frame_total_count = jnp.sum(valid_tubelet_count).astype(jnp.float32)
    head_mask = (frame_index == 0).astype(jnp.float32)
    pooled_gradient, grad_final_gain, grad_final_shift, grad_proj = head_pull(grad_unit)
    grad_block, grad_learn_gain, grad_learn_shift, grad_map = learner_pull(
        (
            pooled_gradient,
            jnp.full((CLIPS_PER_BATCH,), DECAY_PENALTY / frame_total_count, jnp.float32),
        )
    )
    grad_mlp = to_bfloat(grad_block)
    grad_down_bias = jnp.sum(grad_mlp.astype(jnp.float32), (0, 1))
    grad_w_down = jnp.einsum(
        "cpf,cpd->fd", hidden_low, grad_mlp, preferred_element_type=jnp.float32
    )
    grad_hidden = jnp.einsum("cpd,fd->cpf", grad_mlp, w_down, preferred_element_type=jnp.float32)
    (grad_pre,) = gelu_pull(grad_hidden)
    grad_pre_low = to_bfloat(grad_pre)
    grad_up_bias = jnp.sum(grad_pre_low.astype(jnp.float32), (0, 1))
    grad_w_up = jnp.einsum(
        "cpd,cpf->df", normed_two, grad_pre_low, preferred_element_type=jnp.float32
    )
    grad_normed_two = jnp.einsum(
        "cpf,df->cpd", grad_pre_low, w_up, preferred_element_type=jnp.float32
    )
    grad_in_two, grad_gain_two, grad_shift_two = norm_backward(grad_normed_two, vec_f[2], saved_two)
    grad_second = grad_block + grad_in_two
    grad_attn = to_bfloat(grad_second)
    grad_out_bias = jnp.sum(grad_attn.astype(jnp.float32), (0, 1))
    grad_w_out = jnp.einsum(
        "cpe,cpd->ed", attended_reduced, grad_attn, preferred_element_type=jnp.float32
    )
    grad_attended = to_bfloat(
        jnp.einsum("cpd,ed->cpe", grad_attn, w_out, preferred_element_type=jnp.float32)
    ).reshape(CLIPS_PER_BATCH, PATCHES_THIRD_2, HEAD_COUNT, HEAD_FEATURES)
    row_delta = jnp.einsum("cqhd,chqd->chq", grad_attended.astype(jnp.float32), head_attended_rows)
    zeroed_query = jnp.zeros(
        (CLIPS_PER_BATCH, PATCHES_THIRD_2, HEAD_COUNT, HEAD_FEATURES), jnp.float32
    )
    query_kv_piece = lax.all_gather(kv_local, "frame", axis=1, tiled=True)
    count_blocks, query_block_rows = block_plan(query_kv_piece.shape[1])

    def query_one_block(block_index, query_gradient):
        block_start = block_index * query_block_rows
        key_value_block = lax.dynamic_slice_in_dim(
            query_kv_piece, block_index * query_block_rows, query_block_rows, 1
        )
        scores, key_ok, head_keys, head_values = block_scores(key_value_block, block_start)
        prob_tile = jnp.where(key_ok, jnp.exp(scores - log_sum[..., None]), 0.0)
        grad_prob = jnp.einsum(
            "cqhd,ckhd->chqk", grad_attended, head_values, preferred_element_type=jnp.float32
        )
        grad_score = to_bfloat(prob_tile * (grad_prob - row_delta[..., None]))
        return (
            query_gradient
            + jnp.einsum(
                "chqk,ckhd->cqhd", grad_score, head_keys, preferred_element_type=jnp.float32
            )
            * score_scale
        )

    query_gradient = lax.fori_loop(0, count_blocks, query_one_block, zeroed_query)
    own_keys = kv_local[..., :width_of_model].reshape(
        CLIPS_PER_BATCH, PATCHES_THIRD_2, HEAD_COUNT, HEAD_FEATURES
    )
    own_values = kv_local[..., width_of_model:].reshape(
        CLIPS_PER_BATCH, PATCHES_THIRD_2, HEAD_COUNT, HEAD_FEATURES
    )
    own_ok = key_mask(frame_index * PATCHES_THIRD_2, PATCHES_THIRD_2)[:, None, None, :]
    row_pieces = (
        query_matrix.astype(jnp.float32),
        grad_attended.astype(jnp.float32),
        log_sum.transpose(0, 2, 1),
        row_delta.transpose(0, 2, 1),
    )
    query_piece = lax.all_gather(
        row_pieces[0].astype(jnp.bfloat16), "frame", axis=1, tiled=True
    ).astype(jnp.float32)
    grad_out_piece = lax.all_gather(
        row_pieces[1].astype(jnp.bfloat16), "frame", axis=1, tiled=True
    ).astype(jnp.float32)
    lse_piece = lax.all_gather(
        row_pieces[2].astype(jnp.bfloat16), "frame", axis=1, tiled=True
    ).astype(jnp.float32)
    delta_piece = lax.all_gather(
        row_pieces[3].astype(jnp.bfloat16), "frame", axis=1, tiled=True
    ).astype(jnp.float32)
    count_blocks, own_block_rows = block_plan(query_piece.shape[1])

    def own_one_block(block_index, running):
        key_gradient, value_gradient = running
        offset = block_index * own_block_rows
        query_block = to_bfloat(lax.dynamic_slice_in_dim(query_piece, offset, own_block_rows, 1))
        grad_out_block = to_bfloat(
            lax.dynamic_slice_in_dim(grad_out_piece, offset, own_block_rows, 1)
        )
        lse_block = lax.dynamic_slice_in_dim(lse_piece, offset, own_block_rows, 1).transpose(
            0, 2, 1
        )
        delta_block = lax.dynamic_slice_in_dim(delta_piece, offset, own_block_rows, 1).transpose(
            0, 2, 1
        )
        scores = (
            jnp.einsum("cqhd,ckhd->chqk", query_block, own_keys, preferred_element_type=jnp.float32)
            * score_scale
        )
        scores = jnp.where(own_ok, scores, -1e30)
        prob_tile = jnp.where(own_ok, jnp.exp(scores - lse_block[..., None]), 0.0)
        grad_prob = jnp.einsum(
            "cqhd,ckhd->chqk", grad_out_block, own_values, preferred_element_type=jnp.float32
        )
        grad_score = to_bfloat(prob_tile * (grad_prob - delta_block[..., None]))
        key_gradient = (
            key_gradient
            + jnp.einsum(
                "chqk,cqhd->ckhd", grad_score, query_block, preferred_element_type=jnp.float32
            )
            * score_scale
        )
        value_gradient = value_gradient + jnp.einsum(
            "chqk,cqhd->ckhd",
            to_bfloat(prob_tile),
            grad_out_block,
            preferred_element_type=jnp.float32,
        )
        return (key_gradient, value_gradient)

    grad_key_own, grad_value_own = lax.fori_loop(
        0, count_blocks, own_one_block, (zeroed_query, zeroed_query)
    )
    gradient_key_value_local = to_bfloat(
        jnp.concatenate(
            [
                grad_key_own.reshape(CLIPS_PER_BATCH, PATCHES_THIRD_2, width_of_model),
                grad_value_own.reshape(CLIPS_PER_BATCH, PATCHES_THIRD_2, width_of_model),
            ],
            -1,
        )
    )
    gradient_query_key_value = jnp.concatenate(
        [
            to_bfloat(query_gradient).reshape(CLIPS_PER_BATCH, PATCHES_THIRD_2, width_of_model),
            gradient_key_value_local,
        ],
        -1,
    )
    grad_query_bias = jnp.sum(
        gradient_query_key_value[..., :width_of_model].astype(jnp.float32), (0, 1)
    )
    grad_value_bias = jnp.sum(
        gradient_query_key_value[..., 2 * width_of_model :].astype(jnp.float32), (0, 1)
    )
    grad_w_qkv = jnp.einsum(
        "cpd,cpe->de", normed_one, gradient_query_key_value, preferred_element_type=jnp.float32
    )
    grad_normed_one = jnp.einsum(
        "cpe,de->cpd", gradient_query_key_value, w_qkv, preferred_element_type=jnp.float32
    )
    grad_in_one, grad_gain_one, grad_shift_one = norm_backward(grad_normed_one, vec_f[0], saved_one)
    gradient_entry = grad_second + grad_in_one
    gradient_entry_low = to_bfloat(gradient_entry).reshape(
        CLIPS_PER_BATCH * PATCHES_THIRD_2, width_of_model
    )
    grad_w_embed = jnp.einsum(
        "rt,rd->td", rows_of_pixels, gradient_entry_low, preferred_element_type=jnp.float32
    )
    grad_embed_bias = jnp.sum(gradient_entry, (0, 1))
    grad_pos_space = jnp.zeros((P0 + P1 + PATCHES_THIRD_2, width_of_model), jnp.float32)
    current = lax.dynamic_slice_in_dim(grad_pos_space, start_rows[0], PATCHES_THIRD_2, 0)
    grad_pos_space = lax.dynamic_update_slice_in_dim(
        grad_pos_space, current + gradient_entry[0], start_rows[0], 0
    )
    grad_pos_time = lax.dynamic_update_slice_in_dim(
        jnp.zeros((TMAX, width_of_model), jnp.float32), grad_embed_bias[None], frame_index, 0
    )
    grad_vectors = jnp.stack(
        [
            grad_gain_one,
            grad_shift_one,
            grad_gain_two,
            grad_shift_two,
            grad_learn_gain,
            grad_learn_shift,
            grad_final_gain * head_mask,
            grad_final_shift * head_mask,
            grad_embed_bias,
            grad_query_bias,
            grad_value_bias,
            grad_out_bias,
            grad_down_bias,
        ]
    )
    flat_grad = jnp.concatenate(
        [
            piece_grad.reshape(-1)
            for piece_grad in (
                grad_w_embed,
                grad_w_qkv,
                grad_w_out,
                grad_w_up,
                grad_w_down,
                grad_proj * head_mask,
                grad_map,
                grad_pos_space,
                grad_pos_time,
                grad_vectors,
                grad_up_bias,
            )
        ]
    )
    grad_shard = lax.psum_scatter(flat_grad, ("batch", "frame"), scatter_dimension=0, tiled=True)
    contrast_keep = jnp.where(frame_index == 0, contrast_part, 0.0)
    square_sum, contrast_total = lax.psum(
        (jnp.sum(grad_shard * grad_shard), contrast_keep), ("batch", "frame")
    )
    grad_norm = jnp.sqrt(square_sum)
    loss_value = contrast_total + DECAY_PENALTY * jnp.sum(correlation_all) / frame_total_count
    clipped = grad_shard * jnp.minimum(1.0, CLIP_AT / grad_norm)
    new_first = BETA_ONE * first_moment + (1.0 - BETA_ONE) * clipped
    new_second = BETA_TWO * second_moment + (1.0 - BETA_TWO) * clipped * clipped
    step_count = adam_step[0].astype(jnp.float32)
    update = (
        new_first
        / (1.0 - BETA_ONE**step_count)
        / (jnp.sqrt(new_second / (1.0 - BETA_TWO**step_count)) + ADAM_EPS)
    )
    new_master = master - RATE * (update + DECAY * master)
    return (new_master, new_first, new_second, to_bfloat(new_master), loss_value, grad_norm)


MESH = pl.DeviceIdType.MESH
T=144
SPA=32

class Sends:
    def __init__(self, sem): self.sem=sem; self.n=0; self.items=[]
    def go(self, src, dst, rsem, dev, pred=None):
        c = pltpu.make_async_remote_copy(src_ref=src, dst_ref=dst, send_sem=self.sem.at[self.n], recv_sem=rsem, device_id=dev, device_id_type=MESH)
        self.n += 1
        if pred is None: c.start()
        else:
            @pl.when(pred)
            def _(): c.start()
        self.items.append((c,pred))
    def prep(self, src, dst, rsem, dev, pred=None):
        c = pltpu.make_async_remote_copy(src_ref=src, dst_ref=dst, send_sem=self.sem.at[self.n], recv_sem=rsem, device_id=dev, device_id_type=MESH)
        self.n += 1
        self.items.append((c,pred))
        def fire():
            if pred is None: c.start()
            else:
                @pl.when(pred)
                def _(): c.start()
        return fire
    def drain(self):
        for c,pred in self.items:
            if pred is None: c.wait_send()
            else:
                @pl.when(pred)
                def _(): c.wait_send()

def both(a,b):
    if a is None: return b
    if b is None: return a
    return jnp.logical_and(a,b)

def make_ag(spa=SPA):
    A=(0,spa); A1=(0,spa//2); A2=(spa//2,spa//2)
    nb=T-spa
    B=(spa,nb); B1=(spa,nb//2); B2=(spa+nb//2,nb//2)
    FULL=(0,T)
    def kernel(x_ref, out, ssem, lsem, zB, xB, yB, xBh, yBh, pA, zA, pown, pzB, pxB, pyB, pxBh, pyBh, ppA, pzA):
        b=lax.axis_index("batch"); f=lax.axis_index("frame")
        x=b%2; y=b//2; z=f//2; c=f%2
        bx=y*2+(1-x); by=(1-y)*2+x; bd=(1-y)*2+(1-x)
        X=(bx,f); Y=(by,f); Pn=(b,z*2+(1-c)); UP=(b,f+2); DN=(b,f-2)
        up=z<3; dn=z>0
        bar=pltpu.get_barrier_semaphore()
        for d,p in ((X,None),(Y,None),(Pn,None),(UP,up),(DN,dn)):
            if p is None: pl.semaphore_signal(bar,inc=1,device_id=d,device_id_type=MESH)
            else:
                @pl.when(p)
                def _(): pl.semaphore_signal(bar,inc=1,device_id=d,device_id_type=MESH)
        pl.semaphore_wait(bar, 4+(z*(3-z)+1)//3)
        S=Sends(ssem)
        def blk(bb,zz,part): return out.at[bb*8+zz*2+c, pl.ds(part[0],part[1])]
        def send(bb,zz,part,rsem,dev,pred=None,own=False):
            dst=blk(bb,zz,part)
            src=x_ref.at[pl.ds(part[0],part[1])] if own else dst
            S.go(src,dst,rsem,dev,pred)
        def wait(bb,zz,part,rsem):
            r=blk(bb,zz,part)
            pltpu.make_async_remote_copy(src_ref=r,dst_ref=r,send_sem=ssem.at[0],recv_sem=rsem,device_id=Pn,device_id_type=MESH).wait_recv()
        def waitp(pred,*a):
            if pred is None: wait(*a)
            else:
                @pl.when(pred)
                def _(): wait(*a)
        lc=pltpu.make_async_copy(x_ref, blk(b,z,FULL), lsem);
        send(b,z,A,pA.at[0],X,own=True); send(b,z,A,pA.at[1],Y,own=True)
        send(b,z,B,zB.at[z],UP,up,True); send(b,z,B,zB.at[z],DN,dn,True)
        send(b,z,B,xB.at[z],X,own=True); send(b,z,B,yB.at[z],Y,own=True)
        send(b,z,A,zA.at[z,0],UP,up,True); send(b,z,A,zA.at[z,0],DN,dn,True)
        send(b,z,FULL,pown.at[0],Pn,own=True)
        lc.start()
        pz=[]
        def pwait(*a): pz.append(a)
        pwait(None,b,z,FULL,pown.at[0])
        def zfwdA(bb,part,i,ps):
            send(bb,z,part,zA.at[z,i],UP,up); send(bb,z,part,zA.at[z,i],DN,dn)
            send(bb,z,part,ps,Pn); pwait(None,bb,z,part,ps)
        wait(bx,z,A,pA.at[0]); send(bx,z,A1,pA.at[2],Y); zfwdA(bx,A,1,ppA.at[0])
        wait(by,z,A,pA.at[1]); send(by,z,A2,pA.at[3],X); zfwdA(by,A,2,ppA.at[1])
        wait(bd,z,A1,pA.at[2]); zfwdA(bd,A1,3,ppA.at[2])
        wait(bd,z,A2,pA.at[3]); zfwdA(bd,A2,4,ppA.at[3])
        def xyB(zz,pred):
            waitp(pred,bx,zz,B,xB.at[zz]); send(bx,zz,B1,yBh.at[zz],Y,pred); send(bx,zz,B,pxB.at[zz],Pn,pred); pwait(pred,bx,zz,B,pxB.at[zz])
            waitp(pred,by,zz,B,yB.at[zz]); send(by,zz,B2,xBh.at[zz],X,pred); send(by,zz,B,pyB.at[zz],Pn,pred); pwait(pred,by,zz,B,pyB.at[zz])
        xyB(z,None)
        for d in (1,2,3):
            for s in (1,-1):
                zz=z+s*d
                pred=(zz<4) if s>0 else (zz>=0)
                nxt,np_=(DN,dn) if s>0 else (UP,up)
                waitp(pred,b,zz,B,zB.at[zz])
                send(b,zz,B,zB.at[zz],nxt,both(pred,np_))
                send(b,zz,B,xB.at[zz],X,pred); send(b,zz,B,yB.at[zz],Y,pred)
                send(b,zz,B,pzB.at[zz],Pn,pred); pwait(pred,b,zz,B,pzB.at[zz])
            for s in (1,-1):
                zz=z+s*d
                pred=(zz<4) if s>0 else (zz>=0)
                nxt,np_=(DN,dn) if s>0 else (UP,up)
                for i,(bb,part) in enumerate(((b,A),(bx,A),(by,A),(bd,A1),(bd,A2))):
                    waitp(pred,bb,zz,part,zA.at[zz,i]); send(bb,zz,part,zA.at[zz,i],nxt,both(pred,np_))
                    send(bb,zz,part,pzA.at[zz,i],Pn,pred); pwait(pred,bb,zz,part,pzA.at[zz,i])
            for s in (1,-1):
                zz=z+s*d
                pred=(zz<4) if s>0 else (zz>=0)
                xyB(zz,pred)
        for zz in range(4):
            wait(bd,zz,B1,yBh.at[zz]); send(bd,zz,B1,pyBh.at[zz],Pn); pwait(None,bd,zz,B1,pyBh.at[zz])
            wait(bd,zz,B2,xBh.at[zz]); send(bd,zz,B2,pxBh.at[zz],Pn); pwait(None,bd,zz,B2,pxBh.at[zz])
        for a in pz: waitp(*a)
        lc.wait()
        S.drain()
    D=pltpu.SemaphoreType.DMA
    def ag(xin, cid=0):
        return pl.pallas_call(kernel, out_shape=jax.ShapeDtypeStruct((32,T,16,128),jnp.bfloat16),
            in_specs=[pl.BlockSpec(memory_space=pltpu.VMEM)], out_specs=pl.BlockSpec(memory_space=pl.ANY),
            scratch_shapes=[D((160,)),D]+[D((4,))]*5+[D((4,)),D((4,5)),D((1,))]+[D((4,))]*5+[D((4,)),D((4,5))],
            compiler_params=pltpu.CompilerParams(collective_id=cid,has_side_effects=True))(xin)
    return ag


def make_rsx(spa=16):
    nb=T-spa
    A=(0,spa); A1=(0,spa//2); A2=(spa//2,spa//2)
    B=(spa,nb); B1=(spa,nb//2); B2=(spa+nb//2,nb//2)
    FULL=(0,T)
    def kernel(pix, h1, att, h2, act, dx0, dqkv, dattn, dpre, dmlp, tail, gout, nout,
               PS, R, h2T, LX, LY, LHX, LHY, LZB, LZA, LPA, out, C, CB_, CR_, NB, ssem, psem, stsem, csem, nsem, nsend, s_hx, s_hy, s_x, s_y, s_zb, s_za, s_pa):
        b=lax.axis_index("batch"); f=lax.axis_index("frame")
        x=b%2; y=b//2; z=f//2; c=f%2
        bx=y*2+(1-x); by=(1-y)*2+x; bd=(1-y)*2+(1-x)
        X=(bx,f); Y=(by,f); Pn=(b,z*2+(1-c)); UP=(b,f+2); DN=(b,f-2)
        up=z<3; dn=z>0
        t=z//2
        k=b*8+f
        def dev_of(kk): return (kk//8,kk%8)
        bar=pltpu.get_barrier_semaphore()
        def greet(d,_):
            pl.semaphore_signal(bar,inc=1,device_id=dev_of((k+d)%32),device_id_type=MESH); return 0
        lax.fori_loop(1,32,greet,0)
        zo=[3*(1-t), 2-t, (1-z)*(1-t)+(5-z)*t, z]
        order=[]
        for zz in zo: order += [(bd,zz)]
        for zz in zo: order += [(bx,zz),(by,zz)]
        for zz in zo: order += [(b,zz)]
        h2T[...]=h2[...].T
        TN_=(((0,),(0,)),((),()))
        def put(dst,r,m):
            rows=r.shape[0]
            r=r.astype(jnp.bfloat16)
            for s in range(rows//16):
                for j in range(m):
                    dst[s*m+j]=r[s*16:(s+1)*16,j*128:(j+1)*128]
        def col(a,i,n): return a[:,pl.ds(pl.multiple_of(i*n,128),n)]
        def comp(kk,dst):
            def mm(a,bb_,dims): return lax.dot_general(a,bb_,dims,preferred_element_type=jnp.float32)
            @pl.when(kk<4)
            def _(): put(dst,mm(col(pix,kk,384),dx0[...],TN_),6)
            @pl.when(jnp.logical_and(kk>=4,kk<10))
            def _(): put(dst,mm(col(h1,kk-4,128),dqkv[...],TN_),18)
            @pl.when(jnp.logical_and(kk>=10,kk<12))
            def _(): put(dst,mm(col(att,kk-10,384),dattn[...],TN_),6)
            @pl.when(jnp.logical_and(kk>=12,kk<20))
            def _(): put(dst,mm(h2T[pl.ds(pl.multiple_of((kk-12)*96,16),96)],dpre[...],(((1,),(0,)),((),()))),24)
            @pl.when(jnp.logical_and(kk>=20,kk<28))
            def _(): put(dst,mm(col(act,kk-20,384),dmlp[...],TN_),6)
            @pl.when(kk>=28)
            def _():
                def cp(i,_):
                    ds=pl.ds(i*8,8); dst[ds]=tail[kk-28,ds]; return 0
                lax.fori_loop(0,T//8,cp,0)
        def pick(i):
            g=jnp.where(i<4,i,jnp.where(i<12,(i-4)//2,i-12))
            zz=jnp.where(g==0,zo[0],jnp.where(g==1,zo[1],jnp.where(g==2,zo[2],zo[3])))
            bb=jnp.where(i<4,bd,jnp.where(i<12,jnp.where(i%2==0,bx,by),b))
            return bb,zz
        def pcopy(i):
            bb,zz=pick(i)
            return pltpu.make_async_remote_copy(src_ref=PS.at[16+i%4],dst_ref=R.at[bb,zz],send_sem=stsem.at[i%4],recv_sem=psem.at[bb,zz],device_id=Pn,device_id_type=MESH)
        S=Sends(ssem)
        def acc(dst, srcs, n, step=8):
            def body(i,_):
                ds=pl.ds(i*step,step)
                v=srcs[0][ds].astype(jnp.float32)
                for s in srcs[1:]: v=v+s[ds].astype(jnp.float32)
                dst[ds]=v.astype(dst.dtype)
                return 0
            lax.fori_loop(0,n//step,body,0)
        def sub(ref,part): return ref.at[pl.ds(part[0],part[1])]
        def ready(i):
            bb,zz=order[i]
            pltpu.make_async_remote_copy(src_ref=R.at[bb,zz],dst_ref=R.at[bb,zz],send_sem=ssem.at[0],recv_sem=psem.at[bb,zz],device_id=Pn,device_id_type=MESH).wait_recv()
        def wrecv(ref,sem):
            pltpu.make_async_remote_copy(src_ref=ref,dst_ref=ref,send_sem=ssem.at[0],recv_sem=sem,device_id=Pn,device_id_type=MESH).wait_recv()
        plan={}
        def at(h,fn): plan.setdefault(h,[]).append(fn)
        def diag(i,zz):
            f1=S.prep(sub(PS.at[bd*4+zz],B1), LHY.at[zz], s_hy.at[zz], Y)
            f2=S.prep(sub(PS.at[bd*4+zz],B2), LHX.at[zz], s_hx.at[zz], X)
            def fn():
                ready(i)
                acc(sub(PS.at[bd*4+zz],B), [sub(PS.at[bd*4+zz],B), sub(R.at[bd,zz],B)], nb)
                f1(); f2()
            return fn
        def chainA(bi,bb,ds=(3,2,1)):
            fns=[]
            for d in ds:
                for s in (1,-1):
                    zz=z+s*d
                    pred=(zz<4) if s>0 else (zz>=0)
                    frm=dn if s>0 else up
                    dev=UP if s>0 else DN
                    di=0 if s>0 else 1
                    fire=S.prep(sub(PS.at[bb*4+zz],A), LZA.at[di,zz,bi], s_za.at[di,zz,bi], dev, pred)
                    def fn(zz=zz,pred=pred,frm=frm,di=di,fire=fire):
                        @pl.when(jnp.logical_and(pred,frm))
                        def _():
                            wrecv(LZA.at[di,zz,bi], s_za.at[di,zz,bi])
                            acc(sub(PS.at[bb*4+zz],A),[sub(PS.at[bb*4+zz],A),sub(R.at[bb,zz],A),LZA.at[di,zz,bi]],spa)
                        @pl.when(jnp.logical_and(pred,jnp.logical_not(frm)))
                        def _():
                            acc(sub(PS.at[bb*4+zz],A),[sub(PS.at[bb*4+zz],A),sub(R.at[bb,zz],A)],spa)
                        fire()
                    fns.append(fn)
            return fns
        def sides(i,zz):
            fx=S.prep(sub(PS.at[bx*4+zz],B), LX.at[zz], s_x.at[zz], X)
            fy=S.prep(sub(PS.at[by*4+zz],B), LY.at[zz], s_y.at[zz], Y)
            def fn():
                ready(4+2*i); ready(5+2*i)
                wrecv(LHY.at[zz], s_hy.at[zz])
                acc(sub(PS.at[bx*4+zz],B1),[sub(PS.at[bx*4+zz],B1),sub(R.at[bx,zz],B1),LHY.at[zz]],nb//2)
                acc(sub(PS.at[bx*4+zz],B2),[sub(PS.at[bx*4+zz],B2),sub(R.at[bx,zz],B2)],nb//2)
                fx()
                wrecv(LHX.at[zz], s_hx.at[zz])
                acc(sub(PS.at[by*4+zz],B2),[sub(PS.at[by*4+zz],B2),sub(R.at[by,zz],B2),LHX.at[zz]],nb//2)
                acc(sub(PS.at[by*4+zz],B1),[sub(PS.at[by*4+zz],B1),sub(R.at[by,zz],B1)],nb//2)
                fy()
            return fn
        for i,zz in enumerate(zo): at(2*i+3,diag(i,zz))
        for j,d in enumerate((3,2,1)):
            for fn in chainA(0,bd,(d,)): at(10+2*j,fn)
        for i,zz in enumerate(zo): at(13+4*i,sides(i,zz))
        for bi,bb in ((1,bx),(2,by)):
            for j,d in enumerate((3,2,1)):
                for fn in chainA(bi,bb,(d,)): at(26+2*j,fn)
        def produce(h,_):
            i=h//2; own=h%2
            bb,zz=pick(i)
            @pl.when(own==0)
            def _():
                @pl.when(i>=4)
                def _(): pcopy(i-4).wait_send()
            kk=bb*8+zz*2+jnp.where(own==1,c,1-c)
            comp(kk,PS.at[jnp.where(own==1,bb*4+zz,16+i%4)])
            @pl.when(own==0)
            def _():
                @pl.when(i==0)
                def _(): pl.semaphore_wait(bar,31)
                pcopy(i).start()
            for hh,fns in sorted(plan.items()):
                @pl.when(h==hh)
                def _():
                    for fn in fns: fn()
            return 0
        lax.fori_loop(0,32,produce,0)
        for i in range(4): ready(12+i)
        for fn in chainA(3,b): fn()
        for i,zz in enumerate(zo[:3]):
            wrecv(LX.at[zz],s_x.at[zz]); wrecv(LY.at[zz],s_y.at[zz])
            isup=zz>z
            inc=jnp.logical_or(jnp.logical_and(isup,dn),jnp.logical_and(jnp.logical_not(isup),up))
            di=jnp.where(isup,0,1)
            base=[sub(PS.at[b*4+zz],B),sub(R.at[b,zz],B),LX.at[zz],LY.at[zz]]
            @pl.when(inc)
            def _():
                wrecv(LZB.at[di,zz],s_zb.at[di,zz])
                acc(sub(PS.at[b*4+zz],B),base+[LZB.at[di,zz]],nb)
            @pl.when(jnp.logical_not(inc))
            def _(): acc(sub(PS.at[b*4+zz],B),base,nb)
            S.go(sub(PS.at[b*4+zz],B),LZB.at[0,zz],s_zb.at[0,zz],UP,isup)
            S.go(sub(PS.at[b*4+zz],B),LZB.at[1,zz],s_zb.at[1,zz],DN,jnp.logical_not(isup))
        def totA(bi,bb,part,extra=(),dst=None):
            dst = dst if dst is not None else sub(PS.at[bb*4+z],part)
            srcs=[sub(PS.at[bb*4+z],part),sub(R.at[bb,z],part)]+list(extra)
            o=part[0]; n=part[1]
            l0=LZA.at[0,z,bi,pl.ds(o,n)]; l1=LZA.at[1,z,bi,pl.ds(o,n)]
            @pl.when(jnp.logical_and(up,dn))
            def _(): acc(dst,srcs+[l0,l1],n)
            @pl.when(jnp.logical_not(up))
            def _(): acc(dst,srcs+[l0],n)
            @pl.when(jnp.logical_not(dn))
            def _(): acc(dst,srcs+[l1],n)
        for bi in range(4):
            @pl.when(dn)
            def _(): wrecv(LZA.at[0,z,bi],s_za.at[0,z,bi])
            @pl.when(up)
            def _(): wrecv(LZA.at[1,z,bi],s_za.at[1,z,bi])
            if bi==0:
                totA(0,bd,A1); S.go(sub(PS.at[bd*4+z],A1),LPA.at[0,pl.ds(0,spa//2)],s_pa.at[0],Y)
                totA(0,bd,A2); S.go(sub(PS.at[bd*4+z],A2),LPA.at[1,pl.ds(0,spa//2)],s_pa.at[1],X)
            if bi==1:
                totA(1,bx,A2)
                wrecv(LPA.at[0,pl.ds(0,spa//2)],s_pa.at[0])
                totA(1,bx,A1,[LPA.at[0,pl.ds(0,spa//2)]])
                S.go(sub(PS.at[bx*4+z],A),LPA.at[2],s_pa.at[2],X)
            if bi==2:
                totA(2,by,A1)
                wrecv(LPA.at[1,pl.ds(0,spa//2)],s_pa.at[1])
                totA(2,by,A2,[LPA.at[1,pl.ds(0,spa//2)]])
                S.go(sub(PS.at[by*4+z],A),LPA.at[3],s_pa.at[3],Y)
        wrecv(LX.at[z],s_x.at[z]); wrecv(LY.at[z],s_y.at[z])
        base=[sub(PS.at[b*4+z],B),sub(R.at[b,z],B),LX.at[z],LY.at[z]]
        @pl.when(dn)
        def _(): wrecv(LZB.at[0,z],s_zb.at[0,z])
        @pl.when(up)
        def _(): wrecv(LZB.at[1,z],s_zb.at[1,z])
        @pl.when(jnp.logical_and(up,dn))
        def _(): acc(sub(out,B),base+[LZB.at[0,z],LZB.at[1,z]],nb)
        @pl.when(jnp.logical_not(up))
        def _(): acc(sub(out,B),base+[LZB.at[0,z]],nb)
        @pl.when(jnp.logical_not(dn))
        def _(): acc(sub(out,B),base+[LZB.at[1,z]],nb)
        wrecv(LPA.at[2],s_pa.at[2]); wrecv(LPA.at[3],s_pa.at[3])
        totA(3,b,A,[LPA.at[2],LPA.at[3]],dst=sub(out,A))
        def sq(i,a):
            v=out[i]; v=v*v
            return a+v[:8]+v[8:]
        NB[k]=lax.fori_loop(0,T,sq,jnp.zeros((8,128),jnp.float32))
        def ncopy(d):
            return pltpu.make_async_remote_copy(src_ref=NB.at[k],dst_ref=NB.at[k],send_sem=nsend.at[d],recv_sem=nsem.at[k],device_id=dev_of((k+d)%32),device_id_type=MESH)
        def nstart(d,_):
            ncopy(d).start(); return 0
        lax.fori_loop(1,32,nstart,0)
        CR=1440
        def untile(m,s0,n,t0):
            def body(s,_):
                for j in range(m):
                    C[pl.ds(CR+s0+s*16*m+j,16,stride=m),:]=out[t0+s*m+j]
                return 0
            lax.fori_loop(0,n,body,0)
        def plain(t0,n):
            def body(s,_):
                C[pl.ds(CR+(t0+s)*16,16),:]=out[t0+s]; return 0
            lax.fori_loop(0,n,body,0)
        def within(lo,hi): return jnp.logical_and(k>=lo,k<hi)
        @pl.when(jnp.logical_or(jnp.logical_or(within(0,4),within(10,12)),within(20,28)))
        def _(): untile(6,0,24,0)
        @pl.when(within(4,10))
        def _(): untile(18,0,8,0)
        @pl.when(within(12,20))
        def _(): untile(24,0,6,0)
        @pl.when(k==28)
        def _(): untile(4,0,36,0)
        @pl.when(k==29)
        def _():
            untile(4,0,12,0); plain(48,96)
        @pl.when(k>=30)
        def _(): plain(0,T)
        def carry(i,_):
            CB_[pl.ds(i*96,96)]=C[pl.ds(2304+i*96,96),:].astype(jnp.bfloat16); return 0
        lax.fori_loop(0,CR//96,carry,0)
        def cdesc(): return pltpu.make_async_remote_copy(src_ref=CB_,dst_ref=CR_,send_sem=csem.at[0],recv_sem=csem.at[1],device_id=dev_of((k+1)%32),device_id_type=MESH)
        @pl.when(k<31)
        def _(): cdesc().start()
        C[pl.ds(CR+2304,8),:]=jnp.zeros((8,128),jnp.float32)
        def nwait(d,_):
            kk=(k+d)%32
            wrecv_(NB.at[kk],nsem.at[kk],nsend.at[0],Pn); return 0
        lax.fori_loop(1,32,nwait,0)
        def nsum(i,a): return a+NB[i]
        nout[...]=lax.fori_loop(0,32,nsum,jnp.zeros((8,128),jnp.float32))
        @pl.when(k>0)
        def _():
            wrecv_(CR_,csem.at[1],csem.at[0],Pn)
            def uncarry(i,_):
                C[pl.ds(i*96,96),:]=CR_[pl.ds(i*96,96)].astype(jnp.float32); return 0
            lax.fori_loop(0,CR//96,uncarry,0)
        e=CR*128-(294912-289176)*k
        q=e//128; sh=e%128
        lane=lax.broadcasted_iota(jnp.int32,(96,128),1)
        def slide(i,_):
            r0=q+i*96
            a=pltpu.roll(C[pl.ds(r0,96),:],(128-sh)%128,1); b_=pltpu.roll(C[pl.ds(r0+1,96),:],(128-sh)%128,1)
            gout[pl.ds(i*96,96),:]=jnp.where(lane<128-sh,a,b_)
            return 0
        lax.fori_loop(0,24,slide,0)
        @pl.when(k<31)
        def _(): cdesc().wait_send()
        def ndone(d,_):
            ncopy(d).wait_send(); return 0
        lax.fori_loop(1,32,ndone,0)
        for i in range(12,16): pcopy(i).wait_send()
        S.drain()
    D=pltpu.SemaphoreType.DMA
    V=lambda *s: pltpu.VMEM(s+(16,128),jnp.bfloat16)
    VMs=pl.BlockSpec(memory_space=pltpu.VMEM)
    def rs(*args, cid=1):
        return pl.pallas_call(kernel, out_shape=(jax.ShapeDtypeStruct((2304,128),jnp.float32),jax.ShapeDtypeStruct((8,128),jnp.float32)),
            in_specs=[VMs]*11, out_specs=(VMs,VMs),
            scratch_shapes=[V(20,T),V(4,4,T),pltpu.VMEM((768,400),jnp.bfloat16),V(4,nb),V(4,nb),V(4,nb//2),V(4,nb//2),V(2,4,nb),V(2,4,4,spa),V(4,spa),
              pltpu.VMEM((T,16,128),jnp.float32),pltpu.VMEM((3752,128),jnp.float32),pltpu.VMEM((1440,128),jnp.bfloat16),pltpu.VMEM((1440,128),jnp.bfloat16),pltpu.VMEM((32,8,128),jnp.float32),
              D((80,)),D((4,4)),D((4,)),D((2,)),D((32,)),D((32,)),D((4,)),D((4,)),D((4,)),D((4,)),D((2,4)),D((2,4,4)),D((4,))],
            compiler_params=pltpu.CompilerParams(collective_id=cid,has_side_effects=True,vmem_limit_bytes=63*1024*1024))(*args)
    return rs

def wrecv_(ref,sem,ssem,dev):
    pltpu.make_async_remote_copy(src_ref=ref,dst_ref=ref,send_sem=ssem,recv_sem=sem,device_id=dev,device_id_type=MESH).wait_recv()


TOK=400; CB=208; NK=3200; NQ=1600; SUB=80; PADQ=512; CH=640
ROWS={"q":0,"k":400,"v":800,"qc":1200,"kc":1408,"vc":1616}
NT=(((1,),(1,)),((),())); NN=(((1,),(0,)),((),())); TN=(((0,),(0,)),((),()))
f32=jnp.float32; bf16=jnp.bfloat16

def dot(a,b,dims): return lax.dot_general(a,b,dims,preferred_element_type=f32)

def mesh_pos():
    b=lax.axis_index("batch"); f=lax.axis_index("frame")
    return b,f//2,f%2

def zbarrier(b,z,c):
    bar=pltpu.get_barrier_semaphore()
    for d in (1,2,3):
        pl.semaphore_signal(bar,inc=1,device_id=(b,((z+d)%4)*2+c),device_id_type=MESH)
    pl.semaphore_signal(bar,inc=1,device_id=(b,z*2+1-c),device_id_type=MESH)
    pl.semaphore_wait(bar,4)

def wrecv(ref,sem,dev):
    pltpu.make_async_remote_copy(src_ref=ref,dst_ref=ref,send_sem=sem,recv_sem=sem,device_id=dev,device_id_type=MESH).wait_recv()

def others(z):
    return [((z+d)%4) for d in (2,1,3)]

def unpack_c(src, dst, row):
    v=src.astype(f32)
    lane=lax.broadcasted_iota(jnp.int32,(CB,128),1)
    lo=jnp.where(lane<64,v,0.0)
    hi=jnp.where(lane<64,pltpu.roll(v,64,1),0.0)
    dst[pl.ds(row,CB)]=lo.astype(bf16)
    dst[pl.ds(row+CB,TOK-CB)]=hi[:TOK-CB].astype(bf16)

def pack_c(lo, hi):
    hi=jnp.concatenate([hi,jnp.zeros((2*CB-TOK,128),f32)],0)
    lane=lax.broadcasted_iota(jnp.int32,(CB,128),1)
    return jnp.where(lane<64,lo,pltpu.roll(hi,64,1)).astype(bf16)

def key_lanes(v, free, ok):
    e=lax.broadcasted_iota(jnp.int32,v.shape,1)-free
    v=jnp.where(jnp.logical_and(e>=1,e<4),1.0,v)
    return jnp.where(e==0,jnp.where(ok,0.0,-1e30),v)

def value_lanes(v, free):
    e=lax.broadcasted_iota(jnp.int32,v.shape,1)-free
    return jnp.where(jnp.logical_and(e>=0,e<3),1.0,v)

def three_lanes(v, free, col):
    hi=col.astype(bf16).astype(f32); mid=(col-hi).astype(bf16).astype(f32); lo=col-hi-mid
    e=lax.broadcasted_iota(jnp.int32,v.shape,1)-free
    return jnp.where(e==0,hi,jnp.where(e==1,mid,jnp.where(e==2,lo,v)))

def one_lane(v, free):
    e=lax.broadcasted_iota(jnp.int32,v.shape,1)-free
    return jnp.where(e==0,1.0,v)

def fwd_kernel(lims, sp, og, Q, KA, KB, VA, VB, QC, KC, VC, OA, OC, LA, LC,
               K, V, QCp, KCp, VCp, OB, OCp, S, Pb, ssem, lsem, osem, rq, rk, rv, rqc, rkc, rvc, pk, pv, pkc, pvc, ro, roc):
    b,z,c=mesh_pos()
    Pn=(b,z*2+1-c)
    dev=lambda zz:(b,zz*2+c)
    row=lambda zz: pl.multiple_of(zz*TOK,16)
    krow=lambda zz: pl.multiple_of((c*4+zz)*TOK,16)
    pkrow=lambda zz: pl.multiple_of(((1-c)*4+zz)*TOK,16)
    zbarrier(b,z,c)
    X=Sends(ssem)
    part=lambda g,n,ln: sp.at[g,pl.ds(ROWS[n],ln)]
    loc=[]
    def lcopy(src,dst):
        cp=pltpu.make_async_copy(src,dst,lsem.at[len(loc)]); cp.start(); loc.append(cp)
    for zz in others(z):
        X.go(part(zz,"kc",CB),KCp.at[c*4+z],rkc.at[z],dev(zz))
        X.go(part(zz,"qc",CB),QCp.at[z],rqc.at[z],dev(zz))
        X.go(part(zz,"vc",CB),VCp.at[c*4+z],rvc.at[z],dev(zz))
    lcopy(part(z,"kc",CB),KCp.at[c*4+z]); lcopy(part(z,"qc",CB),QCp.at[z]); lcopy(part(z,"vc",CB),VCp.at[c*4+z])
    X.go(part(z,"kc",CB),KCp.at[c*4+z],pkc.at[z],Pn)
    X.go(part(z,"vc",CB),VCp.at[c*4+z],pvc.at[z],Pn)
    for zz in others(z):
        X.go(part(zz,"k",TOK),K.at[pl.ds(krow(z),TOK)],rk.at[z],dev(zz))
        X.go(part(zz,"v",TOK),V.at[pl.ds(krow(z),TOK)],rv.at[z],dev(zz))
        X.go(part(zz,"q",TOK),Q.at[pl.ds(row(z),TOK)],rq.at[z],dev(zz))
    lcopy(part(z,"k",TOK),K.at[pl.ds(krow(z),TOK)])
    lcopy(part(z,"q",TOK),Q.at[pl.ds(row(z),TOK)])
    lcopy(part(z,"v",TOK),V.at[pl.ds(krow(z),TOK)])
    X.go(part(z,"k",TOK),K.at[pl.ds(krow(z),TOK)],pk.at[z],Pn)
    X.go(part(z,"v",TOK),V.at[pl.ds(krow(z),TOK)],pv.at[z],Pn)
    lane=lax.broadcasted_iota(jnp.int32,(TOK,128),1)
    patch=lax.broadcasted_iota(jnp.int32,(TOK,128),0)
    def key_ok(i):
        return patch<jnp.where((i%4)*2+i//4<lims[1],lims[0],0)
    def widen(i,_):
        ds=pl.ds(pl.multiple_of(i*TOK,16),TOK)
        ok=key_ok(i)
        kk=K[ds].astype(f32); vv=V[ds].astype(f32)
        ka=jnp.where(lane<64,kk,0.0); va=jnp.where(lane<64,vv,0.0)
        KA[ds]=key_lanes(ka,64,ok).astype(bf16); KB[ds]=key_lanes(kk-ka,0,ok).astype(bf16)
        VA[ds]=value_lanes(va,64).astype(bf16); VB[ds]=value_lanes(vv-va,0).astype(bf16)
        return 0
    def softmax(slot):
        def sub(i,carry):
            ds=pl.ds(pl.multiple_of(i*SUB,16),SUB)
            m=jnp.max(S[slot,ds,:],-1,keepdims=True)
            Pb[slot,ds,:]=jnp.exp(S[slot,ds,:]-m).astype(bf16)
            return m
        return jnp.concatenate([sub(i,0) for i in range(TOK//SUB)],0)
    for zz in [((z+d)%4) for d in (1,3,2)]:
        kr=KCp.at[c*4+zz]; vr=VCp.at[c*4+zz]
        wrecv(kr,rkc.at[zz],Pn); X.go(kr,kr,pkc.at[zz],Pn)
        wrecv(vr,rvc.at[zz],Pn); X.go(vr,vr,pvc.at[zz],Pn)
        wrecv(QCp.at[zz],rqc.at[zz],Pn)
    for cp in loc[:3]: cp.wait()
    for zz in range(4):
        wrecv(KCp.at[(1-c)*4+zz],pkc.at[zz],Pn); wrecv(VCp.at[(1-c)*4+zz],pvc.at[zz],Pn)
    def unp(i,_):
        r=pl.multiple_of(i*TOK,16)
        unpack_c(KCp[i],KC,r); unpack_c(VCp[i],VC,r)
        ds=pl.ds(r,TOK)
        KC[ds]=key_lanes(KC[ds].astype(f32),64,key_ok(i)).astype(bf16)
        VC[ds]=value_lanes(VC[ds].astype(f32),64).astype(bf16)
        return 0
    lax.fori_loop(0,8,unp,0)
    def unq(i,_):
        unpack_c(QCp[i],QC,pl.multiple_of(i*TOK,16)); return 0
    lax.fori_loop(0,4,unq,0)
    def cblock(i,_):
        ds=pl.ds(pl.multiple_of(i*TOK,16),TOK)
        S[0]=dot(one_lane(QC[ds].astype(f32),64).astype(bf16),KC[...],NT)
        ma=softmax(0)
        o=dot(Pb[0],VC[...],NN)
        la=o[:,64:65]
        o=o/la
        OC[ds]=o
        LC[ds]=jnp.broadcast_to(ma+jnp.log(la),(TOK,128))
        OCp[i]=pack_c(o[:CB],o[CB:])
        return 0
    lax.fori_loop(0,4,cblock,0)
    for zz in others(z):
        X.go(OCp.at[zz],og.at[z,pl.ds(TOK,CB)],roc.at[z],dev(zz))
    lc=pltpu.make_async_copy(OCp.at[z],og.at[z,pl.ds(TOK,CB)],lsem.at[7]); lc.start()
    for zz in [((z+d)%4) for d in (1,3,2)]:
        kr=K.at[pl.ds(krow(zz),TOK)]; vr=V.at[pl.ds(krow(zz),TOK)]
        wrecv(kr,rk.at[zz],Pn); X.go(kr,kr,pk.at[zz],Pn)
        wrecv(vr,rv.at[zz],Pn); X.go(vr,vr,pv.at[zz],Pn)
    for zz in range(4):
        r=K.at[pl.ds(pkrow(zz),TOK)]; wrecv(r,pk.at[zz],Pn)
        r=V.at[pl.ds(pkrow(zz),TOK)]; wrecv(r,pv.at[zz],Pn)
    for zz in [((z+d)%4) for d in (1,2,3)]:
        wrecv(Q.at[pl.ds(row(zz),TOK)],rq.at[zz],Pn)
    for cp in loc[3:6]: cp.wait()
    lax.fori_loop(0,8,widen,0)
    def turn(i): return (z+jnp.where(i==0,2,jnp.where(i==1,1,jnp.where(i==2,3,0))))%4
    def ocopy(i):
        zz=turn(i)
        return pltpu.make_async_remote_copy(src_ref=OB.at[pl.ds(row(zz),TOK)],dst_ref=og.at[z,pl.ds(0,TOK)],send_sem=osem.at[i],recv_sem=ro.at[z],device_id=dev(zz),device_id_type=MESH)
    def pairblock(i,_):
        ds=pl.ds(row(turn(i)),TOK)
        q=Q[ds].astype(f32)
        qa=jnp.where(lane<64,q,0.0)
        S[0]=dot(one_lane(qa,64).astype(bf16),KA[...],NT)
        S[1]=dot(one_lane(q-qa,0).astype(bf16),KB[...],NT)
        ma=softmax(0); mb=softmax(1)
        oa=dot(Pb[0],VA[...],NN); ob=dot(Pb[1],VB[...],NN)
        la=oa[:,64:65]; lb=ob[:,0:1]
        o=jnp.where(lane<64,oa/la,ob/lb)
        OA[ds]=o; OB[ds]=o.astype(bf16)
        LA[ds]=jnp.where(lane<64,ma+jnp.log(la),mb+jnp.log(lb))
        @pl.when(i<3)
        def _(): ocopy(i).start()
        return 0
    lax.fori_loop(0,4,pairblock,0)
    lo=pltpu.make_async_copy(OB.at[pl.ds(row(z),TOK)],og.at[z,pl.ds(0,TOK)],lsem.at[6]); lo.start()
    for d in (1,2,3):
        zz=(z+d)%4
        wrecv(og.at[zz,pl.ds(0,TOK)],ro.at[zz],Pn)
        wrecv(og.at[zz,pl.ds(TOK,CB)],roc.at[zz],Pn)
    lo.wait(); lc.wait()
    for i in range(3): ocopy(i).wait_send()
    X.drain()

D=pltpu.SemaphoreType.DMA
def vb(*s): return pltpu.VMEM(s,bf16)
def vf(*s): return pltpu.VMEM(s,f32)
VM=pl.BlockSpec(memory_space=pltpu.VMEM)
SM=pl.BlockSpec(memory_space=pltpu.SMEM)
def sds(*s,d=bf16): return jax.ShapeDtypeStruct(s,d)

def attn_fwd(sp,lims,cid):
    return pl.pallas_call(fwd_kernel,
        out_shape=(sds(4,TOK+CB,128),sds(NQ,128),sds(NK,128),sds(NK,128),sds(NK,128),sds(NK,128),sds(NQ,128),sds(NK,128),sds(NK,128),
                   sds(NQ,128,d=f32),sds(NQ,128,d=f32),sds(NQ,128,d=f32),sds(NQ,128,d=f32)),
        in_specs=[SM,VM],out_specs=[VM]*13,
        scratch_shapes=[vb(NK,128),vb(NK,128),vb(4,CB,128),vb(8,CB,128),vb(8,CB,128),vb(NQ,128),vb(4,CB,128),vf(2,TOK,NK),vb(2,TOK,NK),
            D((48,)),D((8,)),D((3,))]+[D((4,))]*12,
        compiler_params=pltpu.CompilerParams(collective_id=cid,has_side_effects=True,vmem_limit_bytes=60*1024*1024))(lims,sp)

def bwd_kernel(dog, Q, KA, KB, VA, VB, QC, KC, VC, OA, OC, LA, LC, dsp,
               DO, DOCp, DOC, S, P, DS, DKT, DVT, TT, DQ, DQC, XK, XV, YK, YV, SK, SV, HK, HV, XKC, XVC, YKC, YVC, HKC, HVC,
               ssem, lsem, qsem, rd, rdc, px, ho):
    b,z,c=mesh_pos()
    Pn=(b,z*2+1-c)
    dev=lambda zz:(b,zz*2+c)
    row=lambda zz: pl.multiple_of(zz*TOK,16)
    zbarrier(b,z,c)
    X=Sends(ssem)
    loc=[]
    def lcopy(src,dst):
        cp=pltpu.make_async_copy(src,dst,lsem.at[len(loc)]); cp.start(); loc.append(cp); return cp
    for zz in others(z):
        X.go(dog.at[zz,pl.ds(0,TOK)],DO.at[pl.ds(row(z),TOK)],rd.at[z],dev(zz))
    for zz in others(z):
        X.go(dog.at[zz,pl.ds(TOK,CB)],DOCp.at[z],rdc.at[z],dev(zz))
    l1=lcopy(dog.at[z,pl.ds(0,TOK)],DO.at[pl.ds(row(z),TOK)])
    l2=lcopy(dog.at[z,pl.ds(TOK,CB)],DOCp.at[z])
    l1.wait(); l2.wait()
    lane=lax.broadcasted_iota(jnp.int32,(TOK,128),1)
    def zero(ref):
        def bodyz(i,_):
            ref[:,pl.ds(pl.multiple_of(i*640,128),640)]=jnp.zeros((128,640),f32); return 0
        lax.fori_loop(0,NK//640,bodyz,0)
    def grads(q,k,v,do,lse,delta,free):
        qx=three_lanes(one_lane(q,free),free+1,-lse).astype(bf16)
        dx=three_lanes(do,free,-delta).astype(bf16)
        tail=jnp.zeros((PADQ-TOK,128),bf16)
        q=jnp.concatenate([q.astype(bf16),tail],0); do=jnp.concatenate([do.astype(bf16),tail],0)
        def scores(j):
            ks=pl.ds(j*CH,CH)
            S[j%2,0]=dot(qx,k[ks],NT)
            S[j%2,1]=dot(dx,v[ks],NT)
        scores(0)
        dq=jnp.zeros((TOK,128),f32)
        for j in range(NK//CH):
            if (j+1)*CH<NK: scores(j+1)
            t=j%2; ks=pl.ds(j*CH,CH)
            for i in range(TOK//16):
                ds=pl.ds(i*16,16)
                p=jnp.exp(S[t,0,ds,:])
                P[t,ds,:]=p.astype(bf16)
                DS[t,ds,:]=(p*S[t,1,ds,:]).astype(bf16)
            DKT[:,ks]+=dot(q,DS[t],TN)
            DVT[:,ks]+=dot(do,P[t],TN)
            dq=dq+dot(DS[t,pl.ds(0,TOK)],k[ks],NN)
        return dq
    def home(src,r0,n,si):
        for zz in others(z):
            X.go(src(zz),dsp.at[z,pl.ds(r0,n)],ho.at[si,z],dev(zz))
        lcopy(src(z),dsp.at[z,pl.ds(r0,n)])
    mine=c*NQ; theirs=(1-c)*NQ
    def split(acc, x, own):
        def tr(i,_):
            TT[pl.ds(pl.multiple_of(i*640,16),640)]=acc[:,pl.ds(pl.multiple_of(i*640,128),640)].T
            return 0
        lax.fori_loop(0,NK//640,tr,0)
        def cut(i,_):
            r=pl.multiple_of(i*TOK,16)
            x[pl.ds(r,TOK)]=TT[pl.ds(pl.multiple_of(theirs+i*TOK,16),TOK)].astype(bf16)
            own[pl.ds(r,TOK)]=TT[pl.ds(pl.multiple_of(mine+i*TOK,16),TOK)]
            return 0
        lax.fori_loop(0,4,cut,0)
    for t in range(2):
        P[t,pl.ds(TOK,PADQ-TOK)]=jnp.zeros((PADQ-TOK,CH),bf16)
        DS[t,pl.ds(TOK,PADQ-TOK)]=jnp.zeros((PADQ-TOK,CH),bf16)
    zero(DKT); zero(DVT)
    def pairblock(i,_):
        zz=(z+i)%4
        @pl.when(i>0)
        def _(): wrecv(DO.at[pl.ds(row(zz),TOK)],rd.at[zz],Pn)
        ds=pl.ds(row(zz),TOK)
        q=Q[ds].astype(f32); do=DO[ds].astype(f32)
        dof=do*OA[ds]
        da=jnp.sum(jnp.where(lane<64,dof,0.0),-1,keepdims=True)
        db=jnp.sum(jnp.where(lane<64,0.0,dof),-1,keepdims=True)
        qa=jnp.where(lane<64,q,0.0); doa=jnp.where(lane<64,do,0.0)
        ga=grads(qa,KA,VA,doa,LA[ds,0:1],da,64)
        gb=grads(q-qa,KB,VB,do-doa,LA[ds,64:65],db,0)
        DQ[ds]=(jnp.where(lane<64,ga,gb)*0.125).astype(bf16)
        @pl.when(i>0)
        def _(): qcopy(i).start()
        return 0
    def qcopy(i):
        zz=(z+i)%4
        return pltpu.make_async_remote_copy(src_ref=DQ.at[pl.ds(row(zz),TOK)],dst_ref=dsp.at[z,pl.ds(0,TOK)],send_sem=qsem.at[i],recv_sem=ho.at[0,z],device_id=dev(zz),device_id_type=MESH)
    lax.fori_loop(0,4,pairblock,0)
    lcopy(DQ.at[pl.ds(row(z),TOK)],dsp.at[z,pl.ds(0,TOK)])
    split(DKT,XK,SK); X.go(XK,YK,px.at[0],Pn)
    split(DVT,XV,SV); X.go(XV,YV,px.at[1],Pn)
    def addp(h,own,y):
        def body(i,_):
            ds=pl.ds(pl.multiple_of(i*TOK,16),TOK)
            h[ds]=(own[ds]+y[ds].astype(f32)).astype(bf16)
            return 0
        lax.fori_loop(0,4,body,0)
    wrecv(YK,px.at[0],Pn); addp(HK,SK,YK)
    home(lambda zz: HK.at[pl.ds(row(zz),TOK)],ROWS["k"],TOK,2)
    wrecv(YV,px.at[1],Pn); addp(HV,SV,YV)
    home(lambda zz: HV.at[pl.ds(row(zz),TOK)],ROWS["v"],TOK,3)
    zero(DKT); zero(DVT)
    def cblock(i,_):
        zz=(z+i)%4
        @pl.when(i>0)
        def _(): wrecv(DOCp.at[zz],rdc.at[zz],Pn)
        unpack_c(DOCp[zz],DOC,0)
        ds=pl.ds(row(zz),TOK)
        do=DOC[...].astype(f32)
        delta=jnp.sum(do*OC[ds],-1,keepdims=True)
        g=grads(QC[ds].astype(f32),KC,VC,do,LC[ds,0:1],delta,64)*0.125
        DQC[zz]=pack_c(g[:CB],g[CB:])
        return 0
    lax.fori_loop(0,4,cblock,0)
    home(lambda zz: DQC.at[zz],ROWS["qc"],CB,1)
    def splitc(acc, x, own):
        def tr(i,_):
            TT[pl.ds(pl.multiple_of(i*640,16),640)]=acc[:,pl.ds(pl.multiple_of(i*640,128),640)].T
            return 0
        lax.fori_loop(0,NK//640,tr,0)
        def cut(i,_):
            r=theirs+i*TOK
            x[i]=pack_c(TT[pl.ds(pl.multiple_of(r,16),CB)],TT[pl.ds(pl.multiple_of(r+CB,16),TOK-CB)])
            own[pl.ds(pl.multiple_of(i*TOK,16),TOK)]=TT[pl.ds(pl.multiple_of(mine+i*TOK,16),TOK)]
            return 0
        lax.fori_loop(0,4,cut,0)
    splitc(DKT,XKC,SK); X.go(XKC,YKC,px.at[2],Pn)
    splitc(DVT,XVC,SV); X.go(XVC,YVC,px.at[3],Pn)
    def addc(y,own,h):
        def body(i,_):
            unpack_c(y[i],DOC,0)
            r=i*TOK
            t=own[pl.ds(pl.multiple_of(r,16),TOK)]+DOC[...].astype(f32)
            h[i]=pack_c(t[:CB],t[CB:])
            return 0
        lax.fori_loop(0,4,body,0)
    wrecv(YKC,px.at[2],Pn); addc(YKC,SK,HKC)
    home(lambda zz: HKC.at[zz],ROWS["kc"],CB,4)
    wrecv(YVC,px.at[3],Pn); addc(YVC,SV,HVC)
    home(lambda zz: HVC.at[zz],ROWS["vc"],CB,5)
    for si,(r0,n) in enumerate(((0,TOK),(ROWS["qc"],CB),(ROWS["k"],TOK),(ROWS["v"],TOK),(ROWS["kc"],CB),(ROWS["vc"],CB))):
        for d in (1,2,3):
            zz=(z+d)%4
            wrecv(dsp.at[zz,pl.ds(r0,n)],ho.at[si,zz],Pn)
    for cp in loc[2:]: cp.wait()
    for i in range(1,4): qcopy(i).wait_send()
    X.drain()

def attn_bwd(dog,saved,cid):
    return pl.pallas_call(bwd_kernel,
        out_shape=sds(4,3*(TOK+CB),128),
        in_specs=[VM]*13,out_specs=VM,
        scratch_shapes=[vb(NQ,128),vb(4,CB,128),vb(TOK,128),vf(2,2,TOK,CH),vb(2,PADQ,CH),vb(2,PADQ,CH),vf(128,NK),vf(128,NK),vf(NK,128),
            vb(NQ,128),vb(4,CB,128)]+[vb(NQ,128)]*4+[vf(NQ,128)]*2+[vb(NQ,128)]*2+[vb(4,CB,128)]*6+[
            D((32,)),D((10,)),D((4,)),D((4,)),D((4,)),D((4,)),D((6,4))],
        compiler_params=pltpu.CompilerParams(collective_id=cid,has_side_effects=True,vmem_limit_bytes=60*1024*1024))(dog,*saved)


HI=lax.Precision.HIGHEST
DM=768
MTILES=(0,None,1,2,None,3)

def spread(pair, packed):
    lane=lax.broadcasted_iota(jnp.int32,(CB,128),1)
    def mid(g0,g1):
        a=packed(g0).astype(f32); b=packed(g1).astype(f32)
        top=jnp.where(lane<64,a,pltpu.roll(b,64,1))
        low=jnp.where(lane<64,pltpu.roll(a,64,1),b)
        return jnp.concatenate([top,low[:TOK-CB]],0).astype(bf16)
    return [pair(0),mid(0,1),pair(1),pair(2),mid(2,3),pair(3)]

def gather_groups(tiles):
    out=[]
    for g in range(4):
        p=tiles[(0,2,3,5)[g]]
        t=tiles[(1,1,4,4)[g]]
        if g%2: t=pltpu.roll(t,64,1)
        out.append((p.astype(bf16),pack_c(t[:CB],t[CB:])))
    return out

def wcols(W,j,n):
    S=W.shape[0]
    return jnp.concatenate([W[:,j+i].reshape(S*16,128) for i in range(n)],1)

def lnorm(x):
    c=x-jnp.mean(x,-1,keepdims=True)
    inv=lax.rsqrt(jnp.mean(c*c,-1,keepdims=True)+EPSILON)
    return c*inv,inv

def lnorm_back(dy,gain,n,inv):
    g=dy*gain
    return inv*(g-jnp.mean(g,-1,keepdims=True)-n*jnp.mean(g*n,-1,keepdims=True))

def vrow(V,i):
    return jnp.concatenate([V[6*i+j:6*i+j+1,:] for j in range(6)],1)

def colsum(x): return jnp.sum(x,0,keepdims=True)

def front_kernel(start, fidx, pix, G, x0o, h1o, sp, We, Wq, PO, POf, TI, VE, V, TIf, sems):
    cps=[pltpu.make_async_copy(G.at[pl.ds(0,576)],We,sems.at[0]),
         pltpu.make_async_copy(G.at[pl.ds(4224+(48+6*start[0])//16,151)],PO,sems.at[1]),
         pltpu.make_async_copy(G.at[pl.ds(4224+264,3)],TI,sems.at[2]),
         pltpu.make_async_copy(G.at[pl.ds(4512,7)],VE,sems.at[3]),
         pltpu.make_async_copy(G.at[pl.ds(576,864)],Wq,sems.at[4])]
    for cp in cps: cp.start()
    for cp in cps[:4]: cp.wait()
    for i in range(7): V[pl.ds(i*16,16),:]=VE[i].astype(f32)
    for i in range(3): TIf[pl.ds(i*16,16),:]=TI[i].astype(f32)
    def cv(i,_):
        POf[pl.ds(i*16,16),:]=PO[i].astype(f32); return 0
    lax.fori_loop(0,151,cv,0)
    rem=(6*start[0])%16
    W4=We.reshape(96,6,16,128)
    for j in range(3):
        e=dot(pix[...],wcols(W4,2*j,2),NN)
        p=jnp.concatenate([POf[pl.ds(rem+2*j+i,TOK,stride=6),:] for i in range(2)],1)
        tm=jnp.concatenate([TIf[pl.ds(6*fidx[0]+2*j+i,1),:] for i in range(2)],1)
        bb=jnp.concatenate([V[48+2*j+i:49+2*j+i,:] for i in range(2)],1)
        x0o[:,j*256:(j+1)*256]=e+bb+p+tm
    n,inv=lnorm(x0o[...])
    h1=(n*vrow(V,0)+vrow(V,1)).astype(bf16)
    h1o[...]=h1
    cps[4].wait()
    W4=Wq.reshape(48,18,16,128)
    for part in range(3):
        tiles=[]
        for j in range(3):
            r=dot(h1,wcols(W4,part*6+2*j,2),NN)
            if part!=1:
                o=54 if part==0 else 60
                r=r+jnp.concatenate([V[o+2*j+i:o+1+2*j+i,:] for i in range(2)],1)
            r=r.astype(bf16).astype(f32)
            if part==0: r=r*0.125
            tiles+=[r[:,:128],r[:,128:]]
        for g,(p,c) in enumerate(gather_groups(tiles)):
            sp[g,pl.ds(part*TOK,TOK)]=p
            sp[g,pl.ds(3*TOK+part*CB,CB)]=c

ANYS=pl.BlockSpec(memory_space=pl.ANY)
def front(start,fidx,pix,G):
    return pl.pallas_call(front_kernel,
        out_shape=(sds(TOK,DM,d=f32),sds(TOK,DM),sds(4,3*(TOK+CB),128)),
        in_specs=[SM,SM,VM,ANYS],out_specs=(VM,)*3,
        scratch_shapes=[vb(576,16,128),vb(864,16,128),vb(151,16,128),vf(2416,128),vb(3,16,128),vb(7,16,128),vf(112,128),vf(48,128),D((5,))],
        compiler_params=pltpu.CompilerParams(vmem_limit_bytes=60*1024*1024))(start,fidx,pix,G)

def mid_kernel(og, x0, G, wmap, vmask, scal, counts, sel,
               atto, h2o, acto, dpreo, dmlpo, dattno, dsec, dog, vgo, ubo, gmapo, gprojo, losso,
               Wo, Wu, Wd, Wp, VE, V, A2, GP, SLOT, x1s, x2s, sems, ssem, rsem):
    b=lax.axis_index("batch"); f=lax.axis_index("frame"); k=b*8+f
    def dev_of(kk): return (kk//8,kk%8)
    bar=pltpu.get_barrier_semaphore()
    def greet(d,_):
        pl.semaphore_signal(bar,inc=1,device_id=dev_of((k+d)%32),device_id_type=MESH); return 0
    lax.fori_loop(1,32,greet,0)
    cps=[pltpu.make_async_copy(G.at[pl.ds(10*144,288)],Wo,sems.at[0]),
         pltpu.make_async_copy(G.at[pl.ds(4512,7)],VE,sems.at[1]),
         pltpu.make_async_copy(G.at[pl.ds(12*144,1152)],Wu,sems.at[2]),
         pltpu.make_async_copy(G.at[pl.ds(20*144,1152)],Wd,sems.at[3]),
         pltpu.make_async_copy(G.at[pl.ds(28*144,192)],Wp,sems.at[4])]
    for cp in cps: cp.start()
    for j,t in enumerate(spread(lambda g: og[g,pl.ds(0,TOK)],lambda g: og[g,pl.ds(TOK,CB)])):
        atto[:,j*128:(j+1)*128]=t
    cps[0].wait(); cps[1].wait()
    for i in range(7): V[pl.ds(i*16,16),:]=VE[i].astype(f32)
    Wo4=Wo.reshape(48,6,16,128); Wu4=Wu.reshape(48,24,16,128); Wd4=Wd.reshape(192,6,16,128); Wp4=Wp.reshape(48,4,16,128)
    att=atto[...]
    for j in range(3):
        bb=jnp.concatenate([V[66+2*j+i:67+2*j+i,:] for i in range(2)],1)
        x1s[:,j*256:(j+1)*256]=x0[:,j*256:(j+1)*256]+(dot(att,wcols(Wo4,2*j,2),NN)+bb)
    n2,inv2=lnorm(x1s[...])
    h2=(n2*vrow(V,2)+vrow(V,3)).astype(bf16)
    h2o[...]=h2
    x2s[...]=x1s[...]+vrow(V,12)
    cps[2].wait(); cps[3].wait()
    def hid(j,_):
        w=jnp.concatenate([Wu4[:,2*j+i].reshape(768,128) for i in range(2)],1)
        bb=jnp.concatenate([V[pl.ds(78+2*j+i,1),:] for i in range(2)],1)
        u=dot(h2o[...],w,NN)+bb
        phi=0.5*(1.0+lax.erf(u*(0.5**0.5)))
        a=(u*phi).astype(bf16)
        cs=pl.ds(pl.multiple_of(j*256,256),256)
        GP[:,cs]=phi+u*(jnp.exp(-0.5*u*u)*0.3989422804014327)
        acto[:,cs]=a
        wd=Wd4[pl.ds(j*16,16)]
        x2s[...]+=dot(a,jnp.concatenate([wd[:,t].reshape(256,128) for t in range(6)],1),NN)
        return 0
    lax.fori_loop(0,12,hid,0)
    x2=x2s[...]
    nm,invm=lnorm(x2)
    nmap=nm*vrow(V,4)+vrow(V,5)
    lg=lax.dot_general(nmap,wmap[...],NN,precision=HI,preferred_element_type=f32)
    ok=vmask[...]>0.0
    lg=jnp.where(ok,lg,-1e30)
    ex=jnp.where(ok,jnp.exp(lg-jnp.max(lg,0,keepdims=True)),0.0)
    lane8=lax.broadcasted_iota(jnp.int32,(TOK,128),1)<NMAP
    maps=jnp.where(lane8,ex/jnp.sum(ex,0,keepdims=True),0.0)
    r=jnp.sum(maps,-1,keepdims=True)
    sw=scal[0:1,0:1]; inv_total=scal[1:2,0:1]
    pooled=sw*colsum(r*x2)
    corr=sw*colsum(r*r-jnp.sum(maps*maps,-1,keepdims=True))
    slot=[pooled[:,j*128:(j+1)*128] for j in range(6)]+[jnp.broadcast_to(corr,(1,128)),jnp.zeros((1,128),f32)]
    SLOT[k,pl.ds(0,8)]=jnp.concatenate(slot,0)
    SLOT[k,pl.ds(8,8)]=sel[...]
    def xcopy(d):
        return pltpu.make_async_remote_copy(src_ref=SLOT.at[k],dst_ref=SLOT.at[k],send_sem=ssem.at[d],recv_sem=rsem.at[k],device_id=dev_of((k+d)%32),device_id_type=MESH)
    pl.semaphore_wait(bar,31)
    def xs(d,_):
        xcopy(d).start(); return 0
    lax.fori_loop(1,32,xs,0)
    cps[4].wait()
    def xw(d,_):
        kk=(k+d)%32
        wrecv(SLOT.at[kk],rsem.at[kk],(b,f)); return 0
    lax.fori_loop(1,32,xw,0)
    tot=[]
    for cl in range(4):
        t=SLOT[cl*8,pl.ds(0,8)]
        for ff in range(1,8): t=t+SLOT[cl*8+ff,pl.ds(0,8)]
        tot.append(t)
    corr_total=(tot[0]+tot[1]+tot[2]+tot[3])[6:7,0:1]
    pm=jnp.concatenate([jnp.concatenate([t[j:j+1,:] for j in range(6)],1) for t in tot]+[jnp.zeros((4,DM),f32)],0)/counts[:,0:1]
    nf,invf=lnorm(pm)
    hf=nf*vrow(V,6)+vrow(V,7)
    rows=lax.broadcasted_iota(jnp.int32,(8,1),0)
    live=rows<4
    wp=jnp.concatenate([Wp4[:,t].reshape(768,128) for t in range(4)],1).astype(f32)
    e=lax.dot_general(hf,wp,NN,precision=HI,preferred_element_type=f32)
    rn=lax.rsqrt(jnp.sum(e*e,-1,keepdims=True)+1e-06)
    unit=e*rn
    lanes=lax.broadcasted_iota(jnp.int32,(8,128),1)
    gm=jnp.zeros((8,128),f32)
    for j in range(4):
        gm=gm+jnp.where(lanes==j,jnp.sum(unit*unit[j:j+1,:],-1,keepdims=True),0.0)
    selk=[jnp.concatenate([SLOT[cl*8,pl.ds(8+kk,1)] for cl in range(4)]+[jnp.zeros((4,128),f32)],0) for kk in range(5)]
    S=[jnp.sum(s*gm,-1,keepdims=True)/SOFTMAX_TEMPER for s in selk]
    mx=S[0]
    for s in S[1:]: mx=jnp.maximum(mx,s)
    es=[jnp.exp(s-mx) for s in S]
    se=es[0]+es[1]+es[2]+es[3]+es[4]
    contrast=jnp.sum(jnp.where(live,mx+jnp.log(se)-S[0],0.0),0,keepdims=True)*0.25
    losso[...]=jnp.broadcast_to(contrast+DECAY_PENALTY*corr_total*inv_total,(8,128))
    dgm=jnp.zeros((8,128),f32)
    for kk in range(5):
        w=es[kk]/se-(1.0 if kk==0 else 0.0)
        dgm=dgm+jnp.where(live,w,0.0)*selk[kk]
    dgm=dgm*(0.25/SOFTMAX_TEMPER)
    du=jnp.zeros((8,EMB),f32)
    for j in range(4):
        cj=dgm[:,j:j+1]
        du=du+cj*unit[j:j+1,:]
        du=du+jnp.where(rows==j,colsum(cj*unit),0.0)
    de=rn*du-e*(rn*rn*rn)*jnp.sum(e*du,-1,keepdims=True)
    de=jnp.where(live,de,0.0)
    dhf=lax.dot_general(de,wp,NT,precision=HI,preferred_element_type=f32)
    head=jnp.where(k==0,1.0,0.0)
    gp=lax.dot_general(hf,de,TN,precision=HI,preferred_element_type=f32)*head
    gpb=gp.astype(bf16)
    for s in range(48):
        for t in range(4): gprojo[s*4+t]=gpb[s*16:(s+1)*16,t*128:(t+1)*128]
    vgo[6:7,:]=colsum(dhf*nf)*head
    vgo[7:8,:]=colsum(dhf)*head
    dpm=lnorm_back(dhf,vrow(V,6),nf,invf)/counts[:,0:1]
    dpool=colsum(jnp.where(rows==b,dpm,0.0))
    cdec=DECAY_PENALTY*inv_total*sw
    dm=sw*jnp.sum(x2*dpool,-1,keepdims=True)+2.0*cdec*(r-maps)
    dm=jnp.where(lane8,dm,0.0)
    dl=maps*(dm-colsum(maps*dm))
    gmapo[...]=lax.dot_general(nmap,dl,TN,precision=HI,preferred_element_type=f32)
    dnm=lax.dot_general(dl,wmap[...],NT,precision=HI,preferred_element_type=f32)
    vgo[4:5,:]=colsum(dnm*nm)
    vgo[5:6,:]=colsum(dnm)
    dx2=(sw*r)*dpool+lnorm_back(dnm,vrow(V,4),nm,invm)
    dmlp=dx2.astype(bf16)
    dmlpo[...]=dmlp
    vgo[12:13,:]=colsum(dmlp.astype(f32))
    x2s[...]=jnp.zeros((TOK,DM),f32)
    dsec[...]=dx2
    def hidb(j,_):
        cs=pl.ds(pl.multiple_of(j*256,256),256)
        wd=Wd4[pl.ds(j*16,16)]
        da=dot(dmlpo[...],jnp.concatenate([wd[:,t].reshape(256,128) for t in range(6)],1),NT)
        dp=(da*GP[:,cs]).astype(bf16)
        dpreo[:,cs]=dp
        ubo[:,cs]=colsum(dp.astype(f32))
        w=jnp.concatenate([Wu4[:,2*j+i].reshape(768,128) for i in range(2)],1)
        x2s[...]+=dot(dp,w,NT)
        return 0
    lax.fori_loop(0,12,hidb,0)
    dh2=x2s[...]
    n2,inv2=lnorm(x1s[...])
    vgo[2:3,:]=colsum(dh2*n2)
    vgo[3:4,:]=colsum(dh2)
    dx1=dsec[...]+lnorm_back(dh2,vrow(V,2),n2,inv2)
    dsec[...]=dx1
    da_=dx1.astype(bf16)
    dattno[...]=da_
    vgo[11:12,:]=colsum(da_.astype(f32))
    tiles=[]
    for j in range(6):
        w=jnp.concatenate([Wo4[8*j:8*j+8,t].reshape(128,128) for t in range(6)],1)
        tiles.append(dot(da_,w,NT).astype(bf16).astype(f32))
    for g,(p,c) in enumerate(gather_groups(tiles)):
        dog[g,pl.ds(0,TOK)]=p
        dog[g,pl.ds(TOK,CB)]=c
    def xd(d,_):
        xcopy(d).wait_send(); return 0
    lax.fori_loop(1,32,xd,0)

def middle(og,x0,G,wmap,vmask,scal,counts,sel,cid):
    return pl.pallas_call(mid_kernel,
        out_shape=(sds(TOK,DM),sds(TOK,DM),sds(TOK,FFW),sds(TOK,FFW),sds(TOK,DM),sds(TOK,DM),sds(TOK,DM,d=f32),sds(4,TOK+CB,128),
                   sds(16,DM,d=f32),sds(1,FFW,d=f32),sds(DM,128,d=f32),sds(192,16,128),sds(8,128,d=f32)),
        in_specs=[VM,VM,ANYS]+[VM]*5,out_specs=(VM,)*13,
        scratch_shapes=[vb(288,16,128),vb(1152,16,128),vb(1152,16,128),vb(192,16,128),vb(7,16,128),vf(112,128),vf(8,128),vf(TOK,FFW),vf(32,16,128),
            vf(TOK,DM),vf(TOK,DM),D((5,)),D((32,)),D((32,))],
        compiler_params=pltpu.CompilerParams(collective_id=cid,has_side_effects=True,vmem_limit_bytes=63*1024*1024))(og,x0,G,wmap,vmask,scal,counts,sel)

def back_kernel(start, fidx, dsp, G, x0, dsec, vg, ub, gmap, gproj, dqkv, dx0o, tailo, Wq, VE, V, TL, sems):
    cps=[pltpu.make_async_copy(G.at[pl.ds(576,864)],Wq,sems.at[0]),pltpu.make_async_copy(G.at[pl.ds(4512,7)],VE,sems.at[1])]
    for cp in cps: cp.start()
    for part in range(3):
        for j,t in enumerate(spread(lambda g: dsp[g,pl.ds(part*TOK,TOK)],lambda g: dsp[g,pl.ds(3*TOK+part*CB,CB)])):
            dqkv[:,(part*6+j)*128:(part*6+j+1)*128]=t
    def z(i,_):
        TL[pl.ds(i*64,64),:]=jnp.zeros((64,128),f32); return 0
    lax.fori_loop(0,96,z,0)
    for cp in cps: cp.wait()
    for i in range(7): V[pl.ds(i*16,16),:]=VE[i].astype(f32)
    W4=Wq.reshape(48,18,16,128)
    acc=jnp.zeros((TOK,DM),f32)
    for j in range(9):
        acc=acc+dot(dqkv[:,j*256:(j+1)*256],wcols(W4,2*j,2),NT)
    n,inv=lnorm(x0[...])
    ent=dsec[...]+lnorm_back(acc,vrow(V,0),n,inv)
    dx0o[...]=ent.astype(bf16)
    eb=colsum(ent)
    def rowput(i,v):
        for j in range(6): TL[pl.ds(i+j,1),:]=v[:,j*128:(j+1)*128]
    TL[0:48,:]=gmap[...]
    for j in range(6):
        TL[pl.ds(48+6*start[0]+j,TOK,stride=6),:]=ent[:,j*128:(j+1)*128]
    rowput(4224+6*fidx[0],eb)
    vec={0:colsum(acc*n),1:colsum(acc),8:eb,9:colsum(dqkv[:,0:DM].astype(f32)),10:colsum(dqkv[:,2*DM:].astype(f32))}
    for i in range(13):
        rowput(4608+6*i, vec[i] if i in vec else vg[i:i+1,:])
    for j in range(24): TL[4608+78+j:4608+79+j,:]=ub[:,j*128:(j+1)*128]
    def cg(i,_):
        tailo[pl.ds(i*8,8)]=gproj[pl.ds(i*8,8)]; return 0
    lax.fori_loop(0,24,cg,0)
    def ct(i,_):
        tailo[192+i]=TL[pl.ds(pl.multiple_of(i*16,16),16),:].astype(bf16); return 0
    lax.fori_loop(0,384,ct,0)

def back(start,fidx,dsp,G,x0,dsec,vg,ub,gmap,gproj):
    return pl.pallas_call(back_kernel,
        out_shape=(sds(TOK,3*DM),sds(TOK,DM),sds(576,16,128)),
        in_specs=[SM,SM,VM,ANYS]+[VM]*6,out_specs=(VM,)*3,
        scratch_shapes=[vb(864,16,128),vb(7,16,128),vf(112,128),vf(6144,128),D((2,))],
        compiler_params=pltpu.CompilerParams(vmem_limit_bytes=60*1024*1024))(start,fidx,dsp,G,x0,dsec,vg,ub,gmap,gproj)


SHARD = 289176
BLOCK = 294912
SLIDE = BLOCK - SHARD
CARRY = 32 * SLIDE
KEY_ORDER_C = 2


def to_tiles(matrix):
    rows, width = matrix.shape
    m = width // 128
    return matrix.reshape(rows // 16, 16, m, 128).transpose(0, 2, 1, 3).reshape(-1, 16, 128)


def block_to_tiles(flat, k):
    def of(width):
        return lambda v: to_tiles(v.reshape(-1, width))

    def split29(v):
        return jnp.concatenate([to_tiles(v[: 48 * 2048].reshape(-1, 512)), v[48 * 2048 :].reshape(-1, 16, 128)])

    branch = class_of(k)
    return lax.switch(branch, [of(768), of(2304), of(3072), of(512), split29, of(128)], flat)


def class_of(k):
    return jnp.where(
        k < 4, 0, jnp.where(k < 10, 1, jnp.where(k < 12, 0, jnp.where(k < 20, 2, jnp.where(k < 28, 0, jnp.where(k == 28, 3, jnp.where(k == 29, 4, 5))))))
    )


def local_4x8(
    pixels,
    res_class,
    valid_tubelet_count,
    positive,
    negatives,
    master,
    first_moment,
    second_moment,
    adam_step,
):
    D = HEAD_COUNT * HEAD_FEATURES
    both_axes = ("batch", "frame")
    bi = lax.axis_index("batch")
    fi = lax.axis_index("frame")
    k = bi * 8 + fi
    low = to_bfloat(master)
    nxt = lax.ppermute(low[:CARRY], both_axes, [(i + 1, i) for i in range(31)])
    block = lax.dynamic_slice(jnp.concatenate([low, nxt]), (SLIDE * k,), (BLOCK,))
    G = make_ag()(block_to_tiles(block, k), 0)
    flat_tiles = G.reshape(32 * 144, 16, 128)
    w_map = G[29, 48:51].reshape(D, NMAP).astype(jnp.float32)
    w_map = jnp.pad(w_map, ((0, 0), (0, 128 - NMAP)))
    tubelets = lax.dynamic_slice_in_dim(valid_tubelet_count, bi, 1, 0)
    patches = jnp.where(res_class == 0, P0, jnp.where(res_class == 1, P1, PATCHES_THIRD_2)).astype(jnp.int32)
    start_rows = jnp.where(res_class == 0, 0, jnp.where(res_class == 1, P0, P0 + P1)).astype(jnp.int32)
    frame = jnp.full((1,), fi, jnp.int32)
    pix = pixels.reshape(400, TUBELET_PIXELS)
    first_in, h1, sp = front(start_rows, frame, pix, flat_tiles)
    lims = jnp.concatenate([patches, tubelets])
    og, *saved_attn = attn_fwd(sp, lims, 2)
    total_count = jnp.sum(valid_tubelet_count).astype(jnp.float32)
    patch_mask = jnp.broadcast_to((jnp.arange(400, dtype=jnp.int32)[:, None] < patches[0]).astype(jnp.float32), (400, 128))
    slot_weight = (fi < tubelets[0]).astype(jnp.float32)
    scal = jnp.broadcast_to(
        jnp.concatenate([slot_weight[None], 1.0 / total_count[None], jnp.zeros((6,), jnp.float32)])[:, None], (8, 128)
    )
    counts = jnp.broadcast_to(
        jnp.concatenate([(NMAP * valid_tubelet_count).astype(jnp.float32), jnp.ones((4,), jnp.float32)])[:, None], (8, 128)
    )
    ids = jnp.concatenate([positive, negatives[0], jnp.full((3,), -1, jnp.int32)])
    chosen = (ids[:, None] == jnp.arange(128, dtype=jnp.int32)[None]).astype(jnp.float32)
    (attended, h2, hidden_low, g_pre, g_mlp, g_attn, g_second, dog, g_vec, g_up_bias, g_map, g_proj, loss_rows) = middle(
        og, first_in, flat_tiles, w_map, patch_mask, scal, counts, chosen, 4
    )
    loss_value = loss_rows[0, 0]
    dsp = attn_bwd(dog, saved_attn, 3)
    g_qkv, g_entry, tail_tiles = back(
        start_rows, frame, dsp, flat_tiles, first_in, g_second, g_vec, g_up_bias, g_map[:, :NMAP].reshape(48, 128), g_proj
    )
    grad, squares = make_rsx()(
        pix, h1, attended, h2, hidden_low, g_entry, g_qkv, g_attn, g_pre, g_mlp, tail_tiles.reshape(4, 144, 16, 128), cid=1
    )
    grad = grad.reshape(-1)[:SHARD]
    grad_norm = jnp.sqrt(jnp.sum(squares))
    clipped = grad * jnp.minimum(1.0, CLIP_AT / grad_norm)
    new_first = BETA_ONE * first_moment + (1.0 - BETA_ONE) * clipped
    new_second = BETA_TWO * second_moment + (1.0 - BETA_TWO) * clipped * clipped
    step = adam_step[0].astype(jnp.float32)
    update = new_first / (1.0 - BETA_ONE**step) / (jnp.sqrt(new_second / (1.0 - BETA_TWO**step)) + ADAM_EPS)
    new_master = master - RATE * (update + DECAY * master)
    return (new_master, new_first, new_second, to_bfloat(new_master), loss_value, grad_norm)


def solution(mesh):
    fast = dict(mesh.shape) == {"batch": 4, "frame": 8}
    return jax.shard_map(
        local_4x8 if fast else local_any_mesh,
        mesh=mesh,
        in_specs=(
            P("batch", "frame", None, None),
            P("batch"),
            P(),
            P("batch"),
            P("batch", None),
            P(("batch", "frame")),
            P(("batch", "frame")),
            P(("batch", "frame")),
            P(),
        ),
        out_specs=(
            P(("batch", "frame")),
            P(("batch", "frame")),
            P(("batch", "frame")),
            P(("batch", "frame")),
            P(),
            P(),
        ),
        check_vma=False,
    )
```

```python
from functools import partial
import math

import jax
import jax.numpy as jnp
from jax import lax
from jax.experimental import pallas as pl
from jax.experimental.pallas import tpu as pltpu
from jax.sharding import PartitionSpec as P

HEAD_COUNT = 12
HEAD_FEATURES = 64
FFW = 3072
TUBELET_PIXELS = 1536
EMB = 512
NMAP = 8
P0 = 100
P1 = 196
PATCHES_THIRD_2 = 400
TMAX = 64
NVEC = 13
CLIPS_PER_BATCH = 1


EPSILON = 1e-05
SOFTMAX_TEMPER = 0.02
DECAY_PENALTY = 1.0
CLIP_AT = 0.05
RATE = 0.03
DECAY = 0.05
BETA_ONE = 0.9
BETA_TWO = 0.999
ADAM_EPS = 1e-08
HIGH_ACCURACY = lax.Precision.HIGHEST


def to_bfloat(values):
    return values.astype(jnp.bfloat16)


def unpack_flat(flat_vector):
    width_of_model = HEAD_COUNT * HEAD_FEATURES
    dims_list = [
        (TUBELET_PIXELS, width_of_model),
        (width_of_model, 3 * width_of_model),
        (width_of_model, width_of_model),
        (width_of_model, FFW),
        (FFW, width_of_model),
        (width_of_model, EMB),
        (width_of_model, NMAP),
        (P0 + P1 + PATCHES_THIRD_2, width_of_model),
        (TMAX, width_of_model),
        (NVEC, width_of_model),
        (FFW,),
    ]
    pieces = []
    offset = 0
    for dims_of in dims_list:
        length = math.prod(dims_of)
        pieces.append(flat_vector[offset : offset + length].reshape(dims_of))
        offset += length
    return pieces


def norm_forward(inputs, gain_row, shift_row):
    center = inputs - jnp.mean(inputs, -1, keepdims=True)
    inverse = lax.rsqrt(jnp.mean(center * center, -1, keepdims=True) + EPSILON)
    normed = center * inverse
    return (normed * gain_row + shift_row, (normed, inverse))


def norm_backward(grad_out, gain_row, saved_parts):
    normed, inverse = saved_parts
    scaled = grad_out * gain_row
    grad_in = inverse * (
        scaled
        - jnp.mean(scaled, -1, keepdims=True)
        - normed * jnp.mean(scaled * normed, -1, keepdims=True)
    )
    lead_axes = tuple(range(grad_out.ndim - 1))
    return (grad_in, jnp.sum(grad_out * normed, lead_axes), jnp.sum(grad_out, lead_axes))


def block_plan(total_rows):
    shards = total_rows // PATCHES_THIRD_2
    group_size = 4
    return (shards // group_size, group_size * PATCHES_THIRD_2)


def local_any_mesh(
    pixels,
    res_class,
    valid_tubelet_count,
    positive,
    negatives,
    master,
    first_moment,
    second_moment,
    adam_step,
):
    width_of_model = HEAD_COUNT * HEAD_FEATURES
    score_scale = HEAD_FEATURES ** (-0.5)
    every_clip_rows = CLIPS_PER_BATCH * lax.axis_size("batch")
    index_of_batch = lax.axis_index("batch")
    frame_index = lax.axis_index("frame")
    gathered = lax.all_gather(to_bfloat(master), ("batch", "frame"), axis=0, tiled=True)
    w_embed, w_qkv, w_out, w_up, w_down, w_proj, w_map, pos_space, pos_time, vectors, bias_up = (
        unpack_flat(gathered)
    )
    vec_f = vectors.astype(jnp.float32)
    tubelet_stack = lax.dynamic_slice_in_dim(
        valid_tubelet_count, index_of_batch * CLIPS_PER_BATCH, CLIPS_PER_BATCH, 0
    )
    patches = jnp.where(res_class == 0, P0, jnp.where(res_class == 1, P1, PATCHES_THIRD_2)).astype(
        jnp.int32
    )
    start_rows = jnp.where(res_class == 0, 0, jnp.where(res_class == 1, P0, P0 + P1)).astype(
        jnp.int32
    )
    patch_pos = jnp.stack(
        [lax.dynamic_slice_in_dim(pos_space, start_rows[0], PATCHES_THIRD_2, 0)]
    ).astype(jnp.float32)
    time_row = lax.dynamic_slice_in_dim(pos_time, frame_index, 1, 0).astype(jnp.float32)
    rows_of_pixels = pixels.reshape(CLIPS_PER_BATCH * PATCHES_THIRD_2, TUBELET_PIXELS)
    embedded = jnp.dot(rows_of_pixels, w_embed, preferred_element_type=jnp.float32).reshape(
        CLIPS_PER_BATCH, PATCHES_THIRD_2, width_of_model
    )
    first_in = embedded + vec_f[8] + patch_pos + time_row
    normed_one, saved_one = norm_forward(first_in, vec_f[0], vec_f[1])
    normed_one = to_bfloat(normed_one)
    qkv_bias = jnp.concatenate([vec_f[9], jnp.zeros_like(vec_f[9]), vec_f[10]])
    projection_output = to_bfloat(
        jnp.einsum("cpd,de->cpe", normed_one, w_qkv, preferred_element_type=jnp.float32) + qkv_bias
    )
    query_matrix = projection_output[..., :width_of_model].reshape(
        CLIPS_PER_BATCH, PATCHES_THIRD_2, HEAD_COUNT, HEAD_FEATURES
    )
    kv_local = projection_output[..., width_of_model:]

    def key_mask(row_start, count_of_rows):
        row_ids = row_start + jnp.arange(count_of_rows, dtype=jnp.int32)
        return ((row_ids // PATCHES_THIRD_2)[None, :] < tubelet_stack[:, None]) & (
            (row_ids % PATCHES_THIRD_2)[None, :] < patches[:, None]
        )

    def block_scores(key_value_block, block_start):
        count_of_rows = key_value_block.shape[1]
        head_keys = key_value_block[..., :width_of_model].reshape(
            CLIPS_PER_BATCH, count_of_rows, HEAD_COUNT, HEAD_FEATURES
        )
        head_values = key_value_block[..., width_of_model:].reshape(
            CLIPS_PER_BATCH, count_of_rows, HEAD_COUNT, HEAD_FEATURES
        )
        key_ok = key_mask(block_start, count_of_rows)[:, None, None, :]
        scores = (
            jnp.einsum(
                "cqhd,ckhd->chqk", query_matrix, head_keys, preferred_element_type=jnp.float32
            )
            * score_scale
        )
        return (jnp.where(key_ok, scores, -1e30), key_ok, head_keys, head_values)

    forward_init = (
        jnp.full((CLIPS_PER_BATCH, HEAD_COUNT, PATCHES_THIRD_2), -1e30, jnp.float32),
        jnp.zeros((CLIPS_PER_BATCH, HEAD_COUNT, PATCHES_THIRD_2), jnp.float32),
        jnp.zeros((CLIPS_PER_BATCH, HEAD_COUNT, PATCHES_THIRD_2, HEAD_FEATURES), jnp.float32),
    )
    kv_piece = lax.all_gather(kv_local, "frame", axis=1, tiled=True)
    count_blocks, block_rows = block_plan(kv_piece.shape[1])

    def forward_one_block(block_index, running):
        run_max, run_sum, run_acc = running
        block_start = block_index * block_rows
        key_value_block = lax.dynamic_slice_in_dim(
            kv_piece, block_index * block_rows, block_rows, 1
        )
        scores, key_ok, head_keys, head_values = block_scores(key_value_block, block_start)
        new_max = jnp.maximum(run_max, jnp.max(scores, -1))
        factor = jnp.exp(run_max - new_max)
        prob_tile = jnp.where(key_ok, jnp.exp(scores - new_max[..., None]), 0.0)
        run_acc = run_acc * factor[..., None] + jnp.einsum(
            "chqk,ckhd->chqd", to_bfloat(prob_tile), head_values, preferred_element_type=jnp.float32
        )
        return (new_max, run_sum * factor + jnp.sum(prob_tile, -1), run_acc)

    run_max, run_sum, run_acc = lax.fori_loop(0, count_blocks, forward_one_block, forward_init)
    log_sum = run_max + jnp.log(run_sum)
    head_attended_rows = run_acc / run_sum[..., None]
    attended_reduced = to_bfloat(
        head_attended_rows.transpose(0, 2, 1, 3).reshape(
            CLIPS_PER_BATCH, PATCHES_THIRD_2, width_of_model
        )
    )
    second_in = (
        first_in
        + jnp.einsum("cpe,ed->cpd", attended_reduced, w_out, preferred_element_type=jnp.float32)
        + vec_f[11]
    )
    normed_two, saved_two = norm_forward(second_in, vec_f[2], vec_f[3])
    normed_two = to_bfloat(normed_two)
    hidden_pre = jnp.einsum(
        "cpd,df->cpf", normed_two, w_up, preferred_element_type=jnp.float32
    ) + bias_up.astype(jnp.float32)
    hidden_act, gelu_pull = jax.vjp(partial(jax.nn.gelu, approximate=False), hidden_pre)
    hidden_low = to_bfloat(hidden_act)
    block_out = (
        second_in
        + jnp.einsum("cpf,fd->cpd", hidden_low, w_down, preferred_element_type=jnp.float32)
        + vec_f[12]
    )
    valid_patch = jnp.arange(PATCHES_THIRD_2, dtype=jnp.int32)[None, :] < patches[:, None]
    slot_weight = (frame_index < tubelet_stack).astype(jnp.float32)

    def learner(block_in, gain_row, shift_row, map_weight):
        normed, unused = norm_forward(block_in, gain_row, shift_row)
        logits = jnp.einsum("cpd,dm->cpm", normed, map_weight, precision=HIGH_ACCURACY)
        logits = jnp.where(valid_patch[..., None], logits, -1e30)
        token_maps = jax.nn.softmax(logits, axis=1)
        pooled_part = jnp.einsum(
            "c,cpm,cpd->cd", slot_weight, token_maps, block_in, precision=HIGH_ACCURACY
        )
        gram_matrix = jnp.einsum("cpm,cpn->cmn", token_maps, token_maps, precision=HIGH_ACCURACY)
        correlation_part = slot_weight * (
            jnp.sum(gram_matrix, axis=(1, 2)) - jnp.trace(gram_matrix, axis1=1, axis2=2)
        )
        return (pooled_part, correlation_part)

    (pooled_part, correlation_part), learner_pull = jax.vjp(
        learner, block_out, vec_f[4], vec_f[5], w_map.astype(jnp.float32)
    )
    pooled_sum, correlation_sum = lax.psum((pooled_part, correlation_part), "frame")

    def head_map(pooled_in, gain_row, shift_row, proj_weight):
        pooled_mean = pooled_in / (NMAP * tubelet_stack).astype(jnp.float32)[:, None]
        normed, unused = norm_forward(pooled_mean, gain_row, shift_row)
        embedding = jnp.dot(
            normed, proj_weight, precision=HIGH_ACCURACY, preferred_element_type=jnp.float32
        )
        return embedding * lax.rsqrt(jnp.sum(embedding * embedding, -1, keepdims=True) + 1e-06)

    normalized_embedding, head_pull = jax.vjp(
        head_map, pooled_sum, vec_f[6], vec_f[7], w_proj.astype(jnp.float32)
    )
    embed_all, correlation_all = (
        lax.all_gather(normalized_embedding, "batch", axis=0, tiled=True),
        lax.all_gather(correlation_sum, "batch", axis=0, tiled=True),
    )
    selected_rows = jnp.concatenate([positive[:, None], negatives], axis=1)

    def contrast(embedding_input):
        local_row_set = lax.dynamic_slice_in_dim(
            embedding_input, index_of_batch * CLIPS_PER_BATCH, CLIPS_PER_BATCH, 0
        )
        similarity_matrix = (
            jnp.einsum(
                "yg,yeg->ye", local_row_set, embedding_input[selected_rows], precision=HIGH_ACCURACY
            )
            / SOFTMAX_TEMPER
        )
        return (
            jnp.sum(jax.nn.logsumexp(similarity_matrix, axis=1) - similarity_matrix[:, 0])
            / every_clip_rows
        )

    contrast_part, contrast_pull = jax.vjp(contrast, embed_all)
    (grad_embed_all,) = contrast_pull(jnp.ones_like(contrast_part))
    grad_unit = lax.psum_scatter(grad_embed_all, "batch", scatter_dimension=0, tiled=True)
    frame_total_count = jnp.sum(valid_tubelet_count).astype(jnp.float32)
    head_mask = (frame_index == 0).astype(jnp.float32)
    pooled_gradient, grad_final_gain, grad_final_shift, grad_proj = head_pull(grad_unit)
    grad_block, grad_learn_gain, grad_learn_shift, grad_map = learner_pull(
        (
            pooled_gradient,
            jnp.full((CLIPS_PER_BATCH,), DECAY_PENALTY / frame_total_count, jnp.float32),
        )
    )
    grad_mlp = to_bfloat(grad_block)
    grad_down_bias = jnp.sum(grad_mlp.astype(jnp.float32), (0, 1))
    grad_w_down = jnp.einsum(
        "cpf,cpd->fd", hidden_low, grad_mlp, preferred_element_type=jnp.float32
    )
    grad_hidden = jnp.einsum("cpd,fd->cpf", grad_mlp, w_down, preferred_element_type=jnp.float32)
    (grad_pre,) = gelu_pull(grad_hidden)
    grad_pre_low = to_bfloat(grad_pre)
    grad_up_bias = jnp.sum(grad_pre_low.astype(jnp.float32), (0, 1))
    grad_w_up = jnp.einsum(
        "cpd,cpf->df", normed_two, grad_pre_low, preferred_element_type=jnp.float32
    )
    grad_normed_two = jnp.einsum(
        "cpf,df->cpd", grad_pre_low, w_up, preferred_element_type=jnp.float32
    )
    grad_in_two, grad_gain_two, grad_shift_two = norm_backward(grad_normed_two, vec_f[2], saved_two)
    grad_second = grad_block + grad_in_two
    grad_attn = to_bfloat(grad_second)
    grad_out_bias = jnp.sum(grad_attn.astype(jnp.float32), (0, 1))
    grad_w_out = jnp.einsum(
        "cpe,cpd->ed", attended_reduced, grad_attn, preferred_element_type=jnp.float32
    )
    grad_attended = to_bfloat(
        jnp.einsum("cpd,ed->cpe", grad_attn, w_out, preferred_element_type=jnp.float32)
    ).reshape(CLIPS_PER_BATCH, PATCHES_THIRD_2, HEAD_COUNT, HEAD_FEATURES)
    row_delta = jnp.einsum("cqhd,chqd->chq", grad_attended.astype(jnp.float32), head_attended_rows)
    zeroed_query = jnp.zeros(
        (CLIPS_PER_BATCH, PATCHES_THIRD_2, HEAD_COUNT, HEAD_FEATURES), jnp.float32
    )
    query_kv_piece = lax.all_gather(kv_local, "frame", axis=1, tiled=True)
    count_blocks, query_block_rows = block_plan(query_kv_piece.shape[1])

    def query_one_block(block_index, query_gradient):
        block_start = block_index * query_block_rows
        key_value_block = lax.dynamic_slice_in_dim(
            query_kv_piece, block_index * query_block_rows, query_block_rows, 1
        )
        scores, key_ok, head_keys, head_values = block_scores(key_value_block, block_start)
        prob_tile = jnp.where(key_ok, jnp.exp(scores - log_sum[..., None]), 0.0)
        grad_prob = jnp.einsum(
            "cqhd,ckhd->chqk", grad_attended, head_values, preferred_element_type=jnp.float32
        )
        grad_score = to_bfloat(prob_tile * (grad_prob - row_delta[..., None]))
        return (
            query_gradient
            + jnp.einsum(
                "chqk,ckhd->cqhd", grad_score, head_keys, preferred_element_type=jnp.float32
            )
            * score_scale
        )

    query_gradient = lax.fori_loop(0, count_blocks, query_one_block, zeroed_query)
    own_keys = kv_local[..., :width_of_model].reshape(
        CLIPS_PER_BATCH, PATCHES_THIRD_2, HEAD_COUNT, HEAD_FEATURES
    )
    own_values = kv_local[..., width_of_model:].reshape(
        CLIPS_PER_BATCH, PATCHES_THIRD_2, HEAD_COUNT, HEAD_FEATURES
    )
    own_ok = key_mask(frame_index * PATCHES_THIRD_2, PATCHES_THIRD_2)[:, None, None, :]
    row_pieces = (
        query_matrix.astype(jnp.float32),
        grad_attended.astype(jnp.float32),
        log_sum.transpose(0, 2, 1),
        row_delta.transpose(0, 2, 1),
    )
    query_piece = lax.all_gather(
        row_pieces[0].astype(jnp.bfloat16), "frame", axis=1, tiled=True
    ).astype(jnp.float32)
    grad_out_piece = lax.all_gather(
        row_pieces[1].astype(jnp.bfloat16), "frame", axis=1, tiled=True
    ).astype(jnp.float32)
    lse_piece = lax.all_gather(
        row_pieces[2].astype(jnp.bfloat16), "frame", axis=1, tiled=True
    ).astype(jnp.float32)
    delta_piece = lax.all_gather(
        row_pieces[3].astype(jnp.bfloat16), "frame", axis=1, tiled=True
    ).astype(jnp.float32)
    count_blocks, own_block_rows = block_plan(query_piece.shape[1])

    def own_one_block(block_index, running):
        key_gradient, value_gradient = running
        offset = block_index * own_block_rows
        query_block = to_bfloat(lax.dynamic_slice_in_dim(query_piece, offset, own_block_rows, 1))
        grad_out_block = to_bfloat(
            lax.dynamic_slice_in_dim(grad_out_piece, offset, own_block_rows, 1)
        )
        lse_block = lax.dynamic_slice_in_dim(lse_piece, offset, own_block_rows, 1).transpose(
            0, 2, 1
        )
        delta_block = lax.dynamic_slice_in_dim(delta_piece, offset, own_block_rows, 1).transpose(
            0, 2, 1
        )
        scores = (
            jnp.einsum("cqhd,ckhd->chqk", query_block, own_keys, preferred_element_type=jnp.float32)
            * score_scale
        )
        scores = jnp.where(own_ok, scores, -1e30)
        prob_tile = jnp.where(own_ok, jnp.exp(scores - lse_block[..., None]), 0.0)
        grad_prob = jnp.einsum(
            "cqhd,ckhd->chqk", grad_out_block, own_values, preferred_element_type=jnp.float32
        )
        grad_score = to_bfloat(prob_tile * (grad_prob - delta_block[..., None]))
        key_gradient = (
            key_gradient
            + jnp.einsum(
                "chqk,cqhd->ckhd", grad_score, query_block, preferred_element_type=jnp.float32
            )
            * score_scale
        )
        value_gradient = value_gradient + jnp.einsum(
            "chqk,cqhd->ckhd",
            to_bfloat(prob_tile),
            grad_out_block,
            preferred_element_type=jnp.float32,
        )
        return (key_gradient, value_gradient)

    grad_key_own, grad_value_own = lax.fori_loop(
        0, count_blocks, own_one_block, (zeroed_query, zeroed_query)
    )
    gradient_key_value_local = to_bfloat(
        jnp.concatenate(
            [
                grad_key_own.reshape(CLIPS_PER_BATCH, PATCHES_THIRD_2, width_of_model),
                grad_value_own.reshape(CLIPS_PER_BATCH, PATCHES_THIRD_2, width_of_model),
            ],
            -1,
        )
    )
    gradient_query_key_value = jnp.concatenate(
        [
            to_bfloat(query_gradient).reshape(CLIPS_PER_BATCH, PATCHES_THIRD_2, width_of_model),
            gradient_key_value_local,
        ],
        -1,
    )
    grad_query_bias = jnp.sum(
        gradient_query_key_value[..., :width_of_model].astype(jnp.float32), (0, 1)
    )
    grad_value_bias = jnp.sum(
        gradient_query_key_value[..., 2 * width_of_model :].astype(jnp.float32), (0, 1)
    )
    grad_w_qkv = jnp.einsum(
        "cpd,cpe->de", normed_one, gradient_query_key_value, preferred_element_type=jnp.float32
    )
    grad_normed_one = jnp.einsum(
        "cpe,de->cpd", gradient_query_key_value, w_qkv, preferred_element_type=jnp.float32
    )
    grad_in_one, grad_gain_one, grad_shift_one = norm_backward(grad_normed_one, vec_f[0], saved_one)
    gradient_entry = grad_second + grad_in_one
    gradient_entry_low = to_bfloat(gradient_entry).reshape(
        CLIPS_PER_BATCH * PATCHES_THIRD_2, width_of_model
    )
    grad_w_embed = jnp.einsum(
        "rt,rd->td", rows_of_pixels, gradient_entry_low, preferred_element_type=jnp.float32
    )
    grad_embed_bias = jnp.sum(gradient_entry, (0, 1))
    grad_pos_space = jnp.zeros((P0 + P1 + PATCHES_THIRD_2, width_of_model), jnp.float32)
    current = lax.dynamic_slice_in_dim(grad_pos_space, start_rows[0], PATCHES_THIRD_2, 0)
    grad_pos_space = lax.dynamic_update_slice_in_dim(
        grad_pos_space, current + gradient_entry[0], start_rows[0], 0
    )
    grad_pos_time = lax.dynamic_update_slice_in_dim(
        jnp.zeros((TMAX, width_of_model), jnp.float32), grad_embed_bias[None], frame_index, 0
    )
    grad_vectors = jnp.stack(
        [
            grad_gain_one,
            grad_shift_one,
            grad_gain_two,
            grad_shift_two,
            grad_learn_gain,
            grad_learn_shift,
            grad_final_gain * head_mask,
            grad_final_shift * head_mask,
            grad_embed_bias,
            grad_query_bias,
            grad_value_bias,
            grad_out_bias,
            grad_down_bias,
        ]
    )
    flat_grad = jnp.concatenate(
        [
            piece_grad.reshape(-1)
            for piece_grad in (
                grad_w_embed,
                grad_w_qkv,
                grad_w_out,
                grad_w_up,
                grad_w_down,
                grad_proj * head_mask,
                grad_map,
                grad_pos_space,
                grad_pos_time,
                grad_vectors,
                grad_up_bias,
            )
        ]
    )
    grad_shard = lax.psum_scatter(flat_grad, ("batch", "frame"), scatter_dimension=0, tiled=True)
    contrast_keep = jnp.where(frame_index == 0, contrast_part, 0.0)
    square_sum, contrast_total = lax.psum(
        (jnp.sum(grad_shard * grad_shard), contrast_keep), ("batch", "frame")
    )
    grad_norm = jnp.sqrt(square_sum)
    loss_value = contrast_total + DECAY_PENALTY * jnp.sum(correlation_all) / frame_total_count
    clipped = grad_shard * jnp.minimum(1.0, CLIP_AT / grad_norm)
    new_first = BETA_ONE * first_moment + (1.0 - BETA_ONE) * clipped
    new_second = BETA_TWO * second_moment + (1.0 - BETA_TWO) * clipped * clipped
    step_count = adam_step[0].astype(jnp.float32)
    update = (
        new_first
        / (1.0 - BETA_ONE**step_count)
        / (jnp.sqrt(new_second / (1.0 - BETA_TWO**step_count)) + ADAM_EPS)
    )
    new_master = master - RATE * (update + DECAY * master)
    return (new_master, new_first, new_second, to_bfloat(new_master), loss_value, grad_norm)


MESH = pl.DeviceIdType.MESH
T=144
SPA=32

class Sends:
    def __init__(self, sem): self.sem=sem; self.n=0; self.items=[]
    def go(self, src, dst, rsem, dev, pred=None):
        c = pltpu.make_async_remote_copy(src_ref=src, dst_ref=dst, send_sem=self.sem.at[self.n], recv_sem=rsem, device_id=dev, device_id_type=MESH)
        self.n += 1
        if pred is None: c.start()
        else:
            @pl.when(pred)
            def _(): c.start()
        self.items.append((c,pred))
    def prep(self, src, dst, rsem, dev, pred=None):
        c = pltpu.make_async_remote_copy(src_ref=src, dst_ref=dst, send_sem=self.sem.at[self.n], recv_sem=rsem, device_id=dev, device_id_type=MESH)
        self.n += 1
        self.items.append((c,pred))
        def fire():
            if pred is None: c.start()
            else:
                @pl.when(pred)
                def _(): c.start()
        return fire
    def drain(self):
        for c,pred in self.items:
            if pred is None: c.wait_send()
            else:
                @pl.when(pred)
                def _(): c.wait_send()

def both(a,b):
    if a is None: return b
    if b is None: return a
    return jnp.logical_and(a,b)

def make_ag(spa=SPA):
    A=(0,spa); A1=(0,spa//2); A2=(spa//2,spa//2)
    nb=T-spa
    B=(spa,nb); B1=(spa,nb//2); B2=(spa+nb//2,nb//2)
    FULL=(0,T)
    def kernel(x_ref, out, ssem, lsem, zB, xB, yB, xBh, yBh, pA, zA, pown, pzB, pxB, pyB, pxBh, pyBh, ppA, pzA):
        b=lax.axis_index("batch"); f=lax.axis_index("frame")
        x=b%2; y=b//2; z=f//2; c=f%2
        bx=y*2+(1-x); by=(1-y)*2+x; bd=(1-y)*2+(1-x)
        X=(bx,f); Y=(by,f); Pn=(b,z*2+(1-c)); UP=(b,f+2); DN=(b,f-2)
        up=z<3; dn=z>0
        bar=pltpu.get_barrier_semaphore()
        for d,p in ((X,None),(Y,None),(Pn,None),(UP,up),(DN,dn)):
            if p is None: pl.semaphore_signal(bar,inc=1,device_id=d,device_id_type=MESH)
            else:
                @pl.when(p)
                def _(): pl.semaphore_signal(bar,inc=1,device_id=d,device_id_type=MESH)
        pl.semaphore_wait(bar, 4+(z*(3-z)+1)//3)
        S=Sends(ssem)
        def blk(bb,zz,part): return out.at[bb*8+zz*2+c, pl.ds(part[0],part[1])]
        def send(bb,zz,part,rsem,dev,pred=None,own=False):
            dst=blk(bb,zz,part)
            src=x_ref.at[pl.ds(part[0],part[1])] if own else dst
            S.go(src,dst,rsem,dev,pred)
        def wait(bb,zz,part,rsem):
            r=blk(bb,zz,part)
            pltpu.make_async_remote_copy(src_ref=r,dst_ref=r,send_sem=ssem.at[0],recv_sem=rsem,device_id=Pn,device_id_type=MESH).wait_recv()
        def waitp(pred,*a):
            if pred is None: wait(*a)
            else:
                @pl.when(pred)
                def _(): wait(*a)
        lc=pltpu.make_async_copy(x_ref, blk(b,z,FULL), lsem);
        send(b,z,A,pA.at[0],X,own=True); send(b,z,A,pA.at[1],Y,own=True)
        send(b,z,B,zB.at[z],UP,up,True); send(b,z,B,zB.at[z],DN,dn,True)
        send(b,z,B,xB.at[z],X,own=True); send(b,z,B,yB.at[z],Y,own=True)
        send(b,z,A,zA.at[z,0],UP,up,True); send(b,z,A,zA.at[z,0],DN,dn,True)
        send(b,z,FULL,pown.at[0],Pn,own=True)
        lc.start()
        pz=[]
        def pwait(*a): pz.append(a)
        pwait(None,b,z,FULL,pown.at[0])
        def zfwdA(bb,part,i,ps):
            send(bb,z,part,zA.at[z,i],UP,up); send(bb,z,part,zA.at[z,i],DN,dn)
            send(bb,z,part,ps,Pn); pwait(None,bb,z,part,ps)
        wait(bx,z,A,pA.at[0]); send(bx,z,A1,pA.at[2],Y); zfwdA(bx,A,1,ppA.at[0])
        wait(by,z,A,pA.at[1]); send(by,z,A2,pA.at[3],X); zfwdA(by,A,2,ppA.at[1])
        wait(bd,z,A1,pA.at[2]); zfwdA(bd,A1,3,ppA.at[2])
        wait(bd,z,A2,pA.at[3]); zfwdA(bd,A2,4,ppA.at[3])
        def xyB(zz,pred):
            waitp(pred,bx,zz,B,xB.at[zz]); send(bx,zz,B1,yBh.at[zz],Y,pred); send(bx,zz,B,pxB.at[zz],Pn,pred); pwait(pred,bx,zz,B,pxB.at[zz])
            waitp(pred,by,zz,B,yB.at[zz]); send(by,zz,B2,xBh.at[zz],X,pred); send(by,zz,B,pyB.at[zz],Pn,pred); pwait(pred,by,zz,B,pyB.at[zz])
        xyB(z,None)
        for d in (1,2,3):
            for s in (1,-1):
                zz=z+s*d
                pred=(zz<4) if s>0 else (zz>=0)
                nxt,np_=(DN,dn) if s>0 else (UP,up)
                waitp(pred,b,zz,B,zB.at[zz])
                send(b,zz,B,zB.at[zz],nxt,both(pred,np_))
                send(b,zz,B,xB.at[zz],X,pred); send(b,zz,B,yB.at[zz],Y,pred)
                send(b,zz,B,pzB.at[zz],Pn,pred); pwait(pred,b,zz,B,pzB.at[zz])
            for s in (1,-1):
                zz=z+s*d
                pred=(zz<4) if s>0 else (zz>=0)
                nxt,np_=(DN,dn) if s>0 else (UP,up)
                for i,(bb,part) in enumerate(((b,A),(bx,A),(by,A),(bd,A1),(bd,A2))):
                    waitp(pred,bb,zz,part,zA.at[zz,i]); send(bb,zz,part,zA.at[zz,i],nxt,both(pred,np_))
                    send(bb,zz,part,pzA.at[zz,i],Pn,pred); pwait(pred,bb,zz,part,pzA.at[zz,i])
            for s in (1,-1):
                zz=z+s*d
                pred=(zz<4) if s>0 else (zz>=0)
                xyB(zz,pred)
        for zz in range(4):
            wait(bd,zz,B1,yBh.at[zz]); send(bd,zz,B1,pyBh.at[zz],Pn); pwait(None,bd,zz,B1,pyBh.at[zz])
            wait(bd,zz,B2,xBh.at[zz]); send(bd,zz,B2,pxBh.at[zz],Pn); pwait(None,bd,zz,B2,pxBh.at[zz])
        for a in pz: waitp(*a)
        lc.wait()
        S.drain()
    D=pltpu.SemaphoreType.DMA
    def ag(xin, cid=0):
        return pl.pallas_call(kernel, out_shape=jax.ShapeDtypeStruct((32,T,16,128),jnp.bfloat16),
            in_specs=[pl.BlockSpec(memory_space=pltpu.VMEM)], out_specs=pl.BlockSpec(memory_space=pl.ANY),
            scratch_shapes=[D((160,)),D]+[D((4,))]*5+[D((4,)),D((4,5)),D((1,))]+[D((4,))]*5+[D((4,)),D((4,5))],
            compiler_params=pltpu.CompilerParams(collective_id=cid,has_side_effects=True))(xin)
    return ag


def make_rsx(spa=16):
    nb=T-spa
    A=(0,spa); A1=(0,spa//2); A2=(spa//2,spa//2)
    B=(spa,nb); B1=(spa,nb//2); B2=(spa+nb//2,nb//2)
    FULL=(0,T)
    def kernel(pix, h1, att, h2, act, dx0, dqkv, dattn, dpre, dmlp, tail, gout, nout,
               PS, R, h2T, LX, LY, LHX, LHY, LZB, LZA, LPA, out, C, CB_, CR_, NB, ssem, psem, stsem, csem, nsem, nsend, s_hx, s_hy, s_x, s_y, s_zb, s_za, s_pa):
        b=lax.axis_index("batch"); f=lax.axis_index("frame")
        x=b%2; y=b//2; z=f//2; c=f%2
        bx=y*2+(1-x); by=(1-y)*2+x; bd=(1-y)*2+(1-x)
        X=(bx,f); Y=(by,f); Pn=(b,z*2+(1-c)); UP=(b,f+2); DN=(b,f-2)
        up=z<3; dn=z>0
        t=z//2
        k=b*8+f
        def dev_of(kk): return (kk//8,kk%8)
        bar=pltpu.get_barrier_semaphore()
        def greet(d,_):
            pl.semaphore_signal(bar,inc=1,device_id=dev_of((k+d)%32),device_id_type=MESH); return 0
        lax.fori_loop(1,32,greet,0)
        zo=[3*(1-t), 2-t, (1-z)*(1-t)+(5-z)*t, z]
        order=[]
        for zz in zo: order += [(bd,zz)]
        for zz in zo: order += [(bx,zz),(by,zz)]
        for zz in zo: order += [(b,zz)]
        h2T[...]=h2[...].T
        TN_=(((0,),(0,)),((),()))
        def put(dst,r,m):
            rows=r.shape[0]
            r=r.astype(jnp.bfloat16)
            for s in range(rows//16):
                for j in range(m):
                    dst[s*m+j]=r[s*16:(s+1)*16,j*128:(j+1)*128]
        def col(a,i,n): return a[:,pl.ds(pl.multiple_of(i*n,128),n)]
        def comp(kk,dst):
            def mm(a,bb_,dims): return lax.dot_general(a,bb_,dims,preferred_element_type=jnp.float32)
            @pl.when(kk<4)
            def _(): put(dst,mm(col(pix,kk,384),dx0[...],TN_),6)
            @pl.when(jnp.logical_and(kk>=4,kk<10))
            def _(): put(dst,mm(col(h1,kk-4,128),dqkv[...],TN_),18)
            @pl.when(jnp.logical_and(kk>=10,kk<12))
            def _(): put(dst,mm(col(att,kk-10,384),dattn[...],TN_),6)
            @pl.when(jnp.logical_and(kk>=12,kk<20))
            def _(): put(dst,mm(h2T[pl.ds(pl.multiple_of((kk-12)*96,16),96)],dpre[...],(((1,),(0,)),((),()))),24)
            @pl.when(jnp.logical_and(kk>=20,kk<28))
            def _(): put(dst,mm(col(act,kk-20,384),dmlp[...],TN_),6)
            @pl.when(kk>=28)
            def _():
                def cp(i,_):
                    ds=pl.ds(i*8,8); dst[ds]=tail[kk-28,ds]; return 0
                lax.fori_loop(0,T//8,cp,0)
        def pick(i):
            g=jnp.where(i<4,i,jnp.where(i<12,(i-4)//2,i-12))
            zz=jnp.where(g==0,zo[0],jnp.where(g==1,zo[1],jnp.where(g==2,zo[2],zo[3])))
            bb=jnp.where(i<4,bd,jnp.where(i<12,jnp.where(i%2==0,bx,by),b))
            return bb,zz
        def pcopy(i):
            bb,zz=pick(i)
            return pltpu.make_async_remote_copy(src_ref=PS.at[16+i%4],dst_ref=R.at[bb,zz],send_sem=stsem.at[i%4],recv_sem=psem.at[bb,zz],device_id=Pn,device_id_type=MESH)
        S=Sends(ssem)
        def acc(dst, srcs, n, step=8):
            def body(i,_):
                ds=pl.ds(i*step,step)
                v=srcs[0][ds].astype(jnp.float32)
                for s in srcs[1:]: v=v+s[ds].astype(jnp.float32)
                dst[ds]=v.astype(dst.dtype)
                return 0
            lax.fori_loop(0,n//step,body,0)
        def sub(ref,part): return ref.at[pl.ds(part[0],part[1])]
        def ready(i):
            bb,zz=order[i]
            pltpu.make_async_remote_copy(src_ref=R.at[bb,zz],dst_ref=R.at[bb,zz],send_sem=ssem.at[0],recv_sem=psem.at[bb,zz],device_id=Pn,device_id_type=MESH).wait_recv()
        def wrecv(ref,sem):
            pltpu.make_async_remote_copy(src_ref=ref,dst_ref=ref,send_sem=ssem.at[0],recv_sem=sem,device_id=Pn,device_id_type=MESH).wait_recv()
        plan={}
        def at(h,fn): plan.setdefault(h,[]).append(fn)
        def diag(i,zz):
            f1=S.prep(sub(PS.at[bd*4+zz],B1), LHY.at[zz], s_hy.at[zz], Y)
            f2=S.prep(sub(PS.at[bd*4+zz],B2), LHX.at[zz], s_hx.at[zz], X)
            def fn():
                ready(i)
                acc(sub(PS.at[bd*4+zz],B), [sub(PS.at[bd*4+zz],B), sub(R.at[bd,zz],B)], nb)
                f1(); f2()
            return fn
        def chainA(bi,bb,ds=(3,2,1)):
            fns=[]
            for d in ds:
                for s in (1,-1):
                    zz=z+s*d
                    pred=(zz<4) if s>0 else (zz>=0)
                    frm=dn if s>0 else up
                    dev=UP if s>0 else DN
                    di=0 if s>0 else 1
                    fire=S.prep(sub(PS.at[bb*4+zz],A), LZA.at[di,zz,bi], s_za.at[di,zz,bi], dev, pred)
                    def fn(zz=zz,pred=pred,frm=frm,di=di,fire=fire):
                        @pl.when(jnp.logical_and(pred,frm))
                        def _():
                            wrecv(LZA.at[di,zz,bi], s_za.at[di,zz,bi])
                            acc(sub(PS.at[bb*4+zz],A),[sub(PS.at[bb*4+zz],A),sub(R.at[bb,zz],A),LZA.at[di,zz,bi]],spa)
                        @pl.when(jnp.logical_and(pred,jnp.logical_not(frm)))
                        def _():
                            acc(sub(PS.at[bb*4+zz],A),[sub(PS.at[bb*4+zz],A),sub(R.at[bb,zz],A)],spa)
                        fire()
                    fns.append(fn)
            return fns
        def sides(i,zz):
            fx=S.prep(sub(PS.at[bx*4+zz],B), LX.at[zz], s_x.at[zz], X)
            fy=S.prep(sub(PS.at[by*4+zz],B), LY.at[zz], s_y.at[zz], Y)
            def fn():
                ready(4+2*i); ready(5+2*i)
                wrecv(LHY.at[zz], s_hy.at[zz])
                acc(sub(PS.at[bx*4+zz],B1),[sub(PS.at[bx*4+zz],B1),sub(R.at[bx,zz],B1),LHY.at[zz]],nb//2)
                acc(sub(PS.at[bx*4+zz],B2),[sub(PS.at[bx*4+zz],B2),sub(R.at[bx,zz],B2)],nb//2)
                fx()
                wrecv(LHX.at[zz], s_hx.at[zz])
                acc(sub(PS.at[by*4+zz],B2),[sub(PS.at[by*4+zz],B2),sub(R.at[by,zz],B2),LHX.at[zz]],nb//2)
                acc(sub(PS.at[by*4+zz],B1),[sub(PS.at[by*4+zz],B1),sub(R.at[by,zz],B1)],nb//2)
                fy()
            return fn
        for i,zz in enumerate(zo): at(2*i+3,diag(i,zz))
        for j,d in enumerate((3,2,1)):
            for fn in chainA(0,bd,(d,)): at(10+2*j,fn)
        for i,zz in enumerate(zo): at(13+4*i,sides(i,zz))
        for bi,bb in ((1,bx),(2,by)):
            for j,d in enumerate((3,2,1)):
                for fn in chainA(bi,bb,(d,)): at(26+2*j,fn)
        def produce(h,_):
            i=h//2; own=h%2
            bb,zz=pick(i)
            @pl.when(own==0)
            def _():
                @pl.when(i>=4)
                def _(): pcopy(i-4).wait_send()
            kk=bb*8+zz*2+jnp.where(own==1,c,1-c)
            comp(kk,PS.at[jnp.where(own==1,bb*4+zz,16+i%4)])
            @pl.when(own==0)
            def _():
                @pl.when(i==0)
                def _(): pl.semaphore_wait(bar,31)
                pcopy(i).start()
            for hh,fns in sorted(plan.items()):
                @pl.when(h==hh)
                def _():
                    for fn in fns: fn()
            return 0
        lax.fori_loop(0,32,produce,0)
        for i in range(4): ready(12+i)
        for fn in chainA(3,b): fn()
        for i,zz in enumerate(zo[:3]):
            wrecv(LX.at[zz],s_x.at[zz]); wrecv(LY.at[zz],s_y.at[zz])
            isup=zz>z
            inc=jnp.logical_or(jnp.logical_and(isup,dn),jnp.logical_and(jnp.logical_not(isup),up))
            di=jnp.where(isup,0,1)
            base=[sub(PS.at[b*4+zz],B),sub(R.at[b,zz],B),LX.at[zz],LY.at[zz]]
            @pl.when(inc)
            def _():
                wrecv(LZB.at[di,zz],s_zb.at[di,zz])
                acc(sub(PS.at[b*4+zz],B),base+[LZB.at[di,zz]],nb)
            @pl.when(jnp.logical_not(inc))
            def _(): acc(sub(PS.at[b*4+zz],B),base,nb)
            S.go(sub(PS.at[b*4+zz],B),LZB.at[0,zz],s_zb.at[0,zz],UP,isup)
            S.go(sub(PS.at[b*4+zz],B),LZB.at[1,zz],s_zb.at[1,zz],DN,jnp.logical_not(isup))
        def totA(bi,bb,part,extra=(),dst=None):
            dst = dst if dst is not None else sub(PS.at[bb*4+z],part)
            srcs=[sub(PS.at[bb*4+z],part),sub(R.at[bb,z],part)]+list(extra)
            o=part[0]; n=part[1]
            l0=LZA.at[0,z,bi,pl.ds(o,n)]; l1=LZA.at[1,z,bi,pl.ds(o,n)]
            @pl.when(jnp.logical_and(up,dn))
            def _(): acc(dst,srcs+[l0,l1],n)
            @pl.when(jnp.logical_not(up))
            def _(): acc(dst,srcs+[l0],n)
            @pl.when(jnp.logical_not(dn))
            def _(): acc(dst,srcs+[l1],n)
        for bi in range(4):
            @pl.when(dn)
            def _(): wrecv(LZA.at[0,z,bi],s_za.at[0,z,bi])
            @pl.when(up)
            def _(): wrecv(LZA.at[1,z,bi],s_za.at[1,z,bi])
            if bi==0:
                totA(0,bd,A1); S.go(sub(PS.at[bd*4+z],A1),LPA.at[0,pl.ds(0,spa//2)],s_pa.at[0],Y)
                totA(0,bd,A2); S.go(sub(PS.at[bd*4+z],A2),LPA.at[1,pl.ds(0,spa//2)],s_pa.at[1],X)
            if bi==1:
                totA(1,bx,A2)
                wrecv(LPA.at[0,pl.ds(0,spa//2)],s_pa.at[0])
                totA(1,bx,A1,[LPA.at[0,pl.ds(0,spa//2)]])
                S.go(sub(PS.at[bx*4+z],A),LPA.at[2],s_pa.at[2],X)
            if bi==2:
                totA(2,by,A1)
                wrecv(LPA.at[1,pl.ds(0,spa//2)],s_pa.at[1])
                totA(2,by,A2,[LPA.at[1,pl.ds(0,spa//2)]])
                S.go(sub(PS.at[by*4+z],A),LPA.at[3],s_pa.at[3],Y)
        wrecv(LX.at[z],s_x.at[z]); wrecv(LY.at[z],s_y.at[z])
        base=[sub(PS.at[b*4+z],B),sub(R.at[b,z],B),LX.at[z],LY.at[z]]
        @pl.when(dn)
        def _(): wrecv(LZB.at[0,z],s_zb.at[0,z])
        @pl.when(up)
        def _(): wrecv(LZB.at[1,z],s_zb.at[1,z])
        @pl.when(jnp.logical_and(up,dn))
        def _(): acc(sub(out,B),base+[LZB.at[0,z],LZB.at[1,z]],nb)
        @pl.when(jnp.logical_not(up))
        def _(): acc(sub(out,B),base+[LZB.at[0,z]],nb)
        @pl.when(jnp.logical_not(dn))
        def _(): acc(sub(out,B),base+[LZB.at[1,z]],nb)
        wrecv(LPA.at[2],s_pa.at[2]); wrecv(LPA.at[3],s_pa.at[3])
        totA(3,b,A,[LPA.at[2],LPA.at[3]],dst=sub(out,A))
        def sq(i,a):
            v=out[i]; v=v*v
            return a+v[:8]+v[8:]
        NB[k]=lax.fori_loop(0,T,sq,jnp.zeros((8,128),jnp.float32))
        def ncopy(d):
            return pltpu.make_async_remote_copy(src_ref=NB.at[k],dst_ref=NB.at[k],send_sem=nsend.at[d],recv_sem=nsem.at[k],device_id=dev_of((k+d)%32),device_id_type=MESH)
        def nstart(d,_):
            ncopy(d).start(); return 0
        lax.fori_loop(1,32,nstart,0)
        CR=1440
        def untile(m,s0,n,t0):
            def body(s,_):
                for j in range(m):
                    C[pl.ds(CR+s0+s*16*m+j,16,stride=m),:]=out[t0+s*m+j]
                return 0
            lax.fori_loop(0,n,body,0)
        def plain(t0,n):
            def body(s,_):
                C[pl.ds(CR+(t0+s)*16,16),:]=out[t0+s]; return 0
            lax.fori_loop(0,n,body,0)
        def within(lo,hi): return jnp.logical_and(k>=lo,k<hi)
        @pl.when(jnp.logical_or(jnp.logical_or(within(0,4),within(10,12)),within(20,28)))
        def _(): untile(6,0,24,0)
        @pl.when(within(4,10))
        def _(): untile(18,0,8,0)
        @pl.when(within(12,20))
        def _(): untile(24,0,6,0)
        @pl.when(k==28)
        def _(): untile(4,0,36,0)
        @pl.when(k==29)
        def _():
            untile(4,0,12,0); plain(48,96)
        @pl.when(k>=30)
        def _(): plain(0,T)
        def carry(i,_):
            CB_[pl.ds(i*96,96)]=C[pl.ds(2304+i*96,96),:].astype(jnp.bfloat16); return 0
        lax.fori_loop(0,CR//96,carry,0)
        def cdesc(): return pltpu.make_async_remote_copy(src_ref=CB_,dst_ref=CR_,send_sem=csem.at[0],recv_sem=csem.at[1],device_id=dev_of((k+1)%32),device_id_type=MESH)
        @pl.when(k<31)
        def _(): cdesc().start()
        C[pl.ds(CR+2304,8),:]=jnp.zeros((8,128),jnp.float32)
        def nwait(d,_):
            kk=(k+d)%32
            wrecv_(NB.at[kk],nsem.at[kk],nsend.at[0],Pn); return 0
        lax.fori_loop(1,32,nwait,0)
        def nsum(i,a): return a+NB[i]
        total=jnp.sum(lax.fori_loop(0,32,nsum,jnp.zeros((8,128),jnp.float32)),0,keepdims=True)
        nout[...]=jnp.broadcast_to(jnp.sum(total,1,keepdims=True),(8,128))
        @pl.when(k>0)
        def _():
            wrecv_(CR_,csem.at[1],csem.at[0],Pn)
            def uncarry(i,_):
                C[pl.ds(i*96,96),:]=CR_[pl.ds(i*96,96)].astype(jnp.float32); return 0
            lax.fori_loop(0,CR//96,uncarry,0)
        e=CR*128-(294912-289176)*k
        q=e//128; sh=e%128
        lane=lax.broadcasted_iota(jnp.int32,(96,128),1)
        def slide(i,_):
            r0=q+i*96
            a=pltpu.roll(C[pl.ds(r0,96),:],(128-sh)%128,1); b_=pltpu.roll(C[pl.ds(r0+1,96),:],(128-sh)%128,1)
            gout[pl.ds(i*96,96),:]=jnp.where(lane<128-sh,a,b_)
            return 0
        lax.fori_loop(0,24,slide,0)
        @pl.when(k<31)
        def _(): cdesc().wait_send()
        def ndone(d,_):
            ncopy(d).wait_send(); return 0
        lax.fori_loop(1,32,ndone,0)
        for i in range(12,16): pcopy(i).wait_send()
        S.drain()
    D=pltpu.SemaphoreType.DMA
    V=lambda *s: pltpu.VMEM(s+(16,128),jnp.bfloat16)
    VMs=pl.BlockSpec(memory_space=pltpu.VMEM)
    def rs(*args, cid=1):
        return pl.pallas_call(kernel, out_shape=(jax.ShapeDtypeStruct((2304,128),jnp.float32),jax.ShapeDtypeStruct((8,128),jnp.float32)),
            in_specs=[VMs]*11, out_specs=(VMs,VMs),
            scratch_shapes=[V(20,T),V(4,4,T),pltpu.VMEM((768,400),jnp.bfloat16),V(4,nb),V(4,nb),V(4,nb//2),V(4,nb//2),V(2,4,nb),V(2,4,4,spa),V(4,spa),
              pltpu.VMEM((T,16,128),jnp.float32),pltpu.VMEM((3752,128),jnp.float32),pltpu.VMEM((1440,128),jnp.bfloat16),pltpu.VMEM((1440,128),jnp.bfloat16),pltpu.VMEM((32,8,128),jnp.float32),
              D((80,)),D((4,4)),D((4,)),D((2,)),D((32,)),D((32,)),D((4,)),D((4,)),D((4,)),D((4,)),D((2,4)),D((2,4,4)),D((4,))],
            compiler_params=pltpu.CompilerParams(collective_id=cid,has_side_effects=True,vmem_limit_bytes=63*1024*1024))(*args)
    return rs

def wrecv_(ref,sem,ssem,dev):
    pltpu.make_async_remote_copy(src_ref=ref,dst_ref=ref,send_sem=ssem,recv_sem=sem,device_id=dev,device_id_type=MESH).wait_recv()


TOK=400; CB=208; NK=3200; NQ=1600; SUB=80; PADQ=512; CH=640
ROWS={"q":0,"k":400,"v":800,"qc":1200,"kc":1408,"vc":1616}
NT=(((1,),(1,)),((),())); NN=(((1,),(0,)),((),())); TN=(((0,),(0,)),((),()))
f32=jnp.float32; bf16=jnp.bfloat16

def dot(a,b,dims): return lax.dot_general(a,b,dims,preferred_element_type=f32)

def mesh_pos():
    b=lax.axis_index("batch"); f=lax.axis_index("frame")
    return b,f//2,f%2

def zbarrier(b,z,c):
    bar=pltpu.get_barrier_semaphore()
    for d in (1,2,3):
        pl.semaphore_signal(bar,inc=1,device_id=(b,((z+d)%4)*2+c),device_id_type=MESH)
    pl.semaphore_signal(bar,inc=1,device_id=(b,z*2+1-c),device_id_type=MESH)
    pl.semaphore_wait(bar,4)

def wrecv(ref,sem,dev):
    pltpu.make_async_remote_copy(src_ref=ref,dst_ref=ref,send_sem=sem,recv_sem=sem,device_id=dev,device_id_type=MESH).wait_recv()

def others(z):
    return [((z+d)%4) for d in (2,1,3)]

def unpack_c(src, dst, row):
    v=src.astype(f32)
    lane=lax.broadcasted_iota(jnp.int32,(CB,128),1)
    lo=jnp.where(lane<64,v,0.0)
    hi=jnp.where(lane<64,pltpu.roll(v,64,1),0.0)
    dst[pl.ds(row,CB)]=lo.astype(bf16)
    dst[pl.ds(row+CB,TOK-CB)]=hi[:TOK-CB].astype(bf16)

def pack_c(lo, hi):
    hi=jnp.concatenate([hi,jnp.zeros((2*CB-TOK,128),f32)],0)
    lane=lax.broadcasted_iota(jnp.int32,(CB,128),1)
    return jnp.where(lane<64,lo,pltpu.roll(hi,64,1)).astype(bf16)

def key_lanes(v, free, ok):
    e=lax.broadcasted_iota(jnp.int32,v.shape,1)-free
    v=jnp.where(jnp.logical_and(e>=1,e<4),1.0,v)
    return jnp.where(e==0,jnp.where(ok,0.0,-1e30),v)

def value_lanes(v, free):
    e=lax.broadcasted_iota(jnp.int32,v.shape,1)-free
    return jnp.where(jnp.logical_and(e>=0,e<3),1.0,v)

def three_lanes(v, free, col):
    hi=col.astype(bf16).astype(f32); mid=(col-hi).astype(bf16).astype(f32); lo=col-hi-mid
    e=lax.broadcasted_iota(jnp.int32,v.shape,1)-free
    return jnp.where(e==0,hi,jnp.where(e==1,mid,jnp.where(e==2,lo,v)))

def one_lane(v, free):
    e=lax.broadcasted_iota(jnp.int32,v.shape,1)-free
    return jnp.where(e==0,1.0,v)

def fwd_kernel(lims, sp, og, Q, KA, KB, VA, VB, QC, KC, VC, OA, OC, LA, LC,
               K, V, QCp, KCp, VCp, OB, OCp, S, Pb, ssem, lsem, osem, rq, rk, rv, rqc, rkc, rvc, pk, pv, pkc, pvc, ro, roc):
    b,z,c=mesh_pos()
    Pn=(b,z*2+1-c)
    dev=lambda zz:(b,zz*2+c)
    row=lambda zz: pl.multiple_of(zz*TOK,16)
    krow=lambda zz: pl.multiple_of((c*4+zz)*TOK,16)
    pkrow=lambda zz: pl.multiple_of(((1-c)*4+zz)*TOK,16)
    zbarrier(b,z,c)
    X=Sends(ssem)
    part=lambda g,n,ln: sp.at[g,pl.ds(ROWS[n],ln)]
    loc=[]
    def lcopy(src,dst):
        cp=pltpu.make_async_copy(src,dst,lsem.at[len(loc)]); cp.start(); loc.append(cp)
    for zz in others(z):
        X.go(part(zz,"kc",CB),KCp.at[c*4+z],rkc.at[z],dev(zz))
        X.go(part(zz,"qc",CB),QCp.at[z],rqc.at[z],dev(zz))
        X.go(part(zz,"vc",CB),VCp.at[c*4+z],rvc.at[z],dev(zz))
    lcopy(part(z,"kc",CB),KCp.at[c*4+z]); lcopy(part(z,"qc",CB),QCp.at[z]); lcopy(part(z,"vc",CB),VCp.at[c*4+z])
    X.go(part(z,"kc",CB),KCp.at[c*4+z],pkc.at[z],Pn)
    X.go(part(z,"vc",CB),VCp.at[c*4+z],pvc.at[z],Pn)
    for zz in others(z):
        X.go(part(zz,"k",TOK),K.at[pl.ds(krow(z),TOK)],rk.at[z],dev(zz))
        X.go(part(zz,"v",TOK),V.at[pl.ds(krow(z),TOK)],rv.at[z],dev(zz))
        X.go(part(zz,"q",TOK),Q.at[pl.ds(row(z),TOK)],rq.at[z],dev(zz))
    lcopy(part(z,"k",TOK),K.at[pl.ds(krow(z),TOK)])
    lcopy(part(z,"q",TOK),Q.at[pl.ds(row(z),TOK)])
    lcopy(part(z,"v",TOK),V.at[pl.ds(krow(z),TOK)])
    X.go(part(z,"k",TOK),K.at[pl.ds(krow(z),TOK)],pk.at[z],Pn)
    X.go(part(z,"v",TOK),V.at[pl.ds(krow(z),TOK)],pv.at[z],Pn)
    lane=lax.broadcasted_iota(jnp.int32,(TOK,128),1)
    patch=lax.broadcasted_iota(jnp.int32,(TOK,128),0)
    def key_ok(i):
        return patch<jnp.where((i%4)*2+i//4<lims[1],lims[0],0)
    def widen(i,_):
        ds=pl.ds(pl.multiple_of(i*TOK,16),TOK)
        ok=key_ok(i)
        kk=K[ds].astype(f32); vv=V[ds].astype(f32)
        ka=jnp.where(lane<64,kk,0.0); va=jnp.where(lane<64,vv,0.0)
        KA[ds]=key_lanes(ka,64,ok).astype(bf16); KB[ds]=key_lanes(kk-ka,0,ok).astype(bf16)
        VA[ds]=value_lanes(va,64).astype(bf16); VB[ds]=value_lanes(vv-va,0).astype(bf16)
        return 0
    def softmax(slot):
        def sub(i,carry):
            ds=pl.ds(pl.multiple_of(i*SUB,16),SUB)
            m=jnp.max(S[slot,ds,:],-1,keepdims=True)
            Pb[slot,ds,:]=jnp.exp(S[slot,ds,:]-m).astype(bf16)
            return m
        return jnp.concatenate([sub(i,0) for i in range(TOK//SUB)],0)
    for zz in [((z+d)%4) for d in (1,3,2)]:
        kr=KCp.at[c*4+zz]; vr=VCp.at[c*4+zz]
        wrecv(kr,rkc.at[zz],Pn); X.go(kr,kr,pkc.at[zz],Pn)
        wrecv(vr,rvc.at[zz],Pn); X.go(vr,vr,pvc.at[zz],Pn)
        wrecv(QCp.at[zz],rqc.at[zz],Pn)
    for cp in loc[:3]: cp.wait()
    for zz in range(4):
        wrecv(KCp.at[(1-c)*4+zz],pkc.at[zz],Pn); wrecv(VCp.at[(1-c)*4+zz],pvc.at[zz],Pn)
    def unp(i,_):
        r=pl.multiple_of(i*TOK,16)
        unpack_c(KCp[i],KC,r); unpack_c(VCp[i],VC,r)
        ds=pl.ds(r,TOK)
        KC[ds]=key_lanes(KC[ds].astype(f32),64,key_ok(i)).astype(bf16)
        VC[ds]=value_lanes(VC[ds].astype(f32),64).astype(bf16)
        return 0
    lax.fori_loop(0,8,unp,0)
    def unq(i,_):
        unpack_c(QCp[i],QC,pl.multiple_of(i*TOK,16)); return 0
    lax.fori_loop(0,4,unq,0)
    def cblock(i,_):
        ds=pl.ds(pl.multiple_of(i*TOK,16),TOK)
        S[0]=dot(one_lane(QC[ds].astype(f32),64).astype(bf16),KC[...],NT)
        ma=softmax(0)
        o=dot(Pb[0],VC[...],NN)
        la=o[:,64:65]
        o=o/la
        OC[ds]=o
        LC[ds]=jnp.broadcast_to(ma+jnp.log(la),(TOK,128))
        OCp[i]=pack_c(o[:CB],o[CB:])
        return 0
    lax.fori_loop(0,4,cblock,0)
    for zz in others(z):
        X.go(OCp.at[zz],og.at[z,pl.ds(TOK,CB)],roc.at[z],dev(zz))
    lc=pltpu.make_async_copy(OCp.at[z],og.at[z,pl.ds(TOK,CB)],lsem.at[7]); lc.start()
    for zz in [((z+d)%4) for d in (1,3,2)]:
        kr=K.at[pl.ds(krow(zz),TOK)]; vr=V.at[pl.ds(krow(zz),TOK)]
        wrecv(kr,rk.at[zz],Pn); X.go(kr,kr,pk.at[zz],Pn)
        wrecv(vr,rv.at[zz],Pn); X.go(vr,vr,pv.at[zz],Pn)
    for zz in range(4):
        r=K.at[pl.ds(pkrow(zz),TOK)]; wrecv(r,pk.at[zz],Pn)
        r=V.at[pl.ds(pkrow(zz),TOK)]; wrecv(r,pv.at[zz],Pn)
    for zz in [((z+d)%4) for d in (1,2,3)]:
        wrecv(Q.at[pl.ds(row(zz),TOK)],rq.at[zz],Pn)
    for cp in loc[3:6]: cp.wait()
    lax.fori_loop(0,8,widen,0)
    def turn(i): return (z+jnp.where(i==0,2,jnp.where(i==1,1,jnp.where(i==2,3,0))))%4
    def ocopy(i):
        zz=turn(i)
        return pltpu.make_async_remote_copy(src_ref=OB.at[pl.ds(row(zz),TOK)],dst_ref=og.at[z,pl.ds(0,TOK)],send_sem=osem.at[i],recv_sem=ro.at[z],device_id=dev(zz),device_id_type=MESH)
    def pairblock(i,_):
        ds=pl.ds(row(turn(i)),TOK)
        q=Q[ds].astype(f32)
        qa=jnp.where(lane<64,q,0.0)
        S[0]=dot(one_lane(qa,64).astype(bf16),KA[...],NT)
        S[1]=dot(one_lane(q-qa,0).astype(bf16),KB[...],NT)
        ma=softmax(0); mb=softmax(1)
        oa=dot(Pb[0],VA[...],NN); ob=dot(Pb[1],VB[...],NN)
        la=oa[:,64:65]; lb=ob[:,0:1]
        o=jnp.where(lane<64,oa/la,ob/lb)
        OA[ds]=o; OB[ds]=o.astype(bf16)
        LA[ds]=jnp.where(lane<64,ma+jnp.log(la),mb+jnp.log(lb))
        @pl.when(i<3)
        def _(): ocopy(i).start()
        return 0
    lax.fori_loop(0,4,pairblock,0)
    lo=pltpu.make_async_copy(OB.at[pl.ds(row(z),TOK)],og.at[z,pl.ds(0,TOK)],lsem.at[6]); lo.start()
    for d in (1,2,3):
        zz=(z+d)%4
        wrecv(og.at[zz,pl.ds(0,TOK)],ro.at[zz],Pn)
        wrecv(og.at[zz,pl.ds(TOK,CB)],roc.at[zz],Pn)
    lo.wait(); lc.wait()
    for i in range(3): ocopy(i).wait_send()
    X.drain()

D=pltpu.SemaphoreType.DMA
def vb(*s): return pltpu.VMEM(s,bf16)
def vf(*s): return pltpu.VMEM(s,f32)
VM=pl.BlockSpec(memory_space=pltpu.VMEM)
SM=pl.BlockSpec(memory_space=pltpu.SMEM)
def sds(*s,d=bf16): return jax.ShapeDtypeStruct(s,d)

def attn_fwd(sp,lims,cid):
    return pl.pallas_call(fwd_kernel,
        out_shape=(sds(4,TOK+CB,128),sds(NQ,128),sds(NK,128),sds(NK,128),sds(NK,128),sds(NK,128),sds(NQ,128),sds(NK,128),sds(NK,128),
                   sds(NQ,128,d=f32),sds(NQ,128,d=f32),sds(NQ,128,d=f32),sds(NQ,128,d=f32)),
        in_specs=[SM,VM],out_specs=[VM]*13,
        scratch_shapes=[vb(NK,128),vb(NK,128),vb(4,CB,128),vb(8,CB,128),vb(8,CB,128),vb(NQ,128),vb(4,CB,128),vf(2,TOK,NK),vb(2,TOK,NK),
            D((48,)),D((8,)),D((3,))]+[D((4,))]*12,
        compiler_params=pltpu.CompilerParams(collective_id=cid,has_side_effects=True,vmem_limit_bytes=60*1024*1024))(lims,sp)

def bwd_kernel(dog, Q, KA, KB, VA, VB, QC, KC, VC, OA, OC, LA, LC, dsp,
               DO, DOCp, DOC, S, P, DS, DKT, DVT, TT, DQ, DQC, XK, XV, YK, YV, SK, SV, HK, HV, XKC, XVC, YKC, YVC, HKC, HVC,
               ssem, lsem, qsem, rd, rdc, px, ho):
    b,z,c=mesh_pos()
    Pn=(b,z*2+1-c)
    dev=lambda zz:(b,zz*2+c)
    row=lambda zz: pl.multiple_of(zz*TOK,16)
    zbarrier(b,z,c)
    X=Sends(ssem)
    loc=[]
    def lcopy(src,dst):
        cp=pltpu.make_async_copy(src,dst,lsem.at[len(loc)]); cp.start(); loc.append(cp); return cp
    for zz in others(z):
        X.go(dog.at[zz,pl.ds(0,TOK)],DO.at[pl.ds(row(z),TOK)],rd.at[z],dev(zz))
    for zz in others(z):
        X.go(dog.at[zz,pl.ds(TOK,CB)],DOCp.at[z],rdc.at[z],dev(zz))
    l1=lcopy(dog.at[z,pl.ds(0,TOK)],DO.at[pl.ds(row(z),TOK)])
    l2=lcopy(dog.at[z,pl.ds(TOK,CB)],DOCp.at[z])
    l1.wait(); l2.wait()
    lane=lax.broadcasted_iota(jnp.int32,(TOK,128),1)
    def zero(ref):
        def bodyz(i,_):
            ref[:,pl.ds(pl.multiple_of(i*640,128),640)]=jnp.zeros((128,640),f32); return 0
        lax.fori_loop(0,NK//640,bodyz,0)
    def grads(q,k,v,do,lse,delta,free):
        qx=three_lanes(one_lane(q,free),free+1,-lse).astype(bf16)
        dx=three_lanes(do,free,-delta).astype(bf16)
        tail=jnp.zeros((PADQ-TOK,128),bf16)
        q=jnp.concatenate([q.astype(bf16),tail],0); do=jnp.concatenate([do.astype(bf16),tail],0)
        def scores(j):
            ks=pl.ds(j*CH,CH)
            S[j%2,0]=dot(qx,k[ks],NT)
            S[j%2,1]=dot(dx,v[ks],NT)
        scores(0)
        dq=jnp.zeros((TOK,128),f32)
        for j in range(NK//CH):
            if (j+1)*CH<NK: scores(j+1)
            t=j%2; ks=pl.ds(j*CH,CH)
            for i in range(TOK//16):
                ds=pl.ds(i*16,16)
                p=jnp.exp(S[t,0,ds,:])
                P[t,ds,:]=p.astype(bf16)
                DS[t,ds,:]=(p*S[t,1,ds,:]).astype(bf16)
            DKT[:,ks]+=dot(q,DS[t],TN)
            DVT[:,ks]+=dot(do,P[t],TN)
            dq=dq+dot(DS[t,pl.ds(0,TOK)],k[ks],NN)
        return dq
    def home(src,r0,n,si):
        for zz in others(z):
            X.go(src(zz),dsp.at[z,pl.ds(r0,n)],ho.at[si,z],dev(zz))
        lcopy(src(z),dsp.at[z,pl.ds(r0,n)])
    mine=c*NQ; theirs=(1-c)*NQ
    def split(acc, x, own):
        def tr(i,_):
            TT[pl.ds(pl.multiple_of(i*640,16),640)]=acc[:,pl.ds(pl.multiple_of(i*640,128),640)].T
            return 0
        lax.fori_loop(0,NK//640,tr,0)
        def cut(i,_):
            r=pl.multiple_of(i*TOK,16)
            x[pl.ds(r,TOK)]=TT[pl.ds(pl.multiple_of(theirs+i*TOK,16),TOK)].astype(bf16)
            own[pl.ds(r,TOK)]=TT[pl.ds(pl.multiple_of(mine+i*TOK,16),TOK)]
            return 0
        lax.fori_loop(0,4,cut,0)
    for t in range(2):
        P[t,pl.ds(TOK,PADQ-TOK)]=jnp.zeros((PADQ-TOK,CH),bf16)
        DS[t,pl.ds(TOK,PADQ-TOK)]=jnp.zeros((PADQ-TOK,CH),bf16)
    zero(DKT); zero(DVT)
    def pairblock(i,_):
        zz=(z+i)%4
        @pl.when(i>0)
        def _(): wrecv(DO.at[pl.ds(row(zz),TOK)],rd.at[zz],Pn)
        ds=pl.ds(row(zz),TOK)
        q=Q[ds].astype(f32); do=DO[ds].astype(f32)
        dof=do*OA[ds]
        da=jnp.sum(jnp.where(lane<64,dof,0.0),-1,keepdims=True)
        db=jnp.sum(jnp.where(lane<64,0.0,dof),-1,keepdims=True)
        qa=jnp.where(lane<64,q,0.0); doa=jnp.where(lane<64,do,0.0)
        ga=grads(qa,KA,VA,doa,LA[ds,0:1],da,64)
        gb=grads(q-qa,KB,VB,do-doa,LA[ds,64:65],db,0)
        DQ[ds]=(jnp.where(lane<64,ga,gb)*0.125).astype(bf16)
        @pl.when(i>0)
        def _(): qcopy(i).start()
        return 0
    def qcopy(i):
        zz=(z+i)%4
        return pltpu.make_async_remote_copy(src_ref=DQ.at[pl.ds(row(zz),TOK)],dst_ref=dsp.at[z,pl.ds(0,TOK)],send_sem=qsem.at[i],recv_sem=ho.at[0,z],device_id=dev(zz),device_id_type=MESH)
    lax.fori_loop(0,4,pairblock,0)
    lcopy(DQ.at[pl.ds(row(z),TOK)],dsp.at[z,pl.ds(0,TOK)])
    split(DKT,XK,SK); X.go(XK,YK,px.at[0],Pn)
    split(DVT,XV,SV); X.go(XV,YV,px.at[1],Pn)
    def addp(h,own,y):
        def body(i,_):
            ds=pl.ds(pl.multiple_of(i*TOK,16),TOK)
            h[ds]=(own[ds]+y[ds].astype(f32)).astype(bf16)
            return 0
        lax.fori_loop(0,4,body,0)
    wrecv(YK,px.at[0],Pn); addp(HK,SK,YK)
    home(lambda zz: HK.at[pl.ds(row(zz),TOK)],ROWS["k"],TOK,2)
    wrecv(YV,px.at[1],Pn); addp(HV,SV,YV)
    home(lambda zz: HV.at[pl.ds(row(zz),TOK)],ROWS["v"],TOK,3)
    zero(DKT); zero(DVT)
    def cblock(i,_):
        zz=(z+i)%4
        @pl.when(i>0)
        def _(): wrecv(DOCp.at[zz],rdc.at[zz],Pn)
        unpack_c(DOCp[zz],DOC,0)
        ds=pl.ds(row(zz),TOK)
        do=DOC[...].astype(f32)
        delta=jnp.sum(do*OC[ds],-1,keepdims=True)
        g=grads(QC[ds].astype(f32),KC,VC,do,LC[ds,0:1],delta,64)*0.125
        DQC[zz]=pack_c(g[:CB],g[CB:])
        return 0
    lax.fori_loop(0,4,cblock,0)
    home(lambda zz: DQC.at[zz],ROWS["qc"],CB,1)
    def splitc(acc, x, own):
        def tr(i,_):
            TT[pl.ds(pl.multiple_of(i*640,16),640)]=acc[:,pl.ds(pl.multiple_of(i*640,128),640)].T
            return 0
        lax.fori_loop(0,NK//640,tr,0)
        def cut(i,_):
            r=theirs+i*TOK
            x[i]=pack_c(TT[pl.ds(pl.multiple_of(r,16),CB)],TT[pl.ds(pl.multiple_of(r+CB,16),TOK-CB)])
            own[pl.ds(pl.multiple_of(i*TOK,16),TOK)]=TT[pl.ds(pl.multiple_of(mine+i*TOK,16),TOK)]
            return 0
        lax.fori_loop(0,4,cut,0)
    splitc(DKT,XKC,SK); X.go(XKC,YKC,px.at[2],Pn)
    splitc(DVT,XVC,SV); X.go(XVC,YVC,px.at[3],Pn)
    def addc(y,own,h):
        def body(i,_):
            unpack_c(y[i],DOC,0)
            r=i*TOK
            t=own[pl.ds(pl.multiple_of(r,16),TOK)]+DOC[...].astype(f32)
            h[i]=pack_c(t[:CB],t[CB:])
            return 0
        lax.fori_loop(0,4,body,0)
    wrecv(YKC,px.at[2],Pn); addc(YKC,SK,HKC)
    home(lambda zz: HKC.at[zz],ROWS["kc"],CB,4)
    wrecv(YVC,px.at[3],Pn); addc(YVC,SV,HVC)
    home(lambda zz: HVC.at[zz],ROWS["vc"],CB,5)
    for si,(r0,n) in enumerate(((0,TOK),(ROWS["qc"],CB),(ROWS["k"],TOK),(ROWS["v"],TOK),(ROWS["kc"],CB),(ROWS["vc"],CB))):
        for d in (1,2,3):
            zz=(z+d)%4
            wrecv(dsp.at[zz,pl.ds(r0,n)],ho.at[si,zz],Pn)
    for cp in loc[2:]: cp.wait()
    for i in range(1,4): qcopy(i).wait_send()
    X.drain()

def attn_bwd(dog,saved,cid):
    return pl.pallas_call(bwd_kernel,
        out_shape=sds(4,3*(TOK+CB),128),
        in_specs=[VM]*13,out_specs=VM,
        scratch_shapes=[vb(NQ,128),vb(4,CB,128),vb(TOK,128),vf(2,2,TOK,CH),vb(2,PADQ,CH),vb(2,PADQ,CH),vf(128,NK),vf(128,NK),vf(NK,128),
            vb(NQ,128),vb(4,CB,128)]+[vb(NQ,128)]*4+[vf(NQ,128)]*2+[vb(NQ,128)]*2+[vb(4,CB,128)]*6+[
            D((32,)),D((10,)),D((4,)),D((4,)),D((4,)),D((4,)),D((6,4))],
        compiler_params=pltpu.CompilerParams(collective_id=cid,has_side_effects=True,vmem_limit_bytes=60*1024*1024))(dog,*saved)


HI=lax.Precision.HIGHEST
DM=768
MTILES=(0,None,1,2,None,3)

def spread(pair, packed):
    lane=lax.broadcasted_iota(jnp.int32,(CB,128),1)
    def mid(g0,g1):
        a=packed(g0).astype(f32); b=packed(g1).astype(f32)
        top=jnp.where(lane<64,a,pltpu.roll(b,64,1))
        low=jnp.where(lane<64,pltpu.roll(a,64,1),b)
        return jnp.concatenate([top,low[:TOK-CB]],0).astype(bf16)
    return [pair(0),mid(0,1),pair(1),pair(2),mid(2,3),pair(3)]

def gather_groups(tiles):
    out=[]
    for g in range(4):
        p=tiles[(0,2,3,5)[g]]
        t=tiles[(1,1,4,4)[g]]
        if g%2: t=pltpu.roll(t,64,1)
        out.append((p.astype(bf16),pack_c(t[:CB],t[CB:])))
    return out

def wcols(W,j,n):
    S=W.shape[0]
    return jnp.concatenate([W[:,j+i].reshape(S*16,128) for i in range(n)],1)

def lnorm(x):
    c=x-jnp.mean(x,-1,keepdims=True)
    inv=lax.rsqrt(jnp.mean(c*c,-1,keepdims=True)+EPSILON)
    return c*inv,inv

def lnorm_back(dy,gain,n,inv):
    g=dy*gain
    return inv*(g-jnp.mean(g,-1,keepdims=True)-n*jnp.mean(g*n,-1,keepdims=True))

def vrow(V,i):
    return jnp.concatenate([V[6*i+j:6*i+j+1,:] for j in range(6)],1)

def colsum(x): return jnp.sum(x,0,keepdims=True)

def front_kernel(start, fidx, pix, G, x0o, h1o, sp, We, Wq, PO, POf, TI, VE, V, TIf, sems):
    cps=[pltpu.make_async_copy(G.at[pl.ds(0,576)],We,sems.at[0]),
         pltpu.make_async_copy(G.at[pl.ds(4224+(48+6*start[0])//16,151)],PO,sems.at[1]),
         pltpu.make_async_copy(G.at[pl.ds(4224+264,3)],TI,sems.at[2]),
         pltpu.make_async_copy(G.at[pl.ds(4512,7)],VE,sems.at[3]),
         pltpu.make_async_copy(G.at[pl.ds(576,864)],Wq,sems.at[4])]
    for cp in cps: cp.start()
    for cp in cps[:4]: cp.wait()
    for i in range(7): V[pl.ds(i*16,16),:]=VE[i].astype(f32)
    for i in range(3): TIf[pl.ds(i*16,16),:]=TI[i].astype(f32)
    def cv(i,_):
        POf[pl.ds(i*16,16),:]=PO[i].astype(f32); return 0
    lax.fori_loop(0,151,cv,0)
    rem=(6*start[0])%16
    W4=We.reshape(96,6,16,128)
    for j in range(3):
        e=dot(pix[...],wcols(W4,2*j,2),NN)
        p=jnp.concatenate([POf[pl.ds(rem+2*j+i,TOK,stride=6),:] for i in range(2)],1)
        tm=jnp.concatenate([TIf[pl.ds(6*fidx[0]+2*j+i,1),:] for i in range(2)],1)
        bb=jnp.concatenate([V[48+2*j+i:49+2*j+i,:] for i in range(2)],1)
        x0o[:,j*256:(j+1)*256]=e+bb+p+tm
    n,inv=lnorm(x0o[...])
    h1=(n*vrow(V,0)+vrow(V,1)).astype(bf16)
    h1o[...]=h1
    cps[4].wait()
    W4=Wq.reshape(48,18,16,128)
    for part in range(3):
        tiles=[]
        for j in range(3):
            r=dot(h1,wcols(W4,part*6+2*j,2),NN)
            if part!=1:
                o=54 if part==0 else 60
                r=r+jnp.concatenate([V[o+2*j+i:o+1+2*j+i,:] for i in range(2)],1)
            r=r.astype(bf16).astype(f32)
            if part==0: r=r*0.125
            tiles+=[r[:,:128],r[:,128:]]
        for g,(p,c) in enumerate(gather_groups(tiles)):
            sp[g,pl.ds(part*TOK,TOK)]=p
            sp[g,pl.ds(3*TOK+part*CB,CB)]=c

ANYS=pl.BlockSpec(memory_space=pl.ANY)
def front(start,fidx,pix,G):
    return pl.pallas_call(front_kernel,
        out_shape=(sds(TOK,DM,d=f32),sds(TOK,DM),sds(4,3*(TOK+CB),128)),
        in_specs=[SM,SM,VM,ANYS],out_specs=(VM,)*3,
        scratch_shapes=[vb(576,16,128),vb(864,16,128),vb(151,16,128),vf(2416,128),vb(3,16,128),vb(7,16,128),vf(112,128),vf(48,128),D((5,))],
        compiler_params=pltpu.CompilerParams(vmem_limit_bytes=60*1024*1024))(start,fidx,pix,G)

def mid_kernel(lims, og, x0, G, wmap, scal, counts, sel,
               atto, h2o, acto, dpreo, dmlpo, dattno, dsec, dog, vgo, ubo, gmapo, gprojo, losso,
               Wo, Wu, Wd, Wp, VE, V, A2, GP, SLOT, x1s, x2s, sems, ssem, rsem):
    b=lax.axis_index("batch"); f=lax.axis_index("frame"); k=b*8+f
    def dev_of(kk): return (kk//8,kk%8)
    bar=pltpu.get_barrier_semaphore()
    def greet(d,_):
        pl.semaphore_signal(bar,inc=1,device_id=dev_of((k+d)%32),device_id_type=MESH); return 0
    lax.fori_loop(1,32,greet,0)
    cps=[pltpu.make_async_copy(G.at[pl.ds(10*144,288)],Wo,sems.at[0]),
         pltpu.make_async_copy(G.at[pl.ds(4512,7)],VE,sems.at[1]),
         pltpu.make_async_copy(G.at[pl.ds(12*144,1152)],Wu,sems.at[2]),
         pltpu.make_async_copy(G.at[pl.ds(20*144,1152)],Wd,sems.at[3]),
         pltpu.make_async_copy(G.at[pl.ds(28*144,192)],Wp,sems.at[4])]
    for cp in cps: cp.start()
    for j,t in enumerate(spread(lambda g: og[g,pl.ds(0,TOK)],lambda g: og[g,pl.ds(TOK,CB)])):
        atto[:,j*128:(j+1)*128]=t
    cps[0].wait(); cps[1].wait()
    for i in range(7): V[pl.ds(i*16,16),:]=VE[i].astype(f32)
    Wo4=Wo.reshape(48,6,16,128); Wu4=Wu.reshape(48,24,16,128); Wd4=Wd.reshape(192,6,16,128); Wp4=Wp.reshape(48,4,16,128)
    att=atto[...]
    for j in range(3):
        bb=jnp.concatenate([V[66+2*j+i:67+2*j+i,:] for i in range(2)],1)
        x1s[:,j*256:(j+1)*256]=x0[:,j*256:(j+1)*256]+(dot(att,wcols(Wo4,2*j,2),NN)+bb)
    n2,inv2=lnorm(x1s[...])
    h2=(n2*vrow(V,2)+vrow(V,3)).astype(bf16)
    h2o[...]=h2
    x2s[...]=x1s[...]+vrow(V,12)
    cps[2].wait(); cps[3].wait()
    def hid(j,_):
        w=jnp.concatenate([Wu4[:,2*j+i].reshape(768,128) for i in range(2)],1)
        bb=jnp.concatenate([V[pl.ds(78+2*j+i,1),:] for i in range(2)],1)
        u=dot(h2o[...],w,NN)+bb
        phi=0.5*(1.0+lax.erf(u*(0.5**0.5)))
        a=(u*phi).astype(bf16)
        cs=pl.ds(pl.multiple_of(j*256,256),256)
        GP[:,cs]=phi+u*(jnp.exp(-0.5*u*u)*0.3989422804014327)
        acto[:,cs]=a
        wd=Wd4[pl.ds(j*16,16)]
        x2s[...]+=dot(a,jnp.concatenate([wd[:,t].reshape(256,128) for t in range(6)],1),NN)
        return 0
    lax.fori_loop(0,12,hid,0)
    x2=x2s[...]
    nm,invm=lnorm(x2)
    nmap=nm*vrow(V,4)+vrow(V,5)
    lg=lax.dot_general(nmap,wmap[...],NN,precision=HI,preferred_element_type=f32)
    ok=lax.broadcasted_iota(jnp.int32,(TOK,128),0)<lims[0]
    lg=jnp.where(ok,lg,-1e30)
    ex=jnp.where(ok,jnp.exp(lg-jnp.max(lg,0,keepdims=True)),0.0)
    lane8=lax.broadcasted_iota(jnp.int32,(TOK,128),1)<NMAP
    maps=jnp.where(lane8,ex/jnp.sum(ex,0,keepdims=True),0.0)
    r=jnp.sum(maps,-1,keepdims=True)
    sw=scal[0:1,0:1]; inv_total=scal[1:2,0:1]
    pooled=sw*colsum(r*x2)
    corr=sw*colsum(r*r-jnp.sum(maps*maps,-1,keepdims=True))
    slot=[pooled[:,j*128:(j+1)*128] for j in range(6)]+[jnp.broadcast_to(corr,(1,128)),jnp.zeros((1,128),f32)]
    SLOT[k,pl.ds(0,8)]=jnp.concatenate(slot,0)
    SLOT[k,pl.ds(8,8)]=sel[...]
    def xcopy(d):
        return pltpu.make_async_remote_copy(src_ref=SLOT.at[k],dst_ref=SLOT.at[k],send_sem=ssem.at[d],recv_sem=rsem.at[k],device_id=dev_of((k+d)%32),device_id_type=MESH)
    pl.semaphore_wait(bar,31)
    def xs(d,_):
        xcopy(d).start(); return 0
    lax.fori_loop(1,32,xs,0)
    cps[4].wait()
    def xw(d,_):
        kk=(k+d)%32
        wrecv(SLOT.at[kk],rsem.at[kk],(b,f)); return 0
    lax.fori_loop(1,32,xw,0)
    tot=[]
    for cl in range(4):
        t=SLOT[cl*8,pl.ds(0,8)]
        for ff in range(1,8): t=t+SLOT[cl*8+ff,pl.ds(0,8)]
        tot.append(t)
    corr_total=(tot[0]+tot[1]+tot[2]+tot[3])[6:7,0:1]
    pm=jnp.concatenate([jnp.concatenate([t[j:j+1,:] for j in range(6)],1) for t in tot]+[jnp.zeros((4,DM),f32)],0)/counts[:,0:1]
    nf,invf=lnorm(pm)
    hf=nf*vrow(V,6)+vrow(V,7)
    rows=lax.broadcasted_iota(jnp.int32,(8,1),0)
    live=rows<4
    wp=jnp.concatenate([Wp4[:,t].reshape(768,128) for t in range(4)],1).astype(f32)
    e=lax.dot_general(hf,wp,NN,precision=HI,preferred_element_type=f32)
    rn=lax.rsqrt(jnp.sum(e*e,-1,keepdims=True)+1e-06)
    unit=e*rn
    lanes=lax.broadcasted_iota(jnp.int32,(8,128),1)
    gm=jnp.zeros((8,128),f32)
    for j in range(4):
        gm=gm+jnp.where(lanes==j,jnp.sum(unit*unit[j:j+1,:],-1,keepdims=True),0.0)
    selk=[jnp.concatenate([SLOT[cl*8,pl.ds(8+kk,1)] for cl in range(4)]+[jnp.zeros((4,128),f32)],0) for kk in range(5)]
    S=[jnp.sum(s*gm,-1,keepdims=True)/SOFTMAX_TEMPER for s in selk]
    mx=S[0]
    for s in S[1:]: mx=jnp.maximum(mx,s)
    es=[jnp.exp(s-mx) for s in S]
    se=es[0]+es[1]+es[2]+es[3]+es[4]
    contrast=jnp.sum(jnp.where(live,mx+jnp.log(se)-S[0],0.0),0,keepdims=True)*0.25
    losso[...]=jnp.broadcast_to(contrast+DECAY_PENALTY*corr_total*inv_total,(8,128))
    dgm=jnp.zeros((8,128),f32)
    for kk in range(5):
        w=es[kk]/se-(1.0 if kk==0 else 0.0)
        dgm=dgm+jnp.where(live,w,0.0)*selk[kk]
    dgm=dgm*(0.25/SOFTMAX_TEMPER)
    du=jnp.zeros((8,EMB),f32)
    for j in range(4):
        cj=dgm[:,j:j+1]
        du=du+cj*unit[j:j+1,:]
        du=du+jnp.where(rows==j,colsum(cj*unit),0.0)
    de=rn*du-e*(rn*rn*rn)*jnp.sum(e*du,-1,keepdims=True)
    de=jnp.where(live,de,0.0)
    dhf=lax.dot_general(de,wp,NT,precision=HI,preferred_element_type=f32)
    head=jnp.where(k==0,1.0,0.0)
    gp=lax.dot_general(hf,de,TN,precision=HI,preferred_element_type=f32)*head
    gpb=gp.astype(bf16)
    for s in range(48):
        for t in range(4): gprojo[s*4+t]=gpb[s*16:(s+1)*16,t*128:(t+1)*128]
    vgo[6:7,:]=colsum(dhf*nf)*head
    vgo[7:8,:]=colsum(dhf)*head
    dpm=lnorm_back(dhf,vrow(V,6),nf,invf)/counts[:,0:1]
    dpool=colsum(jnp.where(rows==b,dpm,0.0))
    cdec=DECAY_PENALTY*inv_total*sw
    dm=sw*jnp.sum(x2*dpool,-1,keepdims=True)+2.0*cdec*(r-maps)
    dm=jnp.where(lane8,dm,0.0)
    dl=maps*(dm-colsum(maps*dm))
    gmapo[...]=lax.dot_general(nmap,dl,TN,precision=HI,preferred_element_type=f32)
    dnm=lax.dot_general(dl,wmap[...],NT,precision=HI,preferred_element_type=f32)
    vgo[4:5,:]=colsum(dnm*nm)
    vgo[5:6,:]=colsum(dnm)
    dx2=(sw*r)*dpool+lnorm_back(dnm,vrow(V,4),nm,invm)
    dmlp=dx2.astype(bf16)
    dmlpo[...]=dmlp
    vgo[12:13,:]=colsum(dmlp.astype(f32))
    x2s[...]=jnp.zeros((TOK,DM),f32)
    dsec[...]=dx2
    def hidb(j,_):
        cs=pl.ds(pl.multiple_of(j*256,256),256)
        wd=Wd4[pl.ds(j*16,16)]
        da=dot(dmlpo[...],jnp.concatenate([wd[:,t].reshape(256,128) for t in range(6)],1),NT)
        dp=(da*GP[:,cs]).astype(bf16)
        dpreo[:,cs]=dp
        ubo[:,cs]=colsum(dp.astype(f32))
        w=jnp.concatenate([Wu4[:,2*j+i].reshape(768,128) for i in range(2)],1)
        x2s[...]+=dot(dp,w,NT)
        return 0
    lax.fori_loop(0,12,hidb,0)
    dh2=x2s[...]
    n2,inv2=lnorm(x1s[...])
    vgo[2:3,:]=colsum(dh2*n2)
    vgo[3:4,:]=colsum(dh2)
    dx1=dsec[...]+lnorm_back(dh2,vrow(V,2),n2,inv2)
    dsec[...]=dx1
    da_=dx1.astype(bf16)
    dattno[...]=da_
    vgo[11:12,:]=colsum(da_.astype(f32))
    tiles=[]
    for j in range(6):
        w=jnp.concatenate([Wo4[8*j:8*j+8,t].reshape(128,128) for t in range(6)],1)
        tiles.append(dot(da_,w,NT).astype(bf16).astype(f32))
    for g,(p,c) in enumerate(gather_groups(tiles)):
        dog[g,pl.ds(0,TOK)]=p
        dog[g,pl.ds(TOK,CB)]=c
    def xd(d,_):
        xcopy(d).wait_send(); return 0
    lax.fori_loop(1,32,xd,0)

def middle(lims,og,x0,G,wmap,scal,counts,sel,cid):
    return pl.pallas_call(mid_kernel,
        out_shape=(sds(TOK,DM),sds(TOK,DM),sds(TOK,FFW),sds(TOK,FFW),sds(TOK,DM),sds(TOK,DM),sds(TOK,DM,d=f32),sds(4,TOK+CB,128),
                   sds(16,DM,d=f32),sds(1,FFW,d=f32),sds(DM,128,d=f32),sds(192,16,128),sds(8,128,d=f32)),
        in_specs=[SM,VM,VM,ANYS]+[VM]*4,out_specs=(VM,)*13,
        scratch_shapes=[vb(288,16,128),vb(1152,16,128),vb(1152,16,128),vb(192,16,128),vb(7,16,128),vf(112,128),vf(8,128),vf(TOK,FFW),vf(32,16,128),
            vf(TOK,DM),vf(TOK,DM),D((5,)),D((32,)),D((32,))],
        compiler_params=pltpu.CompilerParams(collective_id=cid,has_side_effects=True,vmem_limit_bytes=63*1024*1024))(lims,og,x0,G,wmap,scal,counts,sel)

def back_kernel(start, fidx, dsp, G, x0, dsec, vg, ub, gmap, gproj, dqkv, dx0o, tailo, Wq, VE, V, TL, sems):
    cps=[pltpu.make_async_copy(G.at[pl.ds(576,864)],Wq,sems.at[0]),pltpu.make_async_copy(G.at[pl.ds(4512,7)],VE,sems.at[1])]
    for cp in cps: cp.start()
    for part in range(3):
        for j,t in enumerate(spread(lambda g: dsp[g,pl.ds(part*TOK,TOK)],lambda g: dsp[g,pl.ds(3*TOK+part*CB,CB)])):
            dqkv[:,(part*6+j)*128:(part*6+j+1)*128]=t
    def z(i,_):
        TL[pl.ds(i*64,64),:]=jnp.zeros((64,128),f32); return 0
    lax.fori_loop(0,96,z,0)
    for cp in cps: cp.wait()
    for i in range(7): V[pl.ds(i*16,16),:]=VE[i].astype(f32)
    W4=Wq.reshape(48,18,16,128)
    acc=jnp.zeros((TOK,DM),f32)
    for j in range(9):
        acc=acc+dot(dqkv[:,j*256:(j+1)*256],wcols(W4,2*j,2),NT)
    n,inv=lnorm(x0[...])
    ent=dsec[...]+lnorm_back(acc,vrow(V,0),n,inv)
    dx0o[...]=ent.astype(bf16)
    eb=colsum(ent)
    def rowput(i,v):
        for j in range(6): TL[pl.ds(i+j,1),:]=v[:,j*128:(j+1)*128]
    TL[0:48,:]=gmap[...]
    for j in range(6):
        TL[pl.ds(48+6*start[0]+j,TOK,stride=6),:]=ent[:,j*128:(j+1)*128]
    rowput(4224+6*fidx[0],eb)
    vec={0:colsum(acc*n),1:colsum(acc),8:eb,9:colsum(dqkv[:,0:DM].astype(f32)),10:colsum(dqkv[:,2*DM:].astype(f32))}
    for i in range(13):
        rowput(4608+6*i, vec[i] if i in vec else vg[i:i+1,:])
    for j in range(24): TL[4608+78+j:4608+79+j,:]=ub[:,j*128:(j+1)*128]
    def cg(i,_):
        tailo[pl.ds(i*8,8)]=gproj[pl.ds(i*8,8)]; return 0
    lax.fori_loop(0,24,cg,0)
    def ct(i,_):
        tailo[192+i]=TL[pl.ds(pl.multiple_of(i*16,16),16),:].astype(bf16); return 0
    lax.fori_loop(0,384,ct,0)

def back(start,fidx,dsp,G,x0,dsec,vg,ub,gmap,gproj):
    return pl.pallas_call(back_kernel,
        out_shape=(sds(TOK,3*DM),sds(TOK,DM),sds(576,16,128)),
        in_specs=[SM,SM,VM,ANYS]+[VM]*6,out_specs=(VM,)*3,
        scratch_shapes=[vb(864,16,128),vb(7,16,128),vf(112,128),vf(6144,128),D((2,))],
        compiler_params=pltpu.CompilerParams(vmem_limit_bytes=60*1024*1024))(start,fidx,dsp,G,x0,dsec,vg,ub,gmap,gproj)


SHARD = 289176
BLOCK = 294912
SLIDE = BLOCK - SHARD
CARRY = 32 * SLIDE
KEY_ORDER_C = 2


def to_tiles(matrix):
    rows, width = matrix.shape
    m = width // 128
    return matrix.reshape(rows // 16, 16, m, 128).transpose(0, 2, 1, 3).reshape(-1, 16, 128)


def block_to_tiles(flat, k):
    def of(width):
        return lambda v: to_tiles(v.reshape(-1, width))

    def split29(v):
        return jnp.concatenate([to_tiles(v[: 48 * 2048].reshape(-1, 512)), v[48 * 2048 :].reshape(-1, 16, 128)])

    branch = class_of(k)
    return lax.switch(branch, [of(768), of(2304), of(3072), of(512), split29, of(128)], flat)


def class_of(k):
    return jnp.where(
        k < 4, 0, jnp.where(k < 10, 1, jnp.where(k < 12, 0, jnp.where(k < 20, 2, jnp.where(k < 28, 0, jnp.where(k == 28, 3, jnp.where(k == 29, 4, 5))))))
    )


def local_4x8(
    pixels,
    res_class,
    valid_tubelet_count,
    positive,
    negatives,
    master,
    first_moment,
    second_moment,
    adam_step,
):
    D = HEAD_COUNT * HEAD_FEATURES
    both_axes = ("batch", "frame")
    bi = lax.axis_index("batch")
    fi = lax.axis_index("frame")
    k = bi * 8 + fi
    low = to_bfloat(master)
    nxt = lax.ppermute(low[:CARRY], both_axes, [(i + 1, i) for i in range(31)])
    block = lax.dynamic_slice(jnp.concatenate([low, nxt]), (SLIDE * k,), (BLOCK,))
    G = make_ag()(block_to_tiles(block, k), 0)
    flat_tiles = G.reshape(32 * 144, 16, 128)
    w_map = G[29, 48:51].reshape(D, NMAP).astype(jnp.float32)
    w_map = jnp.pad(w_map, ((0, 0), (0, 128 - NMAP)))
    tubelets = lax.dynamic_slice_in_dim(valid_tubelet_count, bi, 1, 0)
    patches = jnp.where(res_class == 0, P0, jnp.where(res_class == 1, P1, PATCHES_THIRD_2)).astype(jnp.int32)
    start_rows = jnp.where(res_class == 0, 0, jnp.where(res_class == 1, P0, P0 + P1)).astype(jnp.int32)
    frame = jnp.full((1,), fi, jnp.int32)
    pix = pixels.reshape(400, TUBELET_PIXELS)
    first_in, h1, sp = front(start_rows, frame, pix, flat_tiles)
    lims = jnp.concatenate([patches, tubelets])
    og, *saved_attn = attn_fwd(sp, lims, 2)
    total_count = jnp.sum(valid_tubelet_count).astype(jnp.float32)
    slot_weight = (fi < tubelets[0]).astype(jnp.float32)
    scal = jnp.broadcast_to(
        jnp.concatenate([slot_weight[None], 1.0 / total_count[None], jnp.zeros((6,), jnp.float32)])[:, None], (8, 128)
    )
    counts = jnp.broadcast_to(
        jnp.concatenate([(NMAP * valid_tubelet_count).astype(jnp.float32), jnp.ones((4,), jnp.float32)])[:, None], (8, 128)
    )
    ids = jnp.concatenate([positive, negatives[0], jnp.full((3,), -1, jnp.int32)])
    chosen = (ids[:, None] == jnp.arange(128, dtype=jnp.int32)[None]).astype(jnp.float32)
    (attended, h2, hidden_low, g_pre, g_mlp, g_attn, g_second, dog, g_vec, g_up_bias, g_map, g_proj, loss_rows) = middle(
        lims, og, first_in, flat_tiles, w_map, scal, counts, chosen, 4
    )
    loss_value = loss_rows[0, 0]
    dsp = attn_bwd(dog, saved_attn, 3)
    g_qkv, g_entry, tail_tiles = back(
        start_rows, frame, dsp, flat_tiles, first_in, g_second, g_vec, g_up_bias, g_map[:, :NMAP].reshape(48, 128), g_proj
    )
    grad, squares = make_rsx()(
        pix, h1, attended, h2, hidden_low, g_entry, g_qkv, g_attn, g_pre, g_mlp, tail_tiles.reshape(4, 144, 16, 128), cid=1
    )
    grad = grad.reshape(-1)[:SHARD]
    grad_norm = jnp.sqrt(squares[0, 0])
    clipped = grad * jnp.minimum(1.0, CLIP_AT / grad_norm)
    new_first = BETA_ONE * first_moment + (1.0 - BETA_ONE) * clipped
    new_second = BETA_TWO * second_moment + (1.0 - BETA_TWO) * clipped * clipped
    step = adam_step[0].astype(jnp.float32)
    update = new_first / (1.0 - BETA_ONE**step) / (jnp.sqrt(new_second / (1.0 - BETA_TWO**step)) + ADAM_EPS)
    new_master = master - RATE * (update + DECAY * master)
    return (new_master, new_first, new_second, to_bfloat(new_master), loss_value, grad_norm)


def solution(mesh):
    fast = dict(mesh.shape) == {"batch": 4, "frame": 8}
    return jax.shard_map(
        local_4x8 if fast else local_any_mesh,
        mesh=mesh,
        in_specs=(
            P("batch", "frame", None, None),
            P("batch"),
            P(),
            P("batch"),
            P("batch", None),
            P(("batch", "frame")),
            P(("batch", "frame")),
            P(("batch", "frame")),
            P(),
        ),
        out_specs=(
            P(("batch", "frame")),
            P(("batch", "frame")),
            P(("batch", "frame")),
            P(("batch", "frame")),
            P(),
            P(),
        ),
        check_vma=False,
    )
```
